32 devices in a mesh: vid: 2 (over core), txt: 4 (over y, x), head: 4 (over z).
Axes of the slice: x: 2, y: 2, z: 4, core: 2. Of those that a mesh axis runs over, the one named last changes fastest.
Arguments:
- latents: bfloat16 [32, 128, 768], P('txt', 'vid'), may hold values from -6 to 6
- video_tokens: bfloat16 [32, 1024, 768], P('txt', 'vid'), may hold values from -6 to 6
- caption_tokens: bfloat16 [32, 64, 768], P('vid', 'txt'), may hold values from -6 to 6
- caption_len: int32 [32], P('vid'), may hold values from 5 to 60
- key_mask: int32 [32, 64], P('vid', 'txt'), may hold values 0 or 1
- drop_flags: int32 [32], P('txt'), may hold values 0 or 1
- gain_latent: float32 [768], replicated, may hold values from 0.5 to 1.5
- gain_tokens: float32 [768], replicated, may hold values from 0.5 to 1.5
- gain_mlp: float32 [768], replicated, may hold values from 0.5 to 1.5
- query_weight: bfloat16 [768, 768], P(None, 'head'), may hold values from -0.21875 to 0.21875
- key_matrix: bfloat16 [768, 768], P(None, 'head'), may hold values from -0.21875 to 0.21875
- value_matrix: bfloat16 [768, 768], P(None, 'head'), may hold values from -0.21875 to 0.21875
- out_weight: bfloat16 [768, 768], P('head'), may hold values from -6 to 6
- up_weight: bfloat16 [768, 3072], P(None, 'head'), may hold values from -0.21875 to 0.21875
- down_weight: bfloat16 [3072, 768], P('head'), may hold values from -0.109375 to 0.109375
- cotangent: bfloat16 [32, 128, 768], P('txt', 'vid'), may hold values from -6 to 6
Outputs:
- latents_out: bfloat16 [32, 128, 768], P('txt', 'vid')
- latent_grad: float32 [32, 128, 768], P('txt', 'vid')
- video_grad: float32 [32, 1024, 768], P('txt', 'vid')
- caption_grad: float32 [32, 64, 768], P('vid', 'txt')
- grad_query: float32 [768, 768], P(None, 'head')
- grad_key: float32 [768, 768], P(None, 'head')
- grad_value: float32 [768, 768], P(None, 'head')
- grad_out: float32 [768, 768], P('head')
- grad_up: float32 [768, 3072], P(None, 'head')
- grad_down: float32 [3072, 768], P('head')
- grad_gain_latent: float32 [768], replicated
- grad_gain_tokens: float32 [768], replicated
- grad_gain_mlp: float32 [768], replicated
- kept_count: int32 [], replicated
The draws below stay inside these ranges and needn't reach their ends.
All inputs are finite; a program needn't handle non-finite values. No bound on the sum of `key_mask` or of `drop_flags` on one device may be relied on, other than what follows from the above.
Results may differ from the reference program's by a relative error of at most 0.012.
Values may be sent and summed in bfloat16 or wider, within the bound.
No kernel may reach another device: no remote copies, remote signals or barrier semaphores. Data moves between devices by JAX's collectives and lax.ppermute only.
A program may use at most 128 MiB of HBM per device.

```python
import jax
import jax.numpy as jnp
from jax import lax

D = 768
HEADS = 12
FF = 3072
LAT = 128
CAP = 64
VIDEO = 1024
ITEMS = 32


def plant(entries, rng, least, largest):
    place = [jax.random.randint(jax.random.fold_in(rng, axis), (), 0, length) for axis, length in enumerate(entries.shape)]
    longest = entries.shape.index(max(entries.shape))
    next_to = place[:longest] + [(place[longest] + 1) % entries.shape[longest]] + place[longest + 1:]
    return entries.at[tuple(place)].set(least).at[tuple(next_to)].set(largest)


def block_levels(stream_key, dims, split, low, top_value):
    factor_of = 1.0
    for axis_at, blocks in split:
        draws = jax.random.uniform(jax.random.fold_in(jax.random.fold_in(stream_key, 6), axis_at), (blocks,), jnp.float32, low / len(split), top_value / len(split))
        factor_of = factor_of * jnp.repeat(jnp.exp(draws), dims[axis_at] // blocks).reshape((-1,) + (1,) * (len(dims) - 1 - axis_at))
    return factor_of


def centred(key, shape, width, reach, split=(), kind=jnp.bfloat16):
    drawn = jax.random.normal(key, shape, jnp.float32) * width
    if len(split) > 0:
        drawn = block_levels(key, shape, split, -0.22, 0.18) * drawn
    return jnp.clip(drawn, min=-reach, max=reach).astype(kind)


def setup_inputs(seed: int = 0) -> dict:
    streams_of = jax.random.split(jax.random.key(seed), 17)
    latents = centred(streams_of[0], (ITEMS, LAT, D), 1.0, 6.0, ((0, 4), (1, 2)))
    video_tokens = centred(streams_of[1], (ITEMS, VIDEO, D), 1.0, 6.0, ((0, 4), (1, 2)))
    caption_tokens = centred(streams_of[2], (ITEMS, CAP, D), 1.0, 6.0, ((0, 2), (1, 4)))
    caption_len = plant(jax.random.randint(streams_of[3], (ITEMS,), max(1, CAP // 12), CAP - 3), jax.random.fold_in(streams_of[3], 1), max(1, CAP // 12), (CAP - 3) - 1).astype(jnp.int32)
    key_mask = plant((jax.random.randint(streams_of[4], (ITEMS, CAP), 0, 8) < 7).astype(jnp.int32), jax.random.fold_in(streams_of[4], 1), 0, 1)
    drop_flags = plant((jax.random.randint(streams_of[5], (ITEMS,), 0, 4) < 1).astype(jnp.int32), jax.random.fold_in(streams_of[5], 1), 0, 1)
    gain_latent = jnp.clip(1.0 + 0.1 * jax.random.normal(streams_of[6], (D,), jnp.float32), 0.5, 1.5)
    gain_tokens = jnp.clip(1.0 + 0.1 * jax.random.normal(streams_of[7], (D,), jnp.float32), 0.5, 1.5)
    gain_mlp = jnp.clip(1.0 + 0.1 * jax.random.normal(streams_of[8], (D,), jnp.float32), 0.5, 1.5)
    query_weight = centred(streams_of[9], (D, D), D ** -0.5, 0.21875, ((1, 4),))
    key_matrix = centred(streams_of[10], (D, D), D ** -0.5, 0.21875, ((1, 4),))
    value_matrix = centred(streams_of[11], (D, D), D ** -0.5, 0.21875, ((1, 4),))
    out_weight = centred(streams_of[12], (D, D), 1 ** -0.5, 6.0, ((0, 4),))
    up_weight = centred(streams_of[13], (D, FF), D ** -0.5, 0.21875, ((1, 4),))
    down_weight = centred(streams_of[14], (FF, D), FF ** -0.5, 0.109375, ((0, 4),))
    cotangent = centred(streams_of[15], (ITEMS, LAT, D), 1.0, 6.0, ((0, 4), (1, 2)))
    return {"latents": latents, "video_tokens": video_tokens, "caption_tokens": caption_tokens, "caption_len": caption_len, "key_mask": key_mask, "drop_flags": drop_flags, "gain_latent": gain_latent, "gain_tokens": gain_tokens, "gain_mlp": gain_mlp, "query_weight": query_weight, "key_matrix": key_matrix, "value_matrix": value_matrix, "out_weight": out_weight, "up_weight": up_weight, "down_weight": down_weight, "cotangent": cotangent}


@jax.custom_vjp
def low(v):
    return lax.optimization_barrier(v.astype(jnp.bfloat16)).astype(jnp.float32)

@jax.custom_vjp
def low_back(v):
    return v

def low_keep(v):
    return (low(v), None)

def low_pass(kept, grad):
    return (grad,)

def back_keep(v):
    return (v, None)

def back_low(kept, grad):
    return (low(grad),)
low.defvjp(low_keep, low_pass)
low_back.defvjp(back_keep, back_low)

def layer_norm(values, gain):
    center = values - lax.optimization_barrier(jnp.mean(values, axis=-1, keepdims=True))
    spread = lax.optimization_barrier(jnp.mean(center * center, axis=-1, keepdims=True))
    return center * lax.rsqrt(spread + 1e-05) * gain

def product(left, right):
    return jnp.einsum('ird,de->ire', left, right, precision=lax.Precision.HIGHEST)

def reference(latents, video_tokens, caption_tokens, caption_len, key_mask, drop_flags, gain_latent, gain_tokens, gain_mlp, query_weight, key_matrix, value_matrix, out_weight, up_weight, down_weight, cotangent):
    head_size = D // HEADS
    scale = 1.0 / head_size ** 0.5
    keep = (1 - drop_flags).astype(jnp.float32)
    slots = jnp.arange(CAP, dtype=jnp.int32)
    cap_valid = (slots[None, :] < caption_len[:, None]) & (key_mask == 1)
    valid = jnp.concatenate([jnp.ones((ITEMS, VIDEO), dtype=bool), cap_valid], axis=1)

    def attend(block):
        query_item, key_item, value_item, valid_item = block
        query_heads = query_item.reshape(LAT, HEADS, head_size)
        key_heads = key_item.reshape(-1, HEADS, head_size)
        value_heads = value_item.reshape(-1, HEADS, head_size)
        scores = jnp.einsum('lhe,khe->hlk', query_heads, key_heads, precision=lax.Precision.HIGHEST) * scale
        scores = low_back(scores)
        scores = jnp.where(valid_item[None, None, :], scores, -1e+30)
        peak = lax.optimization_barrier(jnp.max(scores, axis=-1, keepdims=True))
        expo = jnp.exp(scores - peak)
        probs = low(expo / lax.optimization_barrier(jnp.sum(expo, axis=-1, keepdims=True)))
        result = jnp.einsum('hlk,khe->lhe', probs, value_heads, precision=lax.Precision.HIGHEST)
        return result.reshape(LAT, D)

    def forward(lat_in, vid_in, cap_in, gain_one, gain_two, gain_three, w_query, w_key, w_value, w_out, w_up, w_down):
        lat_norm = low(layer_norm(lat_in, gain_one))
        queries = low(low_back(product(lat_norm, w_query)))
        tokens = jnp.concatenate([vid_in, cap_in], axis=1)
        tok_norm = low(layer_norm(tokens, gain_two))
        keys = low(low_back(product(tok_norm, w_key)))
        value_rows = low(low_back(product(tok_norm, w_value)))
        attended = lax.map(jax.checkpoint(attend), (queries, keys, value_rows, valid))
        mixed_in = low(low_back(attended * keep[:, None, None]))
        after_attn = lat_in + low_back(product(mixed_in, w_out))
        mlp_norm = low(layer_norm(after_attn, gain_three))
        pre_act = low_back(product(mlp_norm, w_up))
        activ = low(jax.nn.gelu(pre_act, approximate=False))
        return after_attn + product(activ, w_down)
    primals = (latents.astype(jnp.float32), video_tokens.astype(jnp.float32), caption_tokens.astype(jnp.float32), gain_latent, gain_tokens, gain_mlp, query_weight.astype(jnp.float32), key_matrix.astype(jnp.float32), value_matrix.astype(jnp.float32), out_weight.astype(jnp.float32), up_weight.astype(jnp.float32), down_weight.astype(jnp.float32))
    output, pullback = jax.vjp(forward, *primals)
    grads = pullback(cotangent.astype(jnp.float32))
    kept_count = jnp.sum(1 - drop_flags).astype(jnp.int32)
    return (output.astype(jnp.bfloat16), grads[0], grads[1], grads[2], grads[6], grads[7], grads[8], grads[9], grads[10], grads[11], grads[3], grads[4], grads[5], kept_count)
```

```python
import math

import jax
import jax.numpy as jnp
from jax import lax
from jax.experimental import pallas as pl
from jax.experimental.pallas import tpu as pltpu
from jax.sharding import PartitionSpec as P

D = 768
HEADS = 12


def combined_all(part, axis, combine):
    gathered = jax.tree.map(lambda a: lax.all_gather(a, axis), part)

    def take(source):
        return jax.tree.map(lambda a: lax.dynamic_index_in_dim(a, source, 0, False), gathered)

    return lax.fori_loop(
        1, lax.axis_size(axis), lambda source, state: combine(state, take(source)), take(0)
    )


def layer_norm(values, gain):
    center = values - jnp.mean(values, axis=-1, keepdims=True)
    spread = jnp.mean(center * center, axis=-1, keepdims=True)
    return center * lax.rsqrt(spread + 1e-05) * gain


def norm_back(values, gain, upstream):
    result, pullback = jax.vjp(layer_norm, values, gain)
    return pullback(upstream)


def gelu_exact(values):
    return jax.nn.gelu(values, approximate=False)


def combine_stats(first, second):
    peak = jnp.maximum(first[0], second[0])
    total = first[1] * jnp.exp(first[0] - peak) + second[1] * jnp.exp(second[0] - peak)
    return (peak, total)


def to_blocks(whole, vid_count, txt_count):
    items, rows, width = whole.shape
    split = whole.reshape(txt_count, items // txt_count, vid_count, rows // vid_count, width)
    return split.transpose(2, 0, 1, 3, 4).reshape(
        vid_count * txt_count, items // txt_count, rows // vid_count, width
    )


def from_blocks(blocked, vid_count, txt_count):
    count, items_here, rows_here, width = blocked.shape
    split = blocked.reshape(vid_count, txt_count, items_here, rows_here, width)
    return split.transpose(1, 2, 0, 3, 4).reshape(
        txt_count * items_here, vid_count * rows_here, width
    )


def place_sum(whole, part, start):
    current = lax.dynamic_slice_in_dim(whole, start, part.shape[0], 0)
    return lax.dynamic_update_slice_in_dim(whole, current + part, start, 0)


def place_stats(peak_all, total_all, peak, total, start):
    old_peak = lax.dynamic_slice_in_dim(peak_all, start, peak.shape[0], 0)
    old_total = lax.dynamic_slice_in_dim(total_all, start, peak.shape[0], 0)
    new_peak, new_total = combine_stats((old_peak, old_total), (peak, total))
    peak_all = lax.dynamic_update_slice_in_dim(peak_all, new_peak, start, 0)
    total_all = lax.dynamic_update_slice_in_dim(total_all, new_total, start, 0)
    return (peak_all, total_all)


def take_rows(whole, start, count):
    return lax.dynamic_slice_in_dim(whole, start, count, 0)


def local_general(
    latents,
    video_tokens,
    caption_tokens,
    caption_len,
    key_mask,
    drop_flags,
    gain_latent,
    gain_tokens,
    gain_mlp,
    query_weight,
    key_matrix,
    value_matrix,
    out_weight,
    up_weight,
    down_weight,
    cotangent,
):
    vid_count = lax.axis_size("vid")
    txt_count = lax.axis_size("txt")
    vid_index = lax.axis_index("vid")
    txt_index = lax.axis_index("txt")
    items_here = latents.shape[0]
    cap_items = caption_tokens.shape[0]
    items_total = items_here * txt_count
    head_width = query_weight.shape[1]
    head_size = D // HEADS
    heads_here = head_width // head_size
    scale = 1.0 / math.sqrt(head_size)
    video_here = video_tokens.shape[1]
    cap_here = caption_tokens.shape[1]
    video_start = txt_index * items_here
    cap_start = vid_index * cap_items
    keep = (1 - drop_flags).astype(jnp.float32)
    slots = txt_index * cap_here + jnp.arange(cap_here, dtype=jnp.int32)
    cap_valid = (slots[None, :] < caption_len[:, None]) & (key_mask == 1)
    cap_mask = cap_valid[:, None, None, :]

    def split_heads(values):
        return values.reshape(values.shape[0], values.shape[1], heads_here, head_size)

    lat_float = latents.astype(jnp.float32)
    lat_norm = layer_norm(lat_float, gain_latent).astype(jnp.bfloat16)
    queries = jnp.einsum(
        "bld,de->ble", lat_norm, query_weight, preferred_element_type=jnp.float32
    ).astype(jnp.bfloat16)
    all_queries = from_blocks(
        lax.all_gather(queries[None], ("vid", "txt"), axis=0, tiled=True), vid_count, txt_count
    )
    lat_total = all_queries.shape[1]
    video_queries = take_rows(all_queries, video_start, items_here)
    cap_queries = take_rows(all_queries, cap_start, cap_items)
    video_float = video_tokens.astype(jnp.float32)
    cap_float = caption_tokens.astype(jnp.float32)
    video_normed = layer_norm(video_float, gain_tokens).astype(jnp.bfloat16)
    caption_normed = layer_norm(cap_float, gain_tokens).astype(jnp.bfloat16)
    video_keys = jnp.einsum(
        "flc,co->flo", video_normed, key_matrix, preferred_element_type=jnp.float32
    ).astype(jnp.bfloat16)
    video_values = jnp.einsum(
        "flc,co->flo", video_normed, value_matrix, preferred_element_type=jnp.float32
    ).astype(jnp.bfloat16)
    cap_keys = jnp.einsum(
        "flc,co->flo", caption_normed, key_matrix, preferred_element_type=jnp.float32
    ).astype(jnp.bfloat16)
    cap_values = jnp.einsum(
        "flc,co->flo", caption_normed, value_matrix, preferred_element_type=jnp.float32
    ).astype(jnp.bfloat16)
    video_scores = (
        jnp.einsum(
            "blhe,bkhe->bhlk",
            split_heads(video_queries),
            split_heads(video_keys),
            preferred_element_type=jnp.float32,
        )
        * scale
    )
    cap_scores = (
        jnp.einsum(
            "blhe,bkhe->bhlk",
            split_heads(cap_queries),
            split_heads(cap_keys),
            preferred_element_type=jnp.float32,
        )
        * scale
    )
    cap_scores = jnp.where(cap_mask, cap_scores, -1e30)
    video_peak = jnp.max(video_scores, axis=-1)
    video_total = jnp.sum(jnp.exp(video_scores - video_peak[..., None]), axis=-1)
    cap_peak = jnp.max(cap_scores, axis=-1)
    cap_total = jnp.sum(
        jnp.where(cap_mask, jnp.exp(cap_scores - cap_peak[..., None]), 0.0), axis=-1
    )
    peak_all = jnp.full((items_total, heads_here, lat_total), -1e30, jnp.float32)
    total_all = jnp.zeros((items_total, heads_here, lat_total), jnp.float32)
    peak_all, total_all = place_stats(peak_all, total_all, video_peak, video_total, video_start)
    peak_all, total_all = place_stats(peak_all, total_all, cap_peak, cap_total, cap_start)
    peak, total = combined_all((peak_all, total_all), ("vid", "txt"), combine_stats)
    video_probs = (
        jnp.exp(video_scores - take_rows(peak, video_start, items_here)[..., None])
        / take_rows(total, video_start, items_here)[..., None]
    )
    cap_probs = jnp.where(
        cap_mask,
        jnp.exp(cap_scores - take_rows(peak, cap_start, cap_items)[..., None])
        / take_rows(total, cap_start, cap_items)[..., None],
        0.0,
    )
    video_low = video_probs.astype(jnp.bfloat16)
    cap_low = cap_probs.astype(jnp.bfloat16)
    video_part = jnp.einsum(
        "bhlk,bkhe->blhe", video_low, split_heads(video_values), preferred_element_type=jnp.float32
    ).reshape(items_here, lat_total, head_width)
    cap_part = jnp.einsum(
        "bhlk,bkhe->blhe", cap_low, split_heads(cap_values), preferred_element_type=jnp.float32
    ).reshape(cap_items, lat_total, head_width)
    value_all = jnp.zeros((items_total, lat_total, head_width), jnp.float32)
    value_all = place_sum(place_sum(value_all, video_part, video_start), cap_part, cap_start)
    attended = lax.psum_scatter(
        to_blocks(value_all, vid_count, txt_count), ("vid", "txt"), scatter_dimension=0, tiled=True
    )[0]
    mixed_in = (attended * keep[:, None, None]).astype(jnp.bfloat16)
    branch = lax.psum(
        jnp.einsum("ble,ed->bld", mixed_in, out_weight, preferred_element_type=jnp.float32), "head"
    )
    after_attn = lat_float + branch
    mlp_norm = layer_norm(after_attn, gain_mlp).astype(jnp.bfloat16)
    pre_act = jnp.einsum("bld,df->blf", mlp_norm, up_weight, preferred_element_type=jnp.float32)
    activ = gelu_exact(pre_act).astype(jnp.bfloat16)
    growth = lax.psum(
        jnp.einsum("blf,fd->bld", activ, down_weight, preferred_element_type=jnp.float32).astype(
            jnp.bfloat16
        ),
        "head",
    ).astype(jnp.float32)
    latents_out = (after_attn + growth).astype(jnp.bfloat16)
    grad_down = jnp.einsum("blf,bld->fd", activ, cotangent, preferred_element_type=jnp.float32)
    d_activ = jnp.einsum("bld,fd->blf", cotangent, down_weight, preferred_element_type=jnp.float32)
    d_pre = jax.vjp(gelu_exact, pre_act)[1](d_activ)[0].astype(jnp.bfloat16)
    grad_up = jnp.einsum("bld,blf->df", mlp_norm, d_pre, preferred_element_type=jnp.float32)
    d_mlp_norm = lax.psum(
        jnp.einsum("blf,df->bld", d_pre, up_weight, preferred_element_type=jnp.float32), "head"
    )
    d_after_norm, grad_gain_mlp = norm_back(after_attn, gain_mlp, d_mlp_norm)
    d_after = cotangent.astype(jnp.float32) + d_after_norm
    d_branch = d_after.astype(jnp.bfloat16)
    grad_out = jnp.einsum("ble,bld->ed", mixed_in, d_branch, preferred_element_type=jnp.float32)
    d_att = (
        jnp.einsum("bld,ed->ble", d_branch, out_weight, preferred_element_type=jnp.float32)
        * keep[:, None, None]
    ).astype(jnp.bfloat16)
    all_d_att = from_blocks(
        lax.all_gather(d_att[None], ("vid", "txt"), axis=0, tiled=True), vid_count, txt_count
    )
    video_d_att = split_heads(take_rows(all_d_att, video_start, items_here))
    cap_d_att = split_heads(take_rows(all_d_att, cap_start, cap_items))
    video_dprobs = jnp.einsum(
        "blhe,bkhe->bhlk",
        video_d_att,
        split_heads(video_values),
        preferred_element_type=jnp.float32,
    )
    cap_dprobs = jnp.einsum(
        "blhe,bkhe->bhlk", cap_d_att, split_heads(cap_values), preferred_element_type=jnp.float32
    )
    delta_all = jnp.zeros((items_total, heads_here, lat_total), jnp.float32)
    delta_all = place_sum(delta_all, jnp.sum(video_probs * video_dprobs, axis=-1), video_start)
    delta_all = place_sum(delta_all, jnp.sum(cap_probs * cap_dprobs, axis=-1), cap_start)
    delta = lax.psum(delta_all, ("vid", "txt"))
    video_dscores = (
        video_probs * (video_dprobs - take_rows(delta, video_start, items_here)[..., None])
    ).astype(jnp.bfloat16)
    cap_dscores = (
        cap_probs * (cap_dprobs - take_rows(delta, cap_start, cap_items)[..., None])
    ).astype(jnp.bfloat16)
    video_dq = (
        jnp.einsum(
            "bhlk,bkhe->blhe",
            video_dscores,
            split_heads(video_keys),
            preferred_element_type=jnp.float32,
        )
        * scale
    ).reshape(items_here, lat_total, head_width)
    cap_dq = (
        jnp.einsum(
            "bhlk,bkhe->blhe",
            cap_dscores,
            split_heads(cap_keys),
            preferred_element_type=jnp.float32,
        )
        * scale
    ).reshape(cap_items, lat_total, head_width)
    query_all = jnp.zeros((items_total, lat_total, head_width), jnp.float32)
    query_all = place_sum(place_sum(query_all, video_dq, video_start), cap_dq, cap_start)
    d_queries = lax.psum_scatter(
        to_blocks(query_all, vid_count, txt_count), ("vid", "txt"), scatter_dimension=0, tiled=True
    )[0].astype(jnp.bfloat16)
    video_key_grad = (
        (
            jnp.einsum(
                "bhlk,blhe->bkhe",
                video_dscores,
                split_heads(video_queries),
                preferred_element_type=jnp.float32,
            )
            * scale
        )
        .reshape(items_here, video_here, head_width)
        .astype(jnp.bfloat16)
    )
    video_value_grad = (
        jnp.einsum("bhlk,blhe->bkhe", video_low, video_d_att, preferred_element_type=jnp.float32)
        .reshape(items_here, video_here, head_width)
        .astype(jnp.bfloat16)
    )
    caption_key_grad = (
        (
            jnp.einsum(
                "bhlk,blhe->bkhe",
                cap_dscores,
                split_heads(cap_queries),
                preferred_element_type=jnp.float32,
            )
            * scale
        )
        .reshape(cap_items, cap_here, head_width)
        .astype(jnp.bfloat16)
    )
    caption_value_grad = (
        jnp.einsum("bhlk,blhe->bkhe", cap_low, cap_d_att, preferred_element_type=jnp.float32)
        .reshape(cap_items, cap_here, head_width)
        .astype(jnp.bfloat16)
    )
    grad_query = jnp.einsum("bld,ble->de", lat_norm, d_queries, preferred_element_type=jnp.float32)
    d_lat_norm = lax.psum(
        jnp.einsum("ble,de->bld", d_queries, query_weight, preferred_element_type=jnp.float32),
        "head",
    )
    d_lat_back, grad_gain_latent = norm_back(lat_float, gain_latent, d_lat_norm)
    latent_grad = d_after + d_lat_back
    grad_key = jnp.einsum(
        "zsg,zsv->gv", video_normed, video_key_grad, preferred_element_type=jnp.float32
    ) + jnp.einsum(
        "zsg,zsv->gv", caption_normed, caption_key_grad, preferred_element_type=jnp.float32
    )
    grad_value = jnp.einsum(
        "zsg,zsv->gv", video_normed, video_value_grad, preferred_element_type=jnp.float32
    ) + jnp.einsum(
        "zsg,zsv->gv", caption_normed, caption_value_grad, preferred_element_type=jnp.float32
    )
    video_term = jnp.einsum(
        "ayt,ot->ayo", video_key_grad, key_matrix, preferred_element_type=jnp.float32
    ) + jnp.einsum(
        "ayt,ot->ayo", video_value_grad, value_matrix, preferred_element_type=jnp.float32
    )
    cap_term = jnp.einsum(
        "ayt,ot->ayo", caption_key_grad, key_matrix, preferred_element_type=jnp.float32
    ) + jnp.einsum(
        "ayt,ot->ayo", caption_value_grad, value_matrix, preferred_element_type=jnp.float32
    )
    d_video_norm, d_cap_norm = lax.psum((video_term, cap_term), "head")
    video_grad, video_gain_part = norm_back(video_float, gain_tokens, d_video_norm)
    caption_grad, cap_gain_part = norm_back(cap_float, gain_tokens, d_cap_norm)
    grad_gain_tokens = video_gain_part + cap_gain_part
    kept_here = jnp.sum(keep)
    (
        grad_query,
        grad_key,
        grad_value,
        grad_out,
        grad_up,
        grad_down,
        grad_gain_latent,
        grad_gain_tokens,
        grad_gain_mlp,
        kept_total,
    ) = lax.psum(
        (
            grad_query,
            grad_key,
            grad_value,
            grad_out,
            grad_up,
            grad_down,
            grad_gain_latent,
            grad_gain_tokens,
            grad_gain_mlp,
            kept_here,
        ),
        ("vid", "txt"),
    )
    kept_count = (kept_total / vid_count).astype(jnp.int32)
    return (
        latents_out,
        latent_grad,
        video_grad,
        caption_grad,
        grad_query,
        grad_key,
        grad_value,
        grad_out,
        grad_up,
        grad_down,
        grad_gain_latent,
        grad_gain_tokens,
        grad_gain_mlp,
        kept_count,
    )


def swap_cores(values):
    return lax.ppermute(values, "vid", [(0, 1), (1, 0)])


def head_shift(values, shift, count):
    return lax.ppermute(values, "head", [(i, (i - shift) % count) for i in range(count)])


def take_block(values, index, size, axis=0):
    return lax.dynamic_slice_in_dim(values, index * size, size, axis)


def sum_over_head(part, place, count):
    low = part.astype(jnp.bfloat16)
    total = lax.dynamic_index_in_dim(part, place, 0, False)
    for shift in range(1, count):
        chunk = lax.dynamic_index_in_dim(low, (place - shift) % count, 0, False)
        total = total + head_shift(chunk, shift, count).astype(jnp.float32)
    total = total.astype(jnp.bfloat16)
    result = lax.dynamic_update_index_in_dim(jnp.zeros_like(low), total, place, 0)
    for shift in range(1, count):
        result = lax.dynamic_update_index_in_dim(
            result, head_shift(total, shift, count), (place + shift) % count, 0
        )
    return result


def caption_perm(step, vid_count, txt_count, cores):
    pairs = []
    for v in range(vid_count):
        for t in range(txt_count):
            block = (t + step) % txt_count
            dest_txt = v * (txt_count // vid_count) + block // cores
            dest_vid = block % cores
            pairs.append((v * txt_count + t, dest_vid * txt_count + dest_txt))
    return pairs


PAIR = 128
F32 = jnp.float32
BF16 = jnp.bfloat16


def dot_nt(a, b):
    return lax.dot_general(a, b, (((1,), (1,)), ((), ())), preferred_element_type=F32)


def dot_nn(a, b):
    return lax.dot_general(a, b, (((1,), (0,)), ((), ())), preferred_element_type=F32)


def dot_tn(a, b):
    return lax.dot_general(a, b, (((0,), (0,)), ((), ())), preferred_element_type=F32)


def square(ref):
    return ref[...].reshape(D, D)


def two_heads(values):
    low = lax.broadcasted_iota(jnp.int32, values.shape, 1) < PAIR // 2
    zero = jnp.zeros_like(values)
    return jnp.concatenate([jnp.where(low, values, zero), jnp.where(low, zero, values)], axis=0)


def from_two_heads(both):
    n = both.shape[1] // 2
    first = lax.broadcasted_iota(jnp.int32, (PAIR, n), 0) < PAIR // 2
    return jnp.where(first, both[:, :n], both[:, n:]).T


def chunk_list(video, cap, size):
    return [(start, size) for start in range(0, video, size)] + [(video, cap)]


def norm_kernel(s_ref, own_ref, other_ref, cap_ref, gain_ref, out_ref):
    gain = gain_ref[...]
    start = 0
    for ref in (own_ref, other_ref, cap_ref):
        rows = ref.shape[0]
        for at in range(0, rows, 64):
            out_ref[pl.ds(start + at, 64), :] = layer_norm(
                ref[pl.ds(at, 64), :].astype(F32), gain
            ).astype(BF16)
        start += rows


def forward_kernel(
    s_ref, tok_ref, lat_ref, mask_ref, wq_ref, wk_ref, wv_ref, wo_ref, gain_lat_ref, gain_mlp_ref,
    q_ref, latn_ref, k_ref, v_ref, lse_ref, o_ref, mix_ref, after_ref, mlpn_ref, s_scr,
):
    item = pl.program_id(0)
    lat = lat_ref[...].astype(F32)
    latn = layer_norm(lat, gain_lat_ref[...]).astype(BF16)
    latn_ref[...] = latn
    q_ref[...] = (dot_nt(latn, square(wq_ref)).astype(BF16).astype(F32) * 0.125).astype(BF16)
    keys = tok_ref.shape[0]
    cap = mask_ref.shape[0]
    step = keys // 4

    def project(c, carry):
        rows = pl.ds(pl.multiple_of(c * step, 16), step)
        k_ref[rows, :] = dot_nt(tok_ref[rows, :], square(wk_ref)).astype(BF16)
        v_ref[rows, :] = dot_nt(tok_ref[rows, :], square(wv_ref)).astype(BF16)
        return carry

    lax.fori_loop(0, 4, project, 0)
    chunks = chunk_list(keys - cap, cap, 256)

    def pair(p, carry):
        cols = pl.ds(pl.multiple_of(p * PAIR, PAIR), PAIR)
        q2 = two_heads(q_ref[:, cols])
        peak = None
        for start, size in chunks:
            rows = pl.ds(start, size)
            s = dot_nt(k_ref[rows, cols], q2)
            if start == keys - cap:
                mask = mask_ref[...]
                s = jnp.where(jnp.concatenate([mask, mask], axis=1) > 0.5, s, -1e30)
            s_scr[rows, :] = s
            top = jnp.max(s, axis=0, keepdims=True)
            peak = top if peak is None else jnp.maximum(peak, top)
        total = jnp.zeros_like(peak)
        out = jnp.zeros((PAIR, q2.shape[0]), F32)
        for start, size in chunks:
            rows = pl.ds(start, size)
            e = jnp.exp(s_scr[rows, :] - peak)
            total = total + jnp.sum(e, axis=0, keepdims=True)
            out = out + dot_tn(v_ref[rows, cols], e.astype(BF16))
        o_ref[:, cols] = from_two_heads(out / total)
        lse_ref[pl.ds(p, 1), :] = peak + jnp.log(total)
        return carry

    lax.fori_loop(0, D // PAIR, pair, 0)
    keep = (1 - s_ref[1 + item]).astype(F32)
    mixed = (o_ref[...] * keep).astype(BF16)
    mix_ref[...] = mixed
    after = lat + dot_nn(mixed, square(wo_ref))
    after_ref[...] = after
    mlpn_ref[...] = layer_norm(after, gain_mlp_ref[...]).astype(BF16)


def backward_kernel(
    s_ref, q_ref, k_ref, v_ref, lse_ref, o_ref, datt_ref, own_ref, other_ref, cap_ref, mask_ref,
    wk_ref, wv_ref, gain_ref,
    dq_ref, dk_ref, dv_ref, own_out, other_out, cap_out, gain_out,
):
    item = pl.program_id(0)
    keys = k_ref.shape[0]
    cap = mask_ref.shape[0]
    chunks = chunk_list(keys - cap, cap, 256)

    def pair(p, carry):
        cols = pl.ds(pl.multiple_of(p * PAIR, PAIR), PAIR)
        q2 = two_heads(q_ref[:, cols])
        d_att = datt_ref[:, cols]
        d2 = two_heads(d_att)
        prod = (d_att.astype(F32) * o_ref[:, cols]).T
        delta = jnp.concatenate(
            [
                jnp.sum(prod[: PAIR // 2], axis=0, keepdims=True),
                jnp.sum(prod[PAIR // 2 :], axis=0, keepdims=True),
            ],
            axis=1,
        )
        lse = lse_ref[pl.ds(p, 1), :]
        dq = jnp.zeros((PAIR, q2.shape[0]), F32)
        for start, size in chunks:
            rows = pl.ds(start, size)
            k = k_ref[rows, cols]
            s = dot_nt(k, q2)
            d_probs = dot_nt(v_ref[rows, cols], d2)
            if start == keys - cap:
                mask = mask_ref[...]
                s = jnp.where(jnp.concatenate([mask, mask], axis=1) > 0.5, s, -1e30)
            probs = jnp.exp(s - lse)
            d_scores = (probs * (d_probs - delta)).astype(BF16)
            dv_ref[rows, cols] = dot_nn(probs.astype(BF16), d2).astype(BF16)
            dk_ref[rows, cols] = dot_nn(d_scores, q2).astype(BF16)
            dq = dq + dot_tn(k, d_scores)
        dq_ref[:, cols] = (from_two_heads(dq) * 0.125).astype(BF16)
        return carry

    lax.fori_loop(0, D // PAIR, pair, 0)
    gain = gain_ref[...]

    @pl.when(item == 0)
    def _():
        gain_out[...] = jnp.zeros_like(gain_out)

    start = 0
    for ref, out, size in ((own_ref, own_out, 256), (other_ref, other_out, 256), (cap_ref, cap_out, cap)):
        def chunk(c, carry, ref=ref, out=out, size=size, start=start):
            rows = pl.ds(pl.multiple_of(c * size, 16), size)
            key_rows = pl.ds(pl.multiple_of(start + c * size, 16), size)
            up = dot_nn(dk_ref[key_rows, :], square(wk_ref)) + dot_nn(
                dv_ref[key_rows, :], square(wv_ref)
            )
            x = ref[rows, :].astype(F32)
            center = x - jnp.mean(x, axis=-1, keepdims=True)
            rate = lax.rsqrt(jnp.mean(center * center, axis=-1, keepdims=True) + 1e-05)
            hat = center * rate
            gain_out[pl.ds(0, 1), :] += jnp.sum(up * hat, axis=0, keepdims=True)
            scaled = up * gain
            first = jnp.mean(scaled, axis=-1, keepdims=True)
            second = jnp.mean(scaled * hat, axis=-1, keepdims=True)
            out[rows, :] = (rate * (scaled - first - hat * second)).astype(out.dtype)
            return carry

        lax.fori_loop(0, ref.shape[0] // size, chunk, 0)
        start += ref.shape[0]


def place_kernel(s_ref, whole_ref, part_ref, out_ref):
    out_ref[...] = part_ref[...].astype(out_ref.dtype)


def local(
    latents,
    video_tokens,
    caption_tokens,
    caption_len,
    key_mask,
    drop_flags,
    gain_latent,
    gain_tokens,
    gain_mlp,
    query_weight,
    key_matrix,
    value_matrix,
    out_weight,
    up_weight,
    down_weight,
    cotangent,
):
    txt_count = lax.axis_size("txt")
    head_count = lax.axis_size("head")
    core = lax.axis_index("vid")
    place = lax.axis_index("txt")
    z = lax.axis_index("head")
    items_here = latents.shape[0]
    own = items_here // 2
    lat_half = latents.shape[1]
    lat_rows = 2 * lat_half
    video_here = video_tokens.shape[1]
    cap_here = caption_tokens.shape[1]
    cap_rows = cap_here * txt_count
    keys_here = 2 * video_here + cap_rows
    head_width = query_weight.shape[1]

    def dot(spec, a, b):
        return jnp.einsum(spec, a, b, preferred_element_type=F32)

    packed = jnp.stack([query_weight.T, key_matrix.T, value_matrix.T, out_weight])
    half = take_block(packed, core, 2)
    mine = jnp.zeros((head_count,) + half.shape, BF16)
    mine = lax.dynamic_update_index_in_dim(mine, half, z, 0)
    for shift in range(1, head_count):
        mine = lax.dynamic_update_index_in_dim(
            mine, head_shift(half, shift, head_count), (z + shift) % head_count, 0
        )
    weights = jnp.zeros((2,) + mine.shape, BF16)
    weights = lax.dynamic_update_index_in_dim(weights, mine, core, 0)
    weights = lax.dynamic_update_index_in_dim(weights, swap_cores(mine), 1 - core, 0)

    video_other = swap_cores(take_block(video_tokens, 1 - core, own))
    both = jnp.concatenate([latents, cotangent], axis=1)
    both_own = take_block(both, core, own)
    both_other = swap_cores(take_block(both, 1 - core, own))
    lat = jnp.concatenate([both_own[:, :lat_half], both_other[:, :lat_half]], axis=1)
    cot = jnp.concatenate([both_own[:, lat_half:], both_other[:, lat_half:]], axis=1)
    drop_own = take_block(drop_flags, core, own)
    keep = (1 - drop_own).astype(F32)
    scalars = jnp.concatenate([core[None].astype(jnp.int32), drop_own])

    place_slots = place * cap_here + jnp.arange(cap_here, dtype=jnp.int32)
    cap_valid = (place_slots[None, :] < caption_len[:, None]) & (key_mask == 1)
    cap_flags = jnp.zeros((caption_tokens.shape[0], 1, D), BF16)
    cap_flags = cap_flags.at[:, 0, :cap_here].set(cap_valid.astype(BF16))
    cap_message = jnp.concatenate([caption_tokens, cap_flags], axis=1)
    cap_parts = []
    for step in range(txt_count):
        block = take_block(cap_message, (place + step) % txt_count, own)
        cap_parts.append(
            lax.ppermute(block, ("vid", "txt"), caption_perm(step, 2, txt_count, 2))
        )
    cap = jnp.concatenate([part[:, :cap_here] for part in cap_parts], axis=1)
    valid = jnp.concatenate([part[:, cap_here, :cap_here] for part in cap_parts], axis=1)
    mask = jnp.broadcast_to(valid.astype(F32)[:, :, None], (own, cap_rows, lat_rows))

    def item_spec(rows, width=D):
        return pl.BlockSpec((None, rows, width), lambda i, s: (i, 0, 0))

    def own_spec(rows):
        return pl.BlockSpec((None, rows, D), lambda i, s: (s[0] * own + i, 0, 0))

    def weight_spec(m):
        return pl.BlockSpec(
            (None, head_count, None, head_width, D),
            lambda i, s: (m // 2, 0, m % 2, 0, 0),
            pipeline_mode=pl.Buffered(1),
        )

    row_spec = pl.BlockSpec((1, D), lambda i, s: (0, 0))

    def call(kernel, name, ins, outs, operands, scratch=(), aliases={}):
        return pl.pallas_call(
            kernel,
            name=name,
            grid_spec=pltpu.PrefetchScalarGridSpec(
                num_scalar_prefetch=1,
                grid=(own,),
                in_specs=ins,
                out_specs=[spec for spec, _, _ in outs],
                scratch_shapes=list(scratch),
            ),
            out_shape=[jax.ShapeDtypeStruct(shape, dtype) for _, shape, dtype in outs],
            input_output_aliases=aliases,
            compiler_params=pltpu.CompilerParams(vmem_limit_bytes=56 << 20),
        )(scalars, *operands)

    def item_out(rows, dtype, width=D):
        return (item_spec(rows, width), (own, rows, width), dtype)

    gain_lat_row = gain_latent[None]
    gain_tok_row = gain_tokens[None]
    gain_mlp_row = gain_mlp[None]
    (tok_norm,) = call(
        norm_kernel,
        "token_norm",
        [own_spec(video_here), item_spec(video_here), item_spec(cap_rows), row_spec],
        [item_out(keys_here, BF16)],
        (video_tokens, video_other, cap, gain_tok_row),
    )
    queries, lat_norm, keys, values, lse, attended, mixed_in, after_attn, mlp_norm = call(
        forward_kernel,
        "attention_forward",
        [item_spec(keys_here), item_spec(lat_rows), item_spec(cap_rows, lat_rows)]
        + [weight_spec(m) for m in range(4)]
        + [row_spec, row_spec],
        [
            item_out(lat_rows, BF16),
            item_out(lat_rows, BF16),
            item_out(keys_here, BF16),
            item_out(keys_here, BF16),
            item_out(8, F32, 2 * lat_rows),
            item_out(lat_rows, F32),
            item_out(lat_rows, BF16),
            item_out(lat_rows, F32),
            item_out(lat_rows, BF16),
        ],
        (tok_norm, lat, mask, weights, weights, weights, weights, gain_lat_row, gain_mlp_row),
        [pltpu.VMEM((keys_here, 2 * lat_rows), F32)],
    )

    pre_act = dot("bld,df->blf", mlp_norm, up_weight)
    activ, gelu_pull = jax.vjp(gelu_exact, pre_act)
    activ = activ.astype(BF16)
    d_pre = gelu_pull(dot("bld,fd->blf", cot, down_weight))[0].astype(BF16)
    d_mlp_norm = sum_over_head(dot("blf,df->bld", d_pre, up_weight), z, head_count)
    activ, d_mlp_norm = lax.optimization_barrier((activ, d_mlp_norm))
    growth = lax.psum(dot("blf,fd->bld", activ, down_weight).astype(BF16), "head")
    grad_down = dot("blf,bld->fd", activ, cot)
    grad_up = dot("bld,blf->df", mlp_norm, d_pre)
    out_mine = (after_attn + growth.astype(F32)).astype(BF16)

    d_after_norm, gain_mlp_part = norm_back_rows(after_attn, gain_mlp, d_mlp_norm.astype(F32))
    d_after = cot.astype(F32) + d_after_norm
    d_branch = d_after.astype(BF16)
    w_query = weights[0, :, 0].reshape(D, D)
    w_out = weights[1, :, 1].reshape(D, D)
    d_att = (dot("bld,ed->ble", d_branch, w_out) * keep[:, None, None]).astype(BF16)
    d_queries, d_keys, d_values, video_grad, other_back, cap_back, gain_tok_part = call(
        backward_kernel,
        "attention_backward",
        [
            item_spec(lat_rows),
            item_spec(keys_here),
            item_spec(keys_here),
            item_spec(8, 2 * lat_rows),
            item_spec(lat_rows),
            item_spec(lat_rows),
            own_spec(video_here),
            item_spec(video_here),
            item_spec(cap_rows),
            item_spec(cap_rows, lat_rows),
            weight_spec(1),
            weight_spec(2),
            row_spec,
        ],
        [
            item_out(lat_rows, BF16),
            item_out(keys_here, BF16),
            item_out(keys_here, BF16),
            (own_spec(video_here), video_tokens.shape, F32),
            item_out(video_here, BF16),
            item_out(cap_rows, BF16),
            (pl.BlockSpec((8, D), lambda i, s: (0, 0)), (8, D), F32),
        ],
        (
            queries, keys, values, lse, attended, d_att, video_tokens, video_other, cap, mask,
            weights, weights, gain_tok_row,
        ),
    )
    other_here = swap_cores(other_back)
    (video_grad,) = call(
        place_kernel,
        "place_rows",
        [pl.BlockSpec(memory_space=pl.ANY), item_spec(video_here)],
        [
            (
                pl.BlockSpec((None, video_here, D), lambda i, s: ((1 - s[0]) * own + i, 0, 0)),
                video_tokens.shape,
                F32,
            )
        ],
        (video_grad, other_here),
        aliases={1: 0},
    )
    caption_grad = jnp.zeros((txt_count, own, cap_here, D), F32)
    for step in range(txt_count):
        perm = [(b, a) for a, b in caption_perm(step, 2, txt_count, 2)]
        part = lax.ppermute(
            cap_back[:, step * cap_here : (step + 1) * cap_here], ("vid", "txt"), perm
        )
        caption_grad = lax.dynamic_update_index_in_dim(
            caption_grad, part.astype(F32), (place + step) % txt_count, 0
        )
    caption_grad = caption_grad.reshape(caption_tokens.shape)

    d_lat_norm = dot("ble,ed->bld", d_queries, w_query)
    d_lat_back, gain_lat_part = norm_back_rows(lat.astype(F32), gain_latent, d_lat_norm)
    lat_grad_mine = d_after + d_lat_back

    def mine_cols(array):
        return lax.dynamic_slice_in_dim(array, z * head_width, head_width, array.ndim - 1)

    grad_out = dot("ble,bld->ed", mine_cols(mixed_in), d_branch)
    grad_query = dot("bld,ble->de", lat_norm, mine_cols(d_queries))
    grad_key = dot("bld,ble->de", tok_norm, mine_cols(d_keys))
    grad_value = dot("bld,ble->de", tok_norm, mine_cols(d_values))
    extra = jnp.zeros((8, D), F32)
    extra = extra.at[0].set(jnp.sum(gain_mlp_part, axis=0)).at[1].set(jnp.sum(keep))
    grad_up, grad_down, out_rows = lax.psum(
        (grad_up, grad_down, jnp.concatenate([grad_out, extra])), ("vid", "txt")
    )
    gains = jnp.stack([jnp.sum(gain_lat_part, axis=0), gain_tok_part[0]])
    gains = gains.reshape(2 * D // head_width, head_width)
    late = jnp.concatenate([grad_query, grad_key, grad_value, gains])
    late = lax.psum(late.astype(BF16), ("vid", "txt")).astype(F32)
    gains = late[3 * D :].reshape(2, D)

    def give_back(values):
        other = swap_cores(values[:, lat_half:].astype(BF16)).astype(values.dtype)
        whole = jnp.zeros((items_here, lat_half, D), values.dtype)
        whole = lax.dynamic_update_slice_in_dim(whole, values[:, :lat_half], core * own, 0)
        return lax.dynamic_update_slice_in_dim(whole, other, (1 - core) * own, 0)

    latents_out = give_back(out_mine)
    latent_grad = give_back(lat_grad_mine)
    kept_count = out_rows[head_width + 1, 0].astype(jnp.int32)
    return (
        latents_out,
        latent_grad,
        video_grad,
        caption_grad,
        late[:D],
        late[D : 2 * D],
        late[2 * D : 3 * D],
        out_rows[:head_width],
        grad_up,
        grad_down,
        gains[0],
        gains[1],
        out_rows[head_width],
        kept_count,
    )


def norm_back_rows(values, gain, upstream):
    mean = jnp.mean(values, axis=-1, keepdims=True)
    center = values - mean
    rate = lax.rsqrt(jnp.mean(center * center, axis=-1, keepdims=True) + 1e-05)
    hat = center * rate
    scaled = upstream * gain
    first = jnp.mean(scaled, axis=-1, keepdims=True)
    second = jnp.mean(scaled * hat, axis=-1, keepdims=True)
    return rate * (scaled - first - hat * second), jnp.sum(upstream * hat, axis=-2)


def fits(mesh):
    shape = mesh.shape
    return shape["vid"] == 2 and shape["txt"] == 4 and shape["head"] == 4


def solution(mesh):
    in_specs = (
        P("txt", "vid", None),
        P("txt", "vid", None),
        P("vid", "txt", None),
        P("vid"),
        P("vid", "txt"),
        P("txt"),
        P(),
        P(),
        P(),
        P(None, "head"),
        P(None, "head"),
        P(None, "head"),
        P("head", None),
        P(None, "head"),
        P("head", None),
        P("txt", "vid", None),
    )
    out_specs = (
        P("txt", "vid", None),
        P("txt", "vid", None),
        P("txt", "vid", None),
        P("vid", "txt", None),
        P(None, "head"),
        P(None, "head"),
        P(None, "head"),
        P("head", None),
        P(None, "head"),
        P("head", None),
        P(),
        P(),
        P(),
        P(),
    )
    return jax.shard_map(local if fits(mesh) else local_general, mesh=mesh, in_specs=in_specs, out_specs=out_specs, check_vma=False)
```

```python
import math

import jax
import jax.numpy as jnp
from jax import lax
from jax.experimental import pallas as pl
from jax.experimental.pallas import tpu as pltpu
from jax.sharding import PartitionSpec as P

D = 768
HEADS = 12


def combined_all(part, axis, combine):
    gathered = jax.tree.map(lambda a: lax.all_gather(a, axis), part)

    def take(source):
        return jax.tree.map(lambda a: lax.dynamic_index_in_dim(a, source, 0, False), gathered)

    return lax.fori_loop(
        1, lax.axis_size(axis), lambda source, state: combine(state, take(source)), take(0)
    )


def layer_norm(values, gain):
    center = values - jnp.mean(values, axis=-1, keepdims=True)
    spread = jnp.mean(center * center, axis=-1, keepdims=True)
    return center * lax.rsqrt(spread + 1e-05) * gain


def norm_back(values, gain, upstream):
    result, pullback = jax.vjp(layer_norm, values, gain)
    return pullback(upstream)


def gelu_exact(values):
    return jax.nn.gelu(values, approximate=False)


def combine_stats(first, second):
    peak = jnp.maximum(first[0], second[0])
    total = first[1] * jnp.exp(first[0] - peak) + second[1] * jnp.exp(second[0] - peak)
    return (peak, total)


def to_blocks(whole, vid_count, txt_count):
    items, rows, width = whole.shape
    split = whole.reshape(txt_count, items // txt_count, vid_count, rows // vid_count, width)
    return split.transpose(2, 0, 1, 3, 4).reshape(
        vid_count * txt_count, items // txt_count, rows // vid_count, width
    )


def from_blocks(blocked, vid_count, txt_count):
    count, items_here, rows_here, width = blocked.shape
    split = blocked.reshape(vid_count, txt_count, items_here, rows_here, width)
    return split.transpose(1, 2, 0, 3, 4).reshape(
        txt_count * items_here, vid_count * rows_here, width
    )


def place_sum(whole, part, start):
    current = lax.dynamic_slice_in_dim(whole, start, part.shape[0], 0)
    return lax.dynamic_update_slice_in_dim(whole, current + part, start, 0)


def place_stats(peak_all, total_all, peak, total, start):
    old_peak = lax.dynamic_slice_in_dim(peak_all, start, peak.shape[0], 0)
    old_total = lax.dynamic_slice_in_dim(total_all, start, peak.shape[0], 0)
    new_peak, new_total = combine_stats((old_peak, old_total), (peak, total))
    peak_all = lax.dynamic_update_slice_in_dim(peak_all, new_peak, start, 0)
    total_all = lax.dynamic_update_slice_in_dim(total_all, new_total, start, 0)
    return (peak_all, total_all)


def take_rows(whole, start, count):
    return lax.dynamic_slice_in_dim(whole, start, count, 0)


def local_general(
    latents,
    video_tokens,
    caption_tokens,
    caption_len,
    key_mask,
    drop_flags,
    gain_latent,
    gain_tokens,
    gain_mlp,
    query_weight,
    key_matrix,
    value_matrix,
    out_weight,
    up_weight,
    down_weight,
    cotangent,
):
    vid_count = lax.axis_size("vid")
    txt_count = lax.axis_size("txt")
    vid_index = lax.axis_index("vid")
    txt_index = lax.axis_index("txt")
    items_here = latents.shape[0]
    cap_items = caption_tokens.shape[0]
    items_total = items_here * txt_count
    head_width = query_weight.shape[1]
    head_size = D // HEADS
    heads_here = head_width // head_size
    scale = 1.0 / math.sqrt(head_size)
    video_here = video_tokens.shape[1]
    cap_here = caption_tokens.shape[1]
    video_start = txt_index * items_here
    cap_start = vid_index * cap_items
    keep = (1 - drop_flags).astype(jnp.float32)
    slots = txt_index * cap_here + jnp.arange(cap_here, dtype=jnp.int32)
    cap_valid = (slots[None, :] < caption_len[:, None]) & (key_mask == 1)
    cap_mask = cap_valid[:, None, None, :]

    def split_heads(values):
        return values.reshape(values.shape[0], values.shape[1], heads_here, head_size)

    lat_float = latents.astype(jnp.float32)
    lat_norm = layer_norm(lat_float, gain_latent).astype(jnp.bfloat16)
    queries = jnp.einsum(
        "bld,de->ble", lat_norm, query_weight, preferred_element_type=jnp.float32
    ).astype(jnp.bfloat16)
    all_queries = from_blocks(
        lax.all_gather(queries[None], ("vid", "txt"), axis=0, tiled=True), vid_count, txt_count
    )
    lat_total = all_queries.shape[1]
    video_queries = take_rows(all_queries, video_start, items_here)
    cap_queries = take_rows(all_queries, cap_start, cap_items)
    video_float = video_tokens.astype(jnp.float32)
    cap_float = caption_tokens.astype(jnp.float32)
    video_normed = layer_norm(video_float, gain_tokens).astype(jnp.bfloat16)
    caption_normed = layer_norm(cap_float, gain_tokens).astype(jnp.bfloat16)
    video_keys = jnp.einsum(
        "flc,co->flo", video_normed, key_matrix, preferred_element_type=jnp.float32
    ).astype(jnp.bfloat16)
    video_values = jnp.einsum(
        "flc,co->flo", video_normed, value_matrix, preferred_element_type=jnp.float32
    ).astype(jnp.bfloat16)
    cap_keys = jnp.einsum(
        "flc,co->flo", caption_normed, key_matrix, preferred_element_type=jnp.float32
    ).astype(jnp.bfloat16)
    cap_values = jnp.einsum(
        "flc,co->flo", caption_normed, value_matrix, preferred_element_type=jnp.float32
    ).astype(jnp.bfloat16)
    video_scores = (
        jnp.einsum(
            "blhe,bkhe->bhlk",
            split_heads(video_queries),
            split_heads(video_keys),
            preferred_element_type=jnp.float32,
        )
        * scale
    )
    cap_scores = (
        jnp.einsum(
            "blhe,bkhe->bhlk",
            split_heads(cap_queries),
            split_heads(cap_keys),
            preferred_element_type=jnp.float32,
        )
        * scale
    )
    cap_scores = jnp.where(cap_mask, cap_scores, -1e30)
    video_peak = jnp.max(video_scores, axis=-1)
    video_total = jnp.sum(jnp.exp(video_scores - video_peak[..., None]), axis=-1)
    cap_peak = jnp.max(cap_scores, axis=-1)
    cap_total = jnp.sum(
        jnp.where(cap_mask, jnp.exp(cap_scores - cap_peak[..., None]), 0.0), axis=-1
    )
    peak_all = jnp.full((items_total, heads_here, lat_total), -1e30, jnp.float32)
    total_all = jnp.zeros((items_total, heads_here, lat_total), jnp.float32)
    peak_all, total_all = place_stats(peak_all, total_all, video_peak, video_total, video_start)
    peak_all, total_all = place_stats(peak_all, total_all, cap_peak, cap_total, cap_start)
    peak, total = combined_all((peak_all, total_all), ("vid", "txt"), combine_stats)
    video_probs = (
        jnp.exp(video_scores - take_rows(peak, video_start, items_here)[..., None])
        / take_rows(total, video_start, items_here)[..., None]
    )
    cap_probs = jnp.where(
        cap_mask,
        jnp.exp(cap_scores - take_rows(peak, cap_start, cap_items)[..., None])
        / take_rows(total, cap_start, cap_items)[..., None],
        0.0,
    )
    video_low = video_probs.astype(jnp.bfloat16)
    cap_low = cap_probs.astype(jnp.bfloat16)
    video_part = jnp.einsum(
        "bhlk,bkhe->blhe", video_low, split_heads(video_values), preferred_element_type=jnp.float32
    ).reshape(items_here, lat_total, head_width)
    cap_part = jnp.einsum(
        "bhlk,bkhe->blhe", cap_low, split_heads(cap_values), preferred_element_type=jnp.float32
    ).reshape(cap_items, lat_total, head_width)
    value_all = jnp.zeros((items_total, lat_total, head_width), jnp.float32)
    value_all = place_sum(place_sum(value_all, video_part, video_start), cap_part, cap_start)
    attended = lax.psum_scatter(
        to_blocks(value_all, vid_count, txt_count), ("vid", "txt"), scatter_dimension=0, tiled=True
    )[0]
    mixed_in = (attended * keep[:, None, None]).astype(jnp.bfloat16)
    branch = lax.psum(
        jnp.einsum("ble,ed->bld", mixed_in, out_weight, preferred_element_type=jnp.float32), "head"
    )
    after_attn = lat_float + branch
    mlp_norm = layer_norm(after_attn, gain_mlp).astype(jnp.bfloat16)
    pre_act = jnp.einsum("bld,df->blf", mlp_norm, up_weight, preferred_element_type=jnp.float32)
    activ = gelu_exact(pre_act).astype(jnp.bfloat16)
    growth = lax.psum(
        jnp.einsum("blf,fd->bld", activ, down_weight, preferred_element_type=jnp.float32).astype(
            jnp.bfloat16
        ),
        "head",
    ).astype(jnp.float32)
    latents_out = (after_attn + growth).astype(jnp.bfloat16)
    grad_down = jnp.einsum("blf,bld->fd", activ, cotangent, preferred_element_type=jnp.float32)
    d_activ = jnp.einsum("bld,fd->blf", cotangent, down_weight, preferred_element_type=jnp.float32)
    d_pre = jax.vjp(gelu_exact, pre_act)[1](d_activ)[0].astype(jnp.bfloat16)
    grad_up = jnp.einsum("bld,blf->df", mlp_norm, d_pre, preferred_element_type=jnp.float32)
    d_mlp_norm = lax.psum(
        jnp.einsum("blf,df->bld", d_pre, up_weight, preferred_element_type=jnp.float32), "head"
    )
    d_after_norm, grad_gain_mlp = norm_back(after_attn, gain_mlp, d_mlp_norm)
    d_after = cotangent.astype(jnp.float32) + d_after_norm
    d_branch = d_after.astype(jnp.bfloat16)
    grad_out = jnp.einsum("ble,bld->ed", mixed_in, d_branch, preferred_element_type=jnp.float32)
    d_att = (
        jnp.einsum("bld,ed->ble", d_branch, out_weight, preferred_element_type=jnp.float32)
        * keep[:, None, None]
    ).astype(jnp.bfloat16)
    all_d_att = from_blocks(
        lax.all_gather(d_att[None], ("vid", "txt"), axis=0, tiled=True), vid_count, txt_count
    )
    video_d_att = split_heads(take_rows(all_d_att, video_start, items_here))
    cap_d_att = split_heads(take_rows(all_d_att, cap_start, cap_items))
    video_dprobs = jnp.einsum(
        "blhe,bkhe->bhlk",
        video_d_att,
        split_heads(video_values),
        preferred_element_type=jnp.float32,
    )
    cap_dprobs = jnp.einsum(
        "blhe,bkhe->bhlk", cap_d_att, split_heads(cap_values), preferred_element_type=jnp.float32
    )
    delta_all = jnp.zeros((items_total, heads_here, lat_total), jnp.float32)
    delta_all = place_sum(delta_all, jnp.sum(video_probs * video_dprobs, axis=-1), video_start)
    delta_all = place_sum(delta_all, jnp.sum(cap_probs * cap_dprobs, axis=-1), cap_start)
    delta = lax.psum(delta_all, ("vid", "txt"))
    video_dscores = (
        video_probs * (video_dprobs - take_rows(delta, video_start, items_here)[..., None])
    ).astype(jnp.bfloat16)
    cap_dscores = (
        cap_probs * (cap_dprobs - take_rows(delta, cap_start, cap_items)[..., None])
    ).astype(jnp.bfloat16)
    video_dq = (
        jnp.einsum(
            "bhlk,bkhe->blhe",
            video_dscores,
            split_heads(video_keys),
            preferred_element_type=jnp.float32,
        )
        * scale
    ).reshape(items_here, lat_total, head_width)
    cap_dq = (
        jnp.einsum(
            "bhlk,bkhe->blhe",
            cap_dscores,
            split_heads(cap_keys),
            preferred_element_type=jnp.float32,
        )
        * scale
    ).reshape(cap_items, lat_total, head_width)
    query_all = jnp.zeros((items_total, lat_total, head_width), jnp.float32)
    query_all = place_sum(place_sum(query_all, video_dq, video_start), cap_dq, cap_start)
    d_queries = lax.psum_scatter(
        to_blocks(query_all, vid_count, txt_count), ("vid", "txt"), scatter_dimension=0, tiled=True
    )[0].astype(jnp.bfloat16)
    video_key_grad = (
        (
            jnp.einsum(
                "bhlk,blhe->bkhe",
                video_dscores,
                split_heads(video_queries),
                preferred_element_type=jnp.float32,
            )
            * scale
        )
        .reshape(items_here, video_here, head_width)
        .astype(jnp.bfloat16)
    )
    video_value_grad = (
        jnp.einsum("bhlk,blhe->bkhe", video_low, video_d_att, preferred_element_type=jnp.float32)
        .reshape(items_here, video_here, head_width)
        .astype(jnp.bfloat16)
    )
    caption_key_grad = (
        (
            jnp.einsum(
                "bhlk,blhe->bkhe",
                cap_dscores,
                split_heads(cap_queries),
                preferred_element_type=jnp.float32,
            )
            * scale
        )
        .reshape(cap_items, cap_here, head_width)
        .astype(jnp.bfloat16)
    )
    caption_value_grad = (
        jnp.einsum("bhlk,blhe->bkhe", cap_low, cap_d_att, preferred_element_type=jnp.float32)
        .reshape(cap_items, cap_here, head_width)
        .astype(jnp.bfloat16)
    )
    grad_query = jnp.einsum("bld,ble->de", lat_norm, d_queries, preferred_element_type=jnp.float32)
    d_lat_norm = lax.psum(
        jnp.einsum("ble,de->bld", d_queries, query_weight, preferred_element_type=jnp.float32),
        "head",
    )
    d_lat_back, grad_gain_latent = norm_back(lat_float, gain_latent, d_lat_norm)
    latent_grad = d_after + d_lat_back
    grad_key = jnp.einsum(
        "zsg,zsv->gv", video_normed, video_key_grad, preferred_element_type=jnp.float32
    ) + jnp.einsum(
        "zsg,zsv->gv", caption_normed, caption_key_grad, preferred_element_type=jnp.float32
    )
    grad_value = jnp.einsum(
        "zsg,zsv->gv", video_normed, video_value_grad, preferred_element_type=jnp.float32
    ) + jnp.einsum(
        "zsg,zsv->gv", caption_normed, caption_value_grad, preferred_element_type=jnp.float32
    )
    video_term = jnp.einsum(
        "ayt,ot->ayo", video_key_grad, key_matrix, preferred_element_type=jnp.float32
    ) + jnp.einsum(
        "ayt,ot->ayo", video_value_grad, value_matrix, preferred_element_type=jnp.float32
    )
    cap_term = jnp.einsum(
        "ayt,ot->ayo", caption_key_grad, key_matrix, preferred_element_type=jnp.float32
    ) + jnp.einsum(
        "ayt,ot->ayo", caption_value_grad, value_matrix, preferred_element_type=jnp.float32
    )
    d_video_norm, d_cap_norm = lax.psum((video_term, cap_term), "head")
    video_grad, video_gain_part = norm_back(video_float, gain_tokens, d_video_norm)
    caption_grad, cap_gain_part = norm_back(cap_float, gain_tokens, d_cap_norm)
    grad_gain_tokens = video_gain_part + cap_gain_part
    kept_here = jnp.sum(keep)
    (
        grad_query,
        grad_key,
        grad_value,
        grad_out,
        grad_up,
        grad_down,
        grad_gain_latent,
        grad_gain_tokens,
        grad_gain_mlp,
        kept_total,
    ) = lax.psum(
        (
            grad_query,
            grad_key,
            grad_value,
            grad_out,
            grad_up,
            grad_down,
            grad_gain_latent,
            grad_gain_tokens,
            grad_gain_mlp,
            kept_here,
        ),
        ("vid", "txt"),
    )
    kept_count = (kept_total / vid_count).astype(jnp.int32)
    return (
        latents_out,
        latent_grad,
        video_grad,
        caption_grad,
        grad_query,
        grad_key,
        grad_value,
        grad_out,
        grad_up,
        grad_down,
        grad_gain_latent,
        grad_gain_tokens,
        grad_gain_mlp,
        kept_count,
    )


def swap_cores(values):
    return lax.ppermute(values, "vid", [(0, 1), (1, 0)])


def head_shift(values, shift, count):
    return lax.ppermute(values, "head", [(i, (i - shift) % count) for i in range(count)])


def take_block(values, index, size, axis=0):
    return lax.dynamic_slice_in_dim(values, index * size, size, axis)


def sum_over_head(part, place, count):
    low = part.astype(jnp.bfloat16)
    total = lax.dynamic_index_in_dim(part, place, 0, False)
    for shift in range(1, count):
        chunk = lax.dynamic_index_in_dim(low, (place - shift) % count, 0, False)
        total = total + head_shift(chunk, shift, count).astype(jnp.float32)
    total = total.astype(jnp.bfloat16)
    result = lax.dynamic_update_index_in_dim(jnp.zeros_like(low), total, place, 0)
    for shift in range(1, count):
        result = lax.dynamic_update_index_in_dim(
            result, head_shift(total, shift, count), (place + shift) % count, 0
        )
    return result


def sum_over_group(rows, core, place, count):
    half = rows.shape[0] // 2
    part = half // count
    total = take_block(rows, core, half)
    total = total + swap_cores(take_block(rows, 1 - core, half).astype(BF16)).astype(F32)
    low = total.astype(BF16)
    total = take_block(total, place, part)
    for step in range(1, count):
        perm = [(i, (i - step) % count) for i in range(count)]
        chunk = take_block(low, (place - step) % count, part)
        total = total + lax.ppermute(chunk, "txt", perm).astype(F32)
    total = total.astype(BF16)
    mine = lax.dynamic_update_slice_in_dim(jnp.zeros_like(low), total, place * part, 0)
    for step in range(1, count):
        perm = [(i, (i - step) % count) for i in range(count)]
        mine = lax.dynamic_update_slice_in_dim(
            mine, lax.ppermute(total, "txt", perm), (place + step) % count * part, 0
        )
    whole = jnp.zeros(rows.shape, BF16)
    whole = lax.dynamic_update_slice_in_dim(whole, mine, core * half, 0)
    return lax.dynamic_update_slice_in_dim(whole, swap_cores(mine), (1 - core) * half, 0)


def caption_perm(step, vid_count, txt_count, cores):
    pairs = []
    for v in range(vid_count):
        for t in range(txt_count):
            block = (t + step) % txt_count
            dest_txt = v * (txt_count // vid_count) + block // cores
            dest_vid = block % cores
            pairs.append((v * txt_count + t, dest_vid * txt_count + dest_txt))
    return pairs


PAIR = 128
F32 = jnp.float32
BF16 = jnp.bfloat16


def dot_nt(a, b):
    return lax.dot_general(a, b, (((1,), (1,)), ((), ())), preferred_element_type=F32)


def dot_nn(a, b):
    return lax.dot_general(a, b, (((1,), (0,)), ((), ())), preferred_element_type=F32)


def dot_tn(a, b):
    return lax.dot_general(a, b, (((0,), (0,)), ((), ())), preferred_element_type=F32)


def square(ref):
    return ref[...].reshape(D, D)


def two_heads(values):
    low = lax.broadcasted_iota(jnp.int32, values.shape, 1) < PAIR // 2
    zero = jnp.zeros_like(values)
    return jnp.concatenate([jnp.where(low, values, zero), jnp.where(low, zero, values)], axis=0)


def from_two_heads(both):
    n = both.shape[1] // 2
    first = lax.broadcasted_iota(jnp.int32, (PAIR, n), 0) < PAIR // 2
    return jnp.where(first, both[:, :n], both[:, n:]).T


def chunk_list(video, cap, size):
    return [(start, size) for start in range(0, video, size)] + [(video, cap)]


def norm_kernel(s_ref, own_ref, other_ref, cap_ref, lat_ref, gain_ref, gain_lat_ref, out_ref, lat_out):
    gain = gain_ref[...]
    lat_out[...] = layer_norm(lat_ref[...].astype(F32), gain_lat_ref[...]).astype(BF16)
    start = 0
    for ref in (own_ref, other_ref, cap_ref):
        rows = ref.shape[0]
        for at in range(0, rows, 64):
            out_ref[pl.ds(start + at, 64), :] = layer_norm(
                ref[pl.ds(at, 64), :].astype(F32), gain
            ).astype(BF16)
        start += rows


def forward_kernel(s_ref, tok_ref, latn_ref, mask_ref, wq_ref, wk_ref, wv_ref, *refs):
    q_ref, k_ref, v_ref, lse_ref, o_ref, s_scr = refs[-6:]
    keys, width = k_ref.shape
    cap = mask_ref.shape[0]
    step = keys // 4

    def matrix(ref):
        return ref[...].reshape(width, D)

    q_ref[...] = (dot_nt(latn_ref[...], matrix(wq_ref)).astype(BF16).astype(F32) * 0.125).astype(BF16)

    def project(c, carry):
        rows = pl.ds(pl.multiple_of(c * step, 16), step)
        k_ref[rows, :] = dot_nt(tok_ref[rows, :], matrix(wk_ref)).astype(BF16)
        v_ref[rows, :] = dot_nt(tok_ref[rows, :], matrix(wv_ref)).astype(BF16)
        return carry

    lax.fori_loop(0, 4, project, 0)
    chunks = chunk_list(keys - cap, cap, 256)

    def pair(p, carry):
        cols = pl.ds(pl.multiple_of(p * PAIR, PAIR), PAIR)
        q2 = two_heads(q_ref[:, cols])
        peak = None
        for start, size in chunks:
            rows = pl.ds(start, size)
            s = dot_nt(k_ref[rows, cols], q2)
            if start == keys - cap:
                mask = mask_ref[...]
                s = jnp.where(jnp.concatenate([mask, mask], axis=1) > 0.5, s, -1e30)
            s_scr[rows, :] = s
            top = jnp.max(s, axis=0, keepdims=True)
            peak = top if peak is None else jnp.maximum(peak, top)
        total = jnp.zeros_like(peak)
        out = jnp.zeros((PAIR, q2.shape[0]), F32)
        for start, size in chunks:
            rows = pl.ds(start, size)
            e = jnp.exp(s_scr[rows, :] - peak)
            total = total + jnp.sum(e, axis=0, keepdims=True)
            out = out + dot_tn(v_ref[rows, cols], e.astype(BF16))
        o_ref[:, cols] = from_two_heads(out / total)
        lse_ref[pl.ds(p, 1), :] = peak + jnp.log(total)
        return carry

    lax.fori_loop(0, width // PAIR, pair, 0)


def backward_kernel(
    s_ref, q_ref, k_ref, v_ref, lse_ref, o_ref, datt_ref, own_ref, other_ref, cap_ref, mask_ref,
    wk_ref, wv_ref, gain_ref, tok_ref,
    dq_ref, gk_ref, gv_ref, own_out, other_out, cap_out, gain_out, dk_ref, dv_ref,
):
    item = pl.program_id(0)
    keys = k_ref.shape[0]
    cap = mask_ref.shape[0]
    chunks = chunk_list(keys - cap, cap, 256)

    def pair(p, carry):
        cols = pl.ds(pl.multiple_of(p * PAIR, PAIR), PAIR)
        q2 = two_heads(q_ref[:, cols])
        d_att = datt_ref[:, cols]
        d2 = two_heads(d_att)
        prod = (d_att.astype(F32) * o_ref[:, cols]).T
        delta = jnp.concatenate(
            [
                jnp.sum(prod[: PAIR // 2], axis=0, keepdims=True),
                jnp.sum(prod[PAIR // 2 :], axis=0, keepdims=True),
            ],
            axis=1,
        )
        pairs_here = D // PAIR // lse_ref.shape[0]
        lse = lse_ref[p // pairs_here, pl.ds(p % pairs_here, 1), :]
        dq = jnp.zeros((PAIR, q2.shape[0]), F32)
        for start, size in chunks:
            rows = pl.ds(start, size)
            k = k_ref[rows, cols]
            s = dot_nt(k, q2)
            d_probs = dot_nt(v_ref[rows, cols], d2)
            if start == keys - cap:
                mask = mask_ref[...]
                s = jnp.where(jnp.concatenate([mask, mask], axis=1) > 0.5, s, -1e30)
            probs = jnp.exp(s - lse)
            d_scores = (probs * (d_probs - delta)).astype(BF16)
            dv_ref[rows, cols] = dot_nn(probs.astype(BF16), d2).astype(BF16)
            dk_ref[rows, cols] = dot_nn(d_scores, q2).astype(BF16)
            dq = dq + dot_tn(k, d_scores)
        dq_ref[:, cols] = (from_two_heads(dq) * 0.125).astype(BF16)
        return carry

    lax.fori_loop(0, D // PAIR, pair, 0)
    gain = gain_ref[...]

    @pl.when(item == 0)
    def _():
        gain_out[...] = jnp.zeros_like(gain_out)
        gk_ref[...] = jnp.zeros_like(gk_ref)
        gv_ref[...] = jnp.zeros_like(gv_ref)

    window = pl.ds(pl.multiple_of(s_ref[2], PAIR), gk_ref.shape[0])
    gk_ref[...] += dot_tn(dk_ref[:, window], tok_ref[...])
    gv_ref[...] += dot_tn(dv_ref[:, window], tok_ref[...])

    start = 0
    for ref, out, size in ((own_ref, own_out, 256), (other_ref, other_out, 256), (cap_ref, cap_out, cap)):
        def chunk(c, carry, ref=ref, out=out, size=size, start=start):
            rows = pl.ds(pl.multiple_of(c * size, 16), size)
            key_rows = pl.ds(pl.multiple_of(start + c * size, 16), size)
            up = dot_nn(dk_ref[key_rows, :], square(wk_ref)) + dot_nn(
                dv_ref[key_rows, :], square(wv_ref)
            )
            x = ref[rows, :].astype(F32)
            center = x - jnp.mean(x, axis=-1, keepdims=True)
            rate = lax.rsqrt(jnp.mean(center * center, axis=-1, keepdims=True) + 1e-05)
            hat = center * rate
            gain_out[pl.ds(0, 1), :] += jnp.sum(up * hat, axis=0, keepdims=True)
            scaled = up * gain
            first = jnp.mean(scaled, axis=-1, keepdims=True)
            second = jnp.mean(scaled * hat, axis=-1, keepdims=True)
            out[rows, :] = (rate * (scaled - first - hat * second)).astype(out.dtype)
            return carry

        lax.fori_loop(0, ref.shape[0] // size, chunk, 0)
        start += ref.shape[0]


def place_kernel(s_ref, whole_ref, part_ref, out_ref):
    out_ref[...] = part_ref[...].astype(out_ref.dtype)


def local(
    latents,
    video_tokens,
    caption_tokens,
    caption_len,
    key_mask,
    drop_flags,
    gain_latent,
    gain_tokens,
    gain_mlp,
    query_weight,
    key_matrix,
    value_matrix,
    out_weight,
    up_weight,
    down_weight,
    cotangent,
):
    txt_count = lax.axis_size("txt")
    head_count = lax.axis_size("head")
    core = lax.axis_index("vid")
    place = lax.axis_index("txt")
    z = lax.axis_index("head")
    items_here = latents.shape[0]
    own = items_here // 2
    lat_half = latents.shape[1]
    lat_rows = 2 * lat_half
    video_here = video_tokens.shape[1]
    cap_here = caption_tokens.shape[1]
    cap_rows = cap_here * txt_count
    keys_here = 2 * video_here + cap_rows
    head_width = query_weight.shape[1]

    def dot(spec, a, b):
        return jnp.einsum(spec, a, b, preferred_element_type=F32)

    packed = jnp.stack([query_weight.T, key_matrix.T, value_matrix.T, out_weight])
    half = take_block(packed, core, 2)
    up1 = lax.ppermute(half, "head", [(0, 1), (1, 2), (2, 3)])
    down1 = lax.ppermute(half, "head", [(1, 0), (2, 1), (3, 2)])
    partner = jnp.where(z % 2 == 1, up1, down1)
    near_at = z // 2
    zero = jnp.int32(0)
    own_at = z % 2
    part_shape = (2, 2, 2, head_width, D)

    def place_chunk(whole, chunk, at_core, at_chunk):
        chunk = chunk.reshape((-1, 1) + chunk.shape[-3:])
        return lax.dynamic_update_slice(whole, chunk, (at_core, at_chunk, zero, zero, zero))

    near = jnp.zeros(part_shape, BF16)
    near = place_chunk(near, packed.reshape((2, 2) + packed.shape[1:]), zero, own_at)
    near = place_chunk(near, partner, core, 1 - own_at)
    near = place_chunk(near, swap_cores(partner), 1 - core, 1 - own_at)
    up1, down1, half_then = lax.optimization_barrier((up1, down1, half))
    up2 = lax.ppermute(up1, "head", [(1, 2), (2, 3)])
    down2 = lax.ppermute(down1, "head", [(1, 0), (2, 1)])
    up3 = lax.ppermute(half_then, "head", [(0, 3)])
    down3 = lax.ppermute(half_then, "head", [(3, 0)])

    def by_place(*choices):
        low = jnp.where(z == 0, choices[0], choices[1])
        return jnp.where(z < 2, low, jnp.where(z == 2, choices[2], choices[3]))

    far_mine = jnp.stack([by_place(down2, down1, up2, up3), by_place(down3, down2, up1, up2)])
    far = jnp.zeros(part_shape, BF16)
    far = lax.dynamic_update_index_in_dim(far, far_mine, core, 0)
    far = lax.dynamic_update_index_in_dim(far, swap_cores(far_mine), 1 - core, 0)
    weights = jnp.zeros((2,) + part_shape, BF16)
    weights = lax.dynamic_update_index_in_dim(weights, near, near_at, 0)
    weights = lax.dynamic_update_index_in_dim(weights, far, 1 - near_at, 0)

    video_other = swap_cores(take_block(video_tokens, 1 - core, own))
    both = jnp.concatenate([latents, cotangent], axis=1)
    both_own = take_block(both, core, own)
    both_other = swap_cores(take_block(both, 1 - core, own))
    lat = jnp.concatenate([both_own[:, :lat_half], both_other[:, :lat_half]], axis=1)
    cot = jnp.concatenate([both_own[:, lat_half:], both_other[:, lat_half:]], axis=1)
    drop_own = take_block(drop_flags, core, own)
    keep = (1 - drop_own).astype(F32)
    window = z * head_width // PAIR * PAIR
    scalars = jnp.stack([core, near_at, window])
    scalars_far = jnp.stack([core, 1 - near_at, window])

    place_slots = place * cap_here + jnp.arange(cap_here, dtype=jnp.int32)
    cap_valid = (place_slots[None, :] < caption_len[:, None]) & (key_mask == 1)
    cap_flags = jnp.zeros((caption_tokens.shape[0], 1, D), BF16)
    cap_flags = cap_flags.at[:, 0, :cap_here].set(cap_valid.astype(BF16))
    cap_message = jnp.concatenate([caption_tokens, cap_flags], axis=1)
    cap_parts = []
    for step in range(txt_count):
        block = take_block(cap_message, (place + step) % txt_count, own)
        cap_parts.append(
            lax.ppermute(block, ("vid", "txt"), caption_perm(step, 2, txt_count, 2))
        )
    cap = jnp.concatenate([part[:, :cap_here] for part in cap_parts], axis=1)
    valid = jnp.concatenate([part[:, cap_here, :cap_here] for part in cap_parts], axis=1)
    mask = jnp.broadcast_to(valid.astype(F32)[:, :, None], (own, cap_rows, lat_rows))

    def item_spec(rows, width=D):
        return pl.BlockSpec((None, rows, width), lambda i, s: (i, 0, 0))

    def own_spec(rows):
        return pl.BlockSpec((None, rows, D), lambda i, s: (s[0] * own + i, 0, 0))

    def weight_spec(m):
        return pl.BlockSpec(
            (2, None, 2, None, head_width, D),
            lambda i, s: (0, m // 2, 0, m % 2, 0, 0),
            pipeline_mode=pl.Buffered(1),
        )

    def part_spec(m):
        return pl.BlockSpec(
            (None, 2, None, head_width, D),
            lambda i, s: (m // 2, 0, m % 2, 0, 0),
            pipeline_mode=pl.Buffered(1),
        )

    def half_spec(rows):
        return pl.BlockSpec((None, rows, 2 * head_width), lambda i, s: (i, 0, s[1]))

    row_spec = pl.BlockSpec((1, D), lambda i, s: (0, 0))

    def call(kernel, name, ins, outs, operands, micros, scratch=(), aliases={}, scalars=scalars):
        return pl.pallas_call(
            kernel,
            name=name,
            grid_spec=pltpu.PrefetchScalarGridSpec(
                num_scalar_prefetch=1,
                grid=(own,),
                in_specs=ins,
                out_specs=[spec for spec, _, _ in outs],
                scratch_shapes=list(scratch),
            ),
            out_shape=[jax.ShapeDtypeStruct(shape, dtype) for _, shape, dtype in outs],
            input_output_aliases=aliases,
            cost_estimate=pl.CostEstimate(
                flops=micros * 1100 * 10**6, transcendentals=0, bytes_accessed=micros * 10**6
            ),
            compiler_params=pltpu.CompilerParams(vmem_limit_bytes=56 << 20),
        )(scalars, *operands)

    def item_out(rows, dtype, width=D):
        return (item_spec(rows, width), (own, rows, width), dtype)

    gain_lat_row = gain_latent[None]
    gain_tok_row = gain_tokens[None]
    gain_mlp_row = gain_mlp[None]
    tok_norm, lat_norm = call(
        norm_kernel,
        "token_norm",
        [own_spec(video_here), item_spec(video_here), item_spec(cap_rows), item_spec(lat_rows)]
        + [row_spec, row_spec],
        [item_out(keys_here, BF16), item_out(lat_rows, BF16)],
        (video_tokens, video_other, cap, lat, gain_tok_row, gain_lat_row),
        9,
    )

    def forward(part, scalars, before=()):
        return call(
            forward_kernel,
            "attention_forward",
            [item_spec(keys_here), item_spec(lat_rows), item_spec(cap_rows, lat_rows)]
            + [part_spec(m) for m in range(3)]
            + [pl.BlockSpec(memory_space=pl.ANY)] * len(before),
            [
                (half_spec(lat_rows), (own, lat_rows, D), BF16),
                (half_spec(keys_here), (own, keys_here, D), BF16),
                (half_spec(keys_here), (own, keys_here, D), BF16),
                (
                    pl.BlockSpec((None, None, 8, 2 * lat_rows), lambda i, s: (i, s[1], 0, 0)),
                    (own, 2, 8, 2 * lat_rows),
                    F32,
                ),
                (half_spec(lat_rows), (own, lat_rows, D), F32),
            ],
            (tok_norm, lat_norm, mask, part, part, part) + tuple(before),
            23,
            [pltpu.VMEM((keys_here, 2 * lat_rows), F32)],
            {7 + n: n for n in range(len(before))},
            scalars,
        )

    queries, keys, values, lse, attended = forward(far, scalars_far, forward(near, scalars))
    w_query = weights[:, 0, :, 0].reshape(D, D)
    w_out = weights[:, 1, :, 1].reshape(D, D)
    lat_float = lat.astype(F32)
    mixed_in = (attended * keep[:, None, None]).astype(BF16)
    after_attn = lat_float + dot("ble,ed->bld", mixed_in, w_out)
    mlp_norm = layer_norm(after_attn, gain_mlp).astype(BF16)

    pre_act = dot("bld,df->blf", mlp_norm, up_weight)
    activ, gelu_pull = jax.vjp(gelu_exact, pre_act)
    activ = activ.astype(BF16)
    d_pre = gelu_pull(dot("bld,fd->blf", cot, down_weight))[0].astype(BF16)
    d_mlp_norm = sum_over_head(dot("blf,df->bld", d_pre, up_weight), z, head_count)
    activ, d_mlp_norm = lax.optimization_barrier((activ, d_mlp_norm))
    growth = lax.psum(dot("blf,fd->bld", activ, down_weight).astype(BF16), "head")
    grad_down = dot("blf,bld->fd", activ, cot)
    grad_up = dot("bld,blf->df", mlp_norm, d_pre)

    d_after_norm, gain_mlp_part = norm_back_rows(after_attn, gain_mlp, d_mlp_norm.astype(F32))
    d_after = cot.astype(F32) + d_after_norm
    d_branch = d_after.astype(BF16)
    d_att = (dot("bld,ed->ble", d_branch, w_out) * keep[:, None, None]).astype(BF16)
    d_queries, key_rows, value_rows, video_grad, other_back, cap_back, gain_tok_part = call(
        backward_kernel,
        "attention_backward",
        [
            item_spec(lat_rows),
            item_spec(keys_here),
            item_spec(keys_here),
            pl.BlockSpec((None, 2, 8, 2 * lat_rows), lambda i, s: (i, 0, 0, 0)),
            item_spec(lat_rows),
            item_spec(lat_rows),
            own_spec(video_here),
            item_spec(video_here),
            item_spec(cap_rows),
            item_spec(cap_rows, lat_rows),
            weight_spec(1),
            weight_spec(2),
            row_spec,
            item_spec(keys_here),
        ],
        [
            item_out(lat_rows, BF16),
            (pl.BlockSpec((2 * PAIR, D), lambda i, s: (0, 0)), (2 * PAIR, D), F32),
            (pl.BlockSpec((2 * PAIR, D), lambda i, s: (0, 0)), (2 * PAIR, D), F32),
            (own_spec(video_here), video_tokens.shape, F32),
            item_out(video_here, BF16),
            item_out(cap_rows, BF16),
            (pl.BlockSpec((8, D), lambda i, s: (0, 0)), (8, D), F32),
        ],
        (
            queries, keys, values, lse, attended, d_att, video_tokens, video_other, cap, mask,
            weights, weights, gain_tok_row, tok_norm,
        ),
        58,
        [pltpu.VMEM((keys_here, D), BF16), pltpu.VMEM((keys_here, D), BF16)],
    )
    growth, d_queries = lax.optimization_barrier((growth, d_queries))
    out_mine = (after_attn + growth.astype(F32)).astype(BF16)
    other_here = swap_cores(other_back)
    (video_grad,) = call(
        place_kernel,
        "place_rows",
        [pl.BlockSpec(memory_space=pl.ANY), item_spec(video_here)],
        [
            (
                pl.BlockSpec((None, video_here, D), lambda i, s: ((1 - s[0]) * own + i, 0, 0)),
                video_tokens.shape,
                F32,
            )
        ],
        (video_grad, other_here),
        6,
        aliases={1: 0},
    )
    caption_grad = jnp.zeros((txt_count, own, cap_here, D), F32)
    for step in range(txt_count):
        perm = [(b, a) for a, b in caption_perm(step, 2, txt_count, 2)]
        part = lax.ppermute(
            cap_back[:, step * cap_here : (step + 1) * cap_here], ("vid", "txt"), perm
        )
        caption_grad = lax.dynamic_update_index_in_dim(
            caption_grad, part.astype(F32), (place + step) % txt_count, 0
        )
    caption_grad = caption_grad.reshape(caption_tokens.shape)

    d_lat_norm = dot("ble,ed->bld", d_queries, w_query)
    d_lat_back, gain_lat_part = norm_back_rows(lat_float, gain_latent, d_lat_norm)
    lat_grad_mine = d_after + d_lat_back

    def mine_cols(array):
        return lax.dynamic_slice_in_dim(array, z * head_width, head_width, array.ndim - 1)

    def mine_rows(rows):
        return lax.dynamic_slice_in_dim(rows, z * head_width - window, head_width, 0)

    grad_up, grad_down = lax.psum((grad_up.astype(BF16), grad_down.astype(BF16)), ("vid", "txt"))
    grad_out = dot("ble,bld->ed", mine_cols(mixed_in), d_branch)
    grad_query = dot("ble,bld->ed", mine_cols(d_queries), lat_norm)
    gains = jnp.stack(
        [
            jnp.sum(gain_lat_part, axis=0),
            gain_tok_part[0],
            jnp.sum(gain_mlp_part, axis=0),
            jnp.full((D,), jnp.sum(keep)),
        ]
    )
    count = 4 * head_width + gains.shape[0]
    spare = jnp.zeros((-count % (32 * txt_count), D), F32)
    late = jnp.concatenate(
        [grad_query, mine_rows(key_rows), mine_rows(value_rows), grad_out, gains, spare]
    )
    late = sum_over_group(late, core, place, txt_count).astype(F32)
    gains = late[4 * head_width :]

    def give_back(values):
        other = swap_cores(values[:, lat_half:].astype(BF16)).astype(values.dtype)
        whole = jnp.zeros((items_here, lat_half, D), values.dtype)
        whole = lax.dynamic_update_slice_in_dim(whole, values[:, :lat_half], core * own, 0)
        return lax.dynamic_update_slice_in_dim(whole, other, (1 - core) * own, 0)

    latents_out = give_back(out_mine)
    latent_grad = give_back(lat_grad_mine)
    kept_count = gains[3, 0].astype(jnp.int32)
    return (
        latents_out,
        latent_grad,
        video_grad,
        caption_grad,
        late[:head_width].T,
        late[head_width : 2 * head_width].T,
        late[2 * head_width : 3 * head_width].T,
        late[3 * head_width : 4 * head_width],
        grad_up.astype(F32),
        grad_down.astype(F32),
        gains[0],
        gains[1],
        gains[2],
        kept_count,
    )


def norm_back_rows(values, gain, upstream):
    mean = jnp.mean(values, axis=-1, keepdims=True)
    center = values - mean
    rate = lax.rsqrt(jnp.mean(center * center, axis=-1, keepdims=True) + 1e-05)
    hat = center * rate
    scaled = upstream * gain
    first = jnp.mean(scaled, axis=-1, keepdims=True)
    second = jnp.mean(scaled * hat, axis=-1, keepdims=True)
    return rate * (scaled - first - hat * second), jnp.sum(upstream * hat, axis=-2)


def fits(mesh):
    shape = mesh.shape
    return shape["vid"] == 2 and shape["txt"] == 4 and shape["head"] == 4


def solution(mesh):
    in_specs = (
        P("txt", "vid", None),
        P("txt", "vid", None),
        P("vid", "txt", None),
        P("vid"),
        P("vid", "txt"),
        P("txt"),
        P(),
        P(),
        P(),
        P(None, "head"),
        P(None, "head"),
        P(None, "head"),
        P("head", None),
        P(None, "head"),
        P("head", None),
        P("txt", "vid", None),
    )
    out_specs = (
        P("txt", "vid", None),
        P("txt", "vid", None),
        P("txt", "vid", None),
        P("vid", "txt", None),
        P(None, "head"),
        P(None, "head"),
        P(None, "head"),
        P("head", None),
        P(None, "head"),
        P("head", None),
        P(),
        P(),
        P(),
        P(),
    )
    return jax.shard_map(local if fits(mesh) else local_general, mesh=mesh, in_specs=in_specs, out_specs=out_specs, check_vma=False)
```

```python
import functools
import math

import jax
import jax.numpy as jnp
from jax import lax
from jax.experimental import pallas as pl
from jax.experimental.pallas import tpu as pltpu
from jax.sharding import PartitionSpec as P

D = 768
HEADS = 12


def combined_all(part, axis, combine):
    gathered = jax.tree.map(lambda a: lax.all_gather(a, axis), part)

    def take(source):
        return jax.tree.map(lambda a: lax.dynamic_index_in_dim(a, source, 0, False), gathered)

    return lax.fori_loop(
        1, lax.axis_size(axis), lambda source, state: combine(state, take(source)), take(0)
    )


def layer_norm(values, gain):
    center = values - jnp.mean(values, axis=-1, keepdims=True)
    spread = jnp.mean(center * center, axis=-1, keepdims=True)
    return center * lax.rsqrt(spread + 1e-05) * gain


def norm_back(values, gain, upstream):
    result, pullback = jax.vjp(layer_norm, values, gain)
    return pullback(upstream)


def gelu_exact(values):
    return jax.nn.gelu(values, approximate=False)


def combine_stats(first, second):
    peak = jnp.maximum(first[0], second[0])
    total = first[1] * jnp.exp(first[0] - peak) + second[1] * jnp.exp(second[0] - peak)
    return (peak, total)


def to_blocks(whole, vid_count, txt_count):
    items, rows, width = whole.shape
    split = whole.reshape(txt_count, items // txt_count, vid_count, rows // vid_count, width)
    return split.transpose(2, 0, 1, 3, 4).reshape(
        vid_count * txt_count, items // txt_count, rows // vid_count, width
    )


def from_blocks(blocked, vid_count, txt_count):
    count, items_here, rows_here, width = blocked.shape
    split = blocked.reshape(vid_count, txt_count, items_here, rows_here, width)
    return split.transpose(1, 2, 0, 3, 4).reshape(
        txt_count * items_here, vid_count * rows_here, width
    )


def place_sum(whole, part, start):
    current = lax.dynamic_slice_in_dim(whole, start, part.shape[0], 0)
    return lax.dynamic_update_slice_in_dim(whole, current + part, start, 0)


def place_stats(peak_all, total_all, peak, total, start):
    old_peak = lax.dynamic_slice_in_dim(peak_all, start, peak.shape[0], 0)
    old_total = lax.dynamic_slice_in_dim(total_all, start, peak.shape[0], 0)
    new_peak, new_total = combine_stats((old_peak, old_total), (peak, total))
    peak_all = lax.dynamic_update_slice_in_dim(peak_all, new_peak, start, 0)
    total_all = lax.dynamic_update_slice_in_dim(total_all, new_total, start, 0)
    return (peak_all, total_all)


def take_rows(whole, start, count):
    return lax.dynamic_slice_in_dim(whole, start, count, 0)


def local_general(
    latents,
    video_tokens,
    caption_tokens,
    caption_len,
    key_mask,
    drop_flags,
    gain_latent,
    gain_tokens,
    gain_mlp,
    query_weight,
    key_matrix,
    value_matrix,
    out_weight,
    up_weight,
    down_weight,
    cotangent,
):
    vid_count = lax.axis_size("vid")
    txt_count = lax.axis_size("txt")
    vid_index = lax.axis_index("vid")
    txt_index = lax.axis_index("txt")
    items_here = latents.shape[0]
    cap_items = caption_tokens.shape[0]
    items_total = items_here * txt_count
    head_width = query_weight.shape[1]
    head_size = D // HEADS
    heads_here = head_width // head_size
    scale = 1.0 / math.sqrt(head_size)
    video_here = video_tokens.shape[1]
    cap_here = caption_tokens.shape[1]
    video_start = txt_index * items_here
    cap_start = vid_index * cap_items
    keep = (1 - drop_flags).astype(jnp.float32)
    slots = txt_index * cap_here + jnp.arange(cap_here, dtype=jnp.int32)
    cap_valid = (slots[None, :] < caption_len[:, None]) & (key_mask == 1)
    cap_mask = cap_valid[:, None, None, :]

    def split_heads(values):
        return values.reshape(values.shape[0], values.shape[1], heads_here, head_size)

    lat_float = latents.astype(jnp.float32)
    lat_norm = layer_norm(lat_float, gain_latent).astype(jnp.bfloat16)
    queries = jnp.einsum(
        "bld,de->ble", lat_norm, query_weight, preferred_element_type=jnp.float32
    ).astype(jnp.bfloat16)
    all_queries = from_blocks(
        lax.all_gather(queries[None], ("vid", "txt"), axis=0, tiled=True), vid_count, txt_count
    )
    lat_total = all_queries.shape[1]
    video_queries = take_rows(all_queries, video_start, items_here)
    cap_queries = take_rows(all_queries, cap_start, cap_items)
    video_float = video_tokens.astype(jnp.float32)
    cap_float = caption_tokens.astype(jnp.float32)
    video_normed = layer_norm(video_float, gain_tokens).astype(jnp.bfloat16)
    caption_normed = layer_norm(cap_float, gain_tokens).astype(jnp.bfloat16)
    video_keys = jnp.einsum(
        "flc,co->flo", video_normed, key_matrix, preferred_element_type=jnp.float32
    ).astype(jnp.bfloat16)
    video_values = jnp.einsum(
        "flc,co->flo", video_normed, value_matrix, preferred_element_type=jnp.float32
    ).astype(jnp.bfloat16)
    cap_keys = jnp.einsum(
        "flc,co->flo", caption_normed, key_matrix, preferred_element_type=jnp.float32
    ).astype(jnp.bfloat16)
    cap_values = jnp.einsum(
        "flc,co->flo", caption_normed, value_matrix, preferred_element_type=jnp.float32
    ).astype(jnp.bfloat16)
    video_scores = (
        jnp.einsum(
            "blhe,bkhe->bhlk",
            split_heads(video_queries),
            split_heads(video_keys),
            preferred_element_type=jnp.float32,
        )
        * scale
    )
    cap_scores = (
        jnp.einsum(
            "blhe,bkhe->bhlk",
            split_heads(cap_queries),
            split_heads(cap_keys),
            preferred_element_type=jnp.float32,
        )
        * scale
    )
    cap_scores = jnp.where(cap_mask, cap_scores, -1e30)
    video_peak = jnp.max(video_scores, axis=-1)
    video_total = jnp.sum(jnp.exp(video_scores - video_peak[..., None]), axis=-1)
    cap_peak = jnp.max(cap_scores, axis=-1)
    cap_total = jnp.sum(
        jnp.where(cap_mask, jnp.exp(cap_scores - cap_peak[..., None]), 0.0), axis=-1
    )
    peak_all = jnp.full((items_total, heads_here, lat_total), -1e30, jnp.float32)
    total_all = jnp.zeros((items_total, heads_here, lat_total), jnp.float32)
    peak_all, total_all = place_stats(peak_all, total_all, video_peak, video_total, video_start)
    peak_all, total_all = place_stats(peak_all, total_all, cap_peak, cap_total, cap_start)
    peak, total = combined_all((peak_all, total_all), ("vid", "txt"), combine_stats)
    video_probs = (
        jnp.exp(video_scores - take_rows(peak, video_start, items_here)[..., None])
        / take_rows(total, video_start, items_here)[..., None]
    )
    cap_probs = jnp.where(
        cap_mask,
        jnp.exp(cap_scores - take_rows(peak, cap_start, cap_items)[..., None])
        / take_rows(total, cap_start, cap_items)[..., None],
        0.0,
    )
    video_low = video_probs.astype(jnp.bfloat16)
    cap_low = cap_probs.astype(jnp.bfloat16)
    video_part = jnp.einsum(
        "bhlk,bkhe->blhe", video_low, split_heads(video_values), preferred_element_type=jnp.float32
    ).reshape(items_here, lat_total, head_width)
    cap_part = jnp.einsum(
        "bhlk,bkhe->blhe", cap_low, split_heads(cap_values), preferred_element_type=jnp.float32
    ).reshape(cap_items, lat_total, head_width)
    value_all = jnp.zeros((items_total, lat_total, head_width), jnp.float32)
    value_all = place_sum(place_sum(value_all, video_part, video_start), cap_part, cap_start)
    attended = lax.psum_scatter(
        to_blocks(value_all, vid_count, txt_count), ("vid", "txt"), scatter_dimension=0, tiled=True
    )[0]
    mixed_in = (attended * keep[:, None, None]).astype(jnp.bfloat16)
    branch = lax.psum(
        jnp.einsum("ble,ed->bld", mixed_in, out_weight, preferred_element_type=jnp.float32), "head"
    )
    after_attn = lat_float + branch
    mlp_norm = layer_norm(after_attn, gain_mlp).astype(jnp.bfloat16)
    pre_act = jnp.einsum("bld,df->blf", mlp_norm, up_weight, preferred_element_type=jnp.float32)
    activ = gelu_exact(pre_act).astype(jnp.bfloat16)
    growth = lax.psum(
        jnp.einsum("blf,fd->bld", activ, down_weight, preferred_element_type=jnp.float32).astype(
            jnp.bfloat16
        ),
        "head",
    ).astype(jnp.float32)
    latents_out = (after_attn + growth).astype(jnp.bfloat16)
    grad_down = jnp.einsum("blf,bld->fd", activ, cotangent, preferred_element_type=jnp.float32)
    d_activ = jnp.einsum("bld,fd->blf", cotangent, down_weight, preferred_element_type=jnp.float32)
    d_pre = jax.vjp(gelu_exact, pre_act)[1](d_activ)[0].astype(jnp.bfloat16)
    grad_up = jnp.einsum("bld,blf->df", mlp_norm, d_pre, preferred_element_type=jnp.float32)
    d_mlp_norm = lax.psum(
        jnp.einsum("blf,df->bld", d_pre, up_weight, preferred_element_type=jnp.float32), "head"
    )
    d_after_norm, grad_gain_mlp = norm_back(after_attn, gain_mlp, d_mlp_norm)
    d_after = cotangent.astype(jnp.float32) + d_after_norm
    d_branch = d_after.astype(jnp.bfloat16)
    grad_out = jnp.einsum("ble,bld->ed", mixed_in, d_branch, preferred_element_type=jnp.float32)
    d_att = (
        jnp.einsum("bld,ed->ble", d_branch, out_weight, preferred_element_type=jnp.float32)
        * keep[:, None, None]
    ).astype(jnp.bfloat16)
    all_d_att = from_blocks(
        lax.all_gather(d_att[None], ("vid", "txt"), axis=0, tiled=True), vid_count, txt_count
    )
    video_d_att = split_heads(take_rows(all_d_att, video_start, items_here))
    cap_d_att = split_heads(take_rows(all_d_att, cap_start, cap_items))
    video_dprobs = jnp.einsum(
        "blhe,bkhe->bhlk",
        video_d_att,
        split_heads(video_values),
        preferred_element_type=jnp.float32,
    )
    cap_dprobs = jnp.einsum(
        "blhe,bkhe->bhlk", cap_d_att, split_heads(cap_values), preferred_element_type=jnp.float32
    )
    delta_all = jnp.zeros((items_total, heads_here, lat_total), jnp.float32)
    delta_all = place_sum(delta_all, jnp.sum(video_probs * video_dprobs, axis=-1), video_start)
    delta_all = place_sum(delta_all, jnp.sum(cap_probs * cap_dprobs, axis=-1), cap_start)
    delta = lax.psum(delta_all, ("vid", "txt"))
    video_dscores = (
        video_probs * (video_dprobs - take_rows(delta, video_start, items_here)[..., None])
    ).astype(jnp.bfloat16)
    cap_dscores = (
        cap_probs * (cap_dprobs - take_rows(delta, cap_start, cap_items)[..., None])
    ).astype(jnp.bfloat16)
    video_dq = (
        jnp.einsum(
            "bhlk,bkhe->blhe",
            video_dscores,
            split_heads(video_keys),
            preferred_element_type=jnp.float32,
        )
        * scale
    ).reshape(items_here, lat_total, head_width)
    cap_dq = (
        jnp.einsum(
            "bhlk,bkhe->blhe",
            cap_dscores,
            split_heads(cap_keys),
            preferred_element_type=jnp.float32,
        )
        * scale
    ).reshape(cap_items, lat_total, head_width)
    query_all = jnp.zeros((items_total, lat_total, head_width), jnp.float32)
    query_all = place_sum(place_sum(query_all, video_dq, video_start), cap_dq, cap_start)
    d_queries = lax.psum_scatter(
        to_blocks(query_all, vid_count, txt_count), ("vid", "txt"), scatter_dimension=0, tiled=True
    )[0].astype(jnp.bfloat16)
    video_key_grad = (
        (
            jnp.einsum(
                "bhlk,blhe->bkhe",
                video_dscores,
                split_heads(video_queries),
                preferred_element_type=jnp.float32,
            )
            * scale
        )
        .reshape(items_here, video_here, head_width)
        .astype(jnp.bfloat16)
    )
    video_value_grad = (
        jnp.einsum("bhlk,blhe->bkhe", video_low, video_d_att, preferred_element_type=jnp.float32)
        .reshape(items_here, video_here, head_width)
        .astype(jnp.bfloat16)
    )
    caption_key_grad = (
        (
            jnp.einsum(
                "bhlk,blhe->bkhe",
                cap_dscores,
                split_heads(cap_queries),
                preferred_element_type=jnp.float32,
            )
            * scale
        )
        .reshape(cap_items, cap_here, head_width)
        .astype(jnp.bfloat16)
    )
    caption_value_grad = (
        jnp.einsum("bhlk,blhe->bkhe", cap_low, cap_d_att, preferred_element_type=jnp.float32)
        .reshape(cap_items, cap_here, head_width)
        .astype(jnp.bfloat16)
    )
    grad_query = jnp.einsum("bld,ble->de", lat_norm, d_queries, preferred_element_type=jnp.float32)
    d_lat_norm = lax.psum(
        jnp.einsum("ble,de->bld", d_queries, query_weight, preferred_element_type=jnp.float32),
        "head",
    )
    d_lat_back, grad_gain_latent = norm_back(lat_float, gain_latent, d_lat_norm)
    latent_grad = d_after + d_lat_back
    grad_key = jnp.einsum(
        "zsg,zsv->gv", video_normed, video_key_grad, preferred_element_type=jnp.float32
    ) + jnp.einsum(
        "zsg,zsv->gv", caption_normed, caption_key_grad, preferred_element_type=jnp.float32
    )
    grad_value = jnp.einsum(
        "zsg,zsv->gv", video_normed, video_value_grad, preferred_element_type=jnp.float32
    ) + jnp.einsum(
        "zsg,zsv->gv", caption_normed, caption_value_grad, preferred_element_type=jnp.float32
    )
    video_term = jnp.einsum(
        "ayt,ot->ayo", video_key_grad, key_matrix, preferred_element_type=jnp.float32
    ) + jnp.einsum(
        "ayt,ot->ayo", video_value_grad, value_matrix, preferred_element_type=jnp.float32
    )
    cap_term = jnp.einsum(
        "ayt,ot->ayo", caption_key_grad, key_matrix, preferred_element_type=jnp.float32
    ) + jnp.einsum(
        "ayt,ot->ayo", caption_value_grad, value_matrix, preferred_element_type=jnp.float32
    )
    d_video_norm, d_cap_norm = lax.psum((video_term, cap_term), "head")
    video_grad, video_gain_part = norm_back(video_float, gain_tokens, d_video_norm)
    caption_grad, cap_gain_part = norm_back(cap_float, gain_tokens, d_cap_norm)
    grad_gain_tokens = video_gain_part + cap_gain_part
    kept_here = jnp.sum(keep)
    (
        grad_query,
        grad_key,
        grad_value,
        grad_out,
        grad_up,
        grad_down,
        grad_gain_latent,
        grad_gain_tokens,
        grad_gain_mlp,
        kept_total,
    ) = lax.psum(
        (
            grad_query,
            grad_key,
            grad_value,
            grad_out,
            grad_up,
            grad_down,
            grad_gain_latent,
            grad_gain_tokens,
            grad_gain_mlp,
            kept_here,
        ),
        ("vid", "txt"),
    )
    kept_count = (kept_total / vid_count).astype(jnp.int32)
    return (
        latents_out,
        latent_grad,
        video_grad,
        caption_grad,
        grad_query,
        grad_key,
        grad_value,
        grad_out,
        grad_up,
        grad_down,
        grad_gain_latent,
        grad_gain_tokens,
        grad_gain_mlp,
        kept_count,
    )


def swap_cores(values):
    return lax.ppermute(values, "vid", [(0, 1), (1, 0)])


def head_shift(values, shift, count):
    return lax.ppermute(values, "head", [(i, (i - shift) % count) for i in range(count)])


def take_block(values, index, size, axis=0):
    return lax.dynamic_slice_in_dim(values, index * size, size, axis)


def sum_over_head(part, place, count):
    low = part.astype(jnp.bfloat16)
    total = lax.dynamic_index_in_dim(part, place, 0, False)
    for shift in range(1, count):
        chunk = lax.dynamic_index_in_dim(low, (place - shift) % count, 0, False)
        total = total + head_shift(chunk, shift, count).astype(jnp.float32)
    total = total.astype(jnp.bfloat16)
    result = lax.dynamic_update_index_in_dim(jnp.zeros_like(low), total, place, 0)
    for shift in range(1, count):
        result = lax.dynamic_update_index_in_dim(
            result, head_shift(total, shift, count), (place + shift) % count, 0
        )
    return result


def group_steps(count):
    return [(step, [(i, (i - step) % count) for i in range(count)]) for step in range(1, count)]


def reduce_over_cores(rows, core):
    half = rows.shape[0] // 2
    other = swap_cores(take_block(rows, 1 - core, half))
    return take_block(rows, core, half).astype(F32) + other.astype(F32), other


def reduce_over_group(half, place, count):
    part = half.shape[0] // count
    low = half.astype(BF16)
    total = take_block(half, place, part)
    for step, perm in group_steps(count):
        chunk = take_block(low, (place - step) % count, part)
        total = total + lax.ppermute(chunk, "txt", perm).astype(F32)
    return total.astype(BF16)


def gather_group(total, core, place, count):
    part = total.shape[0]
    half = part * count
    mine = jnp.zeros((half, total.shape[1]), BF16)
    mine = lax.dynamic_update_slice_in_dim(mine, total, place * part, 0)
    for step, perm in group_steps(count):
        mine = lax.dynamic_update_slice_in_dim(
            mine, lax.ppermute(total, "txt", perm), (place + step) % count * part, 0
        )
    whole = jnp.zeros((2 * half, total.shape[1]), BF16)
    whole = lax.dynamic_update_slice_in_dim(whole, mine, core * half, 0)
    return lax.dynamic_update_slice_in_dim(whole, swap_cores(mine), (1 - core) * half, 0)


def caption_perm(step, vid_count, txt_count, cores):
    pairs = []
    for v in range(vid_count):
        for t in range(txt_count):
            block = (t + step) % txt_count
            dest_txt = v * (txt_count // vid_count) + block // cores
            dest_vid = block % cores
            pairs.append((v * txt_count + t, dest_vid * txt_count + dest_txt))
    return pairs


PAIR = 128
F32 = jnp.float32
BF16 = jnp.bfloat16


def dot_nt(a, b):
    return lax.dot_general(a, b, (((1,), (1,)), ((), ())), preferred_element_type=F32)


def dot_nn(a, b):
    return lax.dot_general(a, b, (((1,), (0,)), ((), ())), preferred_element_type=F32)


def dot_tn(a, b):
    return lax.dot_general(a, b, (((0,), (0,)), ((), ())), preferred_element_type=F32)


def square(ref):
    return ref[...].reshape(D, D)


def two_heads(values):
    low = lax.broadcasted_iota(jnp.int32, values.shape, 1) < PAIR // 2
    zero = jnp.zeros_like(values)
    return jnp.concatenate([jnp.where(low, values, zero), jnp.where(low, zero, values)], axis=0)


def from_two_heads(both):
    n = both.shape[1] // 2
    first = lax.broadcasted_iota(jnp.int32, (PAIR, n), 0) < PAIR // 2
    return jnp.where(first, both[:, :n], both[:, n:]).T


def chunk_list(video, cap, size):
    return [(start, size) for start in range(0, video, size)] + [(video, cap)]


def norm_kernel(s_ref, own_ref, other_ref, lat_ref, gain_ref, gain_lat_ref, out_ref, lat_out):
    gain = gain_ref[...]
    lat_out[...] = layer_norm(lat_ref[...].astype(F32), gain_lat_ref[...]).astype(BF16)
    start = 0
    for ref in (own_ref, other_ref):
        rows = ref.shape[0]
        for at in range(0, rows, 64):
            out_ref[pl.ds(start + at, 64), :] = layer_norm(
                ref[pl.ds(at, 64), :].astype(F32), gain
            ).astype(BF16)
        start += rows


def forward_kernel(
    s_ref, tok_ref, cap_ref, gain_ref, latn_ref, mask_ref, wq_ref, wk_ref, wv_ref, *refs
):
    q_ref, k_ref, v_ref, lse_ref, o_ref, s_scr = refs[-6:]
    keys, width = k_ref.shape
    cap = mask_ref.shape[0]
    step = (keys - cap) // 4

    def matrix(ref):
        return ref[...].reshape(width, D)

    q_ref[...] = (dot_nt(latn_ref[...], matrix(wq_ref)).astype(BF16).astype(F32) * 0.125).astype(BF16)

    def project(c, carry):
        rows = pl.ds(pl.multiple_of(c * step, 16), step)
        k_ref[rows, :] = dot_nt(tok_ref[rows, :], matrix(wk_ref)).astype(BF16)
        v_ref[rows, :] = dot_nt(tok_ref[rows, :], matrix(wv_ref)).astype(BF16)
        return carry

    lax.fori_loop(0, 4, project, 0)
    cap_rows = pl.ds(keys - cap, cap)
    cap_norm = layer_norm(cap_ref[...].astype(F32), gain_ref[...]).astype(BF16)
    k_ref[cap_rows, :] = dot_nt(cap_norm, matrix(wk_ref)).astype(BF16)
    v_ref[cap_rows, :] = dot_nt(cap_norm, matrix(wv_ref)).astype(BF16)
    chunks = chunk_list(keys - cap, cap, 256)

    def pair(p, carry):
        cols = pl.ds(pl.multiple_of(p * PAIR, PAIR), PAIR)
        q2 = two_heads(q_ref[:, cols])
        peak = None
        for start, size in chunks:
            rows = pl.ds(start, size)
            s = dot_nt(k_ref[rows, cols], q2)
            if start == keys - cap:
                mask = mask_ref[...]
                s = jnp.where(jnp.concatenate([mask, mask], axis=1) > 0.5, s, -1e30)
            s_scr[rows, :] = s
            top = jnp.max(s, axis=0, keepdims=True)
            peak = top if peak is None else jnp.maximum(peak, top)
        total = jnp.zeros_like(peak)
        out = jnp.zeros((PAIR, q2.shape[0]), F32)
        for start, size in chunks:
            rows = pl.ds(start, size)
            e = jnp.exp(s_scr[rows, :] - peak)
            total = total + jnp.sum(e, axis=0, keepdims=True)
            out = out + dot_tn(v_ref[rows, cols], e.astype(BF16))
        o_ref[:, cols] = from_two_heads(out / total)
        lse_ref[pl.ds(p, 1), :] = peak + jnp.log(total)
        return carry

    lax.fori_loop(0, width // PAIR, pair, 0)


def backward_kernel(
    first, s_ref, q_ref, k_ref, v_ref, lse_ref, o_ref, datt_ref, own_ref, other_ref, cap_ref, mask_ref,
    wk_ref, wv_ref, gain_ref, tok_ref, wq_ref, lat_ref, latn_ref, after_ref, gain_lat_ref, *refs
):
    if first:
        own_out, other_out, cap_out, lat_out, sums_ref, gain_out = refs[:6]
    else:
        sums_in, gain_in, ready_ref = refs[:3]
        own_out, other_out, cap_out, lat_out, late_ref = refs[5:10]
        sums_ref, gain_out = refs[-2:]
    dq_ref, dk_ref, dv_ref = refs[6:9] if first else refs[10:13]
    item = pl.program_id(0)
    keys = k_ref.shape[0]
    cap = mask_ref.shape[0]
    chunks = chunk_list(keys - cap, cap, 256)

    def pair(p, carry):
        cols = pl.ds(pl.multiple_of(p * PAIR, PAIR), PAIR)
        q2 = two_heads(q_ref[:, cols])
        d_att = datt_ref[:, cols]
        d2 = two_heads(d_att)
        prod = (d_att.astype(F32) * o_ref[:, cols]).T
        delta = jnp.concatenate(
            [
                jnp.sum(prod[: PAIR // 2], axis=0, keepdims=True),
                jnp.sum(prod[PAIR // 2 :], axis=0, keepdims=True),
            ],
            axis=1,
        )
        pairs_here = D // PAIR // lse_ref.shape[0]
        lse = lse_ref[p // pairs_here, pl.ds(p % pairs_here, 1), :]
        dq = jnp.zeros((PAIR, q2.shape[0]), F32)
        for start, size in chunks:
            rows = pl.ds(start, size)
            k = k_ref[rows, cols]
            s = dot_nt(k, q2)
            d_probs = dot_nt(v_ref[rows, cols], d2)
            if start == keys - cap:
                mask = mask_ref[...]
                s = jnp.where(jnp.concatenate([mask, mask], axis=1) > 0.5, s, -1e30)
            probs = jnp.exp(s - lse)
            d_scores = (probs * (d_probs - delta)).astype(BF16)
            dv_ref[rows, cols] = dot_nn(probs.astype(BF16), d2).astype(BF16)
            dk_ref[rows, cols] = dot_nn(d_scores, q2).astype(BF16)
            dq = dq + dot_tn(k, d_scores)
        dq_ref[:, cols] = (from_two_heads(dq) * 0.125).astype(BF16)
        return carry

    lax.fori_loop(0, D // PAIR, pair, 0)
    gain = gain_ref[...]

    @pl.when(item == 0)
    def _():
        gain_out[...] = jnp.zeros_like(gain_out) if first else gain_in[...]
        sums_ref[...] = jnp.zeros_like(sums_ref) if first else sums_in[...]

    window = pl.ds(pl.multiple_of(s_ref[2], PAIR), sums_ref.shape[1])
    video_rows = pl.ds(0, keys - cap)
    cap_rows = pl.ds(keys - cap, cap)
    cap_norm = layer_norm(cap_ref[...].astype(F32), gain).astype(BF16)
    sums_ref[0] += dot_tn(dq_ref[:, window], latn_ref[...])
    for n, ref in ((1, dk_ref), (2, dv_ref)):
        sums_ref[n] += dot_tn(ref[video_rows, window], tok_ref[...]) + dot_tn(
            ref[cap_rows, window], cap_norm
        )

    def norm_back(x, up, gain, row):
        center = x - jnp.mean(x, axis=-1, keepdims=True)
        rate = lax.rsqrt(jnp.mean(center * center, axis=-1, keepdims=True) + 1e-05)
        hat = center * rate
        gain_out[pl.ds(row, 1), :] += jnp.sum(up * hat, axis=0, keepdims=True)
        scaled = up * gain
        first = jnp.mean(scaled, axis=-1, keepdims=True)
        second = jnp.mean(scaled * hat, axis=-1, keepdims=True)
        return rate * (scaled - first - hat * second)

    half = lat_out.shape[0]
    lat_grad = after_ref[...] + norm_back(
        lat_ref[...].astype(F32), dot_nn(dq_ref[...], square(wq_ref)), gain_lat_ref[...], 1
    )
    lat_out[...] = lat_grad[:half]
    other_out[pl.ds(other_ref.shape[0], half), :] = lat_grad[half:].astype(BF16)

    start = 0
    for ref, out, size in ((own_ref, own_out, 256), (other_ref, other_out, 256), (cap_ref, cap_out, cap)):
        def chunk(c, carry, ref=ref, out=out, size=size, start=start):
            rows = pl.ds(pl.multiple_of(c * size, 16), size)
            key_rows = pl.ds(pl.multiple_of(start + c * size, 16), size)
            up = dot_nn(dk_ref[key_rows, :], square(wk_ref)) + dot_nn(
                dv_ref[key_rows, :], square(wv_ref)
            )
            back = norm_back(ref[rows, :].astype(F32), up, gain, 0)
            out[rows, :] = back.astype(out.dtype)
            return carry

        lax.fori_loop(0, ref.shape[0] // size, chunk, 0)
        start += ref.shape[0]

    if first:
        return

    @pl.when(item == pl.num_programs(0) - 1)
    def _():
        width = D // 4
        mine = pl.ds(pl.multiple_of(s_ref[3], PAIR // 2), width)
        for n in range(3):
            late_ref[pl.ds(n * width, width), :] = sums_ref[n, mine, :].astype(BF16)
        ready = ready_ref.shape[0]
        late_ref[pl.ds(3 * width, ready), :] = ready_ref[...]
        gains = jnp.concatenate([gain_out[...], jnp.zeros((8, D), F32)], axis=0)
        late_ref[pl.ds(3 * width + ready, 16), :] = gains.astype(BF16)
        spare = late_ref.shape[0] - 3 * width - ready - 16
        late_ref[pl.ds(3 * width + ready + 16, spare), :] = jnp.zeros((spare, D), BF16)


def place_kernel(s_ref, video_in, lat_in, video_part, lat_part, video_ref, lat_ref):
    video_ref[...] = video_part[...].astype(F32)

    @pl.when(pl.program_id(1) == 0)
    def _():
        lat_ref[...] = lat_part[...].astype(F32)


def local(
    latents,
    video_tokens,
    caption_tokens,
    caption_len,
    key_mask,
    drop_flags,
    gain_latent,
    gain_tokens,
    gain_mlp,
    query_weight,
    key_matrix,
    value_matrix,
    out_weight,
    up_weight,
    down_weight,
    cotangent,
):
    txt_count = lax.axis_size("txt")
    head_count = lax.axis_size("head")
    core = lax.axis_index("vid")
    place_index = lax.axis_index("txt")
    z = lax.axis_index("head")
    items_here = latents.shape[0]
    own = items_here // 2
    lat_half = latents.shape[1]
    lat_rows = 2 * lat_half
    video_here = video_tokens.shape[1]
    cap_here = caption_tokens.shape[1]
    cap_rows = cap_here * txt_count
    keys_here = 2 * video_here + cap_rows
    head_width = query_weight.shape[1]

    def dot(spec, a, b):
        return jnp.einsum(spec, a, b, preferred_element_type=F32)

    packed = jnp.stack([query_weight.T, key_matrix.T, value_matrix.T, out_weight])
    half = take_block(packed, core, 2)
    up1 = lax.ppermute(half, "head", [(0, 1), (1, 2), (2, 3)])
    down1 = lax.ppermute(half, "head", [(1, 0), (2, 1), (3, 2)])
    near_at = z // 2
    zero = jnp.int32(0)
    own_at = z % 2
    part_shape = (2, 2, 2, head_width, D)

    def place_chunk(whole, chunk, at_core, at_chunk):
        chunk = chunk.reshape((-1, 1) + chunk.shape[-3:])
        return lax.dynamic_update_slice(whole, chunk, (at_core, at_chunk, zero, zero, zero))

    video_other = swap_cores(take_block(video_tokens, 1 - core, own))
    both = jnp.concatenate([latents, cotangent], axis=1)
    both_own = take_block(both, core, own)
    both_other = swap_cores(take_block(both, 1 - core, own))
    lat = jnp.concatenate([both_own[:, :lat_half], both_other[:, :lat_half]], axis=1)
    cot = jnp.concatenate([both_own[:, lat_half:], both_other[:, lat_half:]], axis=1)
    drop_own = take_block(drop_flags, core, own)
    keep = (1 - drop_own).astype(F32)
    window = z * head_width // PAIR * PAIR
    inside = z * head_width - window
    scalars = jnp.stack([core, near_at, window, inside])
    scalars_far = jnp.stack([core, 1 - near_at, window, inside])

    place_slots = place_index * cap_here + jnp.arange(cap_here, dtype=jnp.int32)
    cap_valid = (place_slots[None, :] < caption_len[:, None]) & (key_mask == 1)
    cap_flags = jnp.zeros((caption_tokens.shape[0], 1, D), BF16)
    cap_flags = cap_flags.at[:, 0, :cap_here].set(cap_valid.astype(BF16))
    cap_message = jnp.concatenate([caption_tokens, cap_flags], axis=1)
    cap_parts = []
    for step in range(txt_count):
        block = take_block(cap_message, (place_index + step) % txt_count, own)
        cap_parts.append(
            lax.ppermute(block, ("vid", "txt"), caption_perm(step, 2, txt_count, 2))
        )
    cap = jnp.concatenate([part[:, :cap_here] for part in cap_parts], axis=1)
    valid = jnp.concatenate([part[:, cap_here, :cap_here] for part in cap_parts], axis=1)
    mask = jnp.broadcast_to(valid.astype(F32)[:, :, None], (own, cap_rows, lat_rows))

    def item_spec(rows, width=D, first=0):
        return pl.BlockSpec((None, rows, width), lambda i, s: (first + i, 0, 0))

    def own_spec(rows, first=0):
        return pl.BlockSpec((None, rows, D), lambda i, s: (s[0] * own + first + i, 0, 0))

    def whole_spec(*shape):
        return pl.BlockSpec(shape, lambda i, s: (0,) * len(shape))

    def weight_spec(m):
        return pl.BlockSpec(
            (2, None, 2, None, head_width, D),
            lambda i, s: (0, m // 2, 0, m % 2, 0, 0),
            pipeline_mode=pl.Buffered(1),
        )

    def part_spec(m):
        return pl.BlockSpec(
            (None, 2, None, head_width, D),
            lambda i, s: (m // 2, 0, m % 2, 0, 0),
            pipeline_mode=pl.Buffered(1),
        )

    def half_spec(rows):
        return pl.BlockSpec((None, rows, 2 * head_width), lambda i, s: (i, 0, s[1]))

    row_spec = pl.BlockSpec((1, D), lambda i, s: (0, 0))

    def call(kernel, name, ins, outs, operands, micros, scratch=(), aliases={}, scalars=scalars, grid=own):
        return pl.pallas_call(
            kernel,
            name=name,
            grid_spec=pltpu.PrefetchScalarGridSpec(
                num_scalar_prefetch=1,
                grid=(grid,),
                in_specs=ins,
                out_specs=[spec for spec, _, _ in outs],
                scratch_shapes=list(scratch),
            ),
            out_shape=[jax.ShapeDtypeStruct(shape, dtype) for _, shape, dtype in outs],
            input_output_aliases=aliases,
            cost_estimate=pl.CostEstimate(
                flops=micros * 1100 * 10**6, transcendentals=0, bytes_accessed=micros * 10**6
            ),
            compiler_params=pltpu.CompilerParams(vmem_limit_bytes=56 << 20),
        )(scalars, *operands)

    def item_out(rows, dtype, width=D):
        return (item_spec(rows, width), (own, rows, width), dtype)

    gain_lat_row = gain_latent[None]
    gain_tok_row = gain_tokens[None]
    gain_mlp_row = gain_mlp[None]
    tok_norm, lat_norm = call(
        norm_kernel,
        "token_norm",
        [own_spec(video_here), item_spec(video_here), item_spec(lat_rows), row_spec, row_spec],
        [item_out(2 * video_here, BF16), item_out(lat_rows, BF16)],
        (video_tokens, video_other, lat, gain_tok_row, gain_lat_row),
        9,
    )
    tok_norm, up1, down1 = lax.optimization_barrier((tok_norm, up1, down1))
    partner = jnp.where(z % 2 == 1, up1, down1)
    near = jnp.zeros(part_shape, BF16)
    near = place_chunk(near, packed.reshape((2, 2) + packed.shape[1:]), zero, own_at)
    near = place_chunk(near, partner, core, 1 - own_at)
    near = place_chunk(near, swap_cores(partner), 1 - core, 1 - own_at)

    half_then, _ = lax.optimization_barrier((half, up1))
    up2 = lax.ppermute(up1, "head", [(1, 2), (2, 3)])
    down2 = lax.ppermute(down1, "head", [(1, 0), (2, 1)])
    up3 = lax.ppermute(half_then, "head", [(0, 3)])
    down3 = lax.ppermute(half_then, "head", [(3, 0)])

    def forward(part, scalars, before=()):
        return call(
            forward_kernel,
            "attention_forward",
            [item_spec(2 * video_here), item_spec(cap_rows), row_spec, item_spec(lat_rows)]
            + [item_spec(cap_rows, lat_rows)]
            + [part_spec(m) for m in range(3)]
            + [pl.BlockSpec(memory_space=pl.ANY)] * len(before),
            [
                (half_spec(lat_rows), (own, lat_rows, D), BF16),
                (half_spec(keys_here), (own, keys_here, D), BF16),
                (half_spec(keys_here), (own, keys_here, D), BF16),
                (
                    pl.BlockSpec((None, None, 8, 2 * lat_rows), lambda i, s: (i, s[1], 0, 0)),
                    (own, 2, 8, 2 * lat_rows),
                    F32,
                ),
                (half_spec(lat_rows), (own, lat_rows, D), F32),
            ],
            (tok_norm, cap, gain_tok_row, lat_norm, mask, part, part, part) + tuple(before),
            23,
            [pltpu.VMEM((keys_here, 2 * lat_rows), F32)],
            {9 + n: n for n in range(len(before))},
            scalars,
        )

    before = forward(near, scalars)
    before, up2, down2, up3, down3 = lax.optimization_barrier((before, up2, down2, up3, down3))

    def by_place(*choices):
        low = jnp.where(z == 0, choices[0], choices[1])
        return jnp.where(z < 2, low, jnp.where(z == 2, choices[2], choices[3]))

    far_mine = jnp.stack([by_place(down2, down1, up2, up3), by_place(down3, down2, up1, up2)])
    far = jnp.zeros(part_shape, BF16)
    far = lax.dynamic_update_index_in_dim(far, far_mine, core, 0)
    far = lax.dynamic_update_index_in_dim(far, swap_cores(far_mine), 1 - core, 0)
    weights = jnp.zeros((2,) + part_shape, BF16)
    weights = lax.dynamic_update_index_in_dim(weights, near, near_at, 0)
    weights = lax.dynamic_update_index_in_dim(weights, far, 1 - near_at, 0)
    queries, keys, values, lse, attended = forward(far, scalars_far, before)
    w_query = weights[:, 0, :, 0].reshape(D, D)
    w_out = weights[:, 1, :, 1].reshape(D, D)
    lat_float = lat.astype(F32)
    mixed_in = (attended * keep[:, None, None]).astype(BF16)
    after_attn = lat_float + dot("ble,ed->bld", mixed_in, w_out)
    mlp_norm = layer_norm(after_attn, gain_mlp).astype(BF16)

    pre_act = dot("bld,df->blf", mlp_norm, up_weight)
    activ, gelu_pull = jax.vjp(gelu_exact, pre_act)
    activ = activ.astype(BF16)
    d_pre = gelu_pull(dot("bld,fd->blf", cot, down_weight))[0].astype(BF16)
    d_mlp_part = dot("blf,df->bld", d_pre, up_weight)
    d_mlp_part, activ, d_pre = lax.optimization_barrier((d_mlp_part, activ, d_pre))
    d_mlp_norm = sum_over_head(d_mlp_part, z, head_count)
    grad_down = dot("blf,bld->fd", activ, cot).astype(BF16)
    grad_up = dot("bld,blf->df", mlp_norm, d_pre).astype(BF16)
    activ, d_mlp_norm, grad_up, grad_down = lax.optimization_barrier(
        (activ, d_mlp_norm, grad_up, grad_down)
    )
    grad_up, grad_down = lax.psum((grad_up, grad_down), ("vid", "txt"))
    growth = lax.psum(dot("blf,fd->bld", activ, down_weight).astype(BF16), "head")

    d_after_norm, gain_mlp_part = norm_back_rows(after_attn, gain_mlp, d_mlp_norm.astype(F32))
    d_after = cot.astype(F32) + d_after_norm
    d_branch = d_after.astype(BF16)
    d_att = (dot("bld,ed->ble", d_branch, w_out) * keep[:, None, None]).astype(BF16)
    mixed_mine = lax.dynamic_slice_in_dim(mixed_in, z * head_width, head_width, 2)
    grad_out = dot("ble,bld->ed", mixed_mine, d_branch)
    ready = jnp.concatenate(
        [
            grad_out,
            jnp.sum(gain_mlp_part, axis=0)[None],
            jnp.full((1, D), jnp.sum(keep)),
            jnp.zeros((14, D), F32),
        ]
    ).astype(BF16)
    late_size = 4 * head_width + 32
    late_size = late_size + -late_size % (32 * txt_count)
    some = own // 2

    def backward(at, before=(), operands=()):
        first = at == 0
        sums_shape = (3, 2 * PAIR, D)
        outs = [
            (own_spec(video_here, at), video_tokens.shape, F32),
            (item_spec(video_here + lat_half), (some, video_here + lat_half, D), BF16),
            (item_spec(cap_rows), (some, cap_rows, D), BF16),
            (own_spec(lat_half, at), latents.shape, F32),
        ]
        scratch = [
            pltpu.VMEM((lat_rows, D), BF16),
            pltpu.VMEM((keys_here, D), BF16),
            pltpu.VMEM((keys_here, D), BF16),
        ]
        if first:
            ins = []
            outs = outs + [(whole_spec(*sums_shape), sums_shape, F32), (whole_spec(8, D), (8, D), F32)]
        else:
            ins = [whole_spec(*sums_shape), whole_spec(8, D), whole_spec(*ready.shape)]
            ins = ins + [pl.BlockSpec(memory_space=pl.ANY)] * len(before)
            outs = outs + [(whole_spec(late_size, D), (late_size, D), BF16)]
            scratch = scratch + [pltpu.VMEM(sums_shape, F32), pltpu.VMEM((8, D), F32)]
        return call(
            functools.partial(backward_kernel, first),
            "attention_backward",
            [
                item_spec(lat_rows, D, at),
                item_spec(keys_here, D, at),
                item_spec(keys_here, D, at),
                pl.BlockSpec((None, 2, 8, 2 * lat_rows), lambda i, s: (at + i, 0, 0, 0)),
                item_spec(lat_rows, D, at),
                item_spec(lat_rows, D, at),
                own_spec(video_here, at),
                item_spec(video_here, D, at),
                item_spec(cap_rows, D, at),
                item_spec(cap_rows, lat_rows, at),
                weight_spec(1),
                weight_spec(2),
                row_spec,
                item_spec(2 * video_here, D, at),
                weight_spec(0),
                item_spec(lat_rows, D, at),
                item_spec(lat_rows, D, at),
                item_spec(lat_rows, D, at),
                row_spec,
            ]
            + ins,
            outs,
            (
                queries, keys, values, lse, attended, d_att, video_tokens, video_other, cap, mask,
                weights, weights, gain_tok_row, tok_norm, weights, lat, lat_norm, d_after,
                gain_lat_row,
            )
            + tuple(operands)
            + tuple(before),
            3,
            scratch,
            {} if first else {23: 0, 24: 3},
            grid=some,
        )

    def place(at, video_grad, latent_grad, part):
        piece = video_here // 4
        return pl.pallas_call(
            place_kernel,
            name="place_rows",
            grid_spec=pltpu.PrefetchScalarGridSpec(
                num_scalar_prefetch=1,
                grid=(some, 4),
                in_specs=[
                    pl.BlockSpec(memory_space=pl.ANY),
                    pl.BlockSpec(memory_space=pl.ANY),
                    pl.BlockSpec((None, piece, D), lambda i, r, s: (i, r, 0)),
                    pl.BlockSpec((None, lat_half, D), lambda i, r, s: (i, video_here // lat_half, 0)),
                ],
                out_specs=[
                    pl.BlockSpec((None, piece, D), lambda i, r, s: ((1 - s[0]) * own + at + i, r, 0)),
                    pl.BlockSpec(
                        (None, lat_half, D), lambda i, r, s: ((1 - s[0]) * own + at + i, 0, 0)
                    ),
                ],
            ),
            out_shape=[
                jax.ShapeDtypeStruct(video_tokens.shape, F32),
                jax.ShapeDtypeStruct(latents.shape, F32),
            ],
            input_output_aliases={1: 0, 2: 1},
            cost_estimate=pl.CostEstimate(
                flops=3 * 10**9, transcendentals=0, bytes_accessed=5 * 10**6
            ),
        )(scalars, video_grad, latent_grad, part, part)

    d_att, ready = lax.optimization_barrier((d_att, ready))
    video_grad, back_a, cap_a, latent_grad, sums, gain_sums = backward(0)
    here_a = swap_cores(back_a)
    grad_up, grad_down, sums = lax.optimization_barrier((grad_up, grad_down, sums))
    video_grad, back_b, cap_b, latent_grad, late = backward(
        some, (video_grad, latent_grad), (sums, gain_sums, ready)
    )
    growth, here_a, _ = lax.optimization_barrier((growth, here_a, late))
    late_half, late_swapped = reduce_over_cores(late, core)
    here_b = swap_cores(back_b)
    cap_back = jnp.concatenate([cap_a, cap_b])
    cap_back, _ = lax.optimization_barrier((cap_back, late_swapped))
    late_total = reduce_over_group(late_half, place_index, txt_count)
    video_grad, latent_grad = place(0, video_grad, latent_grad, here_a)
    late_total, video_grad = lax.optimization_barrier((late_total, video_grad))
    late = gather_group(late_total, core, place_index, txt_count).astype(F32)
    video_grad, latent_grad = place(some, video_grad, latent_grad, here_b)
    out_mine = (after_attn + growth.astype(F32)).astype(BF16)
    caption_grad = jnp.zeros((txt_count, own, cap_here, D), F32)
    for step in range(txt_count):
        perm = [(b, a) for a, b in caption_perm(step, 2, txt_count, 2)]
        part = lax.ppermute(
            cap_back[:, step * cap_here : (step + 1) * cap_here], ("vid", "txt"), perm
        )
        caption_grad = lax.dynamic_update_index_in_dim(
            caption_grad, part.astype(F32), (place_index + step) % txt_count, 0
        )
    caption_grad = caption_grad.reshape(caption_tokens.shape)

    gains = late[4 * head_width :]

    def give_back(values):
        other = swap_cores(values[:, lat_half:].astype(BF16)).astype(values.dtype)
        whole = jnp.zeros((items_here, lat_half, D), values.dtype)
        whole = lax.dynamic_update_slice_in_dim(whole, values[:, :lat_half], core * own, 0)
        return lax.dynamic_update_slice_in_dim(whole, other, (1 - core) * own, 0)

    latents_out = give_back(out_mine)
    kept_count = gains[1, 0].astype(jnp.int32)
    return (
        latents_out,
        latent_grad,
        video_grad,
        caption_grad,
        late[:head_width].T,
        late[head_width : 2 * head_width].T,
        late[2 * head_width : 3 * head_width].T,
        late[3 * head_width : 4 * head_width],
        grad_up.astype(F32),
        grad_down.astype(F32),
        gains[17],
        gains[16],
        gains[0],
        kept_count,
    )


def norm_back_rows(values, gain, upstream):
    mean = jnp.mean(values, axis=-1, keepdims=True)
    center = values - mean
    rate = lax.rsqrt(jnp.mean(center * center, axis=-1, keepdims=True) + 1e-05)
    hat = center * rate
    scaled = upstream * gain
    first = jnp.mean(scaled, axis=-1, keepdims=True)
    second = jnp.mean(scaled * hat, axis=-1, keepdims=True)
    return rate * (scaled - first - hat * second), jnp.sum(upstream * hat, axis=-2)


def fits(mesh):
    shape = mesh.shape
    return shape["vid"] == 2 and shape["txt"] == 4 and shape["head"] == 4


def solution(mesh):
    in_specs = (
        P("txt", "vid", None),
        P("txt", "vid", None),
        P("vid", "txt", None),
        P("vid"),
        P("vid", "txt"),
        P("txt"),
        P(),
        P(),
        P(),
        P(None, "head"),
        P(None, "head"),
        P(None, "head"),
        P("head", None),
        P(None, "head"),
        P("head", None),
        P("txt", "vid", None),
    )
    out_specs = (
        P("txt", "vid", None),
        P("txt", "vid", None),
        P("txt", "vid", None),
        P("vid", "txt", None),
        P(None, "head"),
        P(None, "head"),
        P(None, "head"),
        P("head", None),
        P(None, "head"),
        P("head", None),
        P(),
        P(),
        P(),
        P(),
    )
    return jax.shard_map(local if fits(mesh) else local_general, mesh=mesh, in_specs=in_specs, out_specs=out_specs, check_vma=False)
```

```python
import functools
import math

import jax
import jax.numpy as jnp
from jax import lax
from jax.experimental import pallas as pl
from jax.experimental.pallas import tpu as pltpu
from jax.sharding import PartitionSpec as P

D = 768
HEADS = 12


def combined_all(part, axis, combine):
    gathered = jax.tree.map(lambda a: lax.all_gather(a, axis), part)

    def take(source):
        return jax.tree.map(lambda a: lax.dynamic_index_in_dim(a, source, 0, False), gathered)

    return lax.fori_loop(
        1, lax.axis_size(axis), lambda source, state: combine(state, take(source)), take(0)
    )


def layer_norm(values, gain):
    center = values - jnp.mean(values, axis=-1, keepdims=True)
    spread = jnp.mean(center * center, axis=-1, keepdims=True)
    return center * lax.rsqrt(spread + 1e-05) * gain


def norm_back(values, gain, upstream):
    result, pullback = jax.vjp(layer_norm, values, gain)
    return pullback(upstream)


def gelu_exact(values):
    return jax.nn.gelu(values, approximate=False)


def combine_stats(first, second):
    peak = jnp.maximum(first[0], second[0])
    total = first[1] * jnp.exp(first[0] - peak) + second[1] * jnp.exp(second[0] - peak)
    return (peak, total)


def to_blocks(whole, vid_count, txt_count):
    items, rows, width = whole.shape
    split = whole.reshape(txt_count, items // txt_count, vid_count, rows // vid_count, width)
    return split.transpose(2, 0, 1, 3, 4).reshape(
        vid_count * txt_count, items // txt_count, rows // vid_count, width
    )


def from_blocks(blocked, vid_count, txt_count):
    count, items_here, rows_here, width = blocked.shape
    split = blocked.reshape(vid_count, txt_count, items_here, rows_here, width)
    return split.transpose(1, 2, 0, 3, 4).reshape(
        txt_count * items_here, vid_count * rows_here, width
    )


def place_sum(whole, part, start):
    current = lax.dynamic_slice_in_dim(whole, start, part.shape[0], 0)
    return lax.dynamic_update_slice_in_dim(whole, current + part, start, 0)


def place_stats(peak_all, total_all, peak, total, start):
    old_peak = lax.dynamic_slice_in_dim(peak_all, start, peak.shape[0], 0)
    old_total = lax.dynamic_slice_in_dim(total_all, start, peak.shape[0], 0)
    new_peak, new_total = combine_stats((old_peak, old_total), (peak, total))
    peak_all = lax.dynamic_update_slice_in_dim(peak_all, new_peak, start, 0)
    total_all = lax.dynamic_update_slice_in_dim(total_all, new_total, start, 0)
    return (peak_all, total_all)


def take_rows(whole, start, count):
    return lax.dynamic_slice_in_dim(whole, start, count, 0)


def local_general(
    latents,
    video_tokens,
    caption_tokens,
    caption_len,
    key_mask,
    drop_flags,
    gain_latent,
    gain_tokens,
    gain_mlp,
    query_weight,
    key_matrix,
    value_matrix,
    out_weight,
    up_weight,
    down_weight,
    cotangent,
):
    vid_count = lax.axis_size("vid")
    txt_count = lax.axis_size("txt")
    vid_index = lax.axis_index("vid")
    txt_index = lax.axis_index("txt")
    items_here = latents.shape[0]
    cap_items = caption_tokens.shape[0]
    items_total = items_here * txt_count
    head_width = query_weight.shape[1]
    head_size = D // HEADS
    heads_here = head_width // head_size
    scale = 1.0 / math.sqrt(head_size)
    video_here = video_tokens.shape[1]
    cap_here = caption_tokens.shape[1]
    video_start = txt_index * items_here
    cap_start = vid_index * cap_items
    keep = (1 - drop_flags).astype(jnp.float32)
    slots = txt_index * cap_here + jnp.arange(cap_here, dtype=jnp.int32)
    cap_valid = (slots[None, :] < caption_len[:, None]) & (key_mask == 1)
    cap_mask = cap_valid[:, None, None, :]

    def split_heads(values):
        return values.reshape(values.shape[0], values.shape[1], heads_here, head_size)

    lat_float = latents.astype(jnp.float32)
    lat_norm = layer_norm(lat_float, gain_latent).astype(jnp.bfloat16)
    queries = jnp.einsum(
        "bld,de->ble", lat_norm, query_weight, preferred_element_type=jnp.float32
    ).astype(jnp.bfloat16)
    all_queries = from_blocks(
        lax.all_gather(queries[None], ("vid", "txt"), axis=0, tiled=True), vid_count, txt_count
    )
    lat_total = all_queries.shape[1]
    video_queries = take_rows(all_queries, video_start, items_here)
    cap_queries = take_rows(all_queries, cap_start, cap_items)
    video_float = video_tokens.astype(jnp.float32)
    cap_float = caption_tokens.astype(jnp.float32)
    video_normed = layer_norm(video_float, gain_tokens).astype(jnp.bfloat16)
    caption_normed = layer_norm(cap_float, gain_tokens).astype(jnp.bfloat16)
    video_keys = jnp.einsum(
        "flc,co->flo", video_normed, key_matrix, preferred_element_type=jnp.float32
    ).astype(jnp.bfloat16)
    video_values = jnp.einsum(
        "flc,co->flo", video_normed, value_matrix, preferred_element_type=jnp.float32
    ).astype(jnp.bfloat16)
    cap_keys = jnp.einsum(
        "flc,co->flo", caption_normed, key_matrix, preferred_element_type=jnp.float32
    ).astype(jnp.bfloat16)
    cap_values = jnp.einsum(
        "flc,co->flo", caption_normed, value_matrix, preferred_element_type=jnp.float32
    ).astype(jnp.bfloat16)
    video_scores = (
        jnp.einsum(
            "blhe,bkhe->bhlk",
            split_heads(video_queries),
            split_heads(video_keys),
            preferred_element_type=jnp.float32,
        )
        * scale
    )
    cap_scores = (
        jnp.einsum(
            "blhe,bkhe->bhlk",
            split_heads(cap_queries),
            split_heads(cap_keys),
            preferred_element_type=jnp.float32,
        )
        * scale
    )
    cap_scores = jnp.where(cap_mask, cap_scores, -1e30)
    video_peak = jnp.max(video_scores, axis=-1)
    video_total = jnp.sum(jnp.exp(video_scores - video_peak[..., None]), axis=-1)
    cap_peak = jnp.max(cap_scores, axis=-1)
    cap_total = jnp.sum(
        jnp.where(cap_mask, jnp.exp(cap_scores - cap_peak[..., None]), 0.0), axis=-1
    )
    peak_all = jnp.full((items_total, heads_here, lat_total), -1e30, jnp.float32)
    total_all = jnp.zeros((items_total, heads_here, lat_total), jnp.float32)
    peak_all, total_all = place_stats(peak_all, total_all, video_peak, video_total, video_start)
    peak_all, total_all = place_stats(peak_all, total_all, cap_peak, cap_total, cap_start)
    peak, total = combined_all((peak_all, total_all), ("vid", "txt"), combine_stats)
    video_probs = (
        jnp.exp(video_scores - take_rows(peak, video_start, items_here)[..., None])
        / take_rows(total, video_start, items_here)[..., None]
    )
    cap_probs = jnp.where(
        cap_mask,
        jnp.exp(cap_scores - take_rows(peak, cap_start, cap_items)[..., None])
        / take_rows(total, cap_start, cap_items)[..., None],
        0.0,
    )
    video_low = video_probs.astype(jnp.bfloat16)
    cap_low = cap_probs.astype(jnp.bfloat16)
    video_part = jnp.einsum(
        "bhlk,bkhe->blhe", video_low, split_heads(video_values), preferred_element_type=jnp.float32
    ).reshape(items_here, lat_total, head_width)
    cap_part = jnp.einsum(
        "bhlk,bkhe->blhe", cap_low, split_heads(cap_values), preferred_element_type=jnp.float32
    ).reshape(cap_items, lat_total, head_width)
    value_all = jnp.zeros((items_total, lat_total, head_width), jnp.float32)
    value_all = place_sum(place_sum(value_all, video_part, video_start), cap_part, cap_start)
    attended = lax.psum_scatter(
        to_blocks(value_all, vid_count, txt_count), ("vid", "txt"), scatter_dimension=0, tiled=True
    )[0]
    mixed_in = (attended * keep[:, None, None]).astype(jnp.bfloat16)
    branch = lax.psum(
        jnp.einsum("ble,ed->bld", mixed_in, out_weight, preferred_element_type=jnp.float32), "head"
    )
    after_attn = lat_float + branch
    mlp_norm = layer_norm(after_attn, gain_mlp).astype(jnp.bfloat16)
    pre_act = jnp.einsum("bld,df->blf", mlp_norm, up_weight, preferred_element_type=jnp.float32)
    activ = gelu_exact(pre_act).astype(jnp.bfloat16)
    growth = lax.psum(
        jnp.einsum("blf,fd->bld", activ, down_weight, preferred_element_type=jnp.float32).astype(
            jnp.bfloat16
        ),
        "head",
    ).astype(jnp.float32)
    latents_out = (after_attn + growth).astype(jnp.bfloat16)
    grad_down = jnp.einsum("blf,bld->fd", activ, cotangent, preferred_element_type=jnp.float32)
    d_activ = jnp.einsum("bld,fd->blf", cotangent, down_weight, preferred_element_type=jnp.float32)
    d_pre = jax.vjp(gelu_exact, pre_act)[1](d_activ)[0].astype(jnp.bfloat16)
    grad_up = jnp.einsum("bld,blf->df", mlp_norm, d_pre, preferred_element_type=jnp.float32)
    d_mlp_norm = lax.psum(
        jnp.einsum("blf,df->bld", d_pre, up_weight, preferred_element_type=jnp.float32), "head"
    )
    d_after_norm, grad_gain_mlp = norm_back(after_attn, gain_mlp, d_mlp_norm)
    d_after = cotangent.astype(jnp.float32) + d_after_norm
    d_branch = d_after.astype(jnp.bfloat16)
    grad_out = jnp.einsum("ble,bld->ed", mixed_in, d_branch, preferred_element_type=jnp.float32)
    d_att = (
        jnp.einsum("bld,ed->ble", d_branch, out_weight, preferred_element_type=jnp.float32)
        * keep[:, None, None]
    ).astype(jnp.bfloat16)
    all_d_att = from_blocks(
        lax.all_gather(d_att[None], ("vid", "txt"), axis=0, tiled=True), vid_count, txt_count
    )
    video_d_att = split_heads(take_rows(all_d_att, video_start, items_here))
    cap_d_att = split_heads(take_rows(all_d_att, cap_start, cap_items))
    video_dprobs = jnp.einsum(
        "blhe,bkhe->bhlk",
        video_d_att,
        split_heads(video_values),
        preferred_element_type=jnp.float32,
    )
    cap_dprobs = jnp.einsum(
        "blhe,bkhe->bhlk", cap_d_att, split_heads(cap_values), preferred_element_type=jnp.float32
    )
    delta_all = jnp.zeros((items_total, heads_here, lat_total), jnp.float32)
    delta_all = place_sum(delta_all, jnp.sum(video_probs * video_dprobs, axis=-1), video_start)
    delta_all = place_sum(delta_all, jnp.sum(cap_probs * cap_dprobs, axis=-1), cap_start)
    delta = lax.psum(delta_all, ("vid", "txt"))
    video_dscores = (
        video_probs * (video_dprobs - take_rows(delta, video_start, items_here)[..., None])
    ).astype(jnp.bfloat16)
    cap_dscores = (
        cap_probs * (cap_dprobs - take_rows(delta, cap_start, cap_items)[..., None])
    ).astype(jnp.bfloat16)
    video_dq = (
        jnp.einsum(
            "bhlk,bkhe->blhe",
            video_dscores,
            split_heads(video_keys),
            preferred_element_type=jnp.float32,
        )
        * scale
    ).reshape(items_here, lat_total, head_width)
    cap_dq = (
        jnp.einsum(
            "bhlk,bkhe->blhe",
            cap_dscores,
            split_heads(cap_keys),
            preferred_element_type=jnp.float32,
        )
        * scale
    ).reshape(cap_items, lat_total, head_width)
    query_all = jnp.zeros((items_total, lat_total, head_width), jnp.float32)
    query_all = place_sum(place_sum(query_all, video_dq, video_start), cap_dq, cap_start)
    d_queries = lax.psum_scatter(
        to_blocks(query_all, vid_count, txt_count), ("vid", "txt"), scatter_dimension=0, tiled=True
    )[0].astype(jnp.bfloat16)
    video_key_grad = (
        (
            jnp.einsum(
                "bhlk,blhe->bkhe",
                video_dscores,
                split_heads(video_queries),
                preferred_element_type=jnp.float32,
            )
            * scale
        )
        .reshape(items_here, video_here, head_width)
        .astype(jnp.bfloat16)
    )
    video_value_grad = (
        jnp.einsum("bhlk,blhe->bkhe", video_low, video_d_att, preferred_element_type=jnp.float32)
        .reshape(items_here, video_here, head_width)
        .astype(jnp.bfloat16)
    )
    caption_key_grad = (
        (
            jnp.einsum(
                "bhlk,blhe->bkhe",
                cap_dscores,
                split_heads(cap_queries),
                preferred_element_type=jnp.float32,
            )
            * scale
        )
        .reshape(cap_items, cap_here, head_width)
        .astype(jnp.bfloat16)
    )
    caption_value_grad = (
        jnp.einsum("bhlk,blhe->bkhe", cap_low, cap_d_att, preferred_element_type=jnp.float32)
        .reshape(cap_items, cap_here, head_width)
        .astype(jnp.bfloat16)
    )
    grad_query = jnp.einsum("bld,ble->de", lat_norm, d_queries, preferred_element_type=jnp.float32)
    d_lat_norm = lax.psum(
        jnp.einsum("ble,de->bld", d_queries, query_weight, preferred_element_type=jnp.float32),
        "head",
    )
    d_lat_back, grad_gain_latent = norm_back(lat_float, gain_latent, d_lat_norm)
    latent_grad = d_after + d_lat_back
    grad_key = jnp.einsum(
        "zsg,zsv->gv", video_normed, video_key_grad, preferred_element_type=jnp.float32
    ) + jnp.einsum(
        "zsg,zsv->gv", caption_normed, caption_key_grad, preferred_element_type=jnp.float32
    )
    grad_value = jnp.einsum(
        "zsg,zsv->gv", video_normed, video_value_grad, preferred_element_type=jnp.float32
    ) + jnp.einsum(
        "zsg,zsv->gv", caption_normed, caption_value_grad, preferred_element_type=jnp.float32
    )
    video_term = jnp.einsum(
        "ayt,ot->ayo", video_key_grad, key_matrix, preferred_element_type=jnp.float32
    ) + jnp.einsum(
        "ayt,ot->ayo", video_value_grad, value_matrix, preferred_element_type=jnp.float32
    )
    cap_term = jnp.einsum(
        "ayt,ot->ayo", caption_key_grad, key_matrix, preferred_element_type=jnp.float32
    ) + jnp.einsum(
        "ayt,ot->ayo", caption_value_grad, value_matrix, preferred_element_type=jnp.float32
    )
    d_video_norm, d_cap_norm = lax.psum((video_term, cap_term), "head")
    video_grad, video_gain_part = norm_back(video_float, gain_tokens, d_video_norm)
    caption_grad, cap_gain_part = norm_back(cap_float, gain_tokens, d_cap_norm)
    grad_gain_tokens = video_gain_part + cap_gain_part
    kept_here = jnp.sum(keep)
    (
        grad_query,
        grad_key,
        grad_value,
        grad_out,
        grad_up,
        grad_down,
        grad_gain_latent,
        grad_gain_tokens,
        grad_gain_mlp,
        kept_total,
    ) = lax.psum(
        (
            grad_query,
            grad_key,
            grad_value,
            grad_out,
            grad_up,
            grad_down,
            grad_gain_latent,
            grad_gain_tokens,
            grad_gain_mlp,
            kept_here,
        ),
        ("vid", "txt"),
    )
    kept_count = (kept_total / vid_count).astype(jnp.int32)
    return (
        latents_out,
        latent_grad,
        video_grad,
        caption_grad,
        grad_query,
        grad_key,
        grad_value,
        grad_out,
        grad_up,
        grad_down,
        grad_gain_latent,
        grad_gain_tokens,
        grad_gain_mlp,
        kept_count,
    )


def swap_cores(values):
    return lax.ppermute(values, "vid", [(0, 1), (1, 0)])


def head_shift(values, shift, count):
    return lax.ppermute(values, "head", [(i, (i - shift) % count) for i in range(count)])


def take_block(values, index, size, axis=0):
    return lax.dynamic_slice_in_dim(values, index * size, size, axis)


def sum_over_head(part, place, count):
    low = part.astype(jnp.bfloat16)
    total = lax.dynamic_index_in_dim(part, place, 0, False)
    for shift in range(1, count):
        chunk = lax.dynamic_index_in_dim(low, (place - shift) % count, 0, False)
        total = total + head_shift(chunk, shift, count).astype(jnp.float32)
    total = total.astype(jnp.bfloat16)
    result = lax.dynamic_update_index_in_dim(jnp.zeros_like(low), total, place, 0)
    for shift in range(1, count):
        result = lax.dynamic_update_index_in_dim(
            result, head_shift(total, shift, count), (place + shift) % count, 0
        )
    return result


def group_steps(count):
    return [(step, [(i, (i - step) % count) for i in range(count)]) for step in range(1, count)]


def reduce_over_cores(rows, core):
    half = rows.shape[0] // 2
    other = swap_cores(take_block(rows, 1 - core, half))
    return take_block(rows, core, half).astype(F32) + other.astype(F32), other


def reduce_over_group(half, place, count):
    part = half.shape[0] // count
    low = half.astype(BF16)
    total = take_block(half, place, part)
    for step, perm in group_steps(count):
        chunk = take_block(low, (place - step) % count, part)
        total = total + lax.ppermute(chunk, "txt", perm).astype(F32)
    return total.astype(BF16)


def gather_group(total, core, place, count):
    part = total.shape[0]
    half = part * count
    mine = jnp.zeros((half, total.shape[1]), BF16)
    mine = lax.dynamic_update_slice_in_dim(mine, total, place * part, 0)
    for step, perm in group_steps(count):
        mine = lax.dynamic_update_slice_in_dim(
            mine, lax.ppermute(total, "txt", perm), (place + step) % count * part, 0
        )
    whole = jnp.zeros((2 * half, total.shape[1]), BF16)
    whole = lax.dynamic_update_slice_in_dim(whole, mine, core * half, 0)
    return lax.dynamic_update_slice_in_dim(whole, swap_cores(mine), (1 - core) * half, 0)


def caption_perm(step, vid_count, txt_count, cores):
    pairs = []
    for v in range(vid_count):
        for t in range(txt_count):
            block = (t + step) % txt_count
            dest_txt = v * (txt_count // vid_count) + block // cores
            dest_vid = block % cores
            pairs.append((v * txt_count + t, dest_vid * txt_count + dest_txt))
    return pairs


PAIR = 128
F32 = jnp.float32
BF16 = jnp.bfloat16


def dot_nt(a, b):
    return lax.dot_general(a, b, (((1,), (1,)), ((), ())), preferred_element_type=F32)


def dot_nn(a, b):
    return lax.dot_general(a, b, (((1,), (0,)), ((), ())), preferred_element_type=F32)


def dot_tn(a, b):
    return lax.dot_general(a, b, (((0,), (0,)), ((), ())), preferred_element_type=F32)


def square(ref):
    return ref[...].reshape(D, D)


def two_heads(values):
    low = lax.broadcasted_iota(jnp.int32, values.shape, 1) < PAIR // 2
    zero = jnp.zeros_like(values)
    return jnp.concatenate([jnp.where(low, values, zero), jnp.where(low, zero, values)], axis=0)


def from_two_heads(both):
    n = both.shape[1] // 2
    first = lax.broadcasted_iota(jnp.int32, (PAIR, n), 0) < PAIR // 2
    return jnp.where(first, both[:, :n], both[:, n:]).T


def chunk_list(video, cap, size):
    return [(start, size) for start in range(0, video, size)] + [(video, cap)]


def norm_kernel(s_ref, tok_ref, gain_ref, *refs):
    gain = gain_ref[...]
    out_ref = refs[-1]
    for at in range(0, tok_ref.shape[0], 64):
        rows = pl.ds(at, 64)
        out_ref[rows, :] = layer_norm(tok_ref[rows, :].astype(F32), gain).astype(BF16)


def cap_mask(cap_ref):
    mask = cap_ref[:, pl.ds(D, PAIR)]
    return jnp.concatenate([mask, mask], axis=1).astype(F32) > 0.5


def forward_kernel(
    s_ref, tok_ref, cap_ref, gain_ref, lat_ref, gain_lat_ref, wq_ref, wk_ref, wv_ref, *refs
):
    q_ref, k_ref, v_ref, lse_ref, o_ref, s_scr = refs[-6:]
    keys, width = k_ref.shape
    cap = cap_ref.shape[0]
    step = (keys - cap) // 4

    def matrix(ref):
        return ref[...].reshape(width, D)

    latn = layer_norm(lat_ref[...].astype(F32), gain_lat_ref[...]).astype(BF16)
    q_ref[...] = (dot_nt(latn, matrix(wq_ref)).astype(BF16).astype(F32) * 0.125).astype(BF16)

    def project(c, carry):
        rows = pl.ds(pl.multiple_of(c * step, 16), step)
        k_ref[rows, :] = dot_nt(tok_ref[rows, :], matrix(wk_ref)).astype(BF16)
        v_ref[rows, :] = dot_nt(tok_ref[rows, :], matrix(wv_ref)).astype(BF16)
        return carry

    lax.fori_loop(0, 4, project, 0)
    cap_rows = pl.ds(keys - cap, cap)
    cap_norm = layer_norm(cap_ref[:, pl.ds(0, D)].astype(F32), gain_ref[...]).astype(BF16)
    k_ref[cap_rows, :] = dot_nt(cap_norm, matrix(wk_ref)).astype(BF16)
    v_ref[cap_rows, :] = dot_nt(cap_norm, matrix(wv_ref)).astype(BF16)
    chunks = chunk_list(keys - cap, cap, 256)

    def pair(p, carry):
        cols = pl.ds(pl.multiple_of(p * PAIR, PAIR), PAIR)
        q2 = two_heads(q_ref[:, cols])
        peak = None
        for start, size in chunks:
            rows = pl.ds(start, size)
            s = dot_nt(k_ref[rows, cols], q2)
            if start == keys - cap:
                s = jnp.where(cap_mask(cap_ref), s, -1e30)
            s_scr[rows, :] = s
            top = jnp.max(s, axis=0, keepdims=True)
            peak = top if peak is None else jnp.maximum(peak, top)
        total = jnp.zeros_like(peak)
        out = jnp.zeros((PAIR, q2.shape[0]), F32)
        for start, size in chunks:
            rows = pl.ds(start, size)
            e = jnp.exp(s_scr[rows, :] - peak)
            total = total + jnp.sum(e, axis=0, keepdims=True)
            out = out + dot_tn(v_ref[rows, cols], e.astype(BF16))
        o_ref[:, cols] = from_two_heads(out / total)
        lse_ref[pl.ds(p, 1), :] = peak + jnp.log(total)
        return carry

    lax.fori_loop(0, width // PAIR, pair, 0)


def backward_kernel(
    first, s_ref, q_ref, k_ref, v_ref, lse_ref, o_ref, datt_ref, own_ref, other_ref, cap_ref,
    wk_ref, wv_ref, gain_ref, tok_ref, wq_ref, lat_ref, after_ref, gain_lat_ref, *refs
):
    if first:
        own_out, other_out, cap_out, lat_out, sums_ref, gain_out = refs[:6]
    else:
        sums_in, gain_in, ready_ref = refs[:3]
        own_out, other_out, cap_out, lat_out, late_ref = refs[5:10]
        sums_ref, gain_out = refs[-2:]
    dq_ref, dk_ref, dv_ref = refs[6:9] if first else refs[10:13]
    item = pl.program_id(0)
    keys = k_ref.shape[0]
    cap = cap_ref.shape[0]
    chunks = chunk_list(keys - cap, cap, 256)

    def pair(p, carry):
        cols = pl.ds(pl.multiple_of(p * PAIR, PAIR), PAIR)
        q2 = two_heads(q_ref[:, cols])
        d_att = datt_ref[:, cols]
        d2 = two_heads(d_att)
        prod = (d_att.astype(F32) * o_ref[:, cols]).T
        delta = jnp.concatenate(
            [
                jnp.sum(prod[: PAIR // 2], axis=0, keepdims=True),
                jnp.sum(prod[PAIR // 2 :], axis=0, keepdims=True),
            ],
            axis=1,
        )
        pairs_here = D // PAIR // lse_ref.shape[0]
        lse = lse_ref[p // pairs_here, pl.ds(p % pairs_here, 1), :]
        dq = jnp.zeros((PAIR, q2.shape[0]), F32)
        for start, size in chunks:
            rows = pl.ds(start, size)
            k = k_ref[rows, cols]
            s = dot_nt(k, q2)
            d_probs = dot_nt(v_ref[rows, cols], d2)
            if start == keys - cap:
                s = jnp.where(cap_mask(cap_ref), s, -1e30)
            probs = jnp.exp(s - lse)
            d_scores = (probs * (d_probs - delta)).astype(BF16)
            dv_ref[rows, cols] = dot_nn(probs.astype(BF16), d2).astype(BF16)
            dk_ref[rows, cols] = dot_nn(d_scores, q2).astype(BF16)
            dq = dq + dot_tn(k, d_scores)
        dq_ref[:, cols] = (from_two_heads(dq) * 0.125).astype(BF16)
        return carry

    lax.fori_loop(0, D // PAIR, pair, 0)
    gain = gain_ref[...]

    @pl.when(item == 0)
    def _():
        gain_out[...] = jnp.zeros_like(gain_out) if first else gain_in[...]
        sums_ref[...] = jnp.zeros_like(sums_ref) if first else sums_in[...]

    window = pl.ds(pl.multiple_of(s_ref[2], PAIR), sums_ref.shape[1])
    video_rows = pl.ds(0, keys - cap)
    cap_rows = pl.ds(keys - cap, cap)
    cap_norm = layer_norm(cap_ref[:, pl.ds(0, D)].astype(F32), gain).astype(BF16)
    latn = layer_norm(lat_ref[...].astype(F32), gain_lat_ref[...]).astype(BF16)
    sums_ref[0] += dot_tn(dq_ref[:, window], latn)
    for n, ref in ((1, dk_ref), (2, dv_ref)):
        sums_ref[n] += dot_tn(ref[video_rows, window], tok_ref[...]) + dot_tn(
            ref[cap_rows, window], cap_norm
        )

    def norm_back(x, up, gain, row):
        center = x - jnp.mean(x, axis=-1, keepdims=True)
        rate = lax.rsqrt(jnp.mean(center * center, axis=-1, keepdims=True) + 1e-05)
        hat = center * rate
        gain_out[pl.ds(row, 1), :] += jnp.sum(up * hat, axis=0, keepdims=True)
        scaled = up * gain
        first = jnp.mean(scaled, axis=-1, keepdims=True)
        second = jnp.mean(scaled * hat, axis=-1, keepdims=True)
        return rate * (scaled - first - hat * second)

    half = lat_out.shape[0]
    lat_grad = after_ref[...] + norm_back(
        lat_ref[...].astype(F32), dot_nn(dq_ref[...], square(wq_ref)), gain_lat_ref[...], 1
    )
    lat_out[...] = lat_grad[:half]
    other_out[pl.ds(other_ref.shape[0], half), :] = lat_grad[half:].astype(BF16)

    start = 0
    for ref, out, size in ((own_ref, own_out, 256), (other_ref, other_out, 256), (cap_ref, cap_out, cap)):
        def chunk(c, carry, ref=ref, out=out, size=size, start=start):
            rows = pl.ds(pl.multiple_of(c * size, 16), size)
            key_rows = pl.ds(pl.multiple_of(start + c * size, 16), size)
            up = dot_nn(dk_ref[key_rows, :], square(wk_ref)) + dot_nn(
                dv_ref[key_rows, :], square(wv_ref)
            )
            back = norm_back(ref[rows, pl.ds(0, D)].astype(F32), up, gain, 0)
            out[rows, :] = back.astype(out.dtype)
            return carry

        lax.fori_loop(0, ref.shape[0] // size, chunk, 0)
        start += ref.shape[0]

    if first:
        return

    @pl.when(item == pl.num_programs(0) - 1)
    def _():
        width = D // 4
        mine = pl.ds(pl.multiple_of(s_ref[3], PAIR // 2), width)
        for n in range(3):
            late_ref[pl.ds(n * width, width), :] = sums_ref[n, mine, :].astype(BF16)
        ready = ready_ref.shape[0]
        late_ref[pl.ds(3 * width, ready), :] = ready_ref[...]
        gains = jnp.concatenate([gain_out[...], jnp.zeros((8, D), F32)], axis=0)
        late_ref[pl.ds(3 * width + ready, 16), :] = gains.astype(BF16)
        spare = late_ref.shape[0] - 3 * width - ready - 16
        late_ref[pl.ds(3 * width + ready + 16, spare), :] = jnp.zeros((spare, D), BF16)


def place_kernel(s_ref, video_in, lat_in, video_part, lat_part, video_ref, lat_ref):
    video_ref[...] = video_part[...].astype(F32)

    @pl.when(pl.program_id(1) == 0)
    def _():
        lat_ref[...] = lat_part[...].astype(F32)


def local(
    latents,
    video_tokens,
    caption_tokens,
    caption_len,
    key_mask,
    drop_flags,
    gain_latent,
    gain_tokens,
    gain_mlp,
    query_weight,
    key_matrix,
    value_matrix,
    out_weight,
    up_weight,
    down_weight,
    cotangent,
):
    txt_count = lax.axis_size("txt")
    head_count = lax.axis_size("head")
    core = lax.axis_index("vid")
    place_index = lax.axis_index("txt")
    z = lax.axis_index("head")
    items_here = latents.shape[0]
    own = items_here // 2
    lat_half = latents.shape[1]
    lat_rows = 2 * lat_half
    video_here = video_tokens.shape[1]
    cap_here = caption_tokens.shape[1]
    cap_rows = cap_here * txt_count
    keys_here = 2 * video_here + cap_rows
    head_width = query_weight.shape[1]

    def dot(spec, a, b):
        return jnp.einsum(spec, a, b, preferred_element_type=F32)

    packed = jnp.stack([query_weight.T, key_matrix.T, value_matrix.T, out_weight])
    half = take_block(packed, core, 2)
    up1 = lax.ppermute(half, "head", [(0, 1), (1, 2), (2, 3)])
    down1 = lax.ppermute(half, "head", [(1, 0), (2, 1), (3, 2)])
    near_at = z // 2
    zero = jnp.int32(0)
    own_at = z % 2
    part_shape = (2, 2, 2, head_width, D)

    def place_chunk(whole, chunk, at_core, at_chunk):
        chunk = chunk.reshape((-1, 1) + chunk.shape[-3:])
        return lax.dynamic_update_slice(whole, chunk, (at_core, at_chunk, zero, zero, zero))

    video_other = swap_cores(take_block(video_tokens, 1 - core, own))
    both = jnp.concatenate([latents, cotangent], axis=1)
    both_own = take_block(both, core, own)
    both_other = swap_cores(take_block(both, 1 - core, own))
    lat = jnp.concatenate([both_own[:, :lat_half], both_other[:, :lat_half]], axis=1)
    cot = jnp.concatenate([both_own[:, lat_half:], both_other[:, lat_half:]], axis=1)
    drop_own = take_block(drop_flags, core, own)
    keep = (1 - drop_own).astype(F32)
    window = z * head_width // PAIR * PAIR
    inside = z * head_width - window
    scalars = jnp.stack([core, near_at, window, inside])
    scalars_far = jnp.stack([core, 1 - near_at, window, inside])

    place_slots = place_index * cap_here + jnp.arange(cap_here, dtype=jnp.int32)
    cap_valid = (place_slots[None, :] < caption_len[:, None]) & (key_mask == 1)
    flags = jnp.broadcast_to(cap_valid.astype(BF16)[:, :, None], cap_valid.shape + (PAIR,))
    cap_message = jnp.concatenate([caption_tokens, flags], axis=2)
    cap_parts = []
    for step in range(txt_count):
        block = take_block(cap_message, (place_index + step) % txt_count, own)
        cap_parts.append(
            lax.ppermute(block, ("vid", "txt"), caption_perm(step, 2, txt_count, 2))
        )
    def item_spec(rows, width=D, first=0):
        return pl.BlockSpec((None, rows, width), lambda i, s: (first + i, 0, 0))

    def own_spec(rows, first=0):
        return pl.BlockSpec((None, rows, D), lambda i, s: (s[0] * own + first + i, 0, 0))

    def whole_spec(*shape):
        return pl.BlockSpec(shape, lambda i, s: (0,) * len(shape))

    def weight_spec(m):
        return pl.BlockSpec(
            (2, None, 2, None, head_width, D),
            lambda i, s: (0, m // 2, 0, m % 2, 0, 0),
            pipeline_mode=pl.Buffered(1),
        )

    def part_spec(m):
        return pl.BlockSpec(
            (None, 2, None, head_width, D),
            lambda i, s: (m // 2, 0, m % 2, 0, 0),
            pipeline_mode=pl.Buffered(1),
        )

    def half_spec(rows):
        return pl.BlockSpec((None, rows, 2 * head_width), lambda i, s: (i, 0, s[1]))

    row_spec = pl.BlockSpec((1, D), lambda i, s: (0, 0))

    def call(kernel, name, ins, outs, operands, micros, scratch=(), aliases={}, scalars=scalars, grid=own):
        return pl.pallas_call(
            kernel,
            name=name,
            grid_spec=pltpu.PrefetchScalarGridSpec(
                num_scalar_prefetch=1,
                grid=(grid,),
                in_specs=ins,
                out_specs=[spec for spec, _, _ in outs],
                scratch_shapes=list(scratch),
            ),
            out_shape=[jax.ShapeDtypeStruct(shape, dtype) for _, shape, dtype in outs],
            input_output_aliases=aliases,
            cost_estimate=pl.CostEstimate(
                flops=micros * 1100 * 10**6, transcendentals=0, bytes_accessed=micros * 10**6
            ),
            compiler_params=pltpu.CompilerParams(vmem_limit_bytes=56 << 20),
        )(scalars, *operands)

    def item_out(rows, dtype, width=D):
        return (item_spec(rows, width), (own, rows, width), dtype)

    gain_lat_row = gain_latent[None]
    gain_tok_row = gain_tokens[None]
    gain_mlp_row = gain_mlp[None]
    def token_norm(part, spec, tokens, before=()):
        return call(
            norm_kernel,
            "token_norm",
            [spec, row_spec] + [pl.BlockSpec(memory_space=pl.ANY)] * len(before),
            [
                (
                    pl.BlockSpec((None, video_here, D), lambda i, s: (i, part, 0)),
                    (own, 2 * video_here, D),
                    BF16,
                )
            ],
            (tokens, gain_tok_row) + tuple(before),
            5,
            aliases={3: 0} if before else {},
        )

    tok_norm = token_norm(0, own_spec(video_here), video_tokens)
    (tok_norm,) = token_norm(1, item_spec(video_here), video_other, tok_norm)
    tok_norm, up1, down1, cap_parts = lax.optimization_barrier((tok_norm, up1, down1, cap_parts))
    cap = jnp.concatenate(cap_parts, axis=1)
    partner = jnp.where(z % 2 == 1, up1, down1)
    near = jnp.zeros(part_shape, BF16)
    near = place_chunk(near, packed.reshape((2, 2) + packed.shape[1:]), zero, own_at)
    near = place_chunk(near, partner, core, 1 - own_at)
    near = place_chunk(near, swap_cores(partner), 1 - core, 1 - own_at)

    half_then, _ = lax.optimization_barrier((half, up1))
    up2 = lax.ppermute(up1, "head", [(1, 2), (2, 3)])
    down2 = lax.ppermute(down1, "head", [(1, 0), (2, 1)])
    up3 = lax.ppermute(half_then, "head", [(0, 3)])
    down3 = lax.ppermute(half_then, "head", [(3, 0)])

    def forward(part, scalars, before=()):
        return call(
            forward_kernel,
            "attention_forward",
            [item_spec(2 * video_here), item_spec(cap_rows, D + PAIR), row_spec]
            + [item_spec(lat_rows), row_spec]
            + [part_spec(m) for m in range(3)]
            + [pl.BlockSpec(memory_space=pl.ANY)] * len(before),
            [
                (half_spec(lat_rows), (own, lat_rows, D), BF16),
                (half_spec(keys_here), (own, keys_here, D), BF16),
                (half_spec(keys_here), (own, keys_here, D), BF16),
                (
                    pl.BlockSpec((None, None, 8, 2 * lat_rows), lambda i, s: (i, s[1], 0, 0)),
                    (own, 2, 8, 2 * lat_rows),
                    F32,
                ),
                (half_spec(lat_rows), (own, lat_rows, D), F32),
            ],
            (tok_norm, cap, gain_tok_row, lat, gain_lat_row, part, part, part) + tuple(before),
            23,
            [pltpu.VMEM((keys_here, 2 * lat_rows), F32)],
            {9 + n: n for n in range(len(before))},
            scalars,
        )

    before = forward(near, scalars)
    before, up2, down2, up3, down3 = lax.optimization_barrier((before, up2, down2, up3, down3))

    def by_place(*choices):
        low = jnp.where(z == 0, choices[0], choices[1])
        return jnp.where(z < 2, low, jnp.where(z == 2, choices[2], choices[3]))

    far_mine = jnp.stack([by_place(down2, down1, up2, up3), by_place(down3, down2, up1, up2)])
    far = jnp.zeros(part_shape, BF16)
    far = lax.dynamic_update_index_in_dim(far, far_mine, core, 0)
    far = lax.dynamic_update_index_in_dim(far, swap_cores(far_mine), 1 - core, 0)
    def both_halves(near, far):
        whole = jnp.zeros((2,) + near.shape, BF16)
        whole = lax.dynamic_update_index_in_dim(whole, near, near_at, 0)
        return lax.dynamic_update_index_in_dim(whole, far, 1 - near_at, 0)

    queries, keys, values, lse, attended = forward(far, scalars_far, before)
    w_out = both_halves(near[1, :, 1], far[1, :, 1]).reshape(D, D)
    lat_float = lat.astype(F32)
    mixed_in = (attended * keep[:, None, None]).astype(BF16)
    after_attn = lat_float + dot("ble,ed->bld", mixed_in, w_out)
    mlp_norm = layer_norm(after_attn, gain_mlp).astype(BF16)

    pre_act = dot("bld,df->blf", mlp_norm, up_weight)
    activ, gelu_pull = jax.vjp(gelu_exact, pre_act)
    activ = activ.astype(BF16)
    d_pre = gelu_pull(dot("bld,fd->blf", cot, down_weight))[0].astype(BF16)
    d_mlp_part = dot("blf,df->bld", d_pre, up_weight)
    d_mlp_part, activ, d_pre = lax.optimization_barrier((d_mlp_part, activ, d_pre))
    d_mlp_norm = sum_over_head(d_mlp_part, z, head_count)
    grad_down = dot("blf,bld->fd", activ, cot).astype(BF16)
    grad_up = dot("bld,blf->df", mlp_norm, d_pre).astype(BF16)
    near, far, _ = lax.optimization_barrier((near, far, d_mlp_part))
    weights = both_halves(near, far)
    early = jnp.where(core == 0, grad_up, grad_down).astype(F32)
    early = early + swap_cores(jnp.where(core == 0, grad_down, grad_up)).astype(F32)
    activ, d_mlp_norm, early, weights = lax.optimization_barrier(
        (activ, d_mlp_norm, early.astype(BF16), weights)
    )
    early = lax.psum(early, "txt")
    growth = lax.psum(dot("blf,fd->bld", activ, down_weight).astype(BF16), "head")

    d_after_norm, gain_mlp_part = norm_back_rows(after_attn, gain_mlp, d_mlp_norm.astype(F32))
    d_after = cot.astype(F32) + d_after_norm
    d_branch = d_after.astype(BF16)
    d_att = (dot("bld,ed->ble", d_branch, w_out) * keep[:, None, None]).astype(BF16)
    mixed_mine = lax.dynamic_slice_in_dim(mixed_in, z * head_width, head_width, 2)
    grad_out = dot("ble,bld->ed", mixed_mine, d_branch)
    ready = jnp.concatenate(
        [
            grad_out,
            jnp.sum(gain_mlp_part, axis=0)[None],
            jnp.full((1, D), jnp.sum(keep)),
            jnp.zeros((14, D), F32),
        ]
    ).astype(BF16)
    late_size = 4 * head_width + 32
    late_size = late_size + -late_size % (32 * txt_count)
    some = own // 2

    def backward(at, before=(), operands=()):
        first = at == 0
        sums_shape = (3, 2 * PAIR, D)
        outs = [
            (own_spec(video_here, at), video_tokens.shape, F32),
            (item_spec(video_here + lat_half), (some, video_here + lat_half, D), BF16),
            (item_spec(cap_rows), (some, cap_rows, D), BF16),
            (own_spec(lat_half, at), latents.shape, F32),
        ]
        scratch = [
            pltpu.VMEM((lat_rows, D), BF16),
            pltpu.VMEM((keys_here, D), BF16),
            pltpu.VMEM((keys_here, D), BF16),
        ]
        if first:
            ins = []
            outs = outs + [(whole_spec(*sums_shape), sums_shape, F32), (whole_spec(8, D), (8, D), F32)]
        else:
            ins = [whole_spec(*sums_shape), whole_spec(8, D), whole_spec(*ready.shape)]
            ins = ins + [pl.BlockSpec(memory_space=pl.ANY)] * len(before)
            outs = outs + [(whole_spec(late_size, D), (late_size, D), BF16)]
            scratch = scratch + [pltpu.VMEM(sums_shape, F32), pltpu.VMEM((8, D), F32)]
        return call(
            functools.partial(backward_kernel, first),
            "attention_backward",
            [
                item_spec(lat_rows, D, at),
                item_spec(keys_here, D, at),
                item_spec(keys_here, D, at),
                pl.BlockSpec((None, 2, 8, 2 * lat_rows), lambda i, s: (at + i, 0, 0, 0)),
                item_spec(lat_rows, D, at),
                item_spec(lat_rows, D, at),
                own_spec(video_here, at),
                item_spec(video_here, D, at),
                item_spec(cap_rows, D + PAIR, at),
                weight_spec(1),
                weight_spec(2),
                row_spec,
                item_spec(2 * video_here, D, at),
                weight_spec(0),
                item_spec(lat_rows, D, at),
                item_spec(lat_rows, D, at),
                row_spec,
            ]
            + ins,
            outs,
            (
                queries, keys, values, lse, attended, d_att, video_tokens, video_other, cap,
                weights, weights, gain_tok_row, tok_norm, weights, lat, d_after,
                gain_lat_row,
            )
            + tuple(operands)
            + tuple(before),
            3,
            scratch,
            {} if first else {21: 0, 22: 3},
            grid=some,
        )

    def place(at, video_grad, latent_grad, part):
        piece = video_here // 2
        return pl.pallas_call(
            place_kernel,
            name="place_rows",
            grid_spec=pltpu.PrefetchScalarGridSpec(
                num_scalar_prefetch=1,
                grid=(some, 2),
                in_specs=[
                    pl.BlockSpec(memory_space=pl.ANY),
                    pl.BlockSpec(memory_space=pl.ANY),
                    pl.BlockSpec((None, piece, D), lambda i, r, s: (i, r, 0)),
                    pl.BlockSpec((None, lat_half, D), lambda i, r, s: (i, video_here // lat_half, 0)),
                ],
                out_specs=[
                    pl.BlockSpec((None, piece, D), lambda i, r, s: ((1 - s[0]) * own + at + i, r, 0)),
                    pl.BlockSpec(
                        (None, lat_half, D), lambda i, r, s: ((1 - s[0]) * own + at + i, 0, 0)
                    ),
                ],
            ),
            out_shape=[
                jax.ShapeDtypeStruct(video_tokens.shape, F32),
                jax.ShapeDtypeStruct(latents.shape, F32),
            ],
            input_output_aliases={1: 0, 2: 1},
            cost_estimate=pl.CostEstimate(
                flops=3 * 10**9, transcendentals=0, bytes_accessed=5 * 10**6
            ),
        )(scalars, video_grad, latent_grad, part, part)

    d_att, ready = lax.optimization_barrier((d_att, ready))
    video_grad, back_a, cap_a, latent_grad, sums, gain_sums = backward(0)
    here_a = swap_cores(back_a)
    early, sums = lax.optimization_barrier((early, sums))
    video_grad, back_b, cap_b, latent_grad, late = backward(
        some, (video_grad, latent_grad), (sums, gain_sums, ready)
    )
    growth, _ = lax.optimization_barrier((growth, late))
    late_half, late_swapped = reduce_over_cores(late, core)
    here_b = swap_cores(back_b)
    cap_back = jnp.concatenate([cap_a, cap_b])
    cap_back, _ = lax.optimization_barrier((cap_back, late_swapped))
    late_total = reduce_over_group(late_half, place_index, txt_count)
    here_a, _ = lax.optimization_barrier((here_a, late_half))
    early_other = swap_cores(early)
    video_grad, latent_grad = place(0, video_grad, latent_grad, here_a)
    here_b, early, early_other, _ = lax.optimization_barrier((here_b, early, early_other, late_total))
    late = gather_group(late_total, core, place_index, txt_count).astype(F32)
    video_grad, latent_grad = place(some, video_grad, latent_grad, here_b)
    out_mine = (after_attn + growth.astype(F32)).astype(BF16)
    caption_grad = jnp.zeros((txt_count, own, cap_here, D), F32)
    for step in range(txt_count):
        perm = [(b, a) for a, b in caption_perm(step, 2, txt_count, 2)]
        part = lax.ppermute(
            cap_back[:, step * cap_here : (step + 1) * cap_here], ("vid", "txt"), perm
        )
        caption_grad = lax.dynamic_update_index_in_dim(
            caption_grad, part.astype(F32), (place_index + step) % txt_count, 0
        )
    caption_grad = caption_grad.reshape(caption_tokens.shape)

    gains = late[4 * head_width :]

    def give_back(values):
        other = swap_cores(values[:, lat_half:].astype(BF16)).astype(values.dtype)
        whole = jnp.zeros((items_here, lat_half, D), values.dtype)
        whole = lax.dynamic_update_slice_in_dim(whole, values[:, :lat_half], core * own, 0)
        return lax.dynamic_update_slice_in_dim(whole, other, (1 - core) * own, 0)

    latents_out = give_back(out_mine)
    kept_count = gains[1, 0].astype(jnp.int32)
    return (
        latents_out,
        latent_grad,
        video_grad,
        caption_grad,
        late[:head_width].T,
        late[head_width : 2 * head_width].T,
        late[2 * head_width : 3 * head_width].T,
        late[3 * head_width : 4 * head_width],
        jnp.where(core == 0, early, early_other).astype(F32),
        jnp.where(core == 0, early_other, early).astype(F32),
        gains[17],
        gains[16],
        gains[0],
        kept_count,
    )


def norm_back_rows(values, gain, upstream):
    mean = jnp.mean(values, axis=-1, keepdims=True)
    center = values - mean
    rate = lax.rsqrt(jnp.mean(center * center, axis=-1, keepdims=True) + 1e-05)
    hat = center * rate
    scaled = upstream * gain
    first = jnp.mean(scaled, axis=-1, keepdims=True)
    second = jnp.mean(scaled * hat, axis=-1, keepdims=True)
    return rate * (scaled - first - hat * second), jnp.sum(upstream * hat, axis=-2)


def fits(mesh):
    shape = mesh.shape
    return shape["vid"] == 2 and shape["txt"] == 4 and shape["head"] == 4


def solution(mesh):
    in_specs = (
        P("txt", "vid", None),
        P("txt", "vid", None),
        P("vid", "txt", None),
        P("vid"),
        P("vid", "txt"),
        P("txt"),
        P(),
        P(),
        P(),
        P(None, "head"),
        P(None, "head"),
        P(None, "head"),
        P("head", None),
        P(None, "head"),
        P("head", None),
        P("txt", "vid", None),
    )
    out_specs = (
        P("txt", "vid", None),
        P("txt", "vid", None),
        P("txt", "vid", None),
        P("vid", "txt", None),
        P(None, "head"),
        P(None, "head"),
        P(None, "head"),
        P("head", None),
        P(None, "head"),
        P("head", None),
        P(),
        P(),
        P(),
        P(),
    )
    return jax.shard_map(local if fits(mesh) else local_general, mesh=mesh, in_specs=in_specs, out_specs=out_specs, check_vma=False)
```

```python
import functools
import math

import jax
import jax.numpy as jnp
from jax import lax
from jax.experimental import pallas as pl
from jax.experimental.pallas import tpu as pltpu
from jax.sharding import PartitionSpec as P

D = 768
HEADS = 12


def combined_all(part, axis, combine):
    gathered = jax.tree.map(lambda a: lax.all_gather(a, axis), part)

    def take(source):
        return jax.tree.map(lambda a: lax.dynamic_index_in_dim(a, source, 0, False), gathered)

    return lax.fori_loop(
        1, lax.axis_size(axis), lambda source, state: combine(state, take(source)), take(0)
    )


def layer_norm(values, gain):
    center = values - jnp.mean(values, axis=-1, keepdims=True)
    spread = jnp.mean(center * center, axis=-1, keepdims=True)
    return center * lax.rsqrt(spread + 1e-05) * gain


def norm_back(values, gain, upstream):
    result, pullback = jax.vjp(layer_norm, values, gain)
    return pullback(upstream)


def gelu_exact(values):
    return jax.nn.gelu(values, approximate=False)


def combine_stats(first, second):
    peak = jnp.maximum(first[0], second[0])
    total = first[1] * jnp.exp(first[0] - peak) + second[1] * jnp.exp(second[0] - peak)
    return (peak, total)


def to_blocks(whole, vid_count, txt_count):
    items, rows, width = whole.shape
    split = whole.reshape(txt_count, items // txt_count, vid_count, rows // vid_count, width)
    return split.transpose(2, 0, 1, 3, 4).reshape(
        vid_count * txt_count, items // txt_count, rows // vid_count, width
    )


def from_blocks(blocked, vid_count, txt_count):
    count, items_here, rows_here, width = blocked.shape
    split = blocked.reshape(vid_count, txt_count, items_here, rows_here, width)
    return split.transpose(1, 2, 0, 3, 4).reshape(
        txt_count * items_here, vid_count * rows_here, width
    )


def place_sum(whole, part, start):
    current = lax.dynamic_slice_in_dim(whole, start, part.shape[0], 0)
    return lax.dynamic_update_slice_in_dim(whole, current + part, start, 0)


def place_stats(peak_all, total_all, peak, total, start):
    old_peak = lax.dynamic_slice_in_dim(peak_all, start, peak.shape[0], 0)
    old_total = lax.dynamic_slice_in_dim(total_all, start, peak.shape[0], 0)
    new_peak, new_total = combine_stats((old_peak, old_total), (peak, total))
    peak_all = lax.dynamic_update_slice_in_dim(peak_all, new_peak, start, 0)
    total_all = lax.dynamic_update_slice_in_dim(total_all, new_total, start, 0)
    return (peak_all, total_all)


def take_rows(whole, start, count):
    return lax.dynamic_slice_in_dim(whole, start, count, 0)


def local_general(
    latents,
    video_tokens,
    caption_tokens,
    caption_len,
    key_mask,
    drop_flags,
    gain_latent,
    gain_tokens,
    gain_mlp,
    query_weight,
    key_matrix,
    value_matrix,
    out_weight,
    up_weight,
    down_weight,
    cotangent,
):
    vid_count = lax.axis_size("vid")
    txt_count = lax.axis_size("txt")
    vid_index = lax.axis_index("vid")
    txt_index = lax.axis_index("txt")
    items_here = latents.shape[0]
    cap_items = caption_tokens.shape[0]
    items_total = items_here * txt_count
    head_width = query_weight.shape[1]
    head_size = D // HEADS
    heads_here = head_width // head_size
    scale = 1.0 / math.sqrt(head_size)
    video_here = video_tokens.shape[1]
    cap_here = caption_tokens.shape[1]
    video_start = txt_index * items_here
    cap_start = vid_index * cap_items
    keep = (1 - drop_flags).astype(jnp.float32)
    slots = txt_index * cap_here + jnp.arange(cap_here, dtype=jnp.int32)
    cap_valid = (slots[None, :] < caption_len[:, None]) & (key_mask == 1)
    cap_mask = cap_valid[:, None, None, :]

    def split_heads(values):
        return values.reshape(values.shape[0], values.shape[1], heads_here, head_size)

    lat_float = latents.astype(jnp.float32)
    lat_norm = layer_norm(lat_float, gain_latent).astype(jnp.bfloat16)
    queries = jnp.einsum(
        "bld,de->ble", lat_norm, query_weight, preferred_element_type=jnp.float32
    ).astype(jnp.bfloat16)
    all_queries = from_blocks(
        lax.all_gather(queries[None], ("vid", "txt"), axis=0, tiled=True), vid_count, txt_count
    )
    lat_total = all_queries.shape[1]
    video_queries = take_rows(all_queries, video_start, items_here)
    cap_queries = take_rows(all_queries, cap_start, cap_items)
    video_float = video_tokens.astype(jnp.float32)
    cap_float = caption_tokens.astype(jnp.float32)
    video_normed = layer_norm(video_float, gain_tokens).astype(jnp.bfloat16)
    caption_normed = layer_norm(cap_float, gain_tokens).astype(jnp.bfloat16)
    video_keys = jnp.einsum(
        "flc,co->flo", video_normed, key_matrix, preferred_element_type=jnp.float32
    ).astype(jnp.bfloat16)
    video_values = jnp.einsum(
        "flc,co->flo", video_normed, value_matrix, preferred_element_type=jnp.float32
    ).astype(jnp.bfloat16)
    cap_keys = jnp.einsum(
        "flc,co->flo", caption_normed, key_matrix, preferred_element_type=jnp.float32
    ).astype(jnp.bfloat16)
    cap_values = jnp.einsum(
        "flc,co->flo", caption_normed, value_matrix, preferred_element_type=jnp.float32
    ).astype(jnp.bfloat16)
    video_scores = (
        jnp.einsum(
            "blhe,bkhe->bhlk",
            split_heads(video_queries),
            split_heads(video_keys),
            preferred_element_type=jnp.float32,
        )
        * scale
    )
    cap_scores = (
        jnp.einsum(
            "blhe,bkhe->bhlk",
            split_heads(cap_queries),
            split_heads(cap_keys),
            preferred_element_type=jnp.float32,
        )
        * scale
    )
    cap_scores = jnp.where(cap_mask, cap_scores, -1e30)
    video_peak = jnp.max(video_scores, axis=-1)
    video_total = jnp.sum(jnp.exp(video_scores - video_peak[..., None]), axis=-1)
    cap_peak = jnp.max(cap_scores, axis=-1)
    cap_total = jnp.sum(
        jnp.where(cap_mask, jnp.exp(cap_scores - cap_peak[..., None]), 0.0), axis=-1
    )
    peak_all = jnp.full((items_total, heads_here, lat_total), -1e30, jnp.float32)
    total_all = jnp.zeros((items_total, heads_here, lat_total), jnp.float32)
    peak_all, total_all = place_stats(peak_all, total_all, video_peak, video_total, video_start)
    peak_all, total_all = place_stats(peak_all, total_all, cap_peak, cap_total, cap_start)
    peak, total = combined_all((peak_all, total_all), ("vid", "txt"), combine_stats)
    video_probs = (
        jnp.exp(video_scores - take_rows(peak, video_start, items_here)[..., None])
        / take_rows(total, video_start, items_here)[..., None]
    )
    cap_probs = jnp.where(
        cap_mask,
        jnp.exp(cap_scores - take_rows(peak, cap_start, cap_items)[..., None])
        / take_rows(total, cap_start, cap_items)[..., None],
        0.0,
    )
    video_low = video_probs.astype(jnp.bfloat16)
    cap_low = cap_probs.astype(jnp.bfloat16)
    video_part = jnp.einsum(
        "bhlk,bkhe->blhe", video_low, split_heads(video_values), preferred_element_type=jnp.float32
    ).reshape(items_here, lat_total, head_width)
    cap_part = jnp.einsum(
        "bhlk,bkhe->blhe", cap_low, split_heads(cap_values), preferred_element_type=jnp.float32
    ).reshape(cap_items, lat_total, head_width)
    value_all = jnp.zeros((items_total, lat_total, head_width), jnp.float32)
    value_all = place_sum(place_sum(value_all, video_part, video_start), cap_part, cap_start)
    attended = lax.psum_scatter(
        to_blocks(value_all, vid_count, txt_count), ("vid", "txt"), scatter_dimension=0, tiled=True
    )[0]
    mixed_in = (attended * keep[:, None, None]).astype(jnp.bfloat16)
    branch = lax.psum(
        jnp.einsum("ble,ed->bld", mixed_in, out_weight, preferred_element_type=jnp.float32), "head"
    )
    after_attn = lat_float + branch
    mlp_norm = layer_norm(after_attn, gain_mlp).astype(jnp.bfloat16)
    pre_act = jnp.einsum("bld,df->blf", mlp_norm, up_weight, preferred_element_type=jnp.float32)
    activ = gelu_exact(pre_act).astype(jnp.bfloat16)
    growth = lax.psum(
        jnp.einsum("blf,fd->bld", activ, down_weight, preferred_element_type=jnp.float32).astype(
            jnp.bfloat16
        ),
        "head",
    ).astype(jnp.float32)
    latents_out = (after_attn + growth).astype(jnp.bfloat16)
    grad_down = jnp.einsum("blf,bld->fd", activ, cotangent, preferred_element_type=jnp.float32)
    d_activ = jnp.einsum("bld,fd->blf", cotangent, down_weight, preferred_element_type=jnp.float32)
    d_pre = jax.vjp(gelu_exact, pre_act)[1](d_activ)[0].astype(jnp.bfloat16)
    grad_up = jnp.einsum("bld,blf->df", mlp_norm, d_pre, preferred_element_type=jnp.float32)
    d_mlp_norm = lax.psum(
        jnp.einsum("blf,df->bld", d_pre, up_weight, preferred_element_type=jnp.float32), "head"
    )
    d_after_norm, grad_gain_mlp = norm_back(after_attn, gain_mlp, d_mlp_norm)
    d_after = cotangent.astype(jnp.float32) + d_after_norm
    d_branch = d_after.astype(jnp.bfloat16)
    grad_out = jnp.einsum("ble,bld->ed", mixed_in, d_branch, preferred_element_type=jnp.float32)
    d_att = (
        jnp.einsum("bld,ed->ble", d_branch, out_weight, preferred_element_type=jnp.float32)
        * keep[:, None, None]
    ).astype(jnp.bfloat16)
    all_d_att = from_blocks(
        lax.all_gather(d_att[None], ("vid", "txt"), axis=0, tiled=True), vid_count, txt_count
    )
    video_d_att = split_heads(take_rows(all_d_att, video_start, items_here))
    cap_d_att = split_heads(take_rows(all_d_att, cap_start, cap_items))
    video_dprobs = jnp.einsum(
        "blhe,bkhe->bhlk",
        video_d_att,
        split_heads(video_values),
        preferred_element_type=jnp.float32,
    )
    cap_dprobs = jnp.einsum(
        "blhe,bkhe->bhlk", cap_d_att, split_heads(cap_values), preferred_element_type=jnp.float32
    )
    delta_all = jnp.zeros((items_total, heads_here, lat_total), jnp.float32)
    delta_all = place_sum(delta_all, jnp.sum(video_probs * video_dprobs, axis=-1), video_start)
    delta_all = place_sum(delta_all, jnp.sum(cap_probs * cap_dprobs, axis=-1), cap_start)
    delta = lax.psum(delta_all, ("vid", "txt"))
    video_dscores = (
        video_probs * (video_dprobs - take_rows(delta, video_start, items_here)[..., None])
    ).astype(jnp.bfloat16)
    cap_dscores = (
        cap_probs * (cap_dprobs - take_rows(delta, cap_start, cap_items)[..., None])
    ).astype(jnp.bfloat16)
    video_dq = (
        jnp.einsum(
            "bhlk,bkhe->blhe",
            video_dscores,
            split_heads(video_keys),
            preferred_element_type=jnp.float32,
        )
        * scale
    ).reshape(items_here, lat_total, head_width)
    cap_dq = (
        jnp.einsum(
            "bhlk,bkhe->blhe",
            cap_dscores,
            split_heads(cap_keys),
            preferred_element_type=jnp.float32,
        )
        * scale
    ).reshape(cap_items, lat_total, head_width)
    query_all = jnp.zeros((items_total, lat_total, head_width), jnp.float32)
    query_all = place_sum(place_sum(query_all, video_dq, video_start), cap_dq, cap_start)
    d_queries = lax.psum_scatter(
        to_blocks(query_all, vid_count, txt_count), ("vid", "txt"), scatter_dimension=0, tiled=True
    )[0].astype(jnp.bfloat16)
    video_key_grad = (
        (
            jnp.einsum(
                "bhlk,blhe->bkhe",
                video_dscores,
                split_heads(video_queries),
                preferred_element_type=jnp.float32,
            )
            * scale
        )
        .reshape(items_here, video_here, head_width)
        .astype(jnp.bfloat16)
    )
    video_value_grad = (
        jnp.einsum("bhlk,blhe->bkhe", video_low, video_d_att, preferred_element_type=jnp.float32)
        .reshape(items_here, video_here, head_width)
        .astype(jnp.bfloat16)
    )
    caption_key_grad = (
        (
            jnp.einsum(
                "bhlk,blhe->bkhe",
                cap_dscores,
                split_heads(cap_queries),
                preferred_element_type=jnp.float32,
            )
            * scale
        )
        .reshape(cap_items, cap_here, head_width)
        .astype(jnp.bfloat16)
    )
    caption_value_grad = (
        jnp.einsum("bhlk,blhe->bkhe", cap_low, cap_d_att, preferred_element_type=jnp.float32)
        .reshape(cap_items, cap_here, head_width)
        .astype(jnp.bfloat16)
    )
    grad_query = jnp.einsum("bld,ble->de", lat_norm, d_queries, preferred_element_type=jnp.float32)
    d_lat_norm = lax.psum(
        jnp.einsum("ble,de->bld", d_queries, query_weight, preferred_element_type=jnp.float32),
        "head",
    )
    d_lat_back, grad_gain_latent = norm_back(lat_float, gain_latent, d_lat_norm)
    latent_grad = d_after + d_lat_back
    grad_key = jnp.einsum(
        "zsg,zsv->gv", video_normed, video_key_grad, preferred_element_type=jnp.float32
    ) + jnp.einsum(
        "zsg,zsv->gv", caption_normed, caption_key_grad, preferred_element_type=jnp.float32
    )
    grad_value = jnp.einsum(
        "zsg,zsv->gv", video_normed, video_value_grad, preferred_element_type=jnp.float32
    ) + jnp.einsum(
        "zsg,zsv->gv", caption_normed, caption_value_grad, preferred_element_type=jnp.float32
    )
    video_term = jnp.einsum(
        "ayt,ot->ayo", video_key_grad, key_matrix, preferred_element_type=jnp.float32
    ) + jnp.einsum(
        "ayt,ot->ayo", video_value_grad, value_matrix, preferred_element_type=jnp.float32
    )
    cap_term = jnp.einsum(
        "ayt,ot->ayo", caption_key_grad, key_matrix, preferred_element_type=jnp.float32
    ) + jnp.einsum(
        "ayt,ot->ayo", caption_value_grad, value_matrix, preferred_element_type=jnp.float32
    )
    d_video_norm, d_cap_norm = lax.psum((video_term, cap_term), "head")
    video_grad, video_gain_part = norm_back(video_float, gain_tokens, d_video_norm)
    caption_grad, cap_gain_part = norm_back(cap_float, gain_tokens, d_cap_norm)
    grad_gain_tokens = video_gain_part + cap_gain_part
    kept_here = jnp.sum(keep)
    (
        grad_query,
        grad_key,
        grad_value,
        grad_out,
        grad_up,
        grad_down,
        grad_gain_latent,
        grad_gain_tokens,
        grad_gain_mlp,
        kept_total,
    ) = lax.psum(
        (
            grad_query,
            grad_key,
            grad_value,
            grad_out,
            grad_up,
            grad_down,
            grad_gain_latent,
            grad_gain_tokens,
            grad_gain_mlp,
            kept_here,
        ),
        ("vid", "txt"),
    )
    kept_count = (kept_total / vid_count).astype(jnp.int32)
    return (
        latents_out,
        latent_grad,
        video_grad,
        caption_grad,
        grad_query,
        grad_key,
        grad_value,
        grad_out,
        grad_up,
        grad_down,
        grad_gain_latent,
        grad_gain_tokens,
        grad_gain_mlp,
        kept_count,
    )


def swap_cores(values):
    return lax.ppermute(values, "vid", [(0, 1), (1, 0)])


def head_shift(values, shift, count):
    return lax.ppermute(values, "head", [(i, (i - shift) % count) for i in range(count)])


def take_block(values, index, size, axis=0):
    return lax.dynamic_slice_in_dim(values, index * size, size, axis)


def reduce_over_head(part, place, count):
    low = part.astype(BF16)
    total = lax.dynamic_index_in_dim(part, place, 0, False)
    for shift in range(1, count):
        chunk = lax.dynamic_index_in_dim(low, (place - shift) % count, 0, False)
        total = total + head_shift(chunk, shift, count).astype(F32)
    return total.astype(BF16)


def gather_head(total, place, count):
    result = jnp.zeros((count,) + total.shape, BF16)
    result = lax.dynamic_update_index_in_dim(result, total, place, 0)
    for shift in range(1, count):
        result = lax.dynamic_update_index_in_dim(
            result, head_shift(total, shift, count), (place + shift) % count, 0
        )
    return result


def group_steps(count):
    return [(step, [(i, (i - step) % count) for i in range(count)]) for step in range(1, count)]


def reduce_over_cores(rows, core):
    half = rows.shape[0] // 2
    other = swap_cores(take_block(rows, 1 - core, half))
    return take_block(rows, core, half).astype(F32) + other.astype(F32), other


def reduce_over_group(half, place, count):
    part = half.shape[0] // count
    low = half.astype(BF16)
    total = take_block(half, place, part)
    for step, perm in group_steps(count):
        chunk = take_block(low, (place - step) % count, part)
        total = total + lax.ppermute(chunk, "txt", perm).astype(F32)
    return total.astype(BF16)


def gather_group(total, core, place, count):
    part = total.shape[0]
    half = part * count
    mine = jnp.zeros((half, total.shape[1]), BF16)
    mine = lax.dynamic_update_slice_in_dim(mine, total, place * part, 0)
    for step, perm in group_steps(count):
        mine = lax.dynamic_update_slice_in_dim(
            mine, lax.ppermute(total, "txt", perm), (place + step) % count * part, 0
        )
    whole = jnp.zeros((2 * half, total.shape[1]), BF16)
    whole = lax.dynamic_update_slice_in_dim(whole, mine, core * half, 0)
    return lax.dynamic_update_slice_in_dim(whole, swap_cores(mine), (1 - core) * half, 0)


def caption_perm(step, vid_count, txt_count, cores):
    pairs = []
    for v in range(vid_count):
        for t in range(txt_count):
            block = (t + step) % txt_count
            dest_txt = v * (txt_count // vid_count) + block // cores
            dest_vid = block % cores
            pairs.append((v * txt_count + t, dest_vid * txt_count + dest_txt))
    return pairs


PAIR = 128
BACK_COST = 3
F32 = jnp.float32
BF16 = jnp.bfloat16


def dot_nt(a, b):
    return lax.dot_general(a, b, (((1,), (1,)), ((), ())), preferred_element_type=F32)


def dot_nn(a, b):
    return lax.dot_general(a, b, (((1,), (0,)), ((), ())), preferred_element_type=F32)


def dot_tn(a, b):
    return lax.dot_general(a, b, (((0,), (0,)), ((), ())), preferred_element_type=F32)


def square(ref):
    return ref[...].reshape(D, D)


def two_heads(values):
    low = lax.broadcasted_iota(jnp.int32, values.shape, 1) < PAIR // 2
    zero = jnp.zeros_like(values)
    return jnp.concatenate([jnp.where(low, values, zero), jnp.where(low, zero, values)], axis=0)


def from_two_heads(both):
    n = both.shape[1] // 2
    first = lax.broadcasted_iota(jnp.int32, (PAIR, n), 0) < PAIR // 2
    return jnp.where(first, both[:, :n], both[:, n:]).T


def chunk_list(video, cap, size):
    return [(start, size) for start in range(0, video, size)] + [(video, cap)]


def norm_kernel(s_ref, tok_ref, gain_ref, *refs):
    gain = gain_ref[...]
    out_ref = refs[-1]
    for at in range(0, tok_ref.shape[0], 64):
        rows = pl.ds(at, 64)
        out_ref[rows, :] = layer_norm(tok_ref[rows, :].astype(F32), gain).astype(BF16)


def cap_mask(cap_ref):
    mask = cap_ref[:, pl.ds(D, PAIR)]
    return jnp.concatenate([mask, mask], axis=1).astype(F32) > 0.5


def forward_kernel(s_ref, tok_ref, cap_ref, gain_ref, lat_ref, gain_lat_ref, wq_ref, wkv_ref, *refs):
    q_ref, k_ref, v_ref, lse_ref, o_ref, s_scr, e_scr, wkv_scr = refs[-8:]
    keys, width = k_ref.shape
    cap = cap_ref.shape[0]
    step = (keys - cap) // 4
    latn = layer_norm(lat_ref[...].astype(F32), gain_lat_ref[...]).astype(BF16)
    queries = dot_nt(latn, wq_ref[...].reshape(width, D)).astype(BF16).astype(F32)
    q_ref[...] = (queries * 0.125).astype(BF16)

    @pl.when(pl.program_id(0) == 0)
    def _():
        wkv_scr[...] = wkv_ref[...].reshape(2 * width, D).T

    def project(rows, tokens):
        both = dot_nn(tokens, wkv_scr[...]).astype(BF16)
        k_ref[rows, :] = both[:, :width]
        v_ref[rows, :] = both[:, width:]

    def project_video(c, carry):
        rows = pl.ds(pl.multiple_of(c * step, 16), step)
        project(rows, tok_ref[rows, :])
        return carry

    lax.fori_loop(0, 4, project_video, 0)
    cap_rows = pl.ds(keys - cap, cap)
    project(cap_rows, layer_norm(cap_ref[:, pl.ds(0, D)].astype(F32), gain_ref[...]).astype(BF16))
    pieces = [pl.ds(start, 64) for start in range(0, keys, 64)]

    def pair(p, carry):
        cols = pl.ds(pl.multiple_of(p * PAIR, PAIR), PAIR)
        q2 = two_heads(q_ref[:, cols])
        s_scr[...] = dot_nt(k_ref[:, cols], q2)
        s_scr[cap_rows, :] = jnp.where(cap_mask(cap_ref), s_scr[cap_rows, :], -1e30)
        peak = s_scr[pieces[0], :]
        for rows in pieces[1:]:
            peak = jnp.maximum(peak, s_scr[rows, :])
        peak = jnp.max(peak, axis=0, keepdims=True)
        total = jnp.zeros((8, q2.shape[0]), F32)
        for rows in pieces:
            e = jnp.exp(s_scr[rows, :] - peak)
            e_scr[rows, :] = e.astype(BF16)
            total = total + jnp.sum(e.reshape(-1, 8, q2.shape[0]), axis=0)
        total = jnp.sum(total, axis=0, keepdims=True)
        out = dot_tn(v_ref[:, cols], e_scr[...])
        o_ref[:, cols] = from_two_heads(out / total)
        lse_ref[pl.ds(p, 1), :] = peak + jnp.log(total)
        return carry

    lax.fori_loop(0, width // PAIR, pair, 0)


def backward_kernel(
    s_ref, q_ref, k_ref, v_ref, lse_ref, o_ref, datt_ref, own_ref, other_ref, cap_ref,
    wk_ref, wv_ref, gain_ref, tok_ref, wq_ref, lat_ref, after_ref, gain_lat_ref, ready_ref,
    own_out, other_out, cap_out, lat_out, late_ref,
    dq_ref, dk_ref, dv_ref, s_scr, dp_scr, p_scr, ds_scr, up_scr, sums_ref, gain_out,
):
    item = pl.program_id(0)
    keys = k_ref.shape[0]
    cap = cap_ref.shape[0]
    cap_rows = pl.ds(keys - cap, cap)
    pieces = [pl.ds(start, 64) for start in range(0, keys, 64)]

    def pair(p, carry):
        cols = pl.ds(pl.multiple_of(p * PAIR, PAIR), PAIR)
        q2 = two_heads(q_ref[:, cols])
        d_att = datt_ref[:, cols]
        d2 = two_heads(d_att)
        prod = (d_att.astype(F32) * o_ref[:, cols]).T
        delta = jnp.concatenate(
            [
                jnp.sum(prod[: PAIR // 2], axis=0, keepdims=True),
                jnp.sum(prod[PAIR // 2 :], axis=0, keepdims=True),
            ],
            axis=1,
        )
        pairs_here = D // PAIR // lse_ref.shape[0]
        lse = lse_ref[p // pairs_here, pl.ds(p % pairs_here, 1), :]
        s_scr[...] = dot_nt(k_ref[:, cols], q2)
        dp_scr[...] = dot_nt(v_ref[:, cols], d2)
        s_scr[cap_rows, :] = jnp.where(cap_mask(cap_ref), s_scr[cap_rows, :], -1e30)
        for rows in pieces:
            probs = jnp.exp(s_scr[rows, :] - lse)
            p_scr[rows, :] = probs.astype(BF16)
            ds_scr[rows, :] = (probs * (dp_scr[rows, :] - delta)).astype(BF16)
        dv_ref[:, cols] = dot_nn(p_scr[...], d2).astype(BF16)
        dk_ref[:, cols] = dot_nn(ds_scr[...], q2).astype(BF16)
        dq = dot_tn(k_ref[:, cols], ds_scr[...])
        dq_ref[:, cols] = (from_two_heads(dq) * 0.125).astype(BF16)
        return carry

    lax.fori_loop(0, D // PAIR, pair, 0)
    gain = gain_ref[...]

    @pl.when(item == 0)
    def _():
        gain_out[...] = jnp.zeros_like(gain_out)
        sums_ref[...] = jnp.zeros_like(sums_ref)

    wide = sums_ref.shape[0] // 3
    window = pl.ds(pl.multiple_of(s_ref[2], PAIR), wide)
    video_rows = pl.ds(0, keys - cap)
    cap_norm = layer_norm(cap_ref[:, pl.ds(0, D)].astype(F32), gain).astype(BF16)
    latn = layer_norm(lat_ref[...].astype(F32), gain_lat_ref[...]).astype(BF16)
    sums_ref[pl.ds(0, wide), :] += dot_tn(dq_ref[:, window], latn)

    def both(rows):
        return jnp.concatenate([dk_ref[rows, window], dv_ref[rows, window]], axis=1)

    sums_ref[pl.ds(wide, 2 * wide), :] += dot_tn(both(video_rows), tok_ref[...]) + dot_tn(
        both(cap_rows), cap_norm
    )

    def norm_back(x, up, gain, row):
        center = x - jnp.mean(x, axis=-1, keepdims=True)
        rate = lax.rsqrt(jnp.mean(center * center, axis=-1, keepdims=True) + 1e-05)
        hat = center * rate
        gain_out[pl.ds(8 * row, 8), :] += jnp.sum((up * hat).reshape(-1, 8, D), axis=0)
        scaled = up * gain
        first = jnp.mean(scaled, axis=-1, keepdims=True)
        second = jnp.mean(scaled * hat, axis=-1, keepdims=True)
        return rate * (scaled - first - hat * second)

    half = lat_out.shape[0]
    lat_grad = after_ref[...] + norm_back(
        lat_ref[...].astype(F32), dot_nn(dq_ref[...], square(wq_ref)), gain_lat_ref[...], 1
    )
    lat_out[...] = lat_grad[:half]
    other_out[pl.ds(other_ref.shape[0], half), :] = lat_grad[half:].astype(BF16)

    start = 0
    for ref, out, size in ((own_ref, own_out, 256), (other_ref, other_out, 256), (cap_ref, cap_out, cap)):
        def chunk(c, carry, ref=ref, out=out, size=size, start=start):
            rows = pl.ds(pl.multiple_of(c * size, 16), size)
            key_rows = pl.ds(pl.multiple_of(start + c * size, 16), size)
            up_scr[pl.ds(0, size), :] = dot_nn(dk_ref[key_rows, :], square(wk_ref)) + dot_nn(
                dv_ref[key_rows, :], square(wv_ref)
            )
            for at in range(0, size, 32):
                piece = pl.ds(pl.multiple_of(c * size, 16) + at, 32)
                back = norm_back(
                    ref[piece, pl.ds(0, D)].astype(F32), up_scr[pl.ds(at, 32), :], gain, 0
                )
                out[piece, :] = back.astype(out.dtype)
            return carry

        lax.fori_loop(0, ref.shape[0] // size, chunk, 0)
        start += ref.shape[0]

    @pl.when(item == pl.num_programs(0) - 1)
    def _():
        width = D // 4
        for n in range(3):
            mine = pl.ds(pl.multiple_of(s_ref[3] + n * wide, PAIR // 2), width)
            late_ref[pl.ds(n * width, width), :] = sums_ref[mine, :].astype(BF16)
        ready = ready_ref.shape[0]
        late_ref[pl.ds(3 * width, ready), :] = ready_ref[...]
        gains = [jnp.sum(gain_out[pl.ds(8 * row, 8), :], axis=0, keepdims=True) for row in (0, 1)]
        gains = jnp.concatenate(gains + [jnp.zeros((14, D), F32)], axis=0)
        late_ref[pl.ds(3 * width + ready, 16), :] = gains.astype(BF16)
        spare = late_ref.shape[0] - 3 * width - ready - 16
        late_ref[pl.ds(3 * width + ready + 16, spare), :] = jnp.zeros((spare, D), BF16)


def place_kernel(s_ref, video_in, lat_in, video_part, lat_part, video_ref, lat_ref):
    video_ref[...] = video_part[...].astype(F32)

    @pl.when(pl.program_id(1) == 0)
    def _():
        lat_ref[...] = lat_part[...].astype(F32)


def local(
    latents,
    video_tokens,
    caption_tokens,
    caption_len,
    key_mask,
    drop_flags,
    gain_latent,
    gain_tokens,
    gain_mlp,
    query_weight,
    key_matrix,
    value_matrix,
    out_weight,
    up_weight,
    down_weight,
    cotangent,
):
    txt_count = lax.axis_size("txt")
    head_count = lax.axis_size("head")
    core = lax.axis_index("vid")
    place_index = lax.axis_index("txt")
    z = lax.axis_index("head")
    items_here = latents.shape[0]
    own = items_here // 2
    lat_half = latents.shape[1]
    lat_rows = 2 * lat_half
    video_here = video_tokens.shape[1]
    cap_here = caption_tokens.shape[1]
    cap_rows = cap_here * txt_count
    keys_here = 2 * video_here + cap_rows
    head_width = query_weight.shape[1]

    def dot(spec, a, b):
        return jnp.einsum(spec, a, b, preferred_element_type=F32)

    packed = jnp.stack([key_matrix.T, value_matrix.T, query_weight.T, out_weight])
    half = take_block(packed, core, 2)
    up1 = lax.ppermute(half, "head", [(0, 1), (1, 2), (2, 3)])
    down1 = lax.ppermute(half, "head", [(1, 0), (2, 1), (3, 2)])
    near_at = z // 2
    zero = jnp.int32(0)
    own_at = z % 2
    part_shape = (2, 2, 2, head_width, D)

    def place_chunk(whole, chunk, at_core, at_chunk):
        chunk = chunk.reshape((-1, 2, 1) + chunk.shape[-2:])
        return lax.dynamic_update_slice(whole, chunk, (at_core, zero, at_chunk, zero, zero))

    video_other = swap_cores(take_block(video_tokens, 1 - core, own))
    both = jnp.concatenate([latents, cotangent], axis=1)
    both_own = take_block(both, core, own)
    both_other = swap_cores(take_block(both, 1 - core, own))
    lat = jnp.concatenate([both_own[:, :lat_half], both_other[:, :lat_half]], axis=1)
    cot = jnp.concatenate([both_own[:, lat_half:], both_other[:, lat_half:]], axis=1)
    drop_own = take_block(drop_flags, core, own)
    keep = (1 - drop_own).astype(F32)
    window = z * head_width // PAIR * PAIR
    inside = z * head_width - window
    scalars = jnp.stack([core, near_at, window, inside])
    scalars_far = jnp.stack([core, 1 - near_at, window, inside])

    place_slots = place_index * cap_here + jnp.arange(cap_here, dtype=jnp.int32)
    cap_valid = (place_slots[None, :] < caption_len[:, None]) & (key_mask == 1)
    flags = jnp.broadcast_to(cap_valid.astype(BF16)[:, :, None], cap_valid.shape + (PAIR,))
    cap_message = jnp.concatenate([caption_tokens, flags], axis=2)
    cap_parts = []
    for step in range(txt_count):
        block = take_block(cap_message, (place_index + step) % txt_count, own)
        cap_parts.append(
            lax.ppermute(block, ("vid", "txt"), caption_perm(step, 2, txt_count, 2))
        )
    def item_spec(rows, width=D, first=0):
        return pl.BlockSpec((None, rows, width), lambda i, s: (first + i, 0, 0))

    def own_spec(rows, first=0):
        return pl.BlockSpec((None, rows, D), lambda i, s: (s[0] * own + first + i, 0, 0))

    def whole_spec(*shape):
        return pl.BlockSpec(shape, lambda i, s: (0,) * len(shape))

    def weight_spec(m):
        return pl.BlockSpec(
            (2, None, None, 2, head_width, D),
            lambda i, s: (0, m // 2, m % 2, 0, 0, 0),
            pipeline_mode=pl.Buffered(1),
        )

    def part_spec(at_core, first, count):
        return pl.BlockSpec(
            (None, count, 2, head_width, D),
            lambda i, s: (at_core, first, 0, 0, 0),
            pipeline_mode=pl.Buffered(1),
        )

    def half_spec(rows):
        return pl.BlockSpec((None, rows, 2 * head_width), lambda i, s: (i, 0, s[1]))

    row_spec = pl.BlockSpec((1, D), lambda i, s: (0, 0))

    def call(kernel, name, ins, outs, operands, micros, scratch=(), aliases={}, scalars=scalars, grid=own):
        return pl.pallas_call(
            kernel,
            name=name,
            grid_spec=pltpu.PrefetchScalarGridSpec(
                num_scalar_prefetch=1,
                grid=(grid,),
                in_specs=ins,
                out_specs=[spec for spec, _, _ in outs],
                scratch_shapes=list(scratch),
            ),
            out_shape=[jax.ShapeDtypeStruct(shape, dtype) for _, shape, dtype in outs],
            input_output_aliases=aliases,
            cost_estimate=pl.CostEstimate(
                flops=micros * 1100 * 10**6, transcendentals=0, bytes_accessed=micros * 10**6
            ),
            compiler_params=pltpu.CompilerParams(vmem_limit_bytes=56 << 20),
        )(scalars, *operands)

    def item_out(rows, dtype, width=D):
        return (item_spec(rows, width), (own, rows, width), dtype)

    gain_lat_row = gain_latent[None]
    gain_tok_row = gain_tokens[None]
    gain_mlp_row = gain_mlp[None]
    def token_norm(part, spec, tokens, before=()):
        return call(
            norm_kernel,
            "token_norm",
            [spec, row_spec] + [pl.BlockSpec(memory_space=pl.ANY)] * len(before),
            [
                (
                    pl.BlockSpec((None, video_here, D), lambda i, s: (i, part, 0)),
                    (own, 2 * video_here, D),
                    BF16,
                )
            ],
            (tokens, gain_tok_row) + tuple(before),
            5,
            aliases={3: 0} if before else {},
        )

    tok_norm = token_norm(0, own_spec(video_here), video_tokens)
    (tok_norm,) = token_norm(1, item_spec(video_here), video_other, tok_norm)
    tok_norm, up1, down1, cap_parts = lax.optimization_barrier((tok_norm, up1, down1, cap_parts))
    cap = jnp.concatenate(cap_parts, axis=1)
    partner = jnp.where(z % 2 == 1, up1, down1)
    near = jnp.zeros(part_shape, BF16)
    near = place_chunk(near, packed.reshape((2, 2) + packed.shape[1:]), zero, own_at)
    near = place_chunk(near, partner, core, 1 - own_at)
    near = place_chunk(near, swap_cores(partner), 1 - core, 1 - own_at)

    half_then, _ = lax.optimization_barrier((half, up1))
    up2 = lax.ppermute(up1, "head", [(1, 2), (2, 3)])
    down2 = lax.ppermute(down1, "head", [(1, 0), (2, 1)])
    up3 = lax.ppermute(half_then, "head", [(0, 3)])
    down3 = lax.ppermute(half_then, "head", [(3, 0)])

    def forward(part, scalars, before=()):
        return call(
            forward_kernel,
            "attention_forward",
            [item_spec(2 * video_here), item_spec(cap_rows, D + PAIR), row_spec]
            + [item_spec(lat_rows), row_spec]
            + [part_spec(1, 0, 1), part_spec(0, 0, 2)]
            + [pl.BlockSpec(memory_space=pl.ANY)] * len(before),
            [
                (half_spec(lat_rows), (own, lat_rows, D), BF16),
                (half_spec(keys_here), (own, keys_here, D), BF16),
                (half_spec(keys_here), (own, keys_here, D), BF16),
                (
                    pl.BlockSpec((None, None, 8, 2 * lat_rows), lambda i, s: (i, s[1], 0, 0)),
                    (own, 2, 8, 2 * lat_rows),
                    F32,
                ),
                (half_spec(lat_rows), (own, lat_rows, D), F32),
            ],
            (tok_norm, cap, gain_tok_row, lat, gain_lat_row, part, part) + tuple(before),
            23,
            [
                pltpu.VMEM((keys_here, 2 * lat_rows), F32),
                pltpu.VMEM((keys_here, 2 * lat_rows), BF16),
                pltpu.VMEM((D, 4 * head_width), BF16),
            ],
            {8 + n: n for n in range(len(before))},
            scalars,
        )

    before = forward(near, scalars)
    before, up2, down2, up3, down3 = lax.optimization_barrier((before, up2, down2, up3, down3))

    def by_place(*choices):
        low = jnp.where(z == 0, choices[0], choices[1])
        return jnp.where(z < 2, low, jnp.where(z == 2, choices[2], choices[3]))

    far_mine = jnp.stack(
        [by_place(down2, down1, up2, up3), by_place(down3, down2, up1, up2)], axis=1
    )
    far = jnp.zeros(part_shape, BF16)
    far = lax.dynamic_update_index_in_dim(far, far_mine, core, 0)
    far = lax.dynamic_update_index_in_dim(far, swap_cores(far_mine), 1 - core, 0)
    def both_halves(near, far):
        whole = jnp.zeros((2,) + near.shape, BF16)
        whole = lax.dynamic_update_index_in_dim(whole, near, near_at, 0)
        return lax.dynamic_update_index_in_dim(whole, far, 1 - near_at, 0)

    queries, keys, values, lse, attended = forward(far, scalars_far, before)
    w_out = both_halves(near[1, 1], far[1, 1]).reshape(D, D)
    lat_float = lat.astype(F32)
    mixed_in = (attended * keep[:, None, None]).astype(BF16)
    after_attn = lat_float + dot("ble,ed->bld", mixed_in, w_out)
    mlp_norm = layer_norm(after_attn, gain_mlp).astype(BF16)

    pre_act = dot("bld,df->blf", mlp_norm, up_weight)
    activ, gelu_pull = jax.vjp(gelu_exact, pre_act)
    activ = activ.astype(BF16)
    d_pre = gelu_pull(dot("bld,fd->blf", cot, down_weight))[0].astype(BF16)
    d_mlp_part = dot("blf,df->bld", d_pre, up_weight)
    d_mlp_part, activ, d_pre = lax.optimization_barrier((d_mlp_part, activ, d_pre))
    d_mlp_norm = gather_head(reduce_over_head(d_mlp_part, z, head_count), z, head_count)
    grad_down = dot("blf,bld->fd", activ, cot).astype(BF16)
    grad_up = dot("bld,blf->df", mlp_norm, d_pre).astype(BF16)
    near, far, _ = lax.optimization_barrier((near, far, d_mlp_part))
    weights = both_halves(near, far)
    early = jnp.where(core == 0, grad_up, grad_down).astype(F32)
    early = early + swap_cores(jnp.where(core == 0, grad_down, grad_up)).astype(F32)
    activ, d_mlp_norm, early, weights = lax.optimization_barrier(
        (activ, d_mlp_norm, early.astype(BF16), weights)
    )
    early = lax.psum(early, "txt")
    growth = reduce_over_head(dot("blf,fd->bld", activ, down_weight), z, head_count)

    d_after_norm, gain_mlp_part = norm_back_rows(after_attn, gain_mlp, d_mlp_norm.astype(F32))
    d_after = cot.astype(F32) + d_after_norm
    d_branch = d_after.astype(BF16)
    d_att = (dot("bld,ed->ble", d_branch, w_out) * keep[:, None, None]).astype(BF16)
    mixed_mine = lax.dynamic_slice_in_dim(mixed_in, z * head_width, head_width, 2)
    grad_out = dot("ble,bld->ed", mixed_mine, d_branch)
    ready = jnp.concatenate(
        [
            grad_out,
            jnp.sum(gain_mlp_part, axis=0)[None],
            jnp.full((1, D), jnp.sum(keep)),
            jnp.zeros((14, D), F32),
        ]
    ).astype(BF16)
    late_size = 4 * head_width + 32
    late_size = late_size + -late_size % (32 * txt_count)
    pair_shape = (keys_here, 2 * lat_rows)
    d_att, ready = lax.optimization_barrier((d_att, ready))
    video_grad, other_back, cap_back, latent_grad, late = call(
        backward_kernel,
        "attention_backward",
        [
            item_spec(lat_rows),
            item_spec(keys_here),
            item_spec(keys_here),
            pl.BlockSpec((None, 2, 8, 2 * lat_rows), lambda i, s: (i, 0, 0, 0)),
            item_spec(lat_rows),
            item_spec(lat_rows),
            own_spec(video_here),
            item_spec(video_here),
            item_spec(cap_rows, D + PAIR),
            weight_spec(0),
            weight_spec(1),
            row_spec,
            item_spec(2 * video_here),
            weight_spec(2),
            item_spec(lat_rows),
            item_spec(lat_rows),
            row_spec,
            whole_spec(*ready.shape),
        ],
        [
            (own_spec(video_here), video_tokens.shape, F32),
            item_out(video_here + lat_half, BF16),
            item_out(cap_rows, BF16),
            (own_spec(lat_half), latents.shape, F32),
            (whole_spec(late_size, D), (late_size, D), BF16),
        ],
        (
            queries, keys, values, lse, attended, d_att, video_tokens, video_other, cap,
            weights, weights, gain_tok_row, tok_norm, weights, lat, d_after, gain_lat_row, ready,
        ),
        BACK_COST,
        [
            pltpu.VMEM((lat_rows, D), BF16),
            pltpu.VMEM((keys_here, D), BF16),
            pltpu.VMEM((keys_here, D), BF16),
            pltpu.VMEM(pair_shape, F32),
            pltpu.VMEM(pair_shape, F32),
            pltpu.VMEM(pair_shape, BF16),
            pltpu.VMEM(pair_shape, BF16),
            pltpu.VMEM((256, D), F32),
            pltpu.VMEM((6 * PAIR, D), F32),
            pltpu.VMEM((16, D), F32),
        ],
    )
    def place(video_grad, latent_grad, part):
        piece = video_here // 2
        return pl.pallas_call(
            place_kernel,
            name="place_rows",
            grid_spec=pltpu.PrefetchScalarGridSpec(
                num_scalar_prefetch=1,
                grid=(own, 2),
                in_specs=[
                    pl.BlockSpec(memory_space=pl.ANY),
                    pl.BlockSpec(memory_space=pl.ANY),
                    pl.BlockSpec((None, piece, D), lambda i, r, s: (i, r, 0)),
                    pl.BlockSpec((None, lat_half, D), lambda i, r, s: (i, video_here // lat_half, 0)),
                ],
                out_specs=[
                    pl.BlockSpec((None, piece, D), lambda i, r, s: ((1 - s[0]) * own + i, r, 0)),
                    pl.BlockSpec((None, lat_half, D), lambda i, r, s: ((1 - s[0]) * own + i, 0, 0)),
                ],
            ),
            out_shape=[
                jax.ShapeDtypeStruct(video_tokens.shape, F32),
                jax.ShapeDtypeStruct(latents.shape, F32),
            ],
            input_output_aliases={1: 0, 2: 1},
            cost_estimate=pl.CostEstimate(
                flops=6 * 10**9, transcendentals=0, bytes_accessed=10**7
            ),
        )(scalars, video_grad, latent_grad, part, part)

    growth, early, late = lax.optimization_barrier((growth, early, late))
    late_half, late_swapped = reduce_over_cores(late, core)
    other_here = swap_cores(other_back)
    cap_back, _ = lax.optimization_barrier((cap_back, late_swapped))
    late_total = reduce_over_group(late_half, place_index, txt_count)
    early_other = swap_cores(early)
    other_here, _ = lax.optimization_barrier((other_here, late_half))
    growth, _ = lax.optimization_barrier((growth, late_swapped))
    growth = gather_head(growth, z, head_count)
    video_grad, latent_grad = place(video_grad, latent_grad, other_here)
    video_grad, latent_grad, late_total = lax.optimization_barrier(
        (video_grad, latent_grad, late_total)
    )
    late = gather_group(late_total, core, place_index, txt_count).astype(F32)
    out_mine = (after_attn + growth.astype(F32)).astype(BF16)
    caption_grad = jnp.zeros((txt_count, own, cap_here, D), F32)
    for step in range(txt_count):
        perm = [(b, a) for a, b in caption_perm(step, 2, txt_count, 2)]
        part = lax.ppermute(
            cap_back[:, step * cap_here : (step + 1) * cap_here], ("vid", "txt"), perm
        )
        caption_grad = lax.dynamic_update_index_in_dim(
            caption_grad, part.astype(F32), (place_index + step) % txt_count, 0
        )
    caption_grad = caption_grad.reshape(caption_tokens.shape)

    gains = late[4 * head_width :]

    def give_back(values):
        other = swap_cores(values[:, lat_half:].astype(BF16)).astype(values.dtype)
        whole = jnp.zeros((items_here, lat_half, D), values.dtype)
        whole = lax.dynamic_update_slice_in_dim(whole, values[:, :lat_half], core * own, 0)
        return lax.dynamic_update_slice_in_dim(whole, other, (1 - core) * own, 0)

    latents_out = give_back(out_mine)
    kept_count = gains[1, 0].astype(jnp.int32)
    return (
        latents_out,
        latent_grad,
        video_grad,
        caption_grad,
        late[:head_width].T,
        late[head_width : 2 * head_width].T,
        late[2 * head_width : 3 * head_width].T,
        late[3 * head_width : 4 * head_width],
        jnp.where(core == 0, early, early_other).astype(F32),
        jnp.where(core == 0, early_other, early).astype(F32),
        gains[17],
        gains[16],
        gains[0],
        kept_count,
    )


def norm_back_rows(values, gain, upstream):
    mean = jnp.mean(values, axis=-1, keepdims=True)
    center = values - mean
    rate = lax.rsqrt(jnp.mean(center * center, axis=-1, keepdims=True) + 1e-05)
    hat = center * rate
    scaled = upstream * gain
    first = jnp.mean(scaled, axis=-1, keepdims=True)
    second = jnp.mean(scaled * hat, axis=-1, keepdims=True)
    return rate * (scaled - first - hat * second), jnp.sum(upstream * hat, axis=-2)


def fits(mesh):
    shape = mesh.shape
    return shape["vid"] == 2 and shape["txt"] == 4 and shape["head"] == 4


def solution(mesh):
    in_specs = (
        P("txt", "vid", None),
        P("txt", "vid", None),
        P("vid", "txt", None),
        P("vid"),
        P("vid", "txt"),
        P("txt"),
        P(),
        P(),
        P(),
        P(None, "head"),
        P(None, "head"),
        P(None, "head"),
        P("head", None),
        P(None, "head"),
        P("head", None),
        P("txt", "vid", None),
    )
    out_specs = (
        P("txt", "vid", None),
        P("txt", "vid", None),
        P("txt", "vid", None),
        P("vid", "txt", None),
        P(None, "head"),
        P(None, "head"),
        P(None, "head"),
        P("head", None),
        P(None, "head"),
        P("head", None),
        P(),
        P(),
        P(),
        P(),
    )
    return jax.shard_map(local if fits(mesh) else local_general, mesh=mesh, in_specs=in_specs, out_specs=out_specs, check_vma=False)
```

```python
import functools
import math

import jax
import jax.numpy as jnp
from jax import lax
from jax.experimental import pallas as pl
from jax.experimental.pallas import tpu as pltpu
from jax.sharding import PartitionSpec as P

D = 768
HEADS = 12


def combined_all(part, axis, combine):
    gathered = jax.tree.map(lambda a: lax.all_gather(a, axis), part)

    def take(source):
        return jax.tree.map(lambda a: lax.dynamic_index_in_dim(a, source, 0, False), gathered)

    return lax.fori_loop(
        1, lax.axis_size(axis), lambda source, state: combine(state, take(source)), take(0)
    )


def layer_norm(values, gain):
    center = values - jnp.mean(values, axis=-1, keepdims=True)
    spread = jnp.mean(center * center, axis=-1, keepdims=True)
    return center * lax.rsqrt(spread + 1e-05) * gain


def norm_back(values, gain, upstream):
    result, pullback = jax.vjp(layer_norm, values, gain)
    return pullback(upstream)


def gelu_exact(values):
    return jax.nn.gelu(values, approximate=False)


def combine_stats(first, second):
    peak = jnp.maximum(first[0], second[0])
    total = first[1] * jnp.exp(first[0] - peak) + second[1] * jnp.exp(second[0] - peak)
    return (peak, total)


def to_blocks(whole, vid_count, txt_count):
    items, rows, width = whole.shape
    split = whole.reshape(txt_count, items // txt_count, vid_count, rows // vid_count, width)
    return split.transpose(2, 0, 1, 3, 4).reshape(
        vid_count * txt_count, items // txt_count, rows // vid_count, width
    )


def from_blocks(blocked, vid_count, txt_count):
    count, items_here, rows_here, width = blocked.shape
    split = blocked.reshape(vid_count, txt_count, items_here, rows_here, width)
    return split.transpose(1, 2, 0, 3, 4).reshape(
        txt_count * items_here, vid_count * rows_here, width
    )


def place_sum(whole, part, start):
    current = lax.dynamic_slice_in_dim(whole, start, part.shape[0], 0)
    return lax.dynamic_update_slice_in_dim(whole, current + part, start, 0)


def place_stats(peak_all, total_all, peak, total, start):
    old_peak = lax.dynamic_slice_in_dim(peak_all, start, peak.shape[0], 0)
    old_total = lax.dynamic_slice_in_dim(total_all, start, peak.shape[0], 0)
    new_peak, new_total = combine_stats((old_peak, old_total), (peak, total))
    peak_all = lax.dynamic_update_slice_in_dim(peak_all, new_peak, start, 0)
    total_all = lax.dynamic_update_slice_in_dim(total_all, new_total, start, 0)
    return (peak_all, total_all)


def take_rows(whole, start, count):
    return lax.dynamic_slice_in_dim(whole, start, count, 0)


def local_general(
    latents,
    video_tokens,
    caption_tokens,
    caption_len,
    key_mask,
    drop_flags,
    gain_latent,
    gain_tokens,
    gain_mlp,
    query_weight,
    key_matrix,
    value_matrix,
    out_weight,
    up_weight,
    down_weight,
    cotangent,
):
    vid_count = lax.axis_size("vid")
    txt_count = lax.axis_size("txt")
    vid_index = lax.axis_index("vid")
    txt_index = lax.axis_index("txt")
    items_here = latents.shape[0]
    cap_items = caption_tokens.shape[0]
    items_total = items_here * txt_count
    head_width = query_weight.shape[1]
    head_size = D // HEADS
    heads_here = head_width // head_size
    scale = 1.0 / math.sqrt(head_size)
    video_here = video_tokens.shape[1]
    cap_here = caption_tokens.shape[1]
    video_start = txt_index * items_here
    cap_start = vid_index * cap_items
    keep = (1 - drop_flags).astype(jnp.float32)
    slots = txt_index * cap_here + jnp.arange(cap_here, dtype=jnp.int32)
    cap_valid = (slots[None, :] < caption_len[:, None]) & (key_mask == 1)
    cap_mask = cap_valid[:, None, None, :]

    def split_heads(values):
        return values.reshape(values.shape[0], values.shape[1], heads_here, head_size)

    lat_float = latents.astype(jnp.float32)
    lat_norm = layer_norm(lat_float, gain_latent).astype(jnp.bfloat16)
    queries = jnp.einsum(
        "bld,de->ble", lat_norm, query_weight, preferred_element_type=jnp.float32
    ).astype(jnp.bfloat16)
    all_queries = from_blocks(
        lax.all_gather(queries[None], ("vid", "txt"), axis=0, tiled=True), vid_count, txt_count
    )
    lat_total = all_queries.shape[1]
    video_queries = take_rows(all_queries, video_start, items_here)
    cap_queries = take_rows(all_queries, cap_start, cap_items)
    video_float = video_tokens.astype(jnp.float32)
    cap_float = caption_tokens.astype(jnp.float32)
    video_normed = layer_norm(video_float, gain_tokens).astype(jnp.bfloat16)
    caption_normed = layer_norm(cap_float, gain_tokens).astype(jnp.bfloat16)
    video_keys = jnp.einsum(
        "flc,co->flo", video_normed, key_matrix, preferred_element_type=jnp.float32
    ).astype(jnp.bfloat16)
    video_values = jnp.einsum(
        "flc,co->flo", video_normed, value_matrix, preferred_element_type=jnp.float32
    ).astype(jnp.bfloat16)
    cap_keys = jnp.einsum(
        "flc,co->flo", caption_normed, key_matrix, preferred_element_type=jnp.float32
    ).astype(jnp.bfloat16)
    cap_values = jnp.einsum(
        "flc,co->flo", caption_normed, value_matrix, preferred_element_type=jnp.float32
    ).astype(jnp.bfloat16)
    video_scores = (
        jnp.einsum(
            "blhe,bkhe->bhlk",
            split_heads(video_queries),
            split_heads(video_keys),
            preferred_element_type=jnp.float32,
        )
        * scale
    )
    cap_scores = (
        jnp.einsum(
            "blhe,bkhe->bhlk",
            split_heads(cap_queries),
            split_heads(cap_keys),
            preferred_element_type=jnp.float32,
        )
        * scale
    )
    cap_scores = jnp.where(cap_mask, cap_scores, -1e30)
    video_peak = jnp.max(video_scores, axis=-1)
    video_total = jnp.sum(jnp.exp(video_scores - video_peak[..., None]), axis=-1)
    cap_peak = jnp.max(cap_scores, axis=-1)
    cap_total = jnp.sum(
        jnp.where(cap_mask, jnp.exp(cap_scores - cap_peak[..., None]), 0.0), axis=-1
    )
    peak_all = jnp.full((items_total, heads_here, lat_total), -1e30, jnp.float32)
    total_all = jnp.zeros((items_total, heads_here, lat_total), jnp.float32)
    peak_all, total_all = place_stats(peak_all, total_all, video_peak, video_total, video_start)
    peak_all, total_all = place_stats(peak_all, total_all, cap_peak, cap_total, cap_start)
    peak, total = combined_all((peak_all, total_all), ("vid", "txt"), combine_stats)
    video_probs = (
        jnp.exp(video_scores - take_rows(peak, video_start, items_here)[..., None])
        / take_rows(total, video_start, items_here)[..., None]
    )
    cap_probs = jnp.where(
        cap_mask,
        jnp.exp(cap_scores - take_rows(peak, cap_start, cap_items)[..., None])
        / take_rows(total, cap_start, cap_items)[..., None],
        0.0,
    )
    video_low = video_probs.astype(jnp.bfloat16)
    cap_low = cap_probs.astype(jnp.bfloat16)
    video_part = jnp.einsum(
        "bhlk,bkhe->blhe", video_low, split_heads(video_values), preferred_element_type=jnp.float32
    ).reshape(items_here, lat_total, head_width)
    cap_part = jnp.einsum(
        "bhlk,bkhe->blhe", cap_low, split_heads(cap_values), preferred_element_type=jnp.float32
    ).reshape(cap_items, lat_total, head_width)
    value_all = jnp.zeros((items_total, lat_total, head_width), jnp.float32)
    value_all = place_sum(place_sum(value_all, video_part, video_start), cap_part, cap_start)
    attended = lax.psum_scatter(
        to_blocks(value_all, vid_count, txt_count), ("vid", "txt"), scatter_dimension=0, tiled=True
    )[0]
    mixed_in = (attended * keep[:, None, None]).astype(jnp.bfloat16)
    branch = lax.psum(
        jnp.einsum("ble,ed->bld", mixed_in, out_weight, preferred_element_type=jnp.float32), "head"
    )
    after_attn = lat_float + branch
    mlp_norm = layer_norm(after_attn, gain_mlp).astype(jnp.bfloat16)
    pre_act = jnp.einsum("bld,df->blf", mlp_norm, up_weight, preferred_element_type=jnp.float32)
    activ = gelu_exact(pre_act).astype(jnp.bfloat16)
    growth = lax.psum(
        jnp.einsum("blf,fd->bld", activ, down_weight, preferred_element_type=jnp.float32).astype(
            jnp.bfloat16
        ),
        "head",
    ).astype(jnp.float32)
    latents_out = (after_attn + growth).astype(jnp.bfloat16)
    grad_down = jnp.einsum("blf,bld->fd", activ, cotangent, preferred_element_type=jnp.float32)
    d_activ = jnp.einsum("bld,fd->blf", cotangent, down_weight, preferred_element_type=jnp.float32)
    d_pre = jax.vjp(gelu_exact, pre_act)[1](d_activ)[0].astype(jnp.bfloat16)
    grad_up = jnp.einsum("bld,blf->df", mlp_norm, d_pre, preferred_element_type=jnp.float32)
    d_mlp_norm = lax.psum(
        jnp.einsum("blf,df->bld", d_pre, up_weight, preferred_element_type=jnp.float32), "head"
    )
    d_after_norm, grad_gain_mlp = norm_back(after_attn, gain_mlp, d_mlp_norm)
    d_after = cotangent.astype(jnp.float32) + d_after_norm
    d_branch = d_after.astype(jnp.bfloat16)
    grad_out = jnp.einsum("ble,bld->ed", mixed_in, d_branch, preferred_element_type=jnp.float32)
    d_att = (
        jnp.einsum("bld,ed->ble", d_branch, out_weight, preferred_element_type=jnp.float32)
        * keep[:, None, None]
    ).astype(jnp.bfloat16)
    all_d_att = from_blocks(
        lax.all_gather(d_att[None], ("vid", "txt"), axis=0, tiled=True), vid_count, txt_count
    )
    video_d_att = split_heads(take_rows(all_d_att, video_start, items_here))
    cap_d_att = split_heads(take_rows(all_d_att, cap_start, cap_items))
    video_dprobs = jnp.einsum(
        "blhe,bkhe->bhlk",
        video_d_att,
        split_heads(video_values),
        preferred_element_type=jnp.float32,
    )
    cap_dprobs = jnp.einsum(
        "blhe,bkhe->bhlk", cap_d_att, split_heads(cap_values), preferred_element_type=jnp.float32
    )
    delta_all = jnp.zeros((items_total, heads_here, lat_total), jnp.float32)
    delta_all = place_sum(delta_all, jnp.sum(video_probs * video_dprobs, axis=-1), video_start)
    delta_all = place_sum(delta_all, jnp.sum(cap_probs * cap_dprobs, axis=-1), cap_start)
    delta = lax.psum(delta_all, ("vid", "txt"))
    video_dscores = (
        video_probs * (video_dprobs - take_rows(delta, video_start, items_here)[..., None])
    ).astype(jnp.bfloat16)
    cap_dscores = (
        cap_probs * (cap_dprobs - take_rows(delta, cap_start, cap_items)[..., None])
    ).astype(jnp.bfloat16)
    video_dq = (
        jnp.einsum(
            "bhlk,bkhe->blhe",
            video_dscores,
            split_heads(video_keys),
            preferred_element_type=jnp.float32,
        )
        * scale
    ).reshape(items_here, lat_total, head_width)
    cap_dq = (
        jnp.einsum(
            "bhlk,bkhe->blhe",
            cap_dscores,
            split_heads(cap_keys),
            preferred_element_type=jnp.float32,
        )
        * scale
    ).reshape(cap_items, lat_total, head_width)
    query_all = jnp.zeros((items_total, lat_total, head_width), jnp.float32)
    query_all = place_sum(place_sum(query_all, video_dq, video_start), cap_dq, cap_start)
    d_queries = lax.psum_scatter(
        to_blocks(query_all, vid_count, txt_count), ("vid", "txt"), scatter_dimension=0, tiled=True
    )[0].astype(jnp.bfloat16)
    video_key_grad = (
        (
            jnp.einsum(
                "bhlk,blhe->bkhe",
                video_dscores,
                split_heads(video_queries),
                preferred_element_type=jnp.float32,
            )
            * scale
        )
        .reshape(items_here, video_here, head_width)
        .astype(jnp.bfloat16)
    )
    video_value_grad = (
        jnp.einsum("bhlk,blhe->bkhe", video_low, video_d_att, preferred_element_type=jnp.float32)
        .reshape(items_here, video_here, head_width)
        .astype(jnp.bfloat16)
    )
    caption_key_grad = (
        (
            jnp.einsum(
                "bhlk,blhe->bkhe",
                cap_dscores,
                split_heads(cap_queries),
                preferred_element_type=jnp.float32,
            )
            * scale
        )
        .reshape(cap_items, cap_here, head_width)
        .astype(jnp.bfloat16)
    )
    caption_value_grad = (
        jnp.einsum("bhlk,blhe->bkhe", cap_low, cap_d_att, preferred_element_type=jnp.float32)
        .reshape(cap_items, cap_here, head_width)
        .astype(jnp.bfloat16)
    )
    grad_query = jnp.einsum("bld,ble->de", lat_norm, d_queries, preferred_element_type=jnp.float32)
    d_lat_norm = lax.psum(
        jnp.einsum("ble,de->bld", d_queries, query_weight, preferred_element_type=jnp.float32),
        "head",
    )
    d_lat_back, grad_gain_latent = norm_back(lat_float, gain_latent, d_lat_norm)
    latent_grad = d_after + d_lat_back
    grad_key = jnp.einsum(
        "zsg,zsv->gv", video_normed, video_key_grad, preferred_element_type=jnp.float32
    ) + jnp.einsum(
        "zsg,zsv->gv", caption_normed, caption_key_grad, preferred_element_type=jnp.float32
    )
    grad_value = jnp.einsum(
        "zsg,zsv->gv", video_normed, video_value_grad, preferred_element_type=jnp.float32
    ) + jnp.einsum(
        "zsg,zsv->gv", caption_normed, caption_value_grad, preferred_element_type=jnp.float32
    )
    video_term = jnp.einsum(
        "ayt,ot->ayo", video_key_grad, key_matrix, preferred_element_type=jnp.float32
    ) + jnp.einsum(
        "ayt,ot->ayo", video_value_grad, value_matrix, preferred_element_type=jnp.float32
    )
    cap_term = jnp.einsum(
        "ayt,ot->ayo", caption_key_grad, key_matrix, preferred_element_type=jnp.float32
    ) + jnp.einsum(
        "ayt,ot->ayo", caption_value_grad, value_matrix, preferred_element_type=jnp.float32
    )
    d_video_norm, d_cap_norm = lax.psum((video_term, cap_term), "head")
    video_grad, video_gain_part = norm_back(video_float, gain_tokens, d_video_norm)
    caption_grad, cap_gain_part = norm_back(cap_float, gain_tokens, d_cap_norm)
    grad_gain_tokens = video_gain_part + cap_gain_part
    kept_here = jnp.sum(keep)
    (
        grad_query,
        grad_key,
        grad_value,
        grad_out,
        grad_up,
        grad_down,
        grad_gain_latent,
        grad_gain_tokens,
        grad_gain_mlp,
        kept_total,
    ) = lax.psum(
        (
            grad_query,
            grad_key,
            grad_value,
            grad_out,
            grad_up,
            grad_down,
            grad_gain_latent,
            grad_gain_tokens,
            grad_gain_mlp,
            kept_here,
        ),
        ("vid", "txt"),
    )
    kept_count = (kept_total / vid_count).astype(jnp.int32)
    return (
        latents_out,
        latent_grad,
        video_grad,
        caption_grad,
        grad_query,
        grad_key,
        grad_value,
        grad_out,
        grad_up,
        grad_down,
        grad_gain_latent,
        grad_gain_tokens,
        grad_gain_mlp,
        kept_count,
    )


def swap_cores(values):
    return lax.ppermute(values, "vid", [(0, 1), (1, 0)])


def head_shift(values, shift, count):
    return lax.ppermute(values, "head", [(i, (i - shift) % count) for i in range(count)])


def take_block(values, index, size, axis=0):
    return lax.dynamic_slice_in_dim(values, index * size, size, axis)


def reduce_over_head(part, place, count):
    low = part.astype(BF16)
    total = lax.dynamic_index_in_dim(part, place, 0, False)
    for shift in range(1, count):
        chunk = lax.dynamic_index_in_dim(low, (place - shift) % count, 0, False)
        total = total + head_shift(chunk, shift, count).astype(F32)
    return total.astype(BF16)


def gather_head(total, place, count):
    result = jnp.zeros((count,) + total.shape, BF16)
    result = lax.dynamic_update_index_in_dim(result, total, place, 0)
    for shift in range(1, count):
        result = lax.dynamic_update_index_in_dim(
            result, head_shift(total, shift, count), (place + shift) % count, 0
        )
    return result


def group_steps(count):
    return [(step, [(i, (i - step) % count) for i in range(count)]) for step in range(1, count)]


def reduce_over_cores(rows, core):
    half = rows.shape[0] // 2
    other = swap_cores(take_block(rows, 1 - core, half))
    return take_block(rows, core, half).astype(F32) + other.astype(F32), other


def reduce_over_group(half, place, count):
    part = half.shape[0] // count
    low = half.astype(BF16)
    total = take_block(half, place, part)
    for step, perm in group_steps(count):
        chunk = take_block(low, (place - step) % count, part)
        total = total + lax.ppermute(chunk, "txt", perm).astype(F32)
    return total.astype(BF16)


def gather_places(total, place, count):
    part = total.shape[0]
    mine = jnp.zeros((part * count, total.shape[1]), BF16)
    mine = lax.dynamic_update_slice_in_dim(mine, total, place * part, 0)
    for step, perm in group_steps(count):
        mine = lax.dynamic_update_slice_in_dim(
            mine, lax.ppermute(total, "txt", perm), (place + step) % count * part, 0
        )
    return mine


def gather_cores(mine, core):
    half = mine.shape[0]
    whole = jnp.zeros((2 * half, mine.shape[1]), BF16)
    whole = lax.dynamic_update_slice_in_dim(whole, mine, core * half, 0)
    return lax.dynamic_update_slice_in_dim(whole, swap_cores(mine), (1 - core) * half, 0)


def caption_perm(step, vid_count, txt_count, cores):
    pairs = []
    for v in range(vid_count):
        for t in range(txt_count):
            block = (t + step) % txt_count
            dest_txt = v * (txt_count // vid_count) + block // cores
            dest_vid = block % cores
            pairs.append((v * txt_count + t, dest_vid * txt_count + dest_txt))
    return pairs


PAIR = 128
BACK_COST = 3
F32 = jnp.float32
BF16 = jnp.bfloat16


def dot_nt(a, b):
    return lax.dot_general(a, b, (((1,), (1,)), ((), ())), preferred_element_type=F32)


def dot_nn(a, b):
    return lax.dot_general(a, b, (((1,), (0,)), ((), ())), preferred_element_type=F32)


def dot_tn(a, b):
    return lax.dot_general(a, b, (((0,), (0,)), ((), ())), preferred_element_type=F32)


def square(ref):
    return ref[...].reshape(D, D)


def two_heads(values):
    low = lax.broadcasted_iota(jnp.int32, values.shape, 1) < PAIR // 2
    zero = jnp.zeros_like(values)
    return jnp.concatenate([jnp.where(low, values, zero), jnp.where(low, zero, values)], axis=0)


def from_two_heads(both):
    n = both.shape[1] // 2
    first = lax.broadcasted_iota(jnp.int32, (PAIR, n), 0) < PAIR // 2
    return jnp.where(first, both[:, :n], both[:, n:]).T


def chunk_list(video, cap, size):
    return [(start, size) for start in range(0, video, size)] + [(video, cap)]


def norm_kernel(s_ref, own_ref, other_ref, gain_ref, out_ref):
    gain = gain_ref[...]
    start = 0
    for ref in (own_ref, other_ref):
        def chunk(c, carry, ref=ref, start=start):
            for part in range(2):
                at = pl.multiple_of(c * 128, 128) + 64 * part
                out_ref[pl.ds(start + at, 64), :] = layer_norm(
                    ref[pl.ds(at, 64), :].astype(F32), gain
                ).astype(BF16)
            return carry

        lax.fori_loop(0, ref.shape[0] // 128, chunk, 0)
        start += ref.shape[0]


def cap_mask(cap_ref):
    mask = cap_ref[:, pl.ds(D, PAIR)]
    return jnp.concatenate([mask, mask], axis=1).astype(F32) > 0.5


def forward_kernel(s_ref, tok_ref, cap_ref, gain_ref, lat_ref, gain_lat_ref, wq_ref, wkv_ref, *refs):
    q_ref, k_ref, v_ref, lse_ref, o_ref, s_scr, e_scr, wkv_scr = refs[-8:]
    keys, width = k_ref.shape
    cap = cap_ref.shape[0]
    step = (keys - cap) // 4
    latn = layer_norm(lat_ref[...].astype(F32), gain_lat_ref[...]).astype(BF16)
    queries = dot_nt(latn, wq_ref[...].reshape(width, D)).astype(BF16).astype(F32)
    q_ref[...] = (queries * 0.125).astype(BF16)

    @pl.when(pl.program_id(0) == 0)
    def _():
        wkv_scr[...] = wkv_ref[...].reshape(2 * width, D).T

    def project(rows, tokens):
        both = dot_nn(tokens, wkv_scr[...]).astype(BF16)
        k_ref[rows, :] = both[:, :width]
        v_ref[rows, :] = both[:, width:]

    def project_video(c, carry):
        rows = pl.ds(pl.multiple_of(c * step, 16), step)
        project(rows, tok_ref[rows, :])
        return carry

    lax.fori_loop(0, 4, project_video, 0)
    cap_rows = pl.ds(keys - cap, cap)
    project(cap_rows, layer_norm(cap_ref[:, pl.ds(0, D)].astype(F32), gain_ref[...]).astype(BF16))
    pieces = [pl.ds(start, 64) for start in range(0, keys, 64)]

    def pair(p, carry):
        cols = pl.ds(pl.multiple_of(p * PAIR, PAIR), PAIR)
        q2 = two_heads(q_ref[:, cols])
        s_scr[...] = dot_nt(k_ref[:, cols], q2)
        s_scr[cap_rows, :] = jnp.where(cap_mask(cap_ref), s_scr[cap_rows, :], -1e30)
        peak = s_scr[pieces[0], :]
        for rows in pieces[1:]:
            peak = jnp.maximum(peak, s_scr[rows, :])
        peak = jnp.max(peak, axis=0, keepdims=True)
        total = jnp.zeros((8, q2.shape[0]), F32)
        for rows in pieces:
            e = jnp.exp(s_scr[rows, :] - peak)
            e_scr[rows, :] = e.astype(BF16)
            total = total + jnp.sum(e.reshape(-1, 8, q2.shape[0]), axis=0)
        total = jnp.sum(total, axis=0, keepdims=True)
        out = dot_tn(v_ref[:, cols], e_scr[...])
        o_ref[:, cols] = from_two_heads(out / total)
        lse_ref[pl.ds(p, 1), :] = peak + jnp.log(total)
        return carry

    lax.fori_loop(0, width // PAIR, pair, 0)


def backward_kernel(
    s_ref, q_ref, k_ref, v_ref, lse_ref, o_ref, datt_ref, own_ref, other_ref, cap_ref,
    wk_ref, wv_ref, gain_ref, tok_ref, wq_ref, lat_ref, after_ref, gain_lat_ref, ready_ref,
    own_out, other_out, cap_out, lat_out, late_ref,
    dq_ref, dk_ref, dv_ref, s_scr, dp_scr, p_scr, ds_scr, up_scr, sums_ref, gain_out,
):
    item = pl.program_id(0)
    keys = k_ref.shape[0]
    cap = cap_ref.shape[0]
    cap_rows = pl.ds(keys - cap, cap)
    pieces = [pl.ds(start, 64) for start in range(0, keys, 64)]

    def pair(p, carry):
        cols = pl.ds(pl.multiple_of(p * PAIR, PAIR), PAIR)
        q2 = two_heads(q_ref[:, cols])
        d_att = datt_ref[:, cols]
        d2 = two_heads(d_att)
        prod = (d_att.astype(F32) * o_ref[:, cols]).T
        delta = jnp.concatenate(
            [
                jnp.sum(prod[: PAIR // 2], axis=0, keepdims=True),
                jnp.sum(prod[PAIR // 2 :], axis=0, keepdims=True),
            ],
            axis=1,
        )
        pairs_here = D // PAIR // lse_ref.shape[0]
        lse = lse_ref[p // pairs_here, pl.ds(p % pairs_here, 1), :]
        s_scr[...] = dot_nt(k_ref[:, cols], q2)
        dp_scr[...] = dot_nt(v_ref[:, cols], d2)
        s_scr[cap_rows, :] = jnp.where(cap_mask(cap_ref), s_scr[cap_rows, :], -1e30)
        for rows in pieces:
            probs = jnp.exp(s_scr[rows, :] - lse)
            p_scr[rows, :] = probs.astype(BF16)
            ds_scr[rows, :] = (probs * (dp_scr[rows, :] - delta)).astype(BF16)
        dv_ref[:, cols] = dot_nn(p_scr[...], d2).astype(BF16)
        dk_ref[:, cols] = dot_nn(ds_scr[...], q2).astype(BF16)
        dq = dot_tn(k_ref[:, cols], ds_scr[...])
        dq_ref[:, cols] = (from_two_heads(dq) * 0.125).astype(BF16)
        return carry

    lax.fori_loop(0, D // PAIR, pair, 0)
    gain = gain_ref[...]

    @pl.when(item == 0)
    def _():
        gain_out[...] = jnp.zeros_like(gain_out)
        sums_ref[...] = jnp.zeros_like(sums_ref)

    wide = sums_ref.shape[0] // 3
    window = pl.ds(pl.multiple_of(s_ref[2], PAIR), wide)
    video_rows = pl.ds(0, keys - cap)
    cap_norm = layer_norm(cap_ref[:, pl.ds(0, D)].astype(F32), gain).astype(BF16)
    latn = layer_norm(lat_ref[...].astype(F32), gain_lat_ref[...]).astype(BF16)
    sums_ref[pl.ds(0, wide), :] += dot_tn(dq_ref[:, window], latn)

    def both(rows):
        return jnp.concatenate([dk_ref[rows, window], dv_ref[rows, window]], axis=1)

    sums_ref[pl.ds(wide, 2 * wide), :] += dot_tn(both(video_rows), tok_ref[...]) + dot_tn(
        both(cap_rows), cap_norm
    )

    def norm_back(x, up, gain, row):
        center = x - jnp.mean(x, axis=-1, keepdims=True)
        rate = lax.rsqrt(jnp.mean(center * center, axis=-1, keepdims=True) + 1e-05)
        hat = center * rate
        gain_out[pl.ds(8 * row, 8), :] += jnp.sum((up * hat).reshape(-1, 8, D), axis=0)
        scaled = up * gain
        first = jnp.mean(scaled, axis=-1, keepdims=True)
        second = jnp.mean(scaled * hat, axis=-1, keepdims=True)
        return rate * (scaled - first - hat * second)

    half = lat_out.shape[0]
    lat_grad = after_ref[...] + norm_back(
        lat_ref[...].astype(F32), dot_nn(dq_ref[...], square(wq_ref)), gain_lat_ref[...], 1
    )
    lat_out[...] = lat_grad[:half]
    other_out[pl.ds(other_ref.shape[0], half), :] = lat_grad[half:].astype(BF16)

    start = 0
    for ref, out, size in ((own_ref, own_out, 256), (other_ref, other_out, 256), (cap_ref, cap_out, cap)):
        def chunk(c, carry, ref=ref, out=out, size=size, start=start):
            rows = pl.ds(pl.multiple_of(c * size, 16), size)
            key_rows = pl.ds(pl.multiple_of(start + c * size, 16), size)
            up_scr[pl.ds(0, size), :] = dot_nn(dk_ref[key_rows, :], square(wk_ref)) + dot_nn(
                dv_ref[key_rows, :], square(wv_ref)
            )
            for at in range(0, size, 32):
                piece = pl.ds(pl.multiple_of(c * size, 16) + at, 32)
                back = norm_back(
                    ref[piece, pl.ds(0, D)].astype(F32), up_scr[pl.ds(at, 32), :], gain, 0
                )
                out[piece, :] = back.astype(out.dtype)
            return carry

        lax.fori_loop(0, ref.shape[0] // size, chunk, 0)
        start += ref.shape[0]

    @pl.when(item == pl.num_programs(0) - 1)
    def _():
        width = D // 4
        for n in range(3):
            mine = pl.ds(pl.multiple_of(s_ref[3] + n * wide, PAIR // 2), width)
            late_ref[pl.ds(n * width, width), :] = sums_ref[mine, :].astype(BF16)
        ready = ready_ref.shape[0]
        late_ref[pl.ds(3 * width, ready), :] = ready_ref[...]
        gains = [jnp.sum(gain_out[pl.ds(8 * row, 8), :], axis=0, keepdims=True) for row in (0, 1)]
        gains = jnp.concatenate(gains + [jnp.zeros((14, D), F32)], axis=0)
        late_ref[pl.ds(3 * width + ready, 16), :] = gains.astype(BF16)
        spare = late_ref.shape[0] - 3 * width - ready - 16
        late_ref[pl.ds(3 * width + ready + 16, spare), :] = jnp.zeros((spare, D), BF16)


def place_kernel(s_ref, video_in, lat_in, video_part, lat_part, video_ref, lat_ref):
    video_ref[...] = video_part[...].astype(F32)

    @pl.when(pl.program_id(1) == 0)
    def _():
        lat_ref[...] = lat_part[...].astype(F32)


def local(
    latents,
    video_tokens,
    caption_tokens,
    caption_len,
    key_mask,
    drop_flags,
    gain_latent,
    gain_tokens,
    gain_mlp,
    query_weight,
    key_matrix,
    value_matrix,
    out_weight,
    up_weight,
    down_weight,
    cotangent,
):
    txt_count = lax.axis_size("txt")
    head_count = lax.axis_size("head")
    core = lax.axis_index("vid")
    place_index = lax.axis_index("txt")
    z = lax.axis_index("head")
    items_here = latents.shape[0]
    own = items_here // 2
    lat_half = latents.shape[1]
    lat_rows = 2 * lat_half
    video_here = video_tokens.shape[1]
    cap_here = caption_tokens.shape[1]
    cap_rows = cap_here * txt_count
    keys_here = 2 * video_here + cap_rows
    head_width = query_weight.shape[1]

    def dot(spec, a, b):
        return jnp.einsum(spec, a, b, preferred_element_type=F32)

    packed = jnp.stack([key_matrix.T, value_matrix.T, query_weight.T, out_weight])
    half = take_block(packed, core, 2)
    up1 = lax.ppermute(half, "head", [(0, 1), (1, 2), (2, 3)])
    down1 = lax.ppermute(half, "head", [(1, 0), (2, 1), (3, 2)])
    near_at = z // 2
    zero = jnp.int32(0)
    own_at = z % 2
    part_shape = (2, 2, 2, head_width, D)

    def place_chunk(whole, chunk, at_core, at_chunk):
        chunk = chunk.reshape((-1, 2, 1) + chunk.shape[-2:])
        return lax.dynamic_update_slice(whole, chunk, (at_core, zero, at_chunk, zero, zero))

    video_other = swap_cores(take_block(video_tokens, 1 - core, own))
    both = jnp.concatenate([latents, cotangent], axis=1)
    both_own = take_block(both, core, own)
    both_other = swap_cores(take_block(both, 1 - core, own))
    lat = jnp.concatenate([both_own[:, :lat_half], both_other[:, :lat_half]], axis=1)
    cot = jnp.concatenate([both_own[:, lat_half:], both_other[:, lat_half:]], axis=1)
    drop_own = take_block(drop_flags, core, own)
    keep = (1 - drop_own).astype(F32)
    window = z * head_width // PAIR * PAIR
    inside = z * head_width - window
    scalars = jnp.stack([core, near_at, window, inside])
    scalars_far = jnp.stack([core, 1 - near_at, window, inside])

    place_slots = place_index * cap_here + jnp.arange(cap_here, dtype=jnp.int32)
    cap_valid = (place_slots[None, :] < caption_len[:, None]) & (key_mask == 1)
    flags = jnp.broadcast_to(cap_valid.astype(BF16)[:, :, None], cap_valid.shape + (PAIR,))
    cap_message = jnp.concatenate([caption_tokens, flags], axis=2)
    cap_parts = []
    for step in range(txt_count):
        block = take_block(cap_message, (place_index + step) % txt_count, own)
        cap_parts.append(
            lax.ppermute(block, ("vid", "txt"), caption_perm(step, 2, txt_count, 2))
        )
    def item_spec(rows, width=D, first=0):
        return pl.BlockSpec((None, rows, width), lambda i, s: (first + i, 0, 0))

    def own_spec(rows, first=0):
        return pl.BlockSpec((None, rows, D), lambda i, s: (s[0] * own + first + i, 0, 0))

    def whole_spec(*shape):
        return pl.BlockSpec(shape, lambda i, s: (0,) * len(shape))

    def weight_spec(m):
        return pl.BlockSpec(
            (2, None, None, 2, head_width, D),
            lambda i, s: (0, m // 2, m % 2, 0, 0, 0),
            pipeline_mode=pl.Buffered(1),
        )

    def part_spec(at_core, first, count):
        return pl.BlockSpec(
            (None, count, 2, head_width, D),
            lambda i, s: (at_core, first, 0, 0, 0),
            pipeline_mode=pl.Buffered(1),
        )

    def half_spec(rows):
        return pl.BlockSpec((None, rows, 2 * head_width), lambda i, s: (i, 0, s[1]))

    row_spec = pl.BlockSpec((1, D), lambda i, s: (0, 0))

    def call(kernel, name, ins, outs, operands, micros, scratch=(), aliases={}, scalars=scalars, grid=own):
        return pl.pallas_call(
            kernel,
            name=name,
            grid_spec=pltpu.PrefetchScalarGridSpec(
                num_scalar_prefetch=1,
                grid=(grid,),
                in_specs=ins,
                out_specs=[spec for spec, _, _ in outs],
                scratch_shapes=list(scratch),
            ),
            out_shape=[jax.ShapeDtypeStruct(shape, dtype) for _, shape, dtype in outs],
            input_output_aliases=aliases,
            cost_estimate=pl.CostEstimate(
                flops=micros * 1100 * 10**6, transcendentals=0, bytes_accessed=micros * 10**6
            ),
            compiler_params=pltpu.CompilerParams(vmem_limit_bytes=56 << 20),
        )(scalars, *operands)

    def item_out(rows, dtype, width=D):
        return (item_spec(rows, width), (own, rows, width), dtype)

    gain_lat_row = gain_latent[None]
    gain_tok_row = gain_tokens[None]
    gain_mlp_row = gain_mlp[None]
    (tok_norm,) = call(
        norm_kernel,
        "token_norm",
        [own_spec(video_here), item_spec(video_here), row_spec],
        [item_out(2 * video_here, BF16)],
        (video_tokens, video_other, gain_tok_row),
        9,
    )
    tok_norm, up1, down1, cap_parts = lax.optimization_barrier((tok_norm, up1, down1, cap_parts))
    cap = jnp.concatenate(cap_parts, axis=1)
    partner = jnp.where(z % 2 == 1, up1, down1)
    near = jnp.zeros(part_shape, BF16)
    near = place_chunk(near, packed.reshape((2, 2) + packed.shape[1:]), zero, own_at)
    near = place_chunk(near, partner, core, 1 - own_at)
    partner_other = swap_cores(partner)
    near = place_chunk(near, partner_other, 1 - core, 1 - own_at)
    up1, down1, half_then, _ = lax.optimization_barrier((up1, down1, half, partner_other))
    ring_up = lax.ppermute(jnp.where(z == 3, half_then, up1), "head", [(1, 2), (2, 3), (3, 0)])
    ring_down = lax.ppermute(jnp.where(z == 0, half_then, down1), "head", [(1, 0), (2, 1), (0, 3)])

    def forward(part, scalars, before=()):
        return call(
            forward_kernel,
            "attention_forward",
            [item_spec(2 * video_here), item_spec(cap_rows, D + PAIR), row_spec]
            + [item_spec(lat_rows), row_spec]
            + [part_spec(1, 0, 1), part_spec(0, 0, 2)]
            + [pl.BlockSpec(memory_space=pl.ANY)] * len(before),
            [
                (half_spec(lat_rows), (own, lat_rows, D), BF16),
                (half_spec(keys_here), (own, keys_here, D), BF16),
                (half_spec(keys_here), (own, keys_here, D), BF16),
                (
                    pl.BlockSpec((None, None, 8, 2 * lat_rows), lambda i, s: (i, s[1], 0, 0)),
                    (own, 2, 8, 2 * lat_rows),
                    F32,
                ),
                (half_spec(lat_rows), (own, lat_rows, D), F32),
            ],
            (tok_norm, cap, gain_tok_row, lat, gain_lat_row, part, part) + tuple(before),
            23,
            [
                pltpu.VMEM((keys_here, 2 * lat_rows), F32),
                pltpu.VMEM((keys_here, 2 * lat_rows), BF16),
                pltpu.VMEM((D, 4 * head_width), BF16),
            ],
            {8 + n: n for n in range(len(before))},
            scalars,
        )

    before = forward(near, scalars)
    before, up1, down1, ring_up, ring_down = lax.optimization_barrier(
        (before, up1, down1, ring_up, ring_down)
    )
    far_low = jnp.where(z == 1, down1, jnp.where(z == 2, ring_up, ring_down))
    far_high = jnp.where(z == 1, ring_down, jnp.where(z == 2, up1, ring_up))
    far_mine = jnp.stack([far_low, far_high], axis=1)
    far = jnp.zeros(part_shape, BF16)
    far = lax.dynamic_update_index_in_dim(far, far_mine, core, 0)
    far = lax.dynamic_update_index_in_dim(far, swap_cores(far_mine), 1 - core, 0)
    def both_halves(near, far):
        whole = jnp.zeros((2,) + near.shape, BF16)
        whole = lax.dynamic_update_index_in_dim(whole, near, near_at, 0)
        return lax.dynamic_update_index_in_dim(whole, far, 1 - near_at, 0)

    queries, keys, values, lse, attended = forward(far, scalars_far, before)
    w_out = both_halves(near[1, 1], far[1, 1]).reshape(D, D)
    lat_float = lat.astype(F32)
    mixed_in = (attended * keep[:, None, None]).astype(BF16)
    after_attn = lat_float + dot("ble,ed->bld", mixed_in, w_out)
    mlp_norm = layer_norm(after_attn, gain_mlp).astype(BF16)

    pre_act = dot("bld,df->blf", mlp_norm, up_weight)
    activ, gelu_pull = jax.vjp(gelu_exact, pre_act)
    activ = activ.astype(BF16)
    d_pre = gelu_pull(dot("bld,fd->blf", cot, down_weight))[0].astype(BF16)
    d_mlp_part = dot("blf,df->bld", d_pre, up_weight)
    d_mlp_part, activ, d_pre = lax.optimization_barrier((d_mlp_part, activ, d_pre))
    d_mlp_norm = gather_head(reduce_over_head(d_mlp_part, z, head_count), z, head_count)
    grad_down = dot("blf,bld->fd", activ, cot).astype(BF16)
    grad_up = dot("bld,blf->df", mlp_norm, d_pre).astype(BF16)
    near, far, _ = lax.optimization_barrier((near, far, d_mlp_part))
    weights = both_halves(near, far)
    early = jnp.where(core == 0, grad_up, grad_down).astype(F32)
    early = early + swap_cores(jnp.where(core == 0, grad_down, grad_up)).astype(F32)
    growth = dot("blf,fd->bld", activ, down_weight)
    growth, d_mlp_norm, early, weights = lax.optimization_barrier(
        (growth, d_mlp_norm, early.astype(BF16), weights)
    )
    early = lax.psum(early, "txt")
    growth = reduce_over_head(growth, z, head_count)

    d_after_norm, gain_mlp_part = norm_back_rows(after_attn, gain_mlp, d_mlp_norm.astype(F32))
    d_after = cot.astype(F32) + d_after_norm
    d_branch = d_after.astype(BF16)
    d_att = (dot("bld,ed->ble", d_branch, w_out) * keep[:, None, None]).astype(BF16)
    mixed_mine = lax.dynamic_slice_in_dim(mixed_in, z * head_width, head_width, 2)
    grad_out = dot("ble,bld->ed", mixed_mine, d_branch)
    ready = jnp.concatenate(
        [
            grad_out,
            jnp.sum(gain_mlp_part, axis=0)[None],
            jnp.full((1, D), jnp.sum(keep)),
            jnp.zeros((14, D), F32),
        ]
    ).astype(BF16)
    late_size = 4 * head_width + 32
    late_size = late_size + -late_size % (32 * txt_count)
    pair_shape = (keys_here, 2 * lat_rows)
    d_att, ready = lax.optimization_barrier((d_att, ready))
    video_grad, other_back, cap_back, latent_grad, late = call(
        backward_kernel,
        "attention_backward",
        [
            item_spec(lat_rows),
            item_spec(keys_here),
            item_spec(keys_here),
            pl.BlockSpec((None, 2, 8, 2 * lat_rows), lambda i, s: (i, 0, 0, 0)),
            item_spec(lat_rows),
            item_spec(lat_rows),
            own_spec(video_here),
            item_spec(video_here),
            item_spec(cap_rows, D + PAIR),
            weight_spec(0),
            weight_spec(1),
            row_spec,
            item_spec(2 * video_here),
            weight_spec(2),
            item_spec(lat_rows),
            item_spec(lat_rows),
            row_spec,
            whole_spec(*ready.shape),
        ],
        [
            (own_spec(video_here), video_tokens.shape, F32),
            item_out(video_here + lat_half, BF16),
            item_out(cap_rows, BF16),
            (own_spec(lat_half), latents.shape, F32),
            (whole_spec(late_size, D), (late_size, D), BF16),
        ],
        (
            queries, keys, values, lse, attended, d_att, video_tokens, video_other, cap,
            weights, weights, gain_tok_row, tok_norm, weights, lat, d_after, gain_lat_row, ready,
        ),
        BACK_COST,
        [
            pltpu.VMEM((lat_rows, D), BF16),
            pltpu.VMEM((keys_here, D), BF16),
            pltpu.VMEM((keys_here, D), BF16),
            pltpu.VMEM(pair_shape, F32),
            pltpu.VMEM(pair_shape, F32),
            pltpu.VMEM(pair_shape, BF16),
            pltpu.VMEM(pair_shape, BF16),
            pltpu.VMEM((256, D), F32),
            pltpu.VMEM((6 * PAIR, D), F32),
            pltpu.VMEM((16, D), F32),
        ],
    )
    def place(video_grad, latent_grad, part):
        piece = video_here // 2
        return pl.pallas_call(
            place_kernel,
            name="place_rows",
            grid_spec=pltpu.PrefetchScalarGridSpec(
                num_scalar_prefetch=1,
                grid=(own, 2),
                in_specs=[
                    pl.BlockSpec(memory_space=pl.ANY),
                    pl.BlockSpec(memory_space=pl.ANY),
                    pl.BlockSpec((None, piece, D), lambda i, r, s: (i, r, 0)),
                    pl.BlockSpec((None, lat_half, D), lambda i, r, s: (i, video_here // lat_half, 0)),
                ],
                out_specs=[
                    pl.BlockSpec((None, piece, D), lambda i, r, s: ((1 - s[0]) * own + i, r, 0)),
                    pl.BlockSpec((None, lat_half, D), lambda i, r, s: ((1 - s[0]) * own + i, 0, 0)),
                ],
            ),
            out_shape=[
                jax.ShapeDtypeStruct(video_tokens.shape, F32),
                jax.ShapeDtypeStruct(latents.shape, F32),
            ],
            input_output_aliases={1: 0, 2: 1},
            cost_estimate=pl.CostEstimate(
                flops=6 * 10**9, transcendentals=0, bytes_accessed=10**7
            ),
        )(scalars, video_grad, latent_grad, part, part)

    growth, early, late = lax.optimization_barrier((growth, early, late))
    late_half, late_swapped = reduce_over_cores(late, core)
    other_back, early, _ = lax.optimization_barrier((other_back, early, late_swapped))
    other_here = swap_cores(other_back)
    early_other = swap_cores(early)
    late_total = reduce_over_group(late_half, place_index, txt_count)
    late_total, growth, early_other, other_here, cap_back = lax.optimization_barrier(
        (late_total, growth, early_other, other_here, cap_back)
    )
    growth = gather_head(growth, z, head_count)
    cap_parts = []
    for step in range(txt_count):
        perm = [(b, a) for a, b in caption_perm(step, 2, txt_count, 2)]
        cap_parts.append(
            lax.ppermute(cap_back[:, step * cap_here : (step + 1) * cap_here], ("vid", "txt"), perm)
        )
    late = gather_places(late_total, place_index, txt_count)
    video_grad, latent_grad = place(video_grad, latent_grad, other_here)
    late, video_grad, latent_grad, cap_parts, growth = lax.optimization_barrier(
        (late, video_grad, latent_grad, cap_parts, growth)
    )
    late = gather_cores(late, core).astype(F32)
    caption_grad = jnp.zeros((txt_count, own, cap_here, D), F32)
    for step, part in enumerate(cap_parts):
        caption_grad = lax.dynamic_update_index_in_dim(
            caption_grad, part.astype(F32), (place_index + step) % txt_count, 0
        )
    caption_grad = caption_grad.reshape(caption_tokens.shape)
    out_mine = (after_attn + growth.reshape(after_attn.shape).astype(F32)).astype(BF16)
    gains = late[4 * head_width :]

    def give_back(values):
        other = swap_cores(values[:, lat_half:].astype(BF16)).astype(values.dtype)
        whole = jnp.zeros((items_here, lat_half, D), values.dtype)
        whole = lax.dynamic_update_slice_in_dim(whole, values[:, :lat_half], core * own, 0)
        return lax.dynamic_update_slice_in_dim(whole, other, (1 - core) * own, 0)

    latents_out = give_back(out_mine)
    kept_count = gains[1, 0].astype(jnp.int32)
    return (
        latents_out,
        latent_grad,
        video_grad,
        caption_grad,
        late[:head_width].T,
        late[head_width : 2 * head_width].T,
        late[2 * head_width : 3 * head_width].T,
        late[3 * head_width : 4 * head_width],
        jnp.where(core == 0, early, early_other).astype(F32),
        jnp.where(core == 0, early_other, early).astype(F32),
        gains[17],
        gains[16],
        gains[0],
        kept_count,
    )


def norm_back_rows(values, gain, upstream):
    mean = jnp.mean(values, axis=-1, keepdims=True)
    center = values - mean
    rate = lax.rsqrt(jnp.mean(center * center, axis=-1, keepdims=True) + 1e-05)
    hat = center * rate
    scaled = upstream * gain
    first = jnp.mean(scaled, axis=-1, keepdims=True)
    second = jnp.mean(scaled * hat, axis=-1, keepdims=True)
    return rate * (scaled - first - hat * second), jnp.sum(upstream * hat, axis=-2)


def fits(mesh):
    shape = mesh.shape
    return shape["vid"] == 2 and shape["txt"] == 4 and shape["head"] == 4


def solution(mesh):
    in_specs = (
        P("txt", "vid", None),
        P("txt", "vid", None),
        P("vid", "txt", None),
        P("vid"),
        P("vid", "txt"),
        P("txt"),
        P(),
        P(),
        P(),
        P(None, "head"),
        P(None, "head"),
        P(None, "head"),
        P("head", None),
        P(None, "head"),
        P("head", None),
        P("txt", "vid", None),
    )
    out_specs = (
        P("txt", "vid", None),
        P("txt", "vid", None),
        P("txt", "vid", None),
        P("vid", "txt", None),
        P(None, "head"),
        P(None, "head"),
        P(None, "head"),
        P("head", None),
        P(None, "head"),
        P("head", None),
        P(),
        P(),
        P(),
        P(),
    )
    return jax.shard_map(local if fits(mesh) else local_general, mesh=mesh, in_specs=in_specs, out_specs=out_specs, check_vma=False)
```

```python
import functools
import math

import jax
import jax.numpy as jnp
from jax import lax
from jax.experimental import pallas as pl
from jax.experimental.pallas import tpu as pltpu
from jax.sharding import PartitionSpec as P

D = 768
HEADS = 12


def combined_all(part, axis, combine):
    gathered = jax.tree.map(lambda a: lax.all_gather(a, axis), part)

    def take(source):
        return jax.tree.map(lambda a: lax.dynamic_index_in_dim(a, source, 0, False), gathered)

    return lax.fori_loop(
        1, lax.axis_size(axis), lambda source, state: combine(state, take(source)), take(0)
    )


def layer_norm(values, gain):
    center = values - jnp.mean(values, axis=-1, keepdims=True)
    spread = jnp.mean(center * center, axis=-1, keepdims=True)
    return center * lax.rsqrt(spread + 1e-05) * gain


def norm_back(values, gain, upstream):
    result, pullback = jax.vjp(layer_norm, values, gain)
    return pullback(upstream)


def gelu_exact(values):
    return jax.nn.gelu(values, approximate=False)


def combine_stats(first, second):
    peak = jnp.maximum(first[0], second[0])
    total = first[1] * jnp.exp(first[0] - peak) + second[1] * jnp.exp(second[0] - peak)
    return (peak, total)


def to_blocks(whole, vid_count, txt_count):
    items, rows, width = whole.shape
    split = whole.reshape(txt_count, items // txt_count, vid_count, rows // vid_count, width)
    return split.transpose(2, 0, 1, 3, 4).reshape(
        vid_count * txt_count, items // txt_count, rows // vid_count, width
    )


def from_blocks(blocked, vid_count, txt_count):
    count, items_here, rows_here, width = blocked.shape
    split = blocked.reshape(vid_count, txt_count, items_here, rows_here, width)
    return split.transpose(1, 2, 0, 3, 4).reshape(
        txt_count * items_here, vid_count * rows_here, width
    )


def place_sum(whole, part, start):
    current = lax.dynamic_slice_in_dim(whole, start, part.shape[0], 0)
    return lax.dynamic_update_slice_in_dim(whole, current + part, start, 0)


def place_stats(peak_all, total_all, peak, total, start):
    old_peak = lax.dynamic_slice_in_dim(peak_all, start, peak.shape[0], 0)
    old_total = lax.dynamic_slice_in_dim(total_all, start, peak.shape[0], 0)
    new_peak, new_total = combine_stats((old_peak, old_total), (peak, total))
    peak_all = lax.dynamic_update_slice_in_dim(peak_all, new_peak, start, 0)
    total_all = lax.dynamic_update_slice_in_dim(total_all, new_total, start, 0)
    return (peak_all, total_all)


def take_rows(whole, start, count):
    return lax.dynamic_slice_in_dim(whole, start, count, 0)


def local_general(
    latents,
    video_tokens,
    caption_tokens,
    caption_len,
    key_mask,
    drop_flags,
    gain_latent,
    gain_tokens,
    gain_mlp,
    query_weight,
    key_matrix,
    value_matrix,
    out_weight,
    up_weight,
    down_weight,
    cotangent,
):
    vid_count = lax.axis_size("vid")
    txt_count = lax.axis_size("txt")
    vid_index = lax.axis_index("vid")
    txt_index = lax.axis_index("txt")
    items_here = latents.shape[0]
    cap_items = caption_tokens.shape[0]
    items_total = items_here * txt_count
    head_width = query_weight.shape[1]
    head_size = D // HEADS
    heads_here = head_width // head_size
    scale = 1.0 / math.sqrt(head_size)
    video_here = video_tokens.shape[1]
    cap_here = caption_tokens.shape[1]
    video_start = txt_index * items_here
    cap_start = vid_index * cap_items
    keep = (1 - drop_flags).astype(jnp.float32)
    slots = txt_index * cap_here + jnp.arange(cap_here, dtype=jnp.int32)
    cap_valid = (slots[None, :] < caption_len[:, None]) & (key_mask == 1)
    cap_mask = cap_valid[:, None, None, :]

    def split_heads(values):
        return values.reshape(values.shape[0], values.shape[1], heads_here, head_size)

    lat_float = latents.astype(jnp.float32)
    lat_norm = layer_norm(lat_float, gain_latent).astype(jnp.bfloat16)
    queries = jnp.einsum(
        "bld,de->ble", lat_norm, query_weight, preferred_element_type=jnp.float32
    ).astype(jnp.bfloat16)
    all_queries = from_blocks(
        lax.all_gather(queries[None], ("vid", "txt"), axis=0, tiled=True), vid_count, txt_count
    )
    lat_total = all_queries.shape[1]
    video_queries = take_rows(all_queries, video_start, items_here)
    cap_queries = take_rows(all_queries, cap_start, cap_items)
    video_float = video_tokens.astype(jnp.float32)
    cap_float = caption_tokens.astype(jnp.float32)
    video_normed = layer_norm(video_float, gain_tokens).astype(jnp.bfloat16)
    caption_normed = layer_norm(cap_float, gain_tokens).astype(jnp.bfloat16)
    video_keys = jnp.einsum(
        "flc,co->flo", video_normed, key_matrix, preferred_element_type=jnp.float32
    ).astype(jnp.bfloat16)
    video_values = jnp.einsum(
        "flc,co->flo", video_normed, value_matrix, preferred_element_type=jnp.float32
    ).astype(jnp.bfloat16)
    cap_keys = jnp.einsum(
        "flc,co->flo", caption_normed, key_matrix, preferred_element_type=jnp.float32
    ).astype(jnp.bfloat16)
    cap_values = jnp.einsum(
        "flc,co->flo", caption_normed, value_matrix, preferred_element_type=jnp.float32
    ).astype(jnp.bfloat16)
    video_scores = (
        jnp.einsum(
            "blhe,bkhe->bhlk",
            split_heads(video_queries),
            split_heads(video_keys),
            preferred_element_type=jnp.float32,
        )
        * scale
    )
    cap_scores = (
        jnp.einsum(
            "blhe,bkhe->bhlk",
            split_heads(cap_queries),
            split_heads(cap_keys),
            preferred_element_type=jnp.float32,
        )
        * scale
    )
    cap_scores = jnp.where(cap_mask, cap_scores, -1e30)
    video_peak = jnp.max(video_scores, axis=-1)
    video_total = jnp.sum(jnp.exp(video_scores - video_peak[..., None]), axis=-1)
    cap_peak = jnp.max(cap_scores, axis=-1)
    cap_total = jnp.sum(
        jnp.where(cap_mask, jnp.exp(cap_scores - cap_peak[..., None]), 0.0), axis=-1
    )
    peak_all = jnp.full((items_total, heads_here, lat_total), -1e30, jnp.float32)
    total_all = jnp.zeros((items_total, heads_here, lat_total), jnp.float32)
    peak_all, total_all = place_stats(peak_all, total_all, video_peak, video_total, video_start)
    peak_all, total_all = place_stats(peak_all, total_all, cap_peak, cap_total, cap_start)
    peak, total = combined_all((peak_all, total_all), ("vid", "txt"), combine_stats)
    video_probs = (
        jnp.exp(video_scores - take_rows(peak, video_start, items_here)[..., None])
        / take_rows(total, video_start, items_here)[..., None]
    )
    cap_probs = jnp.where(
        cap_mask,
        jnp.exp(cap_scores - take_rows(peak, cap_start, cap_items)[..., None])
        / take_rows(total, cap_start, cap_items)[..., None],
        0.0,
    )
    video_low = video_probs.astype(jnp.bfloat16)
    cap_low = cap_probs.astype(jnp.bfloat16)
    video_part = jnp.einsum(
        "bhlk,bkhe->blhe", video_low, split_heads(video_values), preferred_element_type=jnp.float32
    ).reshape(items_here, lat_total, head_width)
    cap_part = jnp.einsum(
        "bhlk,bkhe->blhe", cap_low, split_heads(cap_values), preferred_element_type=jnp.float32
    ).reshape(cap_items, lat_total, head_width)
    value_all = jnp.zeros((items_total, lat_total, head_width), jnp.float32)
    value_all = place_sum(place_sum(value_all, video_part, video_start), cap_part, cap_start)
    attended = lax.psum_scatter(
        to_blocks(value_all, vid_count, txt_count), ("vid", "txt"), scatter_dimension=0, tiled=True
    )[0]
    mixed_in = (attended * keep[:, None, None]).astype(jnp.bfloat16)
    branch = lax.psum(
        jnp.einsum("ble,ed->bld", mixed_in, out_weight, preferred_element_type=jnp.float32), "head"
    )
    after_attn = lat_float + branch
    mlp_norm = layer_norm(after_attn, gain_mlp).astype(jnp.bfloat16)
    pre_act = jnp.einsum("bld,df->blf", mlp_norm, up_weight, preferred_element_type=jnp.float32)
    activ = gelu_exact(pre_act).astype(jnp.bfloat16)
    growth = lax.psum(
        jnp.einsum("blf,fd->bld", activ, down_weight, preferred_element_type=jnp.float32).astype(
            jnp.bfloat16
        ),
        "head",
    ).astype(jnp.float32)
    latents_out = (after_attn + growth).astype(jnp.bfloat16)
    grad_down = jnp.einsum("blf,bld->fd", activ, cotangent, preferred_element_type=jnp.float32)
    d_activ = jnp.einsum("bld,fd->blf", cotangent, down_weight, preferred_element_type=jnp.float32)
    d_pre = jax.vjp(gelu_exact, pre_act)[1](d_activ)[0].astype(jnp.bfloat16)
    grad_up = jnp.einsum("bld,blf->df", mlp_norm, d_pre, preferred_element_type=jnp.float32)
    d_mlp_norm = lax.psum(
        jnp.einsum("blf,df->bld", d_pre, up_weight, preferred_element_type=jnp.float32), "head"
    )
    d_after_norm, grad_gain_mlp = norm_back(after_attn, gain_mlp, d_mlp_norm)
    d_after = cotangent.astype(jnp.float32) + d_after_norm
    d_branch = d_after.astype(jnp.bfloat16)
    grad_out = jnp.einsum("ble,bld->ed", mixed_in, d_branch, preferred_element_type=jnp.float32)
    d_att = (
        jnp.einsum("bld,ed->ble", d_branch, out_weight, preferred_element_type=jnp.float32)
        * keep[:, None, None]
    ).astype(jnp.bfloat16)
    all_d_att = from_blocks(
        lax.all_gather(d_att[None], ("vid", "txt"), axis=0, tiled=True), vid_count, txt_count
    )
    video_d_att = split_heads(take_rows(all_d_att, video_start, items_here))
    cap_d_att = split_heads(take_rows(all_d_att, cap_start, cap_items))
    video_dprobs = jnp.einsum(
        "blhe,bkhe->bhlk",
        video_d_att,
        split_heads(video_values),
        preferred_element_type=jnp.float32,
    )
    cap_dprobs = jnp.einsum(
        "blhe,bkhe->bhlk", cap_d_att, split_heads(cap_values), preferred_element_type=jnp.float32
    )
    delta_all = jnp.zeros((items_total, heads_here, lat_total), jnp.float32)
    delta_all = place_sum(delta_all, jnp.sum(video_probs * video_dprobs, axis=-1), video_start)
    delta_all = place_sum(delta_all, jnp.sum(cap_probs * cap_dprobs, axis=-1), cap_start)
    delta = lax.psum(delta_all, ("vid", "txt"))
    video_dscores = (
        video_probs * (video_dprobs - take_rows(delta, video_start, items_here)[..., None])
    ).astype(jnp.bfloat16)
    cap_dscores = (
        cap_probs * (cap_dprobs - take_rows(delta, cap_start, cap_items)[..., None])
    ).astype(jnp.bfloat16)
    video_dq = (
        jnp.einsum(
            "bhlk,bkhe->blhe",
            video_dscores,
            split_heads(video_keys),
            preferred_element_type=jnp.float32,
        )
        * scale
    ).reshape(items_here, lat_total, head_width)
    cap_dq = (
        jnp.einsum(
            "bhlk,bkhe->blhe",
            cap_dscores,
            split_heads(cap_keys),
            preferred_element_type=jnp.float32,
        )
        * scale
    ).reshape(cap_items, lat_total, head_width)
    query_all = jnp.zeros((items_total, lat_total, head_width), jnp.float32)
    query_all = place_sum(place_sum(query_all, video_dq, video_start), cap_dq, cap_start)
    d_queries = lax.psum_scatter(
        to_blocks(query_all, vid_count, txt_count), ("vid", "txt"), scatter_dimension=0, tiled=True
    )[0].astype(jnp.bfloat16)
    video_key_grad = (
        (
            jnp.einsum(
                "bhlk,blhe->bkhe",
                video_dscores,
                split_heads(video_queries),
                preferred_element_type=jnp.float32,
            )
            * scale
        )
        .reshape(items_here, video_here, head_width)
        .astype(jnp.bfloat16)
    )
    video_value_grad = (
        jnp.einsum("bhlk,blhe->bkhe", video_low, video_d_att, preferred_element_type=jnp.float32)
        .reshape(items_here, video_here, head_width)
        .astype(jnp.bfloat16)
    )
    caption_key_grad = (
        (
            jnp.einsum(
                "bhlk,blhe->bkhe",
                cap_dscores,
                split_heads(cap_queries),
                preferred_element_type=jnp.float32,
            )
            * scale
        )
        .reshape(cap_items, cap_here, head_width)
        .astype(jnp.bfloat16)
    )
    caption_value_grad = (
        jnp.einsum("bhlk,blhe->bkhe", cap_low, cap_d_att, preferred_element_type=jnp.float32)
        .reshape(cap_items, cap_here, head_width)
        .astype(jnp.bfloat16)
    )
    grad_query = jnp.einsum("bld,ble->de", lat_norm, d_queries, preferred_element_type=jnp.float32)
    d_lat_norm = lax.psum(
        jnp.einsum("ble,de->bld", d_queries, query_weight, preferred_element_type=jnp.float32),
        "head",
    )
    d_lat_back, grad_gain_latent = norm_back(lat_float, gain_latent, d_lat_norm)
    latent_grad = d_after + d_lat_back
    grad_key = jnp.einsum(
        "zsg,zsv->gv", video_normed, video_key_grad, preferred_element_type=jnp.float32
    ) + jnp.einsum(
        "zsg,zsv->gv", caption_normed, caption_key_grad, preferred_element_type=jnp.float32
    )
    grad_value = jnp.einsum(
        "zsg,zsv->gv", video_normed, video_value_grad, preferred_element_type=jnp.float32
    ) + jnp.einsum(
        "zsg,zsv->gv", caption_normed, caption_value_grad, preferred_element_type=jnp.float32
    )
    video_term = jnp.einsum(
        "ayt,ot->ayo", video_key_grad, key_matrix, preferred_element_type=jnp.float32
    ) + jnp.einsum(
        "ayt,ot->ayo", video_value_grad, value_matrix, preferred_element_type=jnp.float32
    )
    cap_term = jnp.einsum(
        "ayt,ot->ayo", caption_key_grad, key_matrix, preferred_element_type=jnp.float32
    ) + jnp.einsum(
        "ayt,ot->ayo", caption_value_grad, value_matrix, preferred_element_type=jnp.float32
    )
    d_video_norm, d_cap_norm = lax.psum((video_term, cap_term), "head")
    video_grad, video_gain_part = norm_back(video_float, gain_tokens, d_video_norm)
    caption_grad, cap_gain_part = norm_back(cap_float, gain_tokens, d_cap_norm)
    grad_gain_tokens = video_gain_part + cap_gain_part
    kept_here = jnp.sum(keep)
    (
        grad_query,
        grad_key,
        grad_value,
        grad_out,
        grad_up,
        grad_down,
        grad_gain_latent,
        grad_gain_tokens,
        grad_gain_mlp,
        kept_total,
    ) = lax.psum(
        (
            grad_query,
            grad_key,
            grad_value,
            grad_out,
            grad_up,
            grad_down,
            grad_gain_latent,
            grad_gain_tokens,
            grad_gain_mlp,
            kept_here,
        ),
        ("vid", "txt"),
    )
    kept_count = (kept_total / vid_count).astype(jnp.int32)
    return (
        latents_out,
        latent_grad,
        video_grad,
        caption_grad,
        grad_query,
        grad_key,
        grad_value,
        grad_out,
        grad_up,
        grad_down,
        grad_gain_latent,
        grad_gain_tokens,
        grad_gain_mlp,
        kept_count,
    )


def swap_cores(values):
    return lax.ppermute(values, "vid", [(0, 1), (1, 0)])


def head_shift(values, shift, count):
    return lax.ppermute(values, "head", [(i, (i - shift) % count) for i in range(count)])


def take_block(values, index, size, axis=0):
    return lax.dynamic_slice_in_dim(values, index * size, size, axis)


def head_chunks(part, place, count):
    low = part.astype(BF16)
    others = [
        lax.dynamic_index_in_dim(low, (place - shift) % count, 0, False)
        for shift in range(1, count)
    ]
    return [lax.dynamic_index_in_dim(part, place, 0, False)] + others


def reduce_over_head(chunks, count):
    total = chunks[0]
    for shift in range(1, count):
        total = total + head_shift(chunks[shift], shift, count).astype(F32)
    return total.astype(BF16)


def gather_head(total, place, count):
    result = jnp.zeros((count,) + total.shape, BF16)
    result = lax.dynamic_update_index_in_dim(result, total, place, 0)
    for shift in range(1, count):
        result = lax.dynamic_update_index_in_dim(
            result, head_shift(total, shift, count), (place + shift) % count, 0
        )
    return result


def group_steps(count):
    return [(step, [(i, (i - step) % count) for i in range(count)]) for step in range(1, count)]


def reduce_over_cores(rows, core):
    half = rows.shape[0] // 2
    other = swap_cores(take_block(rows, 1 - core, half))
    return take_block(rows, core, half).astype(F32) + other.astype(F32), other


def reduce_over_group(half, place, count):
    part = half.shape[0] // count
    low = half.astype(BF16)
    total = take_block(half, place, part)
    for step, perm in group_steps(count):
        chunk = take_block(low, (place - step) % count, part)
        total = total + lax.ppermute(chunk, "txt", perm).astype(F32)
    return total.astype(BF16)


def gather_places(total, place, count):
    part = total.shape[0]
    mine = jnp.zeros((part * count, total.shape[1]), BF16)
    mine = lax.dynamic_update_slice_in_dim(mine, total, place * part, 0)
    for step, perm in group_steps(count):
        mine = lax.dynamic_update_slice_in_dim(
            mine, lax.ppermute(total, "txt", perm), (place + step) % count * part, 0
        )
    return mine


def gather_cores(mine, core):
    half = mine.shape[0]
    whole = jnp.zeros((2 * half, mine.shape[1]), BF16)
    whole = lax.dynamic_update_slice_in_dim(whole, mine, core * half, 0)
    return lax.dynamic_update_slice_in_dim(whole, swap_cores(mine), (1 - core) * half, 0)


def caption_perm(step, vid_count, txt_count, cores):
    pairs = []
    for v in range(vid_count):
        for t in range(txt_count):
            block = (t + step) % txt_count
            dest_txt = v * (txt_count // vid_count) + block // cores
            dest_vid = block % cores
            pairs.append((v * txt_count + t, dest_vid * txt_count + dest_txt))
    return pairs


PAIR = 128
BACK_COST = 3
F32 = jnp.float32
BF16 = jnp.bfloat16


def dot_nt(a, b):
    return lax.dot_general(a, b, (((1,), (1,)), ((), ())), preferred_element_type=F32)


def dot_nn(a, b):
    return lax.dot_general(a, b, (((1,), (0,)), ((), ())), preferred_element_type=F32)


def dot_tn(a, b):
    return lax.dot_general(a, b, (((0,), (0,)), ((), ())), preferred_element_type=F32)


def square(ref):
    return ref[...].reshape(D, D)


def two_heads(values):
    low = lax.broadcasted_iota(jnp.int32, values.shape, 1) < PAIR // 2
    zero = jnp.zeros_like(values)
    return jnp.concatenate([jnp.where(low, values, zero), jnp.where(low, zero, values)], axis=0)


def from_two_heads(both):
    n = both.shape[1] // 2
    first = lax.broadcasted_iota(jnp.int32, (PAIR, n), 0) < PAIR // 2
    return jnp.where(first, both[:, :n], both[:, n:]).T


def chunk_list(video, cap, size):
    return [(start, size) for start in range(0, video, size)] + [(video, cap)]


def norm_kernel(s_ref, own_ref, other_ref, gain_ref, out_ref):
    gain = gain_ref[...]
    start = 0
    for ref in (own_ref, other_ref):
        def chunk(c, carry, ref=ref, start=start):
            for part in range(2):
                at = pl.multiple_of(c * 128, 128) + 64 * part
                out_ref[pl.ds(start + at, 64), :] = layer_norm(
                    ref[pl.ds(at, 64), :].astype(F32), gain
                ).astype(BF16)
            return carry

        lax.fori_loop(0, ref.shape[0] // 128, chunk, 0)
        start += ref.shape[0]


def cap_mask(cap_ref):
    mask = cap_ref[:, pl.ds(D, PAIR)]
    return jnp.concatenate([mask, mask], axis=1).astype(F32) > 0.5


def forward_kernel(s_ref, tok_ref, cap_ref, gain_ref, lat_ref, gain_lat_ref, wq_ref, wkv_ref, *refs):
    q_ref, k_ref, v_ref, lse_ref, o_ref, s_scr, e_scr, wkv_scr = refs[-8:]
    keys, width = k_ref.shape
    cap = cap_ref.shape[0]
    step = (keys - cap) // 4
    latn = layer_norm(lat_ref[...].astype(F32), gain_lat_ref[...]).astype(BF16)
    queries = dot_nt(latn, wq_ref[...].reshape(width, D)).astype(BF16).astype(F32)
    q_ref[...] = (queries * 0.125).astype(BF16)

    @pl.when(pl.program_id(0) == 0)
    def _():
        wkv_scr[...] = wkv_ref[...].reshape(2 * width, D).T

    def project(rows, tokens):
        both = dot_nn(tokens, wkv_scr[...]).astype(BF16)
        k_ref[rows, :] = both[:, :width]
        v_ref[rows, :] = both[:, width:]

    def project_video(c, carry):
        rows = pl.ds(pl.multiple_of(c * step, 16), step)
        project(rows, tok_ref[rows, :])
        return carry

    lax.fori_loop(0, 4, project_video, 0)
    cap_rows = pl.ds(keys - cap, cap)
    project(cap_rows, layer_norm(cap_ref[:, pl.ds(0, D)].astype(F32), gain_ref[...]).astype(BF16))
    pieces = [pl.ds(start, 64) for start in range(0, keys, 64)]

    def pair(p, carry):
        cols = pl.ds(pl.multiple_of(p * PAIR, PAIR), PAIR)
        q2 = two_heads(q_ref[:, cols])
        s_scr[...] = dot_nt(k_ref[:, cols], q2)
        s_scr[cap_rows, :] = jnp.where(cap_mask(cap_ref), s_scr[cap_rows, :], -1e30)
        peak = s_scr[pieces[0], :]
        for rows in pieces[1:]:
            peak = jnp.maximum(peak, s_scr[rows, :])
        peak = jnp.max(peak, axis=0, keepdims=True)
        total = jnp.zeros((8, q2.shape[0]), F32)
        for rows in pieces:
            e = jnp.exp(s_scr[rows, :] - peak)
            e_scr[rows, :] = e.astype(BF16)
            total = total + jnp.sum(e.reshape(-1, 8, q2.shape[0]), axis=0)
        total = jnp.sum(total, axis=0, keepdims=True)
        out = dot_tn(v_ref[:, cols], e_scr[...])
        o_ref[:, cols] = from_two_heads(out / total)
        lse_ref[pl.ds(p, 1), :] = peak + jnp.log(total)
        return carry

    lax.fori_loop(0, width // PAIR, pair, 0)


def backward_kernel(
    s_ref, q_ref, k_ref, v_ref, lse_ref, o_ref, datt_ref, own_ref, other_ref, cap_ref,
    wk_ref, wv_ref, gain_ref, tok_ref, wq_ref, lat_ref, after_ref, gain_lat_ref, ready_ref,
    own_out, other_out, cap_out, lat_out, late_ref,
    dq_ref, dk_ref, dv_ref, s_scr, dp_scr, p_scr, ds_scr, up_scr, sums_ref, gain_out,
):
    item = pl.program_id(0)
    keys = k_ref.shape[0]
    cap = cap_ref.shape[0]
    cap_rows = pl.ds(keys - cap, cap)
    pieces = [pl.ds(start, 64) for start in range(0, keys, 64)]

    def pair(p, carry):
        cols = pl.ds(pl.multiple_of(p * PAIR, PAIR), PAIR)
        q2 = two_heads(q_ref[:, cols])
        d_att = datt_ref[:, cols]
        d2 = two_heads(d_att)
        prod = (d_att.astype(F32) * o_ref[:, cols]).T
        delta = jnp.concatenate(
            [
                jnp.sum(prod[: PAIR // 2], axis=0, keepdims=True),
                jnp.sum(prod[PAIR // 2 :], axis=0, keepdims=True),
            ],
            axis=1,
        )
        pairs_here = D // PAIR // lse_ref.shape[0]
        lse = lse_ref[p // pairs_here, pl.ds(p % pairs_here, 1), :]
        s_scr[...] = dot_nt(k_ref[:, cols], q2)
        dp_scr[...] = dot_nt(v_ref[:, cols], d2)
        s_scr[cap_rows, :] = jnp.where(cap_mask(cap_ref), s_scr[cap_rows, :], -1e30)
        for rows in pieces:
            probs = jnp.exp(s_scr[rows, :] - lse)
            p_scr[rows, :] = probs.astype(BF16)
            ds_scr[rows, :] = (probs * (dp_scr[rows, :] - delta)).astype(BF16)
        dv_ref[:, cols] = dot_nn(p_scr[...], d2).astype(BF16)
        dk_ref[:, cols] = dot_nn(ds_scr[...], q2).astype(BF16)
        dq = dot_tn(k_ref[:, cols], ds_scr[...])
        dq_ref[:, cols] = (from_two_heads(dq) * 0.125).astype(BF16)
        return carry

    lax.fori_loop(0, D // PAIR, pair, 0)
    gain = gain_ref[...]

    @pl.when(item == 0)
    def _():
        gain_out[...] = jnp.zeros_like(gain_out)
        sums_ref[...] = jnp.zeros_like(sums_ref)

    wide = sums_ref.shape[0] // 4
    window = pl.ds(pl.multiple_of(s_ref[2], PAIR), wide)
    video_rows = pl.ds(0, keys - cap)
    cap_norm = layer_norm(cap_ref[:, pl.ds(0, D)].astype(F32), gain).astype(BF16)
    latn = layer_norm(lat_ref[...].astype(F32), gain_lat_ref[...]).astype(BF16)
    sums_ref[pl.ds(0, wide), :] += dot_tn(dq_ref[:, window], latn)
    keep = (1 - s_ref[4 + item]).astype(F32)
    mixed = (o_ref[:, window] * keep).astype(BF16)
    sums_ref[pl.ds(3 * wide, wide), :] += dot_tn(mixed, after_ref[...].astype(BF16))

    def both(rows):
        return jnp.concatenate([dk_ref[rows, window], dv_ref[rows, window]], axis=1)

    sums_ref[pl.ds(wide, 2 * wide), :] += dot_tn(both(video_rows), tok_ref[...]) + dot_tn(
        both(cap_rows), cap_norm
    )

    def norm_back(x, up, gain, row):
        center = x - jnp.mean(x, axis=-1, keepdims=True)
        rate = lax.rsqrt(jnp.mean(center * center, axis=-1, keepdims=True) + 1e-05)
        hat = center * rate
        gain_out[pl.ds(8 * row, 8), :] += jnp.sum((up * hat).reshape(-1, 8, D), axis=0)
        scaled = up * gain
        first = jnp.mean(scaled, axis=-1, keepdims=True)
        second = jnp.mean(scaled * hat, axis=-1, keepdims=True)
        return rate * (scaled - first - hat * second)

    half = lat_out.shape[0]
    lat_grad = after_ref[...] + norm_back(
        lat_ref[...].astype(F32), dot_nn(dq_ref[...], square(wq_ref)), gain_lat_ref[...], 1
    )
    lat_out[...] = lat_grad[:half]
    other_out[pl.ds(other_ref.shape[0], half), :] = lat_grad[half:].astype(BF16)

    start = 0
    for ref, out, size in ((own_ref, own_out, 256), (other_ref, other_out, 256), (cap_ref, cap_out, cap)):
        def chunk(c, carry, ref=ref, out=out, size=size, start=start):
            rows = pl.ds(pl.multiple_of(c * size, 16), size)
            key_rows = pl.ds(pl.multiple_of(start + c * size, 16), size)
            up_scr[pl.ds(0, size), :] = dot_nn(dk_ref[key_rows, :], square(wk_ref)) + dot_nn(
                dv_ref[key_rows, :], square(wv_ref)
            )
            for at in range(0, size, 32):
                piece = pl.ds(pl.multiple_of(c * size, 16) + at, 32)
                back = norm_back(
                    ref[piece, pl.ds(0, D)].astype(F32), up_scr[pl.ds(at, 32), :], gain, 0
                )
                out[piece, :] = back.astype(out.dtype)
            return carry

        lax.fori_loop(0, ref.shape[0] // size, chunk, 0)
        start += ref.shape[0]

    @pl.when(item == pl.num_programs(0) - 1)
    def _():
        width = D // 4
        for n in range(4):
            mine = pl.ds(pl.multiple_of(s_ref[3] + n * wide, PAIR // 2), width)
            late_ref[pl.ds(n * width, width), :] = sums_ref[mine, :].astype(BF16)
        ready = ready_ref.shape[0]
        late_ref[pl.ds(4 * width, ready), :] = ready_ref[...]
        gains = [jnp.sum(gain_out[pl.ds(8 * row, 8), :], axis=0, keepdims=True) for row in (0, 1)]
        gains = jnp.concatenate(gains + [jnp.zeros((14, D), F32)], axis=0)
        late_ref[pl.ds(4 * width + ready, 16), :] = gains.astype(BF16)
        spare = late_ref.shape[0] - 4 * width - ready - 16
        late_ref[pl.ds(4 * width + ready + 16, spare), :] = jnp.zeros((spare, D), BF16)


def place_kernel(s_ref, video_in, lat_in, video_part, lat_part, video_ref, lat_ref):
    video_ref[...] = video_part[...].astype(F32)

    @pl.when(pl.program_id(1) == 0)
    def _():
        lat_ref[...] = lat_part[...].astype(F32)


def local(
    latents,
    video_tokens,
    caption_tokens,
    caption_len,
    key_mask,
    drop_flags,
    gain_latent,
    gain_tokens,
    gain_mlp,
    query_weight,
    key_matrix,
    value_matrix,
    out_weight,
    up_weight,
    down_weight,
    cotangent,
):
    txt_count = lax.axis_size("txt")
    head_count = lax.axis_size("head")
    core = lax.axis_index("vid")
    place_index = lax.axis_index("txt")
    z = lax.axis_index("head")
    items_here = latents.shape[0]
    own = items_here // 2
    lat_half = latents.shape[1]
    lat_rows = 2 * lat_half
    video_here = video_tokens.shape[1]
    cap_here = caption_tokens.shape[1]
    cap_rows = cap_here * txt_count
    keys_here = 2 * video_here + cap_rows
    head_width = query_weight.shape[1]

    def dot(spec, a, b):
        return jnp.einsum(spec, a, b, preferred_element_type=F32)

    packed = jnp.stack([key_matrix.T, value_matrix.T, query_weight.T, out_weight])
    half = take_block(packed, core, 2)
    up1 = lax.ppermute(half, "head", [(0, 1), (1, 2), (2, 3)])
    down1 = lax.ppermute(half, "head", [(1, 0), (2, 1), (3, 2)])
    near_at = z // 2
    zero = jnp.int32(0)
    own_at = z % 2
    part_shape = (2, 2, 2, head_width, D)

    def place_chunk(whole, chunk, at_core, at_chunk):
        chunk = chunk.reshape((-1, 2, 1) + chunk.shape[-2:])
        return lax.dynamic_update_slice(whole, chunk, (at_core, zero, at_chunk, zero, zero))

    both_own = take_block(jnp.concatenate([latents, cotangent], axis=1), core, own)
    video_other = swap_cores(
        jnp.concatenate(
            [take_block(a, 1 - core, own) for a in (video_tokens, latents, cotangent)], axis=1
        )
    )
    both_other = video_other[:, video_here:]
    lat = jnp.concatenate([both_own[:, :lat_half], both_other[:, :lat_half]], axis=1)
    cot = jnp.concatenate([both_own[:, lat_half:], both_other[:, lat_half:]], axis=1)
    drop_own = take_block(drop_flags, core, own)
    keep = (1 - drop_own).astype(F32)
    window = z * head_width // PAIR * PAIR
    inside = z * head_width - window
    scalars = jnp.concatenate([jnp.stack([core, near_at, window, inside]), drop_own])
    scalars_far = jnp.concatenate([jnp.stack([core, 1 - near_at, window, inside]), drop_own])

    place_slots = place_index * cap_here + jnp.arange(cap_here, dtype=jnp.int32)
    cap_valid = (place_slots[None, :] < caption_len[:, None]) & (key_mask == 1)
    flags = jnp.broadcast_to(cap_valid.astype(BF16)[:, :, None], cap_valid.shape + (PAIR,))
    cap_message = jnp.concatenate([caption_tokens, flags], axis=2)
    cap_parts = []
    for step in range(txt_count):
        block = take_block(cap_message, (place_index + step) % txt_count, own)
        cap_parts.append(
            lax.ppermute(block, ("vid", "txt"), caption_perm(step, 2, txt_count, 2))
        )
    def item_spec(rows, width=D, first=0):
        return pl.BlockSpec((None, rows, width), lambda i, s: (first + i, 0, 0))

    def own_spec(rows, first=0):
        return pl.BlockSpec((None, rows, D), lambda i, s: (s[0] * own + first + i, 0, 0))

    def whole_spec(*shape):
        return pl.BlockSpec(shape, lambda i, s: (0,) * len(shape))

    def weight_spec(m):
        return pl.BlockSpec(
            (2, None, None, 2, head_width, D),
            lambda i, s: (0, m // 2, m % 2, 0, 0, 0),
            pipeline_mode=pl.Buffered(1),
        )

    def part_spec(at_core, first, count):
        return pl.BlockSpec(
            (None, count, 2, head_width, D),
            lambda i, s: (at_core, first, 0, 0, 0),
            pipeline_mode=pl.Buffered(1),
        )

    def half_spec(rows):
        return pl.BlockSpec((None, rows, 2 * head_width), lambda i, s: (i, 0, s[1]))

    row_spec = pl.BlockSpec((1, D), lambda i, s: (0, 0))

    def call(kernel, name, ins, outs, operands, micros, scratch=(), aliases={}, scalars=scalars, grid=own):
        return pl.pallas_call(
            kernel,
            name=name,
            grid_spec=pltpu.PrefetchScalarGridSpec(
                num_scalar_prefetch=1,
                grid=(grid,),
                in_specs=ins,
                out_specs=[spec for spec, _, _ in outs],
                scratch_shapes=list(scratch),
            ),
            out_shape=[jax.ShapeDtypeStruct(shape, dtype) for _, shape, dtype in outs],
            input_output_aliases=aliases,
            cost_estimate=pl.CostEstimate(
                flops=micros * 1100 * 10**6, transcendentals=0, bytes_accessed=micros * 10**6
            ),
            compiler_params=pltpu.CompilerParams(vmem_limit_bytes=56 << 20),
        )(scalars, *operands)

    def item_out(rows, dtype, width=D):
        return (item_spec(rows, width), (own, rows, width), dtype)

    gain_lat_row = gain_latent[None]
    gain_tok_row = gain_tokens[None]
    gain_mlp_row = gain_mlp[None]
    (tok_norm,) = call(
        norm_kernel,
        "token_norm",
        [own_spec(video_here), item_spec(video_here), row_spec],
        [item_out(2 * video_here, BF16)],
        (video_tokens, video_other, gain_tok_row),
        9,
    )
    tok_norm, up1, down1, cap_parts = lax.optimization_barrier((tok_norm, up1, down1, cap_parts))
    cap = jnp.concatenate(cap_parts, axis=1)
    partner = jnp.where(z % 2 == 1, up1, down1)
    near = jnp.zeros(part_shape, BF16)
    near = place_chunk(near, packed.reshape((2, 2) + packed.shape[1:]), zero, own_at)
    near = place_chunk(near, partner, core, 1 - own_at)
    partner_other = swap_cores(partner)
    near = place_chunk(near, partner_other, 1 - core, 1 - own_at)
    up1, down1, half_then, _ = lax.optimization_barrier((up1, down1, half, partner_other))
    ring_up = lax.ppermute(jnp.where(z == 3, half_then, up1), "head", [(1, 2), (2, 3), (3, 0)])
    ring_down = lax.ppermute(jnp.where(z == 0, half_then, down1), "head", [(1, 0), (2, 1), (0, 3)])

    def forward(part, scalars, before=()):
        return call(
            forward_kernel,
            "attention_forward",
            [item_spec(2 * video_here), item_spec(cap_rows, D + PAIR), row_spec]
            + [item_spec(lat_rows), row_spec]
            + [part_spec(1, 0, 1), part_spec(0, 0, 2)]
            + [pl.BlockSpec(memory_space=pl.ANY)] * len(before),
            [
                (half_spec(lat_rows), (own, lat_rows, D), BF16),
                (half_spec(keys_here), (own, keys_here, D), BF16),
                (half_spec(keys_here), (own, keys_here, D), BF16),
                (
                    pl.BlockSpec((None, None, 8, 2 * lat_rows), lambda i, s: (i, s[1], 0, 0)),
                    (own, 2, 8, 2 * lat_rows),
                    F32,
                ),
                (half_spec(lat_rows), (own, lat_rows, D), F32),
            ],
            (tok_norm, cap, gain_tok_row, lat, gain_lat_row, part, part) + tuple(before),
            23,
            [
                pltpu.VMEM((keys_here, 2 * lat_rows), F32),
                pltpu.VMEM((keys_here, 2 * lat_rows), BF16),
                pltpu.VMEM((D, 4 * head_width), BF16),
            ],
            {8 + n: n for n in range(len(before))},
            scalars,
        )

    before = forward(near, scalars)
    before, up1, down1, ring_up, ring_down = lax.optimization_barrier(
        (before, up1, down1, ring_up, ring_down)
    )
    far_low = jnp.where(z == 1, down1, jnp.where(z == 2, ring_up, ring_down))
    far_high = jnp.where(z == 1, ring_down, jnp.where(z == 2, up1, ring_up))
    far_mine = jnp.stack([far_low, far_high], axis=1)
    far = jnp.zeros(part_shape, BF16)
    far = lax.dynamic_update_index_in_dim(far, far_mine, core, 0)
    far = lax.dynamic_update_index_in_dim(far, swap_cores(far_mine), 1 - core, 0)
    def both_halves(near, far):
        whole = jnp.zeros((2,) + near.shape, BF16)
        whole = lax.dynamic_update_index_in_dim(whole, near, near_at, 0)
        return lax.dynamic_update_index_in_dim(whole, far, 1 - near_at, 0)

    queries, keys, values, lse, attended = forward(far, scalars_far, before)
    w_out = both_halves(near[1, 1], far[1, 1]).reshape(D, D)
    lat_float = lat.astype(F32)
    mixed_in = (attended * keep[:, None, None]).astype(BF16)
    after_attn = lat_float + dot("ble,ed->bld", mixed_in, w_out)
    mlp_norm = layer_norm(after_attn, gain_mlp).astype(BF16)

    pre_act = dot("bld,df->blf", mlp_norm, up_weight)
    activ, gelu_pull = jax.vjp(gelu_exact, pre_act)
    activ = activ.astype(BF16)
    d_pre = gelu_pull(dot("bld,fd->blf", cot, down_weight))[0].astype(BF16)
    d_mlp_part = dot("blf,df->bld", d_pre, up_weight)
    d_mlp_part, activ, d_pre = lax.optimization_barrier((d_mlp_part, activ, d_pre))
    d_mlp_total = reduce_over_head(head_chunks(d_mlp_part, z, head_count), head_count)
    grad_down = dot("blf,bld->fd", activ, cot).astype(BF16)
    grad_up = dot("bld,blf->df", mlp_norm, d_pre).astype(BF16)
    near, far, _ = lax.optimization_barrier((near, far, d_mlp_part))
    weights = both_halves(near, far)
    early = jnp.where(core == 0, grad_up, grad_down).astype(F32)
    early = early + swap_cores(jnp.where(core == 0, grad_down, grad_up)).astype(F32)
    d_mlp_total, early = lax.optimization_barrier((d_mlp_total, early))
    early = reduce_over_group(early, place_index, txt_count)
    d_mlp_norm = gather_head(d_mlp_total, z, head_count)
    growth = dot("blf,fd->bld", activ, down_weight).astype(BF16)
    growth, d_mlp_norm, weights, early = lax.optimization_barrier(
        (growth, d_mlp_norm, weights, early)
    )
    early = gather_places(early, place_index, txt_count)
    growth = lax.psum(growth, "head")

    d_after_norm, gain_mlp_part = norm_back_rows(after_attn, gain_mlp, d_mlp_norm.astype(F32))
    d_after = cot.astype(F32) + d_after_norm
    d_branch = d_after.astype(BF16)
    d_att = (dot("bld,ed->ble", d_branch, w_out) * keep[:, None, None]).astype(BF16)
    ready = jnp.concatenate(
        [
            jnp.sum(gain_mlp_part, axis=0)[None],
            jnp.full((1, D), jnp.sum(keep)),
            jnp.zeros((14, D), F32),
        ]
    ).astype(BF16)
    late_size = 4 * head_width + 32
    late_size = late_size + -late_size % (32 * txt_count)
    pair_shape = (keys_here, 2 * lat_rows)
    d_att, ready = lax.optimization_barrier((d_att, ready))
    video_grad, other_back, cap_back, latent_grad, late = call(
        backward_kernel,
        "attention_backward",
        [
            item_spec(lat_rows),
            item_spec(keys_here),
            item_spec(keys_here),
            pl.BlockSpec((None, 2, 8, 2 * lat_rows), lambda i, s: (i, 0, 0, 0)),
            item_spec(lat_rows),
            item_spec(lat_rows),
            own_spec(video_here),
            item_spec(video_here),
            item_spec(cap_rows, D + PAIR),
            weight_spec(0),
            weight_spec(1),
            row_spec,
            item_spec(2 * video_here),
            weight_spec(2),
            item_spec(lat_rows),
            item_spec(lat_rows),
            row_spec,
            whole_spec(*ready.shape),
        ],
        [
            (own_spec(video_here), video_tokens.shape, F32),
            item_out(video_here + lat_half, BF16),
            item_out(cap_rows, BF16),
            (own_spec(lat_half), latents.shape, F32),
            (whole_spec(late_size, D), (late_size, D), BF16),
        ],
        (
            queries, keys, values, lse, attended, d_att, video_tokens, video_other, cap,
            weights, weights, gain_tok_row, tok_norm, weights, lat, d_after, gain_lat_row, ready,
        ),
        BACK_COST,
        [
            pltpu.VMEM((lat_rows, D), BF16),
            pltpu.VMEM((keys_here, D), BF16),
            pltpu.VMEM((keys_here, D), BF16),
            pltpu.VMEM(pair_shape, F32),
            pltpu.VMEM(pair_shape, F32),
            pltpu.VMEM(pair_shape, BF16),
            pltpu.VMEM(pair_shape, BF16),
            pltpu.VMEM((256, D), F32),
            pltpu.VMEM((8 * PAIR, D), F32),
            pltpu.VMEM((16, D), F32),
        ],
    )
    def place(video_grad, latent_grad, part):
        piece = video_here
        return pl.pallas_call(
            place_kernel,
            name="place_rows",
            grid_spec=pltpu.PrefetchScalarGridSpec(
                num_scalar_prefetch=1,
                grid=(own, 1),
                in_specs=[
                    pl.BlockSpec(memory_space=pl.ANY),
                    pl.BlockSpec(memory_space=pl.ANY),
                    pl.BlockSpec((None, piece, D), lambda i, r, s: (i, r, 0)),
                    pl.BlockSpec((None, lat_half, D), lambda i, r, s: (i, video_here // lat_half, 0)),
                ],
                out_specs=[
                    pl.BlockSpec((None, piece, D), lambda i, r, s: ((1 - s[0]) * own + i, r, 0)),
                    pl.BlockSpec((None, lat_half, D), lambda i, r, s: ((1 - s[0]) * own + i, 0, 0)),
                ],
            ),
            out_shape=[
                jax.ShapeDtypeStruct(video_tokens.shape, F32),
                jax.ShapeDtypeStruct(latents.shape, F32),
            ],
            input_output_aliases={1: 0, 2: 1},
            cost_estimate=pl.CostEstimate(
                flops=6 * 10**9, transcendentals=0, bytes_accessed=10**7
            ),
        )(scalars, video_grad, latent_grad, part, part)

    early, growth, late = lax.optimization_barrier((early, growth, late))
    late_half, late_swapped = reduce_over_cores(late, core)
    other_back, early, _ = lax.optimization_barrier((other_back, early, late_swapped))
    other_here = swap_cores(other_back)
    early_other = swap_cores(early)
    late_total = reduce_over_group(late_half, place_index, txt_count)
    late_total, early_other, other_here, cap_back = lax.optimization_barrier(
        (late_total, early_other, other_here, cap_back)
    )
    cap_parts = []
    for step in range(txt_count):
        perm = [(b, a) for a, b in caption_perm(step, 2, txt_count, 2)]
        cap_parts.append(
            lax.ppermute(cap_back[:, step * cap_here : (step + 1) * cap_here], ("vid", "txt"), perm)
        )
    late = gather_places(late_total, place_index, txt_count)
    video_grad, latent_grad = place(video_grad, latent_grad, other_here)
    late, video_grad, latent_grad, cap_parts = lax.optimization_barrier(
        (late, video_grad, latent_grad, cap_parts)
    )
    late = gather_cores(late, core).astype(F32)
    caption_grad = jnp.zeros((txt_count, own, cap_here, D), F32)
    for step, part in enumerate(cap_parts):
        caption_grad = lax.dynamic_update_index_in_dim(
            caption_grad, part.astype(F32), (place_index + step) % txt_count, 0
        )
    caption_grad = caption_grad.reshape(caption_tokens.shape)
    out_mine = (after_attn + growth.reshape(after_attn.shape).astype(F32)).astype(BF16)
    gains = late[4 * head_width :]

    def give_back(values):
        other = swap_cores(values[:, lat_half:].astype(BF16)).astype(values.dtype)
        whole = jnp.zeros((items_here, lat_half, D), values.dtype)
        whole = lax.dynamic_update_slice_in_dim(whole, values[:, :lat_half], core * own, 0)
        return lax.dynamic_update_slice_in_dim(whole, other, (1 - core) * own, 0)

    latents_out = give_back(out_mine)
    kept_count = gains[1, 0].astype(jnp.int32)
    return (
        latents_out,
        latent_grad,
        video_grad,
        caption_grad,
        late[:head_width].T,
        late[head_width : 2 * head_width].T,
        late[2 * head_width : 3 * head_width].T,
        late[3 * head_width : 4 * head_width],
        jnp.where(core == 0, early, early_other).astype(F32),
        jnp.where(core == 0, early_other, early).astype(F32),
        gains[17],
        gains[16],
        gains[0],
        kept_count,
    )


def norm_back_rows(values, gain, upstream):
    mean = jnp.mean(values, axis=-1, keepdims=True)
    center = values - mean
    rate = lax.rsqrt(jnp.mean(center * center, axis=-1, keepdims=True) + 1e-05)
    hat = center * rate
    scaled = upstream * gain
    first = jnp.mean(scaled, axis=-1, keepdims=True)
    second = jnp.mean(scaled * hat, axis=-1, keepdims=True)
    return rate * (scaled - first - hat * second), jnp.sum(upstream * hat, axis=-2)


def fits(mesh):
    shape = mesh.shape
    return shape["vid"] == 2 and shape["txt"] == 4 and shape["head"] == 4


def solution(mesh):
    in_specs = (
        P("txt", "vid", None),
        P("txt", "vid", None),
        P("vid", "txt", None),
        P("vid"),
        P("vid", "txt"),
        P("txt"),
        P(),
        P(),
        P(),
        P(None, "head"),
        P(None, "head"),
        P(None, "head"),
        P("head", None),
        P(None, "head"),
        P("head", None),
        P("txt", "vid", None),
    )
    out_specs = (
        P("txt", "vid", None),
        P("txt", "vid", None),
        P("txt", "vid", None),
        P("vid", "txt", None),
        P(None, "head"),
        P(None, "head"),
        P(None, "head"),
        P("head", None),
        P(None, "head"),
        P("head", None),
        P(),
        P(),
        P(),
        P(),
    )
    return jax.shard_map(local if fits(mesh) else local_general, mesh=mesh, in_specs=in_specs, out_specs=out_specs, check_vma=False)
```

```python
import functools
import math

import jax
import jax.numpy as jnp
from jax import lax
from jax.experimental import pallas as pl
from jax.experimental.pallas import tpu as pltpu
from jax.sharding import PartitionSpec as P

D = 768
HEADS = 12


def combined_all(part, axis, combine):
    gathered = jax.tree.map(lambda a: lax.all_gather(a, axis), part)

    def take(source):
        return jax.tree.map(lambda a: lax.dynamic_index_in_dim(a, source, 0, False), gathered)

    return lax.fori_loop(
        1, lax.axis_size(axis), lambda source, state: combine(state, take(source)), take(0)
    )


def layer_norm(values, gain):
    center = values - jnp.mean(values, axis=-1, keepdims=True)
    spread = jnp.mean(center * center, axis=-1, keepdims=True)
    return center * lax.rsqrt(spread + 1e-05) * gain


def norm_back(values, gain, upstream):
    result, pullback = jax.vjp(layer_norm, values, gain)
    return pullback(upstream)


def gelu_exact(values):
    return jax.nn.gelu(values, approximate=False)


def combine_stats(first, second):
    peak = jnp.maximum(first[0], second[0])
    total = first[1] * jnp.exp(first[0] - peak) + second[1] * jnp.exp(second[0] - peak)
    return (peak, total)


def to_blocks(whole, vid_count, txt_count):
    items, rows, width = whole.shape
    split = whole.reshape(txt_count, items // txt_count, vid_count, rows // vid_count, width)
    return split.transpose(2, 0, 1, 3, 4).reshape(
        vid_count * txt_count, items // txt_count, rows // vid_count, width
    )


def from_blocks(blocked, vid_count, txt_count):
    count, items_here, rows_here, width = blocked.shape
    split = blocked.reshape(vid_count, txt_count, items_here, rows_here, width)
    return split.transpose(1, 2, 0, 3, 4).reshape(
        txt_count * items_here, vid_count * rows_here, width
    )


def place_sum(whole, part, start):
    current = lax.dynamic_slice_in_dim(whole, start, part.shape[0], 0)
    return lax.dynamic_update_slice_in_dim(whole, current + part, start, 0)


def place_stats(peak_all, total_all, peak, total, start):
    old_peak = lax.dynamic_slice_in_dim(peak_all, start, peak.shape[0], 0)
    old_total = lax.dynamic_slice_in_dim(total_all, start, peak.shape[0], 0)
    new_peak, new_total = combine_stats((old_peak, old_total), (peak, total))
    peak_all = lax.dynamic_update_slice_in_dim(peak_all, new_peak, start, 0)
    total_all = lax.dynamic_update_slice_in_dim(total_all, new_total, start, 0)
    return (peak_all, total_all)


def take_rows(whole, start, count):
    return lax.dynamic_slice_in_dim(whole, start, count, 0)


def local_general(
    latents,
    video_tokens,
    caption_tokens,
    caption_len,
    key_mask,
    drop_flags,
    gain_latent,
    gain_tokens,
    gain_mlp,
    query_weight,
    key_matrix,
    value_matrix,
    out_weight,
    up_weight,
    down_weight,
    cotangent,
):
    vid_count = lax.axis_size("vid")
    txt_count = lax.axis_size("txt")
    vid_index = lax.axis_index("vid")
    txt_index = lax.axis_index("txt")
    items_here = latents.shape[0]
    cap_items = caption_tokens.shape[0]
    items_total = items_here * txt_count
    head_width = query_weight.shape[1]
    head_size = D // HEADS
    heads_here = head_width // head_size
    scale = 1.0 / math.sqrt(head_size)
    video_here = video_tokens.shape[1]
    cap_here = caption_tokens.shape[1]
    video_start = txt_index * items_here
    cap_start = vid_index * cap_items
    keep = (1 - drop_flags).astype(jnp.float32)
    slots = txt_index * cap_here + jnp.arange(cap_here, dtype=jnp.int32)
    cap_valid = (slots[None, :] < caption_len[:, None]) & (key_mask == 1)
    cap_mask = cap_valid[:, None, None, :]

    def split_heads(values):
        return values.reshape(values.shape[0], values.shape[1], heads_here, head_size)

    lat_float = latents.astype(jnp.float32)
    lat_norm = layer_norm(lat_float, gain_latent).astype(jnp.bfloat16)
    queries = jnp.einsum(
        "bld,de->ble", lat_norm, query_weight, preferred_element_type=jnp.float32
    ).astype(jnp.bfloat16)
    all_queries = from_blocks(
        lax.all_gather(queries[None], ("vid", "txt"), axis=0, tiled=True), vid_count, txt_count
    )
    lat_total = all_queries.shape[1]
    video_queries = take_rows(all_queries, video_start, items_here)
    cap_queries = take_rows(all_queries, cap_start, cap_items)
    video_float = video_tokens.astype(jnp.float32)
    cap_float = caption_tokens.astype(jnp.float32)
    video_normed = layer_norm(video_float, gain_tokens).astype(jnp.bfloat16)
    caption_normed = layer_norm(cap_float, gain_tokens).astype(jnp.bfloat16)
    video_keys = jnp.einsum(
        "flc,co->flo", video_normed, key_matrix, preferred_element_type=jnp.float32
    ).astype(jnp.bfloat16)
    video_values = jnp.einsum(
        "flc,co->flo", video_normed, value_matrix, preferred_element_type=jnp.float32
    ).astype(jnp.bfloat16)
    cap_keys = jnp.einsum(
        "flc,co->flo", caption_normed, key_matrix, preferred_element_type=jnp.float32
    ).astype(jnp.bfloat16)
    cap_values = jnp.einsum(
        "flc,co->flo", caption_normed, value_matrix, preferred_element_type=jnp.float32
    ).astype(jnp.bfloat16)
    video_scores = (
        jnp.einsum(
            "blhe,bkhe->bhlk",
            split_heads(video_queries),
            split_heads(video_keys),
            preferred_element_type=jnp.float32,
        )
        * scale
    )
    cap_scores = (
        jnp.einsum(
            "blhe,bkhe->bhlk",
            split_heads(cap_queries),
            split_heads(cap_keys),
            preferred_element_type=jnp.float32,
        )
        * scale
    )
    cap_scores = jnp.where(cap_mask, cap_scores, -1e30)
    video_peak = jnp.max(video_scores, axis=-1)
    video_total = jnp.sum(jnp.exp(video_scores - video_peak[..., None]), axis=-1)
    cap_peak = jnp.max(cap_scores, axis=-1)
    cap_total = jnp.sum(
        jnp.where(cap_mask, jnp.exp(cap_scores - cap_peak[..., None]), 0.0), axis=-1
    )
    peak_all = jnp.full((items_total, heads_here, lat_total), -1e30, jnp.float32)
    total_all = jnp.zeros((items_total, heads_here, lat_total), jnp.float32)
    peak_all, total_all = place_stats(peak_all, total_all, video_peak, video_total, video_start)
    peak_all, total_all = place_stats(peak_all, total_all, cap_peak, cap_total, cap_start)
    peak, total = combined_all((peak_all, total_all), ("vid", "txt"), combine_stats)
    video_probs = (
        jnp.exp(video_scores - take_rows(peak, video_start, items_here)[..., None])
        / take_rows(total, video_start, items_here)[..., None]
    )
    cap_probs = jnp.where(
        cap_mask,
        jnp.exp(cap_scores - take_rows(peak, cap_start, cap_items)[..., None])
        / take_rows(total, cap_start, cap_items)[..., None],
        0.0,
    )
    video_low = video_probs.astype(jnp.bfloat16)
    cap_low = cap_probs.astype(jnp.bfloat16)
    video_part = jnp.einsum(
        "bhlk,bkhe->blhe", video_low, split_heads(video_values), preferred_element_type=jnp.float32
    ).reshape(items_here, lat_total, head_width)
    cap_part = jnp.einsum(
        "bhlk,bkhe->blhe", cap_low, split_heads(cap_values), preferred_element_type=jnp.float32
    ).reshape(cap_items, lat_total, head_width)
    value_all = jnp.zeros((items_total, lat_total, head_width), jnp.float32)
    value_all = place_sum(place_sum(value_all, video_part, video_start), cap_part, cap_start)
    attended = lax.psum_scatter(
        to_blocks(value_all, vid_count, txt_count), ("vid", "txt"), scatter_dimension=0, tiled=True
    )[0]
    mixed_in = (attended * keep[:, None, None]).astype(jnp.bfloat16)
    branch = lax.psum(
        jnp.einsum("ble,ed->bld", mixed_in, out_weight, preferred_element_type=jnp.float32), "head"
    )
    after_attn = lat_float + branch
    mlp_norm = layer_norm(after_attn, gain_mlp).astype(jnp.bfloat16)
    pre_act = jnp.einsum("bld,df->blf", mlp_norm, up_weight, preferred_element_type=jnp.float32)
    activ = gelu_exact(pre_act).astype(jnp.bfloat16)
    growth = lax.psum(
        jnp.einsum("blf,fd->bld", activ, down_weight, preferred_element_type=jnp.float32).astype(
            jnp.bfloat16
        ),
        "head",
    ).astype(jnp.float32)
    latents_out = (after_attn + growth).astype(jnp.bfloat16)
    grad_down = jnp.einsum("blf,bld->fd", activ, cotangent, preferred_element_type=jnp.float32)
    d_activ = jnp.einsum("bld,fd->blf", cotangent, down_weight, preferred_element_type=jnp.float32)
    d_pre = jax.vjp(gelu_exact, pre_act)[1](d_activ)[0].astype(jnp.bfloat16)
    grad_up = jnp.einsum("bld,blf->df", mlp_norm, d_pre, preferred_element_type=jnp.float32)
    d_mlp_norm = lax.psum(
        jnp.einsum("blf,df->bld", d_pre, up_weight, preferred_element_type=jnp.float32), "head"
    )
    d_after_norm, grad_gain_mlp = norm_back(after_attn, gain_mlp, d_mlp_norm)
    d_after = cotangent.astype(jnp.float32) + d_after_norm
    d_branch = d_after.astype(jnp.bfloat16)
    grad_out = jnp.einsum("ble,bld->ed", mixed_in, d_branch, preferred_element_type=jnp.float32)
    d_att = (
        jnp.einsum("bld,ed->ble", d_branch, out_weight, preferred_element_type=jnp.float32)
        * keep[:, None, None]
    ).astype(jnp.bfloat16)
    all_d_att = from_blocks(
        lax.all_gather(d_att[None], ("vid", "txt"), axis=0, tiled=True), vid_count, txt_count
    )
    video_d_att = split_heads(take_rows(all_d_att, video_start, items_here))
    cap_d_att = split_heads(take_rows(all_d_att, cap_start, cap_items))
    video_dprobs = jnp.einsum(
        "blhe,bkhe->bhlk",
        video_d_att,
        split_heads(video_values),
        preferred_element_type=jnp.float32,
    )
    cap_dprobs = jnp.einsum(
        "blhe,bkhe->bhlk", cap_d_att, split_heads(cap_values), preferred_element_type=jnp.float32
    )
    delta_all = jnp.zeros((items_total, heads_here, lat_total), jnp.float32)
    delta_all = place_sum(delta_all, jnp.sum(video_probs * video_dprobs, axis=-1), video_start)
    delta_all = place_sum(delta_all, jnp.sum(cap_probs * cap_dprobs, axis=-1), cap_start)
    delta = lax.psum(delta_all, ("vid", "txt"))
    video_dscores = (
        video_probs * (video_dprobs - take_rows(delta, video_start, items_here)[..., None])
    ).astype(jnp.bfloat16)
    cap_dscores = (
        cap_probs * (cap_dprobs - take_rows(delta, cap_start, cap_items)[..., None])
    ).astype(jnp.bfloat16)
    video_dq = (
        jnp.einsum(
            "bhlk,bkhe->blhe",
            video_dscores,
            split_heads(video_keys),
            preferred_element_type=jnp.float32,
        )
        * scale
    ).reshape(items_here, lat_total, head_width)
    cap_dq = (
        jnp.einsum(
            "bhlk,bkhe->blhe",
            cap_dscores,
            split_heads(cap_keys),
            preferred_element_type=jnp.float32,
        )
        * scale
    ).reshape(cap_items, lat_total, head_width)
    query_all = jnp.zeros((items_total, lat_total, head_width), jnp.float32)
    query_all = place_sum(place_sum(query_all, video_dq, video_start), cap_dq, cap_start)
    d_queries = lax.psum_scatter(
        to_blocks(query_all, vid_count, txt_count), ("vid", "txt"), scatter_dimension=0, tiled=True
    )[0].astype(jnp.bfloat16)
    video_key_grad = (
        (
            jnp.einsum(
                "bhlk,blhe->bkhe",
                video_dscores,
                split_heads(video_queries),
                preferred_element_type=jnp.float32,
            )
            * scale
        )
        .reshape(items_here, video_here, head_width)
        .astype(jnp.bfloat16)
    )
    video_value_grad = (
        jnp.einsum("bhlk,blhe->bkhe", video_low, video_d_att, preferred_element_type=jnp.float32)
        .reshape(items_here, video_here, head_width)
        .astype(jnp.bfloat16)
    )
    caption_key_grad = (
        (
            jnp.einsum(
                "bhlk,blhe->bkhe",
                cap_dscores,
                split_heads(cap_queries),
                preferred_element_type=jnp.float32,
            )
            * scale
        )
        .reshape(cap_items, cap_here, head_width)
        .astype(jnp.bfloat16)
    )
    caption_value_grad = (
        jnp.einsum("bhlk,blhe->bkhe", cap_low, cap_d_att, preferred_element_type=jnp.float32)
        .reshape(cap_items, cap_here, head_width)
        .astype(jnp.bfloat16)
    )
    grad_query = jnp.einsum("bld,ble->de", lat_norm, d_queries, preferred_element_type=jnp.float32)
    d_lat_norm = lax.psum(
        jnp.einsum("ble,de->bld", d_queries, query_weight, preferred_element_type=jnp.float32),
        "head",
    )
    d_lat_back, grad_gain_latent = norm_back(lat_float, gain_latent, d_lat_norm)
    latent_grad = d_after + d_lat_back
    grad_key = jnp.einsum(
        "zsg,zsv->gv", video_normed, video_key_grad, preferred_element_type=jnp.float32
    ) + jnp.einsum(
        "zsg,zsv->gv", caption_normed, caption_key_grad, preferred_element_type=jnp.float32
    )
    grad_value = jnp.einsum(
        "zsg,zsv->gv", video_normed, video_value_grad, preferred_element_type=jnp.float32
    ) + jnp.einsum(
        "zsg,zsv->gv", caption_normed, caption_value_grad, preferred_element_type=jnp.float32
    )
    video_term = jnp.einsum(
        "ayt,ot->ayo", video_key_grad, key_matrix, preferred_element_type=jnp.float32
    ) + jnp.einsum(
        "ayt,ot->ayo", video_value_grad, value_matrix, preferred_element_type=jnp.float32
    )
    cap_term = jnp.einsum(
        "ayt,ot->ayo", caption_key_grad, key_matrix, preferred_element_type=jnp.float32
    ) + jnp.einsum(
        "ayt,ot->ayo", caption_value_grad, value_matrix, preferred_element_type=jnp.float32
    )
    d_video_norm, d_cap_norm = lax.psum((video_term, cap_term), "head")
    video_grad, video_gain_part = norm_back(video_float, gain_tokens, d_video_norm)
    caption_grad, cap_gain_part = norm_back(cap_float, gain_tokens, d_cap_norm)
    grad_gain_tokens = video_gain_part + cap_gain_part
    kept_here = jnp.sum(keep)
    (
        grad_query,
        grad_key,
        grad_value,
        grad_out,
        grad_up,
        grad_down,
        grad_gain_latent,
        grad_gain_tokens,
        grad_gain_mlp,
        kept_total,
    ) = lax.psum(
        (
            grad_query,
            grad_key,
            grad_value,
            grad_out,
            grad_up,
            grad_down,
            grad_gain_latent,
            grad_gain_tokens,
            grad_gain_mlp,
            kept_here,
        ),
        ("vid", "txt"),
    )
    kept_count = (kept_total / vid_count).astype(jnp.int32)
    return (
        latents_out,
        latent_grad,
        video_grad,
        caption_grad,
        grad_query,
        grad_key,
        grad_value,
        grad_out,
        grad_up,
        grad_down,
        grad_gain_latent,
        grad_gain_tokens,
        grad_gain_mlp,
        kept_count,
    )


def swap_cores(values):
    return lax.ppermute(values, "vid", [(0, 1), (1, 0)])


def head_shift(values, shift, count):
    return lax.ppermute(values, "head", [(i, (i - shift) % count) for i in range(count)])


def take_block(values, index, size, axis=0):
    return lax.dynamic_slice_in_dim(values, index * size, size, axis)


def head_chunks(part, place, count):
    low = part.astype(BF16)
    others = [
        lax.dynamic_index_in_dim(low, (place - shift) % count, 0, False)
        for shift in range(1, count)
    ]
    return [lax.dynamic_index_in_dim(part, place, 0, False)] + others


def head_exchange(chunks, count):
    return [head_shift(chunks[shift], shift, count) for shift in range(1, count)]


def head_sum(own, received):
    for part in received:
        own = own + part.astype(F32)
    return own.astype(BF16)


def gather_head(total, place, count):
    result = jnp.zeros((count,) + total.shape, BF16)
    result = lax.dynamic_update_index_in_dim(result, total, place, 0)
    for shift in range(1, count):
        result = lax.dynamic_update_index_in_dim(
            result, head_shift(total, shift, count), (place + shift) % count, 0
        )
    return result


def group_steps(count):
    return [(step, [(i, (i - step) % count) for i in range(count)]) for step in range(1, count)]


def reduce_over_cores(rows, core):
    half = rows.shape[0] // 2
    other = swap_cores(take_block(rows, 1 - core, half))
    return take_block(rows, core, half).astype(F32) + other.astype(F32), other


def reduce_over_group(half, place, count):
    part = half.shape[0] // count
    low = half.astype(BF16)
    total = take_block(half, place, part)
    for step, perm in group_steps(count):
        chunk = take_block(low, (place - step) % count, part)
        total = total + lax.ppermute(chunk, "txt", perm).astype(F32)
    return total.astype(BF16)


def gather_places(total, place, count):
    part = total.shape[0]
    mine = jnp.zeros((part * count, total.shape[1]), BF16)
    mine = lax.dynamic_update_slice_in_dim(mine, total, place * part, 0)
    for step, perm in group_steps(count):
        mine = lax.dynamic_update_slice_in_dim(
            mine, lax.ppermute(total, "txt", perm), (place + step) % count * part, 0
        )
    return mine


def gather_cores(mine, core):
    half = mine.shape[0]
    whole = jnp.zeros((2 * half, mine.shape[1]), BF16)
    whole = lax.dynamic_update_slice_in_dim(whole, mine, core * half, 0)
    return lax.dynamic_update_slice_in_dim(whole, swap_cores(mine), (1 - core) * half, 0)


def caption_perm(step, vid_count, txt_count, cores):
    pairs = []
    for v in range(vid_count):
        for t in range(txt_count):
            block = (t + step) % txt_count
            dest_txt = v * (txt_count // vid_count) + block // cores
            dest_vid = block % cores
            pairs.append((v * txt_count + t, dest_vid * txt_count + dest_txt))
    return pairs


PAIR = 128
BACK_COST = 3
F32 = jnp.float32
BF16 = jnp.bfloat16


def dot_nt(a, b):
    return lax.dot_general(a, b, (((1,), (1,)), ((), ())), preferred_element_type=F32)


def dot_nn(a, b):
    return lax.dot_general(a, b, (((1,), (0,)), ((), ())), preferred_element_type=F32)


def dot_tn(a, b):
    return lax.dot_general(a, b, (((0,), (0,)), ((), ())), preferred_element_type=F32)


def square(ref):
    return ref[...].reshape(D, D)


def two_heads(values):
    low = lax.broadcasted_iota(jnp.int32, values.shape, 1) < PAIR // 2
    zero = jnp.zeros_like(values)
    return jnp.concatenate([jnp.where(low, values, zero), jnp.where(low, zero, values)], axis=0)


def from_two_heads(both):
    n = both.shape[1] // 2
    first = lax.broadcasted_iota(jnp.int32, (PAIR, n), 0) < PAIR // 2
    return jnp.where(first, both[:, :n], both[:, n:]).T


def chunk_list(video, cap, size):
    return [(start, size) for start in range(0, video, size)] + [(video, cap)]


def norm_kernel(s_ref, own_ref, other_ref, gain_ref, out_ref):
    gain = gain_ref[...]
    start = 0
    for ref in (own_ref, other_ref):
        def chunk(c, carry, ref=ref, start=start):
            for part in range(2):
                at = pl.multiple_of(c * 128, 128) + 64 * part
                out_ref[pl.ds(start + at, 64), :] = layer_norm(
                    ref[pl.ds(at, 64), :].astype(F32), gain
                ).astype(BF16)
            return carry

        lax.fori_loop(0, ref.shape[0] // 128, chunk, 0)
        start += ref.shape[0]


def cap_mask(cap_ref):
    mask = cap_ref[:, pl.ds(D, PAIR)]
    return jnp.concatenate([mask, mask], axis=1).astype(F32) > 0.5


def forward_kernel(s_ref, tok_ref, cap_ref, gain_ref, lat_ref, gain_lat_ref, wq_ref, wkv_ref, *refs):
    q_ref, k_ref, v_ref, lse_ref, o_ref, s_scr, e_scr, wkv_scr = refs[-8:]
    keys, width = k_ref.shape
    cap = cap_ref.shape[0]
    step = (keys - cap) // 4
    latn = layer_norm(lat_ref[...].astype(F32), gain_lat_ref[...]).astype(BF16)
    queries = dot_nt(latn, wq_ref[...].reshape(width, D)).astype(BF16).astype(F32)
    q_ref[...] = (queries * 0.125).astype(BF16)

    @pl.when(pl.program_id(0) == 0)
    def _():
        wkv_scr[...] = wkv_ref[...].reshape(2 * width, D).T

    def project(rows, tokens):
        both = dot_nn(tokens, wkv_scr[...]).astype(BF16)
        k_ref[rows, :] = both[:, :width]
        v_ref[rows, :] = both[:, width:]

    def project_video(c, carry):
        rows = pl.ds(pl.multiple_of(c * step, 16), step)
        project(rows, tok_ref[rows, :])
        return carry

    lax.fori_loop(0, 4, project_video, 0)
    cap_rows = pl.ds(keys - cap, cap)
    project(cap_rows, layer_norm(cap_ref[:, pl.ds(0, D)].astype(F32), gain_ref[...]).astype(BF16))
    pieces = [pl.ds(start, 64) for start in range(0, keys, 64)]

    def pair(p, carry):
        cols = pl.ds(pl.multiple_of(p * PAIR, PAIR), PAIR)
        q2 = two_heads(q_ref[:, cols])
        s_scr[...] = dot_nt(k_ref[:, cols], q2)
        s_scr[cap_rows, :] = jnp.where(cap_mask(cap_ref), s_scr[cap_rows, :], -1e30)
        peak = s_scr[pieces[0], :]
        for rows in pieces[1:]:
            peak = jnp.maximum(peak, s_scr[rows, :])
        peak = jnp.max(peak, axis=0, keepdims=True)
        total = jnp.zeros((8, q2.shape[0]), F32)
        for rows in pieces:
            e = jnp.exp(s_scr[rows, :] - peak)
            e_scr[rows, :] = e.astype(BF16)
            total = total + jnp.sum(e.reshape(-1, 8, q2.shape[0]), axis=0)
        total = jnp.sum(total, axis=0, keepdims=True)
        out = dot_tn(v_ref[:, cols], e_scr[...])
        o_ref[:, cols] = from_two_heads(out / total)
        lse_ref[pl.ds(p, 1), :] = peak + jnp.log(total)
        return carry

    lax.fori_loop(0, width // PAIR, pair, 0)


def backward_kernel(
    s_ref, q_ref, k_ref, v_ref, lse_ref, o_ref, datt_ref, own_ref, other_ref, cap_ref,
    wk_ref, wv_ref, gain_ref, tok_ref, wq_ref, lat_ref, after_ref, gain_lat_ref, ready_ref,
    own_out, other_out, cap_out, lat_out, late_ref,
    dq_ref, dk_ref, dv_ref, s_scr, dp_scr, p_scr, ds_scr, up_scr, sums_ref, gain_out,
):
    item = pl.program_id(0)
    keys = k_ref.shape[0]
    cap = cap_ref.shape[0]
    cap_rows = pl.ds(keys - cap, cap)
    pieces = [pl.ds(start, 64) for start in range(0, keys, 64)]

    def pair(p, carry):
        cols = pl.ds(pl.multiple_of(p * PAIR, PAIR), PAIR)
        q2 = two_heads(q_ref[:, cols])
        d_att = datt_ref[:, cols]
        d2 = two_heads(d_att)
        prod = (d_att.astype(F32) * o_ref[:, cols]).T
        delta = jnp.concatenate(
            [
                jnp.sum(prod[: PAIR // 2], axis=0, keepdims=True),
                jnp.sum(prod[PAIR // 2 :], axis=0, keepdims=True),
            ],
            axis=1,
        )
        pairs_here = D // PAIR // lse_ref.shape[0]
        lse = lse_ref[p // pairs_here, pl.ds(p % pairs_here, 1), :]
        s_scr[...] = dot_nt(k_ref[:, cols], q2)
        dp_scr[...] = dot_nt(v_ref[:, cols], d2)
        s_scr[cap_rows, :] = jnp.where(cap_mask(cap_ref), s_scr[cap_rows, :], -1e30)
        for rows in pieces:
            probs = jnp.exp(s_scr[rows, :] - lse)
            p_scr[rows, :] = probs.astype(BF16)
            ds_scr[rows, :] = (probs * (dp_scr[rows, :] - delta)).astype(BF16)
        dv_ref[:, cols] = dot_nn(p_scr[...], d2).astype(BF16)
        dk_ref[:, cols] = dot_nn(ds_scr[...], q2).astype(BF16)
        dq = dot_tn(k_ref[:, cols], ds_scr[...])
        dq_ref[:, cols] = (from_two_heads(dq) * 0.125).astype(BF16)
        return carry

    lax.fori_loop(0, D // PAIR, pair, 0)
    gain = gain_ref[...]

    @pl.when(item == 0)
    def _():
        gain_out[...] = jnp.zeros_like(gain_out)
        sums_ref[...] = jnp.zeros_like(sums_ref)

    wide = sums_ref.shape[0] // 4
    window = pl.ds(pl.multiple_of(s_ref[2], PAIR), wide)
    video_rows = pl.ds(0, keys - cap)
    cap_norm = layer_norm(cap_ref[:, pl.ds(0, D)].astype(F32), gain).astype(BF16)
    latn = layer_norm(lat_ref[...].astype(F32), gain_lat_ref[...]).astype(BF16)
    sums_ref[pl.ds(0, wide), :] += dot_tn(dq_ref[:, window], latn)
    keep = (1 - s_ref[4 + item]).astype(F32)
    mixed = (o_ref[:, window] * keep).astype(BF16)
    sums_ref[pl.ds(3 * wide, wide), :] += dot_tn(mixed, after_ref[...].astype(BF16))

    def both(rows):
        return jnp.concatenate([dk_ref[rows, window], dv_ref[rows, window]], axis=1)

    sums_ref[pl.ds(wide, 2 * wide), :] += dot_tn(both(video_rows), tok_ref[...]) + dot_tn(
        both(cap_rows), cap_norm
    )

    def norm_back(x, up, gain, row):
        center = x - jnp.mean(x, axis=-1, keepdims=True)
        rate = lax.rsqrt(jnp.mean(center * center, axis=-1, keepdims=True) + 1e-05)
        hat = center * rate
        gain_out[pl.ds(8 * row, 8), :] += jnp.sum((up * hat).reshape(-1, 8, D), axis=0)
        scaled = up * gain
        first = jnp.mean(scaled, axis=-1, keepdims=True)
        second = jnp.mean(scaled * hat, axis=-1, keepdims=True)
        return rate * (scaled - first - hat * second)

    half = lat_out.shape[0]
    lat_grad = after_ref[...] + norm_back(
        lat_ref[...].astype(F32), dot_nn(dq_ref[...], square(wq_ref)), gain_lat_ref[...], 1
    )
    lat_out[...] = lat_grad[:half]
    other_out[pl.ds(other_ref.shape[0], half), :] = lat_grad[half:].astype(BF16)

    start = 0
    for ref, out, size in ((own_ref, own_out, 256), (other_ref, other_out, 256), (cap_ref, cap_out, cap)):
        def chunk(c, carry, ref=ref, out=out, size=size, start=start):
            rows = pl.ds(pl.multiple_of(c * size, 16), size)
            key_rows = pl.ds(pl.multiple_of(start + c * size, 16), size)
            up_scr[pl.ds(0, size), :] = dot_nn(dk_ref[key_rows, :], square(wk_ref)) + dot_nn(
                dv_ref[key_rows, :], square(wv_ref)
            )
            for at in range(0, size, 32):
                piece = pl.ds(pl.multiple_of(c * size, 16) + at, 32)
                back = norm_back(
                    ref[piece, pl.ds(0, D)].astype(F32), up_scr[pl.ds(at, 32), :], gain, 0
                )
                out[piece, :] = back.astype(out.dtype)
            return carry

        lax.fori_loop(0, ref.shape[0] // size, chunk, 0)
        start += ref.shape[0]

    @pl.when(item == pl.num_programs(0) - 1)
    def _():
        width = D // 4
        for n in range(4):
            mine = pl.ds(pl.multiple_of(s_ref[3] + n * wide, PAIR // 2), width)
            late_ref[pl.ds(n * width, width), :] = sums_ref[mine, :].astype(BF16)
        ready = ready_ref.shape[0]
        late_ref[pl.ds(4 * width, ready), :] = ready_ref[...]
        gains = [jnp.sum(gain_out[pl.ds(8 * row, 8), :], axis=0, keepdims=True) for row in (0, 1)]
        gains = jnp.concatenate(gains + [jnp.zeros((14, D), F32)], axis=0)
        late_ref[pl.ds(4 * width + ready, 16), :] = gains.astype(BF16)
        spare = late_ref.shape[0] - 4 * width - ready - 16
        late_ref[pl.ds(4 * width + ready + 16, spare), :] = jnp.zeros((spare, D), BF16)


def place_kernel(s_ref, video_in, lat_in, video_part, lat_part, video_ref, lat_ref):
    video_ref[...] = video_part[...].astype(F32)

    @pl.when(pl.program_id(1) == 0)
    def _():
        lat_ref[...] = lat_part[...].astype(F32)


def local(
    latents,
    video_tokens,
    caption_tokens,
    caption_len,
    key_mask,
    drop_flags,
    gain_latent,
    gain_tokens,
    gain_mlp,
    query_weight,
    key_matrix,
    value_matrix,
    out_weight,
    up_weight,
    down_weight,
    cotangent,
):
    txt_count = lax.axis_size("txt")
    head_count = lax.axis_size("head")
    core = lax.axis_index("vid")
    place_index = lax.axis_index("txt")
    z = lax.axis_index("head")
    items_here = latents.shape[0]
    own = items_here // 2
    lat_half = latents.shape[1]
    lat_rows = 2 * lat_half
    video_here = video_tokens.shape[1]
    cap_here = caption_tokens.shape[1]
    cap_rows = cap_here * txt_count
    keys_here = 2 * video_here + cap_rows
    head_width = query_weight.shape[1]

    def dot(spec, a, b):
        return jnp.einsum(spec, a, b, preferred_element_type=F32)

    packed = jnp.stack([key_matrix.T, value_matrix.T, query_weight.T, out_weight])
    half = take_block(packed, core, 2)
    up1 = lax.ppermute(half, "head", [(0, 1), (1, 2), (2, 3)])
    down1 = lax.ppermute(half, "head", [(1, 0), (2, 1), (3, 2)])
    near_at = z // 2
    zero = jnp.int32(0)
    own_at = z % 2
    part_shape = (2, 2, 2, head_width, D)

    def place_chunk(whole, chunk, at_core, at_chunk):
        chunk = chunk.reshape((-1, 2, 1) + chunk.shape[-2:])
        return lax.dynamic_update_slice(whole, chunk, (at_core, zero, at_chunk, zero, zero))

    both_own = take_block(jnp.concatenate([latents, cotangent], axis=1), core, own)
    video_other = swap_cores(
        jnp.concatenate(
            [take_block(a, 1 - core, own) for a in (video_tokens, latents, cotangent)], axis=1
        )
    )
    both_other = video_other[:, video_here:]
    lat = jnp.concatenate([both_own[:, :lat_half], both_other[:, :lat_half]], axis=1)
    cot = jnp.concatenate([both_own[:, lat_half:], both_other[:, lat_half:]], axis=1)
    drop_own = take_block(drop_flags, core, own)
    keep = (1 - drop_own).astype(F32)
    window = z * head_width // PAIR * PAIR
    inside = z * head_width - window
    scalars = jnp.concatenate([jnp.stack([core, near_at, window, inside]), drop_own])
    scalars_far = jnp.concatenate([jnp.stack([core, 1 - near_at, window, inside]), drop_own])

    place_slots = place_index * cap_here + jnp.arange(cap_here, dtype=jnp.int32)
    cap_valid = (place_slots[None, :] < caption_len[:, None]) & (key_mask == 1)
    flags = jnp.broadcast_to(cap_valid.astype(BF16)[:, :, None], cap_valid.shape + (PAIR,))
    cap_message = jnp.concatenate([caption_tokens, flags], axis=2)
    cap_parts = []
    for step in range(txt_count):
        block = take_block(cap_message, (place_index + step) % txt_count, own)
        cap_parts.append(
            lax.ppermute(block, ("vid", "txt"), caption_perm(step, 2, txt_count, 2))
        )
    def item_spec(rows, width=D, first=0):
        return pl.BlockSpec((None, rows, width), lambda i, s: (first + i, 0, 0))

    def own_spec(rows, first=0):
        return pl.BlockSpec((None, rows, D), lambda i, s: (s[0] * own + first + i, 0, 0))

    def whole_spec(*shape):
        return pl.BlockSpec(shape, lambda i, s: (0,) * len(shape))

    def weight_spec(m):
        return pl.BlockSpec(
            (2, None, None, 2, head_width, D),
            lambda i, s: (0, m // 2, m % 2, 0, 0, 0),
            pipeline_mode=pl.Buffered(1),
        )

    def part_spec(at_core, first, count):
        return pl.BlockSpec(
            (None, count, 2, head_width, D),
            lambda i, s: (at_core, first, 0, 0, 0),
            pipeline_mode=pl.Buffered(1),
        )

    def half_spec(rows):
        return pl.BlockSpec((None, rows, 2 * head_width), lambda i, s: (i, 0, s[1]))

    row_spec = pl.BlockSpec((1, D), lambda i, s: (0, 0))

    def call(kernel, name, ins, outs, operands, micros, scratch=(), aliases={}, scalars=scalars, grid=own):
        return pl.pallas_call(
            kernel,
            name=name,
            grid_spec=pltpu.PrefetchScalarGridSpec(
                num_scalar_prefetch=1,
                grid=(grid,),
                in_specs=ins,
                out_specs=[spec for spec, _, _ in outs],
                scratch_shapes=list(scratch),
            ),
            out_shape=[jax.ShapeDtypeStruct(shape, dtype) for _, shape, dtype in outs],
            input_output_aliases=aliases,
            cost_estimate=pl.CostEstimate(
                flops=micros * 1100 * 10**6, transcendentals=0, bytes_accessed=micros * 10**6
            ),
            compiler_params=pltpu.CompilerParams(vmem_limit_bytes=56 << 20),
        )(scalars, *operands)

    def item_out(rows, dtype, width=D):
        return (item_spec(rows, width), (own, rows, width), dtype)

    gain_lat_row = gain_latent[None]
    gain_tok_row = gain_tokens[None]
    gain_mlp_row = gain_mlp[None]
    (tok_norm,) = call(
        norm_kernel,
        "token_norm",
        [own_spec(video_here), item_spec(video_here), row_spec],
        [item_out(2 * video_here, BF16)],
        (video_tokens, video_other, gain_tok_row),
        9,
    )
    tok_norm, up1, down1, cap_parts = lax.optimization_barrier((tok_norm, up1, down1, cap_parts))
    cap = jnp.concatenate(cap_parts, axis=1)
    partner = jnp.where(z % 2 == 1, up1, down1)
    near = jnp.zeros(part_shape, BF16)
    near = place_chunk(near, packed.reshape((2, 2) + packed.shape[1:]), zero, own_at)
    near = place_chunk(near, partner, core, 1 - own_at)
    partner_other = swap_cores(partner)
    near = place_chunk(near, partner_other, 1 - core, 1 - own_at)
    up1, down1, half_then, _ = lax.optimization_barrier((up1, down1, half, partner_other))
    ring_up = lax.ppermute(jnp.where(z == 3, half_then, up1), "head", [(1, 2), (2, 3), (3, 0)])
    ring_down = lax.ppermute(jnp.where(z == 0, half_then, down1), "head", [(1, 0), (2, 1), (0, 3)])

    def forward(part, scalars, before=()):
        return call(
            forward_kernel,
            "attention_forward",
            [item_spec(2 * video_here), item_spec(cap_rows, D + PAIR), row_spec]
            + [item_spec(lat_rows), row_spec]
            + [part_spec(1, 0, 1), part_spec(0, 0, 2)]
            + [pl.BlockSpec(memory_space=pl.ANY)] * len(before),
            [
                (half_spec(lat_rows), (own, lat_rows, D), BF16),
                (half_spec(keys_here), (own, keys_here, D), BF16),
                (half_spec(keys_here), (own, keys_here, D), BF16),
                (
                    pl.BlockSpec((None, None, 8, 2 * lat_rows), lambda i, s: (i, s[1], 0, 0)),
                    (own, 2, 8, 2 * lat_rows),
                    F32,
                ),
                (half_spec(lat_rows), (own, lat_rows, D), F32),
            ],
            (tok_norm, cap, gain_tok_row, lat, gain_lat_row, part, part) + tuple(before),
            23,
            [
                pltpu.VMEM((keys_here, 2 * lat_rows), F32),
                pltpu.VMEM((keys_here, 2 * lat_rows), BF16),
                pltpu.VMEM((D, 4 * head_width), BF16),
            ],
            {8 + n: n for n in range(len(before))},
            scalars,
        )

    before = forward(near, scalars)
    before, up1, down1, ring_up, ring_down = lax.optimization_barrier(
        (before, up1, down1, ring_up, ring_down)
    )
    far_low = jnp.where(z == 1, down1, jnp.where(z == 2, ring_up, ring_down))
    far_high = jnp.where(z == 1, ring_down, jnp.where(z == 2, up1, ring_up))
    far_mine = jnp.stack([far_low, far_high], axis=1)
    far = jnp.zeros(part_shape, BF16)
    far = lax.dynamic_update_index_in_dim(far, far_mine, core, 0)
    far = lax.dynamic_update_index_in_dim(far, swap_cores(far_mine), 1 - core, 0)
    def both_halves(near, far):
        whole = jnp.zeros((2,) + near.shape, BF16)
        whole = lax.dynamic_update_index_in_dim(whole, near, near_at, 0)
        return lax.dynamic_update_index_in_dim(whole, far, 1 - near_at, 0)

    queries, keys, values, lse, attended = forward(far, scalars_far, before)
    w_out = both_halves(near[1, 1], far[1, 1]).reshape(D, D)
    lat_float = lat.astype(F32)
    mixed_in = (attended * keep[:, None, None]).astype(BF16)
    after_attn = lat_float + dot("ble,ed->bld", mixed_in, w_out)
    mlp_norm = layer_norm(after_attn, gain_mlp).astype(BF16)

    pre_act = dot("bld,df->blf", mlp_norm, up_weight)
    activ, gelu_pull = jax.vjp(gelu_exact, pre_act)
    activ = activ.astype(BF16)
    d_pre = gelu_pull(dot("bld,fd->blf", cot, down_weight))[0].astype(BF16)
    d_mlp_part = dot("blf,df->bld", d_pre, up_weight)
    d_mlp_part, activ, d_pre = lax.optimization_barrier((d_mlp_part, activ, d_pre))
    chunks = head_chunks(d_mlp_part, z, head_count)
    received = head_exchange(chunks, head_count)
    activ, d_pre, received[0] = lax.optimization_barrier((activ, d_pre, received[0]))
    d_mlp_total = head_sum(chunks[0], received)
    grad_down = dot("blf,bld->fd", activ, cot).astype(BF16)
    grad_up = dot("bld,blf->df", mlp_norm, d_pre).astype(BF16)
    near, far, _ = lax.optimization_barrier((near, far, d_mlp_part))
    weights = both_halves(near, far)
    early = jnp.where(core == 0, grad_up, grad_down).astype(F32)
    early = early + swap_cores(jnp.where(core == 0, grad_down, grad_up)).astype(F32)
    d_mlp_norm = gather_head(d_mlp_total, z, head_count)
    activ, _ = lax.optimization_barrier((activ, d_mlp_total))
    growth = head_chunks(dot("blf,fd->bld", activ, down_weight), z, head_count)
    growth, d_mlp_norm, weights, early = lax.optimization_barrier(
        (growth, d_mlp_norm, weights, early.astype(BF16))
    )
    early = lax.psum(early, "txt")
    growth_received = head_exchange(growth, head_count)

    d_after_norm, gain_mlp_part = norm_back_rows(after_attn, gain_mlp, d_mlp_norm.astype(F32))
    d_after = cot.astype(F32) + d_after_norm
    d_branch = d_after.astype(BF16)
    d_att = (dot("bld,ed->ble", d_branch, w_out) * keep[:, None, None]).astype(BF16)
    ready = jnp.concatenate(
        [
            jnp.sum(gain_mlp_part, axis=0)[None],
            jnp.full((1, D), jnp.sum(keep)),
            jnp.zeros((14, D), F32),
        ]
    ).astype(BF16)
    late_size = 4 * head_width + 32
    late_size = late_size + -late_size % (32 * txt_count)
    pair_shape = (keys_here, 2 * lat_rows)
    d_att, ready = lax.optimization_barrier((d_att, ready))
    video_grad, other_back, cap_back, latent_grad, late = call(
        backward_kernel,
        "attention_backward",
        [
            item_spec(lat_rows),
            item_spec(keys_here),
            item_spec(keys_here),
            pl.BlockSpec((None, 2, 8, 2 * lat_rows), lambda i, s: (i, 0, 0, 0)),
            item_spec(lat_rows),
            item_spec(lat_rows),
            own_spec(video_here),
            item_spec(video_here),
            item_spec(cap_rows, D + PAIR),
            weight_spec(0),
            weight_spec(1),
            row_spec,
            item_spec(2 * video_here),
            weight_spec(2),
            item_spec(lat_rows),
            item_spec(lat_rows),
            row_spec,
            whole_spec(*ready.shape),
        ],
        [
            (own_spec(video_here), video_tokens.shape, F32),
            item_out(video_here + lat_half, BF16),
            item_out(cap_rows, BF16),
            (own_spec(lat_half), latents.shape, F32),
            (whole_spec(late_size, D), (late_size, D), BF16),
        ],
        (
            queries, keys, values, lse, attended, d_att, video_tokens, video_other, cap,
            weights, weights, gain_tok_row, tok_norm, weights, lat, d_after, gain_lat_row, ready,
        ),
        BACK_COST,
        [
            pltpu.VMEM((lat_rows, D), BF16),
            pltpu.VMEM((keys_here, D), BF16),
            pltpu.VMEM((keys_here, D), BF16),
            pltpu.VMEM(pair_shape, F32),
            pltpu.VMEM(pair_shape, F32),
            pltpu.VMEM(pair_shape, BF16),
            pltpu.VMEM(pair_shape, BF16),
            pltpu.VMEM((256, D), F32),
            pltpu.VMEM((8 * PAIR, D), F32),
            pltpu.VMEM((16, D), F32),
        ],
    )
    def place(video_grad, latent_grad, part):
        piece = video_here
        return pl.pallas_call(
            place_kernel,
            name="place_rows",
            grid_spec=pltpu.PrefetchScalarGridSpec(
                num_scalar_prefetch=1,
                grid=(own, 1),
                in_specs=[
                    pl.BlockSpec(memory_space=pl.ANY),
                    pl.BlockSpec(memory_space=pl.ANY),
                    pl.BlockSpec((None, piece, D), lambda i, r, s: (i, r, 0)),
                    pl.BlockSpec((None, lat_half, D), lambda i, r, s: (i, video_here // lat_half, 0)),
                ],
                out_specs=[
                    pl.BlockSpec((None, piece, D), lambda i, r, s: ((1 - s[0]) * own + i, r, 0)),
                    pl.BlockSpec((None, lat_half, D), lambda i, r, s: ((1 - s[0]) * own + i, 0, 0)),
                ],
            ),
            out_shape=[
                jax.ShapeDtypeStruct(video_tokens.shape, F32),
                jax.ShapeDtypeStruct(latents.shape, F32),
            ],
            input_output_aliases={1: 0, 2: 1},
            cost_estimate=pl.CostEstimate(
                flops=6 * 10**9, transcendentals=0, bytes_accessed=10**7
            ),
        )(scalars, video_grad, latent_grad, part, part)

    early, growth_received, late = lax.optimization_barrier((early, growth_received, late))
    late_half, late_swapped = reduce_over_cores(late, core)
    other_back, early, _ = lax.optimization_barrier((other_back, early, late_swapped))
    other_here = swap_cores(other_back)
    growth_received, _ = lax.optimization_barrier((growth_received, late_swapped))
    growth = head_sum(growth[0], growth_received)
    early_other = swap_cores(early)
    late_total = reduce_over_group(late_half, place_index, txt_count)
    late_total, growth, early_other, other_here, cap_back = lax.optimization_barrier(
        (late_total, growth, early_other, other_here, cap_back)
    )
    growth = gather_head(growth, z, head_count)
    cap_parts = []
    for step in range(txt_count):
        perm = [(b, a) for a, b in caption_perm(step, 2, txt_count, 2)]
        cap_parts.append(
            lax.ppermute(cap_back[:, step * cap_here : (step + 1) * cap_here], ("vid", "txt"), perm)
        )
    late = gather_places(late_total, place_index, txt_count)
    video_grad, latent_grad = place(video_grad, latent_grad, other_here)
    late, video_grad, latent_grad, cap_parts, growth = lax.optimization_barrier(
        (late, video_grad, latent_grad, cap_parts, growth)
    )
    late = gather_cores(late, core).astype(F32)
    caption_grad = jnp.zeros((txt_count, own, cap_here, D), F32)
    for step, part in enumerate(cap_parts):
        caption_grad = lax.dynamic_update_index_in_dim(
            caption_grad, part.astype(F32), (place_index + step) % txt_count, 0
        )
    caption_grad = caption_grad.reshape(caption_tokens.shape)
    out_mine = (after_attn + growth.reshape(after_attn.shape).astype(F32)).astype(BF16)
    gains = late[4 * head_width :]

    def give_back(values):
        other = swap_cores(values[:, lat_half:].astype(BF16)).astype(values.dtype)
        whole = jnp.zeros((items_here, lat_half, D), values.dtype)
        whole = lax.dynamic_update_slice_in_dim(whole, values[:, :lat_half], core * own, 0)
        return lax.dynamic_update_slice_in_dim(whole, other, (1 - core) * own, 0)

    latents_out = give_back(out_mine)
    kept_count = gains[1, 0].astype(jnp.int32)
    return (
        latents_out,
        latent_grad,
        video_grad,
        caption_grad,
        late[:head_width].T,
        late[head_width : 2 * head_width].T,
        late[2 * head_width : 3 * head_width].T,
        late[3 * head_width : 4 * head_width],
        jnp.where(core == 0, early, early_other).astype(F32),
        jnp.where(core == 0, early_other, early).astype(F32),
        gains[17],
        gains[16],
        gains[0],
        kept_count,
    )


def norm_back_rows(values, gain, upstream):
    mean = jnp.mean(values, axis=-1, keepdims=True)
    center = values - mean
    rate = lax.rsqrt(jnp.mean(center * center, axis=-1, keepdims=True) + 1e-05)
    hat = center * rate
    scaled = upstream * gain
    first = jnp.mean(scaled, axis=-1, keepdims=True)
    second = jnp.mean(scaled * hat, axis=-1, keepdims=True)
    return rate * (scaled - first - hat * second), jnp.sum(upstream * hat, axis=-2)


def fits(mesh):
    shape = mesh.shape
    return shape["vid"] == 2 and shape["txt"] == 4 and shape["head"] == 4


def solution(mesh):
    in_specs = (
        P("txt", "vid", None),
        P("txt", "vid", None),
        P("vid", "txt", None),
        P("vid"),
        P("vid", "txt"),
        P("txt"),
        P(),
        P(),
        P(),
        P(None, "head"),
        P(None, "head"),
        P(None, "head"),
        P("head", None),
        P(None, "head"),
        P("head", None),
        P("txt", "vid", None),
    )
    out_specs = (
        P("txt", "vid", None),
        P("txt", "vid", None),
        P("txt", "vid", None),
        P("vid", "txt", None),
        P(None, "head"),
        P(None, "head"),
        P(None, "head"),
        P("head", None),
        P(None, "head"),
        P("head", None),
        P(),
        P(),
        P(),
        P(),
    )
    return jax.shard_map(local if fits(mesh) else local_general, mesh=mesh, in_specs=in_specs, out_specs=out_specs, check_vma=False)
```

```python
import functools
import math

import jax
import jax.numpy as jnp
from jax import lax
from jax.experimental import pallas as pl
from jax.experimental.pallas import tpu as pltpu
from jax.sharding import PartitionSpec as P

D = 768
HEADS = 12


def combined_all(part, axis, combine):
    gathered = jax.tree.map(lambda a: lax.all_gather(a, axis), part)

    def take(source):
        return jax.tree.map(lambda a: lax.dynamic_index_in_dim(a, source, 0, False), gathered)

    return lax.fori_loop(
        1, lax.axis_size(axis), lambda source, state: combine(state, take(source)), take(0)
    )


def layer_norm(values, gain):
    center = values - jnp.mean(values, axis=-1, keepdims=True)
    spread = jnp.mean(center * center, axis=-1, keepdims=True)
    return center * lax.rsqrt(spread + 1e-05) * gain


def norm_back(values, gain, upstream):
    result, pullback = jax.vjp(layer_norm, values, gain)
    return pullback(upstream)


def gelu_exact(values):
    return jax.nn.gelu(values, approximate=False)


def combine_stats(first, second):
    peak = jnp.maximum(first[0], second[0])
    total = first[1] * jnp.exp(first[0] - peak) + second[1] * jnp.exp(second[0] - peak)
    return (peak, total)


def to_blocks(whole, vid_count, txt_count):
    items, rows, width = whole.shape
    split = whole.reshape(txt_count, items // txt_count, vid_count, rows // vid_count, width)
    return split.transpose(2, 0, 1, 3, 4).reshape(
        vid_count * txt_count, items // txt_count, rows // vid_count, width
    )


def from_blocks(blocked, vid_count, txt_count):
    count, items_here, rows_here, width = blocked.shape
    split = blocked.reshape(vid_count, txt_count, items_here, rows_here, width)
    return split.transpose(1, 2, 0, 3, 4).reshape(
        txt_count * items_here, vid_count * rows_here, width
    )


def place_sum(whole, part, start):
    current = lax.dynamic_slice_in_dim(whole, start, part.shape[0], 0)
    return lax.dynamic_update_slice_in_dim(whole, current + part, start, 0)


def place_stats(peak_all, total_all, peak, total, start):
    old_peak = lax.dynamic_slice_in_dim(peak_all, start, peak.shape[0], 0)
    old_total = lax.dynamic_slice_in_dim(total_all, start, peak.shape[0], 0)
    new_peak, new_total = combine_stats((old_peak, old_total), (peak, total))
    peak_all = lax.dynamic_update_slice_in_dim(peak_all, new_peak, start, 0)
    total_all = lax.dynamic_update_slice_in_dim(total_all, new_total, start, 0)
    return (peak_all, total_all)


def take_rows(whole, start, count):
    return lax.dynamic_slice_in_dim(whole, start, count, 0)


def local_general(
    latents,
    video_tokens,
    caption_tokens,
    caption_len,
    key_mask,
    drop_flags,
    gain_latent,
    gain_tokens,
    gain_mlp,
    query_weight,
    key_matrix,
    value_matrix,
    out_weight,
    up_weight,
    down_weight,
    cotangent,
):
    vid_count = lax.axis_size("vid")
    txt_count = lax.axis_size("txt")
    vid_index = lax.axis_index("vid")
    txt_index = lax.axis_index("txt")
    items_here = latents.shape[0]
    cap_items = caption_tokens.shape[0]
    items_total = items_here * txt_count
    head_width = query_weight.shape[1]
    head_size = D // HEADS
    heads_here = head_width // head_size
    scale = 1.0 / math.sqrt(head_size)
    video_here = video_tokens.shape[1]
    cap_here = caption_tokens.shape[1]
    video_start = txt_index * items_here
    cap_start = vid_index * cap_items
    keep = (1 - drop_flags).astype(jnp.float32)
    slots = txt_index * cap_here + jnp.arange(cap_here, dtype=jnp.int32)
    cap_valid = (slots[None, :] < caption_len[:, None]) & (key_mask == 1)
    cap_mask = cap_valid[:, None, None, :]

    def split_heads(values):
        return values.reshape(values.shape[0], values.shape[1], heads_here, head_size)

    lat_float = latents.astype(jnp.float32)
    lat_norm = layer_norm(lat_float, gain_latent).astype(jnp.bfloat16)
    queries = jnp.einsum(
        "bld,de->ble", lat_norm, query_weight, preferred_element_type=jnp.float32
    ).astype(jnp.bfloat16)
    all_queries = from_blocks(
        lax.all_gather(queries[None], ("vid", "txt"), axis=0, tiled=True), vid_count, txt_count
    )
    lat_total = all_queries.shape[1]
    video_queries = take_rows(all_queries, video_start, items_here)
    cap_queries = take_rows(all_queries, cap_start, cap_items)
    video_float = video_tokens.astype(jnp.float32)
    cap_float = caption_tokens.astype(jnp.float32)
    video_normed = layer_norm(video_float, gain_tokens).astype(jnp.bfloat16)
    caption_normed = layer_norm(cap_float, gain_tokens).astype(jnp.bfloat16)
    video_keys = jnp.einsum(
        "flc,co->flo", video_normed, key_matrix, preferred_element_type=jnp.float32
    ).astype(jnp.bfloat16)
    video_values = jnp.einsum(
        "flc,co->flo", video_normed, value_matrix, preferred_element_type=jnp.float32
    ).astype(jnp.bfloat16)
    cap_keys = jnp.einsum(
        "flc,co->flo", caption_normed, key_matrix, preferred_element_type=jnp.float32
    ).astype(jnp.bfloat16)
    cap_values = jnp.einsum(
        "flc,co->flo", caption_normed, value_matrix, preferred_element_type=jnp.float32
    ).astype(jnp.bfloat16)
    video_scores = (
        jnp.einsum(
            "blhe,bkhe->bhlk",
            split_heads(video_queries),
            split_heads(video_keys),
            preferred_element_type=jnp.float32,
        )
        * scale
    )
    cap_scores = (
        jnp.einsum(
            "blhe,bkhe->bhlk",
            split_heads(cap_queries),
            split_heads(cap_keys),
            preferred_element_type=jnp.float32,
        )
        * scale
    )
    cap_scores = jnp.where(cap_mask, cap_scores, -1e30)
    video_peak = jnp.max(video_scores, axis=-1)
    video_total = jnp.sum(jnp.exp(video_scores - video_peak[..., None]), axis=-1)
    cap_peak = jnp.max(cap_scores, axis=-1)
    cap_total = jnp.sum(
        jnp.where(cap_mask, jnp.exp(cap_scores - cap_peak[..., None]), 0.0), axis=-1
    )
    peak_all = jnp.full((items_total, heads_here, lat_total), -1e30, jnp.float32)
    total_all = jnp.zeros((items_total, heads_here, lat_total), jnp.float32)
    peak_all, total_all = place_stats(peak_all, total_all, video_peak, video_total, video_start)
    peak_all, total_all = place_stats(peak_all, total_all, cap_peak, cap_total, cap_start)
    peak, total = combined_all((peak_all, total_all), ("vid", "txt"), combine_stats)
    video_probs = (
        jnp.exp(video_scores - take_rows(peak, video_start, items_here)[..., None])
        / take_rows(total, video_start, items_here)[..., None]
    )
    cap_probs = jnp.where(
        cap_mask,
        jnp.exp(cap_scores - take_rows(peak, cap_start, cap_items)[..., None])
        / take_rows(total, cap_start, cap_items)[..., None],
        0.0,
    )
    video_low = video_probs.astype(jnp.bfloat16)
    cap_low = cap_probs.astype(jnp.bfloat16)
    video_part = jnp.einsum(
        "bhlk,bkhe->blhe", video_low, split_heads(video_values), preferred_element_type=jnp.float32
    ).reshape(items_here, lat_total, head_width)
    cap_part = jnp.einsum(
        "bhlk,bkhe->blhe", cap_low, split_heads(cap_values), preferred_element_type=jnp.float32
    ).reshape(cap_items, lat_total, head_width)
    value_all = jnp.zeros((items_total, lat_total, head_width), jnp.float32)
    value_all = place_sum(place_sum(value_all, video_part, video_start), cap_part, cap_start)
    attended = lax.psum_scatter(
        to_blocks(value_all, vid_count, txt_count), ("vid", "txt"), scatter_dimension=0, tiled=True
    )[0]
    mixed_in = (attended * keep[:, None, None]).astype(jnp.bfloat16)
    branch = lax.psum(
        jnp.einsum("ble,ed->bld", mixed_in, out_weight, preferred_element_type=jnp.float32), "head"
    )
    after_attn = lat_float + branch
    mlp_norm = layer_norm(after_attn, gain_mlp).astype(jnp.bfloat16)
    pre_act = jnp.einsum("bld,df->blf", mlp_norm, up_weight, preferred_element_type=jnp.float32)
    activ = gelu_exact(pre_act).astype(jnp.bfloat16)
    growth = lax.psum(
        jnp.einsum("blf,fd->bld", activ, down_weight, preferred_element_type=jnp.float32).astype(
            jnp.bfloat16
        ),
        "head",
    ).astype(jnp.float32)
    latents_out = (after_attn + growth).astype(jnp.bfloat16)
    grad_down = jnp.einsum("blf,bld->fd", activ, cotangent, preferred_element_type=jnp.float32)
    d_activ = jnp.einsum("bld,fd->blf", cotangent, down_weight, preferred_element_type=jnp.float32)
    d_pre = jax.vjp(gelu_exact, pre_act)[1](d_activ)[0].astype(jnp.bfloat16)
    grad_up = jnp.einsum("bld,blf->df", mlp_norm, d_pre, preferred_element_type=jnp.float32)
    d_mlp_norm = lax.psum(
        jnp.einsum("blf,df->bld", d_pre, up_weight, preferred_element_type=jnp.float32), "head"
    )
    d_after_norm, grad_gain_mlp = norm_back(after_attn, gain_mlp, d_mlp_norm)
    d_after = cotangent.astype(jnp.float32) + d_after_norm
    d_branch = d_after.astype(jnp.bfloat16)
    grad_out = jnp.einsum("ble,bld->ed", mixed_in, d_branch, preferred_element_type=jnp.float32)
    d_att = (
        jnp.einsum("bld,ed->ble", d_branch, out_weight, preferred_element_type=jnp.float32)
        * keep[:, None, None]
    ).astype(jnp.bfloat16)
    all_d_att = from_blocks(
        lax.all_gather(d_att[None], ("vid", "txt"), axis=0, tiled=True), vid_count, txt_count
    )
    video_d_att = split_heads(take_rows(all_d_att, video_start, items_here))
    cap_d_att = split_heads(take_rows(all_d_att, cap_start, cap_items))
    video_dprobs = jnp.einsum(
        "blhe,bkhe->bhlk",
        video_d_att,
        split_heads(video_values),
        preferred_element_type=jnp.float32,
    )
    cap_dprobs = jnp.einsum(
        "blhe,bkhe->bhlk", cap_d_att, split_heads(cap_values), preferred_element_type=jnp.float32
    )
    delta_all = jnp.zeros((items_total, heads_here, lat_total), jnp.float32)
    delta_all = place_sum(delta_all, jnp.sum(video_probs * video_dprobs, axis=-1), video_start)
    delta_all = place_sum(delta_all, jnp.sum(cap_probs * cap_dprobs, axis=-1), cap_start)
    delta = lax.psum(delta_all, ("vid", "txt"))
    video_dscores = (
        video_probs * (video_dprobs - take_rows(delta, video_start, items_here)[..., None])
    ).astype(jnp.bfloat16)
    cap_dscores = (
        cap_probs * (cap_dprobs - take_rows(delta, cap_start, cap_items)[..., None])
    ).astype(jnp.bfloat16)
    video_dq = (
        jnp.einsum(
            "bhlk,bkhe->blhe",
            video_dscores,
            split_heads(video_keys),
            preferred_element_type=jnp.float32,
        )
        * scale
    ).reshape(items_here, lat_total, head_width)
    cap_dq = (
        jnp.einsum(
            "bhlk,bkhe->blhe",
            cap_dscores,
            split_heads(cap_keys),
            preferred_element_type=jnp.float32,
        )
        * scale
    ).reshape(cap_items, lat_total, head_width)
    query_all = jnp.zeros((items_total, lat_total, head_width), jnp.float32)
    query_all = place_sum(place_sum(query_all, video_dq, video_start), cap_dq, cap_start)
    d_queries = lax.psum_scatter(
        to_blocks(query_all, vid_count, txt_count), ("vid", "txt"), scatter_dimension=0, tiled=True
    )[0].astype(jnp.bfloat16)
    video_key_grad = (
        (
            jnp.einsum(
                "bhlk,blhe->bkhe",
                video_dscores,
                split_heads(video_queries),
                preferred_element_type=jnp.float32,
            )
            * scale
        )
        .reshape(items_here, video_here, head_width)
        .astype(jnp.bfloat16)
    )
    video_value_grad = (
        jnp.einsum("bhlk,blhe->bkhe", video_low, video_d_att, preferred_element_type=jnp.float32)
        .reshape(items_here, video_here, head_width)
        .astype(jnp.bfloat16)
    )
    caption_key_grad = (
        (
            jnp.einsum(
                "bhlk,blhe->bkhe",
                cap_dscores,
                split_heads(cap_queries),
                preferred_element_type=jnp.float32,
            )
            * scale
        )
        .reshape(cap_items, cap_here, head_width)
        .astype(jnp.bfloat16)
    )
    caption_value_grad = (
        jnp.einsum("bhlk,blhe->bkhe", cap_low, cap_d_att, preferred_element_type=jnp.float32)
        .reshape(cap_items, cap_here, head_width)
        .astype(jnp.bfloat16)
    )
    grad_query = jnp.einsum("bld,ble->de", lat_norm, d_queries, preferred_element_type=jnp.float32)
    d_lat_norm = lax.psum(
        jnp.einsum("ble,de->bld", d_queries, query_weight, preferred_element_type=jnp.float32),
        "head",
    )
    d_lat_back, grad_gain_latent = norm_back(lat_float, gain_latent, d_lat_norm)
    latent_grad = d_after + d_lat_back
    grad_key = jnp.einsum(
        "zsg,zsv->gv", video_normed, video_key_grad, preferred_element_type=jnp.float32
    ) + jnp.einsum(
        "zsg,zsv->gv", caption_normed, caption_key_grad, preferred_element_type=jnp.float32
    )
    grad_value = jnp.einsum(
        "zsg,zsv->gv", video_normed, video_value_grad, preferred_element_type=jnp.float32
    ) + jnp.einsum(
        "zsg,zsv->gv", caption_normed, caption_value_grad, preferred_element_type=jnp.float32
    )
    video_term = jnp.einsum(
        "ayt,ot->ayo", video_key_grad, key_matrix, preferred_element_type=jnp.float32
    ) + jnp.einsum(
        "ayt,ot->ayo", video_value_grad, value_matrix, preferred_element_type=jnp.float32
    )
    cap_term = jnp.einsum(
        "ayt,ot->ayo", caption_key_grad, key_matrix, preferred_element_type=jnp.float32
    ) + jnp.einsum(
        "ayt,ot->ayo", caption_value_grad, value_matrix, preferred_element_type=jnp.float32
    )
    d_video_norm, d_cap_norm = lax.psum((video_term, cap_term), "head")
    video_grad, video_gain_part = norm_back(video_float, gain_tokens, d_video_norm)
    caption_grad, cap_gain_part = norm_back(cap_float, gain_tokens, d_cap_norm)
    grad_gain_tokens = video_gain_part + cap_gain_part
    kept_here = jnp.sum(keep)
    (
        grad_query,
        grad_key,
        grad_value,
        grad_out,
        grad_up,
        grad_down,
        grad_gain_latent,
        grad_gain_tokens,
        grad_gain_mlp,
        kept_total,
    ) = lax.psum(
        (
            grad_query,
            grad_key,
            grad_value,
            grad_out,
            grad_up,
            grad_down,
            grad_gain_latent,
            grad_gain_tokens,
            grad_gain_mlp,
            kept_here,
        ),
        ("vid", "txt"),
    )
    kept_count = (kept_total / vid_count).astype(jnp.int32)
    return (
        latents_out,
        latent_grad,
        video_grad,
        caption_grad,
        grad_query,
        grad_key,
        grad_value,
        grad_out,
        grad_up,
        grad_down,
        grad_gain_latent,
        grad_gain_tokens,
        grad_gain_mlp,
        kept_count,
    )


def swap_cores(values):
    return lax.ppermute(values, "vid", [(0, 1), (1, 0)])


def head_shift(values, shift, count):
    return lax.ppermute(values, "head", [(i, (i - shift) % count) for i in range(count)])


def take_block(values, index, size, axis=0):
    return lax.dynamic_slice_in_dim(values, index * size, size, axis)


def head_chunks(part, place, count):
    low = part.astype(BF16)
    others = [
        lax.dynamic_index_in_dim(low, (place - shift) % count, 0, False)
        for shift in range(1, count)
    ]
    return [lax.dynamic_index_in_dim(part, place, 0, False)] + others


def head_exchange(chunks, count):
    return [head_shift(chunks[shift], shift, count) for shift in range(1, count)]


def head_sum(own, received):
    for part in received:
        own = own + part.astype(F32)
    return own.astype(BF16)


def place_head(total, parts, place, count):
    result = jnp.zeros((count,) + total.shape, BF16)
    result = lax.dynamic_update_index_in_dim(result, total, place, 0)
    for shift in range(1, count):
        result = lax.dynamic_update_index_in_dim(
            result, parts[shift - 1], (place + shift) % count, 0
        )
    return result


def gather_head(total, place, count):
    parts = [head_shift(total, shift, count) for shift in range(1, count)]
    return place_head(total, parts, place, count)


def group_steps(count):
    return [(step, [(i, (i - step) % count) for i in range(count)]) for step in range(1, count)]


def reduce_over_cores(rows, core):
    half = rows.shape[0] // 2
    other = swap_cores(take_block(rows, 1 - core, half))
    return take_block(rows, core, half).astype(F32) + other.astype(F32), other


def reduce_over_group(half, place, count):
    part = half.shape[0] // count
    low = half.astype(BF16)
    total = take_block(half, place, part)
    for step, perm in group_steps(count):
        chunk = take_block(low, (place - step) % count, part)
        total = total + lax.ppermute(chunk, "txt", perm).astype(F32)
    return total.astype(BF16)


def gather_places(total, place, count, after):
    part = total.shape[0]
    received = [lax.ppermute(total, "txt", perm) for _, perm in group_steps(count)]
    received[0], after = lax.optimization_barrier((received[0], after))
    mine = jnp.zeros((part * count, total.shape[1]), BF16)
    mine = lax.dynamic_update_slice_in_dim(mine, total, place * part, 0)
    for step in range(1, count):
        mine = lax.dynamic_update_slice_in_dim(
            mine, received[step - 1], (place + step) % count * part, 0
        )
    return mine, after


def gather_cores(mine, core):
    half = mine.shape[0]
    whole = jnp.zeros((2 * half, mine.shape[1]), BF16)
    whole = lax.dynamic_update_slice_in_dim(whole, mine, core * half, 0)
    return lax.dynamic_update_slice_in_dim(whole, swap_cores(mine), (1 - core) * half, 0)


def caption_perm(step, vid_count, txt_count, cores):
    pairs = []
    for v in range(vid_count):
        for t in range(txt_count):
            block = (t + step) % txt_count
            dest_txt = v * (txt_count // vid_count) + block // cores
            dest_vid = block % cores
            pairs.append((v * txt_count + t, dest_vid * txt_count + dest_txt))
    return pairs


PAIR = 128
BACK_COST = 3
F32 = jnp.float32
BF16 = jnp.bfloat16


def dot_nt(a, b):
    return lax.dot_general(a, b, (((1,), (1,)), ((), ())), preferred_element_type=F32)


def dot_nn(a, b):
    return lax.dot_general(a, b, (((1,), (0,)), ((), ())), preferred_element_type=F32)


def dot_tn(a, b):
    return lax.dot_general(a, b, (((0,), (0,)), ((), ())), preferred_element_type=F32)


def square(ref):
    return ref[...].reshape(D, D)


def two_heads(values):
    low = lax.broadcasted_iota(jnp.int32, values.shape, 1) < PAIR // 2
    zero = jnp.zeros_like(values)
    return jnp.concatenate([jnp.where(low, values, zero), jnp.where(low, zero, values)], axis=0)


def from_two_heads(both):
    n = both.shape[1] // 2
    first = lax.broadcasted_iota(jnp.int32, (PAIR, n), 0) < PAIR // 2
    return jnp.where(first, both[:, :n], both[:, n:]).T


def chunk_list(video, cap, size):
    return [(start, size) for start in range(0, video, size)] + [(video, cap)]


def norm_kernel(s_ref, own_ref, other_ref, gain_ref, out_ref):
    gain = gain_ref[...]
    start = 0
    for ref in (own_ref, other_ref):
        def chunk(c, carry, ref=ref, start=start):
            for part in range(2):
                at = pl.multiple_of(c * 128, 128) + 64 * part
                out_ref[pl.ds(start + at, 64), :] = layer_norm(
                    ref[pl.ds(at, 64), :].astype(F32), gain
                ).astype(BF16)
            return carry

        lax.fori_loop(0, ref.shape[0] // 128, chunk, 0)
        start += ref.shape[0]


def cap_mask(cap_ref):
    mask = cap_ref[:, pl.ds(D, PAIR)]
    return jnp.concatenate([mask, mask], axis=1).astype(F32) > 0.5


def forward_kernel(s_ref, tok_ref, cap_ref, gain_ref, lat_ref, gain_lat_ref, wq_ref, wkv_ref, *refs):
    q_ref, k_ref, v_ref, lse_ref, o_ref, s_scr, e_scr, wkv_scr = refs[-8:]
    keys, width = k_ref.shape
    cap = cap_ref.shape[0]
    step = (keys - cap) // 4
    latn = layer_norm(lat_ref[...].astype(F32), gain_lat_ref[...]).astype(BF16)
    queries = dot_nt(latn, wq_ref[...].reshape(width, D)).astype(BF16).astype(F32)
    q_ref[...] = (queries * 0.125).astype(BF16)

    @pl.when(pl.program_id(0) == 0)
    def _():
        wkv_scr[...] = wkv_ref[...].reshape(2 * width, D).T

    def project(rows, tokens):
        both = dot_nn(tokens, wkv_scr[...]).astype(BF16)
        k_ref[rows, :] = both[:, :width]
        v_ref[rows, :] = both[:, width:]

    def project_video(c, carry):
        rows = pl.ds(pl.multiple_of(c * step, 16), step)
        project(rows, tok_ref[rows, :])
        return carry

    lax.fori_loop(0, 4, project_video, 0)
    cap_rows = pl.ds(keys - cap, cap)
    project(cap_rows, layer_norm(cap_ref[:, pl.ds(0, D)].astype(F32), gain_ref[...]).astype(BF16))
    pieces = [pl.ds(start, 64) for start in range(0, keys, 64)]

    def pair(p, carry):
        cols = pl.ds(pl.multiple_of(p * PAIR, PAIR), PAIR)
        q2 = two_heads(q_ref[:, cols])
        s_scr[...] = dot_nt(k_ref[:, cols], q2)
        s_scr[cap_rows, :] = jnp.where(cap_mask(cap_ref), s_scr[cap_rows, :], -1e30)
        peak = s_scr[pieces[0], :]
        for rows in pieces[1:]:
            peak = jnp.maximum(peak, s_scr[rows, :])
        peak = jnp.max(peak, axis=0, keepdims=True)
        total = jnp.zeros((8, q2.shape[0]), F32)
        for rows in pieces:
            e = jnp.exp(s_scr[rows, :] - peak)
            e_scr[rows, :] = e.astype(BF16)
            total = total + jnp.sum(e.reshape(-1, 8, q2.shape[0]), axis=0)
        total = jnp.sum(total, axis=0, keepdims=True)
        out = dot_tn(v_ref[:, cols], e_scr[...])
        o_ref[:, cols] = from_two_heads(out / total)
        lse_ref[pl.ds(p, 1), :] = peak + jnp.log(total)
        return carry

    lax.fori_loop(0, width // PAIR, pair, 0)


def backward_kernel(
    s_ref, q_ref, k_ref, v_ref, lse_ref, o_ref, up_ref, attn_ref, cot_ref, own_ref, other_ref, cap_ref,
    wk_ref, wv_ref, gain_ref, tok_ref, wq_ref, wo_ref, lat_ref, gain_lat_ref, gain_mlp_ref,
    own_out, other_out, cap_out, lat_out, late_ref,
    dq_ref, dk_ref, dv_ref, s_scr, dp_scr, p_scr, ds_scr, up_scr, sums_ref, gain_out,
    datt_ref, after_ref,
):
    item = pl.program_id(0)
    keys = k_ref.shape[0]
    cap = cap_ref.shape[0]
    cap_rows = pl.ds(keys - cap, cap)
    pieces = [pl.ds(start, 64) for start in range(0, keys, 64)]

    @pl.when(item == 0)
    def _():
        gain_out[...] = jnp.zeros_like(gain_out)
        sums_ref[...] = jnp.zeros_like(sums_ref)

    def norm_back(x, up, gain, row):
        center = x - jnp.mean(x, axis=-1, keepdims=True)
        rate = lax.rsqrt(jnp.mean(center * center, axis=-1, keepdims=True) + 1e-05)
        hat = center * rate
        gain_out[pl.ds(8 * row, 8), :] += jnp.sum((up * hat).reshape(-1, 8, D), axis=0)
        scaled = up * gain
        first = jnp.mean(scaled, axis=-1, keepdims=True)
        second = jnp.mean(scaled * hat, axis=-1, keepdims=True)
        return rate * (scaled - first - hat * second)

    keep = (1 - s_ref[4 + item]).astype(F32)
    after_ref[...] = cot_ref[...].astype(F32) + norm_back(
        attn_ref[...], up_ref[...].astype(F32), gain_mlp_ref[...], 2
    )
    d_branch = after_ref[...].astype(BF16)
    datt_ref[...] = (dot_nt(d_branch, square(wo_ref)) * keep).astype(BF16)

    def pair(p, carry):
        cols = pl.ds(pl.multiple_of(p * PAIR, PAIR), PAIR)
        q2 = two_heads(q_ref[:, cols])
        d_att = datt_ref[:, cols]
        d2 = two_heads(d_att)
        prod = (d_att.astype(F32) * o_ref[:, cols]).T
        delta = jnp.concatenate(
            [
                jnp.sum(prod[: PAIR // 2], axis=0, keepdims=True),
                jnp.sum(prod[PAIR // 2 :], axis=0, keepdims=True),
            ],
            axis=1,
        )
        pairs_here = D // PAIR // lse_ref.shape[0]
        lse = lse_ref[p // pairs_here, pl.ds(p % pairs_here, 1), :]
        s_scr[...] = dot_nt(k_ref[:, cols], q2)
        dp_scr[...] = dot_nt(v_ref[:, cols], d2)
        s_scr[cap_rows, :] = jnp.where(cap_mask(cap_ref), s_scr[cap_rows, :], -1e30)
        for rows in pieces:
            probs = jnp.exp(s_scr[rows, :] - lse)
            p_scr[rows, :] = probs.astype(BF16)
            ds_scr[rows, :] = (probs * (dp_scr[rows, :] - delta)).astype(BF16)
        dv_ref[:, cols] = dot_nn(p_scr[...], d2).astype(BF16)
        dk_ref[:, cols] = dot_nn(ds_scr[...], q2).astype(BF16)
        dq = dot_tn(k_ref[:, cols], ds_scr[...])
        dq_ref[:, cols] = (from_two_heads(dq) * 0.125).astype(BF16)
        return carry

    lax.fori_loop(0, D // PAIR, pair, 0)
    gain = gain_ref[...]

    wide = sums_ref.shape[0] // 4
    window = pl.ds(pl.multiple_of(s_ref[2], PAIR), wide)
    video_rows = pl.ds(0, keys - cap)
    cap_norm = layer_norm(cap_ref[:, pl.ds(0, D)].astype(F32), gain).astype(BF16)
    latn = layer_norm(lat_ref[...].astype(F32), gain_lat_ref[...]).astype(BF16)
    sums_ref[pl.ds(0, wide), :] += dot_tn(dq_ref[:, window], latn)
    mixed = (o_ref[:, window] * keep).astype(BF16)
    sums_ref[pl.ds(3 * wide, wide), :] += dot_tn(mixed, after_ref[...].astype(BF16))

    def both(rows):
        return jnp.concatenate([dk_ref[rows, window], dv_ref[rows, window]], axis=1)

    sums_ref[pl.ds(wide, 2 * wide), :] += dot_tn(both(video_rows), tok_ref[...]) + dot_tn(
        both(cap_rows), cap_norm
    )

    half = lat_out.shape[0]
    lat_grad = after_ref[...] + norm_back(
        lat_ref[...].astype(F32), dot_nn(dq_ref[...], square(wq_ref)), gain_lat_ref[...], 1
    )
    lat_out[...] = lat_grad[:half]
    other_out[pl.ds(other_ref.shape[0], half), :] = lat_grad[half:].astype(BF16)

    start = 0
    for ref, out, size in ((own_ref, own_out, 256), (other_ref, other_out, 256), (cap_ref, cap_out, cap)):
        def chunk(c, carry, ref=ref, out=out, size=size, start=start):
            rows = pl.ds(pl.multiple_of(c * size, 16), size)
            key_rows = pl.ds(pl.multiple_of(start + c * size, 16), size)
            up_scr[pl.ds(0, size), :] = dot_nn(dk_ref[key_rows, :], square(wk_ref)) + dot_nn(
                dv_ref[key_rows, :], square(wv_ref)
            )
            for at in range(0, size, 32):
                piece = pl.ds(pl.multiple_of(c * size, 16) + at, 32)
                back = norm_back(
                    ref[piece, pl.ds(0, D)].astype(F32), up_scr[pl.ds(at, 32), :], gain, 0
                )
                out[piece, :] = back.astype(out.dtype)
            return carry

        lax.fori_loop(0, ref.shape[0] // size, chunk, 0)
        start += ref.shape[0]

    @pl.when(item == pl.num_programs(0) - 1)
    def _():
        width = D // 4
        for n in range(4):
            mine = pl.ds(pl.multiple_of(s_ref[3] + n * wide, PAIR // 2), width)
            late_ref[pl.ds(n * width, width), :] = sums_ref[mine, :].astype(BF16)
        gains = [jnp.sum(gain_out[pl.ds(8 * row, 8), :], axis=0, keepdims=True) for row in range(3)]
        kept = 4 - s_ref[4] - s_ref[5] - s_ref[6] - s_ref[7]
        gains.append(jnp.full((1, D), kept.astype(F32)))
        gains = jnp.concatenate(gains + [jnp.zeros((12, D), F32)], axis=0)
        late_ref[pl.ds(4 * width, 16), :] = gains.astype(BF16)
        spare = late_ref.shape[0] - 4 * width - 16
        late_ref[pl.ds(4 * width + 16, spare), :] = jnp.zeros((spare, D), BF16)


def place_kernel(s_ref, video_in, lat_in, video_part, lat_part, video_ref, lat_ref):
    video_ref[...] = video_part[...].astype(F32)

    @pl.when(pl.program_id(1) == 0)
    def _():
        lat_ref[...] = lat_part[...].astype(F32)


def local(
    latents,
    video_tokens,
    caption_tokens,
    caption_len,
    key_mask,
    drop_flags,
    gain_latent,
    gain_tokens,
    gain_mlp,
    query_weight,
    key_matrix,
    value_matrix,
    out_weight,
    up_weight,
    down_weight,
    cotangent,
):
    txt_count = lax.axis_size("txt")
    head_count = lax.axis_size("head")
    core = lax.axis_index("vid")
    place_index = lax.axis_index("txt")
    z = lax.axis_index("head")
    items_here = latents.shape[0]
    own = items_here // 2
    lat_half = latents.shape[1]
    lat_rows = 2 * lat_half
    video_here = video_tokens.shape[1]
    cap_here = caption_tokens.shape[1]
    cap_rows = cap_here * txt_count
    keys_here = 2 * video_here + cap_rows
    head_width = query_weight.shape[1]

    def dot(spec, a, b):
        return jnp.einsum(spec, a, b, preferred_element_type=F32)

    packed = jnp.stack([key_matrix.T, value_matrix.T, query_weight.T, out_weight])
    half = take_block(packed, core, 2)
    up1 = lax.ppermute(half, "head", [(0, 1), (1, 2), (2, 3)])
    down1 = lax.ppermute(half, "head", [(1, 0), (2, 1), (3, 2)])
    near_at = z // 2
    zero = jnp.int32(0)
    own_at = z % 2
    part_shape = (2, 2, 2, head_width, D)

    def place_chunk(whole, chunk, at_core, at_chunk):
        chunk = chunk.reshape((-1, 2, 1) + chunk.shape[-2:])
        return lax.dynamic_update_slice(whole, chunk, (at_core, zero, at_chunk, zero, zero))

    both_own = take_block(jnp.concatenate([latents, cotangent], axis=1), core, own)
    video_other = swap_cores(
        jnp.concatenate(
            [take_block(a, 1 - core, own) for a in (video_tokens, latents, cotangent)], axis=1
        )
    )
    both_other = video_other[:, video_here:]
    lat = jnp.concatenate([both_own[:, :lat_half], both_other[:, :lat_half]], axis=1)
    cot = jnp.concatenate([both_own[:, lat_half:], both_other[:, lat_half:]], axis=1)
    drop_own = take_block(drop_flags, core, own)
    keep = (1 - drop_own).astype(F32)
    window = z * head_width // PAIR * PAIR
    inside = z * head_width - window
    scalars = jnp.concatenate([jnp.stack([core, near_at, window, inside]), drop_own])
    scalars_far = jnp.concatenate([jnp.stack([core, 1 - near_at, window, inside]), drop_own])

    place_slots = place_index * cap_here + jnp.arange(cap_here, dtype=jnp.int32)
    cap_valid = (place_slots[None, :] < caption_len[:, None]) & (key_mask == 1)
    flags = jnp.broadcast_to(cap_valid.astype(BF16)[:, :, None], cap_valid.shape + (PAIR,))
    cap_message = jnp.concatenate([caption_tokens, flags], axis=2)
    cap_parts = []
    for step in range(txt_count):
        block = take_block(cap_message, (place_index + step) % txt_count, own)
        cap_parts.append(
            lax.ppermute(block, ("vid", "txt"), caption_perm(step, 2, txt_count, 2))
        )
    def item_spec(rows, width=D, first=0):
        return pl.BlockSpec((None, rows, width), lambda i, s: (first + i, 0, 0))

    def own_spec(rows, first=0):
        return pl.BlockSpec((None, rows, D), lambda i, s: (s[0] * own + first + i, 0, 0))

    def whole_spec(*shape):
        return pl.BlockSpec(shape, lambda i, s: (0,) * len(shape))

    def weight_spec(m):
        return pl.BlockSpec(
            (2, None, None, 2, head_width, D),
            lambda i, s: (0, m // 2, m % 2, 0, 0, 0),
            pipeline_mode=pl.Buffered(1),
        )

    def part_spec(at_core, first, count):
        return pl.BlockSpec(
            (None, count, 2, head_width, D),
            lambda i, s: (at_core, first, 0, 0, 0),
            pipeline_mode=pl.Buffered(1),
        )

    def half_spec(rows):
        return pl.BlockSpec((None, rows, 2 * head_width), lambda i, s: (i, 0, s[1]))

    row_spec = pl.BlockSpec((1, D), lambda i, s: (0, 0))

    def call(kernel, name, ins, outs, operands, micros, scratch=(), aliases={}, scalars=scalars, grid=own):
        return pl.pallas_call(
            kernel,
            name=name,
            grid_spec=pltpu.PrefetchScalarGridSpec(
                num_scalar_prefetch=1,
                grid=(grid,),
                in_specs=ins,
                out_specs=[spec for spec, _, _ in outs],
                scratch_shapes=list(scratch),
            ),
            out_shape=[jax.ShapeDtypeStruct(shape, dtype) for _, shape, dtype in outs],
            input_output_aliases=aliases,
            cost_estimate=pl.CostEstimate(
                flops=micros * 1100 * 10**6, transcendentals=0, bytes_accessed=micros * 10**6
            ),
            compiler_params=pltpu.CompilerParams(vmem_limit_bytes=56 << 20),
        )(scalars, *operands)

    def item_out(rows, dtype, width=D):
        return (item_spec(rows, width), (own, rows, width), dtype)

    gain_lat_row = gain_latent[None]
    gain_tok_row = gain_tokens[None]
    gain_mlp_row = gain_mlp[None]
    (tok_norm,) = call(
        norm_kernel,
        "token_norm",
        [own_spec(video_here), item_spec(video_here), row_spec],
        [item_out(2 * video_here, BF16)],
        (video_tokens, video_other, gain_tok_row),
        9,
    )
    tok_norm, up1, down1, cap_parts = lax.optimization_barrier((tok_norm, up1, down1, cap_parts))
    cap = jnp.concatenate(cap_parts, axis=1)
    partner = jnp.where(z % 2 == 1, up1, down1)
    near = jnp.zeros(part_shape, BF16)
    near = place_chunk(near, packed.reshape((2, 2) + packed.shape[1:]), zero, own_at)
    near = place_chunk(near, partner, core, 1 - own_at)
    partner_other = swap_cores(partner)
    near = place_chunk(near, partner_other, 1 - core, 1 - own_at)
    up1, down1, half_then, _ = lax.optimization_barrier((up1, down1, half, partner_other))
    ring_up = lax.ppermute(jnp.where(z == 3, half_then, up1), "head", [(1, 2), (2, 3), (3, 0)])
    ring_down = lax.ppermute(jnp.where(z == 0, half_then, down1), "head", [(1, 0), (2, 1), (0, 3)])

    def forward(part, scalars, before=()):
        return call(
            forward_kernel,
            "attention_forward",
            [item_spec(2 * video_here), item_spec(cap_rows, D + PAIR), row_spec]
            + [item_spec(lat_rows), row_spec]
            + [part_spec(1, 0, 1), part_spec(0, 0, 2)]
            + [pl.BlockSpec(memory_space=pl.ANY)] * len(before),
            [
                (half_spec(lat_rows), (own, lat_rows, D), BF16),
                (half_spec(keys_here), (own, keys_here, D), BF16),
                (half_spec(keys_here), (own, keys_here, D), BF16),
                (
                    pl.BlockSpec((None, None, 8, 2 * lat_rows), lambda i, s: (i, s[1], 0, 0)),
                    (own, 2, 8, 2 * lat_rows),
                    F32,
                ),
                (half_spec(lat_rows), (own, lat_rows, D), F32),
            ],
            (tok_norm, cap, gain_tok_row, lat, gain_lat_row, part, part) + tuple(before),
            23,
            [
                pltpu.VMEM((keys_here, 2 * lat_rows), F32),
                pltpu.VMEM((keys_here, 2 * lat_rows), BF16),
                pltpu.VMEM((D, 4 * head_width), BF16),
            ],
            {8 + n: n for n in range(len(before))},
            scalars,
        )

    before = forward(near, scalars)
    before, up1, down1, ring_up, ring_down = lax.optimization_barrier(
        (before, up1, down1, ring_up, ring_down)
    )
    far_low = jnp.where(z == 1, down1, jnp.where(z == 2, ring_up, ring_down))
    far_high = jnp.where(z == 1, ring_down, jnp.where(z == 2, up1, ring_up))
    far_mine = jnp.stack([far_low, far_high], axis=1)
    far = jnp.zeros(part_shape, BF16)
    far = lax.dynamic_update_index_in_dim(far, far_mine, core, 0)
    far = lax.dynamic_update_index_in_dim(far, swap_cores(far_mine), 1 - core, 0)
    def both_halves(near, far):
        whole = jnp.zeros((2,) + near.shape, BF16)
        whole = lax.dynamic_update_index_in_dim(whole, near, near_at, 0)
        return lax.dynamic_update_index_in_dim(whole, far, 1 - near_at, 0)

    queries, keys, values, lse, attended = forward(far, scalars_far, before)
    w_out = both_halves(near[1, 1], far[1, 1]).reshape(D, D)
    lat_float = lat.astype(F32)
    mixed_in = (attended * keep[:, None, None]).astype(BF16)
    after_attn = lat_float + dot("ble,ed->bld", mixed_in, w_out)
    mlp_norm = layer_norm(after_attn, gain_mlp).astype(BF16)

    pre_act = dot("bld,df->blf", mlp_norm, up_weight)
    activ, gelu_pull = jax.vjp(gelu_exact, pre_act)
    activ = activ.astype(BF16)
    d_pre = gelu_pull(dot("bld,fd->blf", cot, down_weight))[0].astype(BF16)
    d_mlp_part = dot("blf,df->bld", d_pre, up_weight)
    d_mlp_part, activ, d_pre = lax.optimization_barrier((d_mlp_part, activ, d_pre))
    chunks = head_chunks(d_mlp_part, z, head_count)
    received = head_exchange(chunks, head_count)
    activ, d_pre, received[0] = lax.optimization_barrier((activ, d_pre, received[0]))
    d_mlp_total = head_sum(chunks[0], received)
    grad_down = dot("blf,bld->fd", activ, cot).astype(BF16)
    grad_up = dot("bld,blf->df", mlp_norm, d_pre).astype(BF16)
    near, far, _ = lax.optimization_barrier((near, far, d_mlp_part))
    weights = both_halves(near, far)
    early = jnp.where(core == 0, grad_up, grad_down).astype(F32)
    early = early + swap_cores(jnp.where(core == 0, grad_down, grad_up)).astype(F32)
    d_mlp_norm = gather_head(d_mlp_total, z, head_count)
    activ, _ = lax.optimization_barrier((activ, d_mlp_total))
    growth = head_chunks(dot("blf,fd->bld", activ, down_weight), z, head_count)
    d_mlp_norm = d_mlp_norm.reshape(after_attn.shape)
    growth, d_mlp_norm, weights, early = lax.optimization_barrier(
        (growth, d_mlp_norm, weights, early.astype(BF16))
    )
    early = lax.psum(early, "txt")
    growth_received = head_exchange(growth, head_count)

    late_size = 4 * head_width + 16
    late_size = late_size + -late_size % (32 * txt_count)
    pair_shape = (keys_here, 2 * lat_rows)
    video_grad, other_back, cap_back, latent_grad, late = call(
        backward_kernel,
        "attention_backward",
        [
            item_spec(lat_rows),
            item_spec(keys_here),
            item_spec(keys_here),
            pl.BlockSpec((None, 2, 8, 2 * lat_rows), lambda i, s: (i, 0, 0, 0)),
            item_spec(lat_rows),
            item_spec(lat_rows),
            item_spec(lat_rows),
            item_spec(lat_rows),
            own_spec(video_here),
            item_spec(video_here),
            item_spec(cap_rows, D + PAIR),
            weight_spec(0),
            weight_spec(1),
            row_spec,
            item_spec(2 * video_here),
            weight_spec(2),
            weight_spec(3),
            item_spec(lat_rows),
            row_spec,
            row_spec,
        ],
        [
            (own_spec(video_here), video_tokens.shape, F32),
            item_out(video_here + lat_half, BF16),
            item_out(cap_rows, BF16),
            (own_spec(lat_half), latents.shape, F32),
            (whole_spec(late_size, D), (late_size, D), BF16),
        ],
        (
            queries, keys, values, lse, attended, d_mlp_norm, after_attn, cot, video_tokens,
            video_other, cap, weights, weights, gain_tok_row, tok_norm, weights, weights, lat,
            gain_lat_row, gain_mlp_row,
        ),
        BACK_COST,
        [
            pltpu.VMEM((lat_rows, D), BF16),
            pltpu.VMEM((keys_here, D), BF16),
            pltpu.VMEM((keys_here, D), BF16),
            pltpu.VMEM(pair_shape, F32),
            pltpu.VMEM(pair_shape, F32),
            pltpu.VMEM(pair_shape, BF16),
            pltpu.VMEM(pair_shape, BF16),
            pltpu.VMEM((256, D), F32),
            pltpu.VMEM((8 * PAIR, D), F32),
            pltpu.VMEM((24, D), F32),
            pltpu.VMEM((lat_rows, D), BF16),
            pltpu.VMEM((lat_rows, D), F32),
        ],
    )
    def place(video_grad, latent_grad, part):
        piece = video_here
        return pl.pallas_call(
            place_kernel,
            name="place_rows",
            grid_spec=pltpu.PrefetchScalarGridSpec(
                num_scalar_prefetch=1,
                grid=(own, 1),
                in_specs=[
                    pl.BlockSpec(memory_space=pl.ANY),
                    pl.BlockSpec(memory_space=pl.ANY),
                    pl.BlockSpec((None, piece, D), lambda i, r, s: (i, r, 0)),
                    pl.BlockSpec((None, lat_half, D), lambda i, r, s: (i, video_here // lat_half, 0)),
                ],
                out_specs=[
                    pl.BlockSpec((None, piece, D), lambda i, r, s: ((1 - s[0]) * own + i, r, 0)),
                    pl.BlockSpec((None, lat_half, D), lambda i, r, s: ((1 - s[0]) * own + i, 0, 0)),
                ],
            ),
            out_shape=[
                jax.ShapeDtypeStruct(video_tokens.shape, F32),
                jax.ShapeDtypeStruct(latents.shape, F32),
            ],
            input_output_aliases={1: 0, 2: 1},
            cost_estimate=pl.CostEstimate(
                flops=6 * 10**9, transcendentals=0, bytes_accessed=10**7
            ),
        )(scalars, video_grad, latent_grad, part, part)

    early, growth_received, late = lax.optimization_barrier((early, growth_received, late))
    late_half, late_swapped = reduce_over_cores(late, core)
    other_back, early, _ = lax.optimization_barrier((other_back, early, late_swapped))
    other_here = swap_cores(other_back)
    growth_received, _ = lax.optimization_barrier((growth_received, late_swapped))
    growth = head_sum(growth[0], growth_received)
    early_other = swap_cores(early)
    late_total = reduce_over_group(late_half, place_index, txt_count)
    late_total, growth, early_other, other_here, cap_back = lax.optimization_barrier(
        (late_total, growth, early_other, other_here, cap_back)
    )
    late, growth = gather_places(late_total, place_index, txt_count, growth)
    growth_parts = [head_shift(growth, shift, head_count) for shift in range(1, head_count)]
    growth_parts[0], cap_back = lax.optimization_barrier((growth_parts[0], cap_back))
    cap_parts = []
    for step in range(txt_count):
        perm = [(b, a) for a, b in caption_perm(step, 2, txt_count, 2)]
        cap_parts.append(
            lax.ppermute(cap_back[:, step * cap_here : (step + 1) * cap_here], ("vid", "txt"), perm)
        )
    video_grad, latent_grad = place(video_grad, latent_grad, other_here)
    late, video_grad, latent_grad, cap_parts, growth_parts = lax.optimization_barrier(
        (late, video_grad, latent_grad, cap_parts, growth_parts)
    )
    growth = place_head(growth, growth_parts, z, head_count)
    late = gather_cores(late, core).astype(F32)
    caption_grad = jnp.zeros((txt_count, own, cap_here, D), F32)
    for step, part in enumerate(cap_parts):
        caption_grad = lax.dynamic_update_index_in_dim(
            caption_grad, part.astype(F32), (place_index + step) % txt_count, 0
        )
    caption_grad = caption_grad.reshape(caption_tokens.shape)
    out_mine = (after_attn + growth.reshape(after_attn.shape).astype(F32)).astype(BF16)
    gains = late[4 * head_width :]

    def give_back(values):
        other = swap_cores(values[:, lat_half:].astype(BF16)).astype(values.dtype)
        whole = jnp.zeros((items_here, lat_half, D), values.dtype)
        whole = lax.dynamic_update_slice_in_dim(whole, values[:, :lat_half], core * own, 0)
        return lax.dynamic_update_slice_in_dim(whole, other, (1 - core) * own, 0)

    latents_out = give_back(out_mine)
    kept_count = gains[3, 0].astype(jnp.int32)
    return (
        latents_out,
        latent_grad,
        video_grad,
        caption_grad,
        late[:head_width].T,
        late[head_width : 2 * head_width].T,
        late[2 * head_width : 3 * head_width].T,
        late[3 * head_width : 4 * head_width],
        jnp.where(core == 0, early, early_other).astype(F32),
        jnp.where(core == 0, early_other, early).astype(F32),
        gains[1],
        gains[0],
        gains[2],
        kept_count,
    )


def fits(mesh):
    shape = mesh.shape
    return shape["vid"] == 2 and shape["txt"] == 4 and shape["head"] == 4


def solution(mesh):
    in_specs = (
        P("txt", "vid", None),
        P("txt", "vid", None),
        P("vid", "txt", None),
        P("vid"),
        P("vid", "txt"),
        P("txt"),
        P(),
        P(),
        P(),
        P(None, "head"),
        P(None, "head"),
        P(None, "head"),
        P("head", None),
        P(None, "head"),
        P("head", None),
        P("txt", "vid", None),
    )
    out_specs = (
        P("txt", "vid", None),
        P("txt", "vid", None),
        P("txt", "vid", None),
        P("vid", "txt", None),
        P(None, "head"),
        P(None, "head"),
        P(None, "head"),
        P("head", None),
        P(None, "head"),
        P("head", None),
        P(),
        P(),
        P(),
        P(),
    )
    return jax.shard_map(local if fits(mesh) else local_general, mesh=mesh, in_specs=in_specs, out_specs=out_specs, check_vma=False)
```

```python
import functools
import math

import jax
import jax.numpy as jnp
from jax import lax
from jax.experimental import pallas as pl
from jax.experimental.pallas import tpu as pltpu
from jax.sharding import PartitionSpec as P

D = 768
HEADS = 12


def combined_all(part, axis, combine):
    gathered = jax.tree.map(lambda a: lax.all_gather(a, axis), part)

    def take(source):
        return jax.tree.map(lambda a: lax.dynamic_index_in_dim(a, source, 0, False), gathered)

    return lax.fori_loop(
        1, lax.axis_size(axis), lambda source, state: combine(state, take(source)), take(0)
    )


def layer_norm(values, gain):
    center = values - jnp.mean(values, axis=-1, keepdims=True)
    spread = jnp.mean(center * center, axis=-1, keepdims=True)
    return center * lax.rsqrt(spread + 1e-05) * gain


def norm_back(values, gain, upstream):
    result, pullback = jax.vjp(layer_norm, values, gain)
    return pullback(upstream)


def gelu_exact(values):
    return jax.nn.gelu(values, approximate=False)


def combine_stats(first, second):
    peak = jnp.maximum(first[0], second[0])
    total = first[1] * jnp.exp(first[0] - peak) + second[1] * jnp.exp(second[0] - peak)
    return (peak, total)


def to_blocks(whole, vid_count, txt_count):
    items, rows, width = whole.shape
    split = whole.reshape(txt_count, items // txt_count, vid_count, rows // vid_count, width)
    return split.transpose(2, 0, 1, 3, 4).reshape(
        vid_count * txt_count, items // txt_count, rows // vid_count, width
    )


def from_blocks(blocked, vid_count, txt_count):
    count, items_here, rows_here, width = blocked.shape
    split = blocked.reshape(vid_count, txt_count, items_here, rows_here, width)
    return split.transpose(1, 2, 0, 3, 4).reshape(
        txt_count * items_here, vid_count * rows_here, width
    )


def place_sum(whole, part, start):
    current = lax.dynamic_slice_in_dim(whole, start, part.shape[0], 0)
    return lax.dynamic_update_slice_in_dim(whole, current + part, start, 0)


def place_stats(peak_all, total_all, peak, total, start):
    old_peak = lax.dynamic_slice_in_dim(peak_all, start, peak.shape[0], 0)
    old_total = lax.dynamic_slice_in_dim(total_all, start, peak.shape[0], 0)
    new_peak, new_total = combine_stats((old_peak, old_total), (peak, total))
    peak_all = lax.dynamic_update_slice_in_dim(peak_all, new_peak, start, 0)
    total_all = lax.dynamic_update_slice_in_dim(total_all, new_total, start, 0)
    return (peak_all, total_all)


def take_rows(whole, start, count):
    return lax.dynamic_slice_in_dim(whole, start, count, 0)


def local_general(
    latents,
    video_tokens,
    caption_tokens,
    caption_len,
    key_mask,
    drop_flags,
    gain_latent,
    gain_tokens,
    gain_mlp,
    query_weight,
    key_matrix,
    value_matrix,
    out_weight,
    up_weight,
    down_weight,
    cotangent,
):
    vid_count = lax.axis_size("vid")
    txt_count = lax.axis_size("txt")
    vid_index = lax.axis_index("vid")
    txt_index = lax.axis_index("txt")
    items_here = latents.shape[0]
    cap_items = caption_tokens.shape[0]
    items_total = items_here * txt_count
    head_width = query_weight.shape[1]
    head_size = D // HEADS
    heads_here = head_width // head_size
    scale = 1.0 / math.sqrt(head_size)
    video_here = video_tokens.shape[1]
    cap_here = caption_tokens.shape[1]
    video_start = txt_index * items_here
    cap_start = vid_index * cap_items
    keep = (1 - drop_flags).astype(jnp.float32)
    slots = txt_index * cap_here + jnp.arange(cap_here, dtype=jnp.int32)
    cap_valid = (slots[None, :] < caption_len[:, None]) & (key_mask == 1)
    cap_mask = cap_valid[:, None, None, :]

    def split_heads(values):
        return values.reshape(values.shape[0], values.shape[1], heads_here, head_size)

    lat_float = latents.astype(jnp.float32)
    lat_norm = layer_norm(lat_float, gain_latent).astype(jnp.bfloat16)
    queries = jnp.einsum(
        "bld,de->ble", lat_norm, query_weight, preferred_element_type=jnp.float32
    ).astype(jnp.bfloat16)
    all_queries = from_blocks(
        lax.all_gather(queries[None], ("vid", "txt"), axis=0, tiled=True), vid_count, txt_count
    )
    lat_total = all_queries.shape[1]
    video_queries = take_rows(all_queries, video_start, items_here)
    cap_queries = take_rows(all_queries, cap_start, cap_items)
    video_float = video_tokens.astype(jnp.float32)
    cap_float = caption_tokens.astype(jnp.float32)
    video_normed = layer_norm(video_float, gain_tokens).astype(jnp.bfloat16)
    caption_normed = layer_norm(cap_float, gain_tokens).astype(jnp.bfloat16)
    video_keys = jnp.einsum(
        "flc,co->flo", video_normed, key_matrix, preferred_element_type=jnp.float32
    ).astype(jnp.bfloat16)
    video_values = jnp.einsum(
        "flc,co->flo", video_normed, value_matrix, preferred_element_type=jnp.float32
    ).astype(jnp.bfloat16)
    cap_keys = jnp.einsum(
        "flc,co->flo", caption_normed, key_matrix, preferred_element_type=jnp.float32
    ).astype(jnp.bfloat16)
    cap_values = jnp.einsum(
        "flc,co->flo", caption_normed, value_matrix, preferred_element_type=jnp.float32
    ).astype(jnp.bfloat16)
    video_scores = (
        jnp.einsum(
            "blhe,bkhe->bhlk",
            split_heads(video_queries),
            split_heads(video_keys),
            preferred_element_type=jnp.float32,
        )
        * scale
    )
    cap_scores = (
        jnp.einsum(
            "blhe,bkhe->bhlk",
            split_heads(cap_queries),
            split_heads(cap_keys),
            preferred_element_type=jnp.float32,
        )
        * scale
    )
    cap_scores = jnp.where(cap_mask, cap_scores, -1e30)
    video_peak = jnp.max(video_scores, axis=-1)
    video_total = jnp.sum(jnp.exp(video_scores - video_peak[..., None]), axis=-1)
    cap_peak = jnp.max(cap_scores, axis=-1)
    cap_total = jnp.sum(
        jnp.where(cap_mask, jnp.exp(cap_scores - cap_peak[..., None]), 0.0), axis=-1
    )
    peak_all = jnp.full((items_total, heads_here, lat_total), -1e30, jnp.float32)
    total_all = jnp.zeros((items_total, heads_here, lat_total), jnp.float32)
    peak_all, total_all = place_stats(peak_all, total_all, video_peak, video_total, video_start)
    peak_all, total_all = place_stats(peak_all, total_all, cap_peak, cap_total, cap_start)
    peak, total = combined_all((peak_all, total_all), ("vid", "txt"), combine_stats)
    video_probs = (
        jnp.exp(video_scores - take_rows(peak, video_start, items_here)[..., None])
        / take_rows(total, video_start, items_here)[..., None]
    )
    cap_probs = jnp.where(
        cap_mask,
        jnp.exp(cap_scores - take_rows(peak, cap_start, cap_items)[..., None])
        / take_rows(total, cap_start, cap_items)[..., None],
        0.0,
    )
    video_low = video_probs.astype(jnp.bfloat16)
    cap_low = cap_probs.astype(jnp.bfloat16)
    video_part = jnp.einsum(
        "bhlk,bkhe->blhe", video_low, split_heads(video_values), preferred_element_type=jnp.float32
    ).reshape(items_here, lat_total, head_width)
    cap_part = jnp.einsum(
        "bhlk,bkhe->blhe", cap_low, split_heads(cap_values), preferred_element_type=jnp.float32
    ).reshape(cap_items, lat_total, head_width)
    value_all = jnp.zeros((items_total, lat_total, head_width), jnp.float32)
    value_all = place_sum(place_sum(value_all, video_part, video_start), cap_part, cap_start)
    attended = lax.psum_scatter(
        to_blocks(value_all, vid_count, txt_count), ("vid", "txt"), scatter_dimension=0, tiled=True
    )[0]
    mixed_in = (attended * keep[:, None, None]).astype(jnp.bfloat16)
    branch = lax.psum(
        jnp.einsum("ble,ed->bld", mixed_in, out_weight, preferred_element_type=jnp.float32), "head"
    )
    after_attn = lat_float + branch
    mlp_norm = layer_norm(after_attn, gain_mlp).astype(jnp.bfloat16)
    pre_act = jnp.einsum("bld,df->blf", mlp_norm, up_weight, preferred_element_type=jnp.float32)
    activ = gelu_exact(pre_act).astype(jnp.bfloat16)
    growth = lax.psum(
        jnp.einsum("blf,fd->bld", activ, down_weight, preferred_element_type=jnp.float32).astype(
            jnp.bfloat16
        ),
        "head",
    ).astype(jnp.float32)
    latents_out = (after_attn + growth).astype(jnp.bfloat16)
    grad_down = jnp.einsum("blf,bld->fd", activ, cotangent, preferred_element_type=jnp.float32)
    d_activ = jnp.einsum("bld,fd->blf", cotangent, down_weight, preferred_element_type=jnp.float32)
    d_pre = jax.vjp(gelu_exact, pre_act)[1](d_activ)[0].astype(jnp.bfloat16)
    grad_up = jnp.einsum("bld,blf->df", mlp_norm, d_pre, preferred_element_type=jnp.float32)
    d_mlp_norm = lax.psum(
        jnp.einsum("blf,df->bld", d_pre, up_weight, preferred_element_type=jnp.float32), "head"
    )
    d_after_norm, grad_gain_mlp = norm_back(after_attn, gain_mlp, d_mlp_norm)
    d_after = cotangent.astype(jnp.float32) + d_after_norm
    d_branch = d_after.astype(jnp.bfloat16)
    grad_out = jnp.einsum("ble,bld->ed", mixed_in, d_branch, preferred_element_type=jnp.float32)
    d_att = (
        jnp.einsum("bld,ed->ble", d_branch, out_weight, preferred_element_type=jnp.float32)
        * keep[:, None, None]
    ).astype(jnp.bfloat16)
    all_d_att = from_blocks(
        lax.all_gather(d_att[None], ("vid", "txt"), axis=0, tiled=True), vid_count, txt_count
    )
    video_d_att = split_heads(take_rows(all_d_att, video_start, items_here))
    cap_d_att = split_heads(take_rows(all_d_att, cap_start, cap_items))
    video_dprobs = jnp.einsum(
        "blhe,bkhe->bhlk",
        video_d_att,
        split_heads(video_values),
        preferred_element_type=jnp.float32,
    )
    cap_dprobs = jnp.einsum(
        "blhe,bkhe->bhlk", cap_d_att, split_heads(cap_values), preferred_element_type=jnp.float32
    )
    delta_all = jnp.zeros((items_total, heads_here, lat_total), jnp.float32)
    delta_all = place_sum(delta_all, jnp.sum(video_probs * video_dprobs, axis=-1), video_start)
    delta_all = place_sum(delta_all, jnp.sum(cap_probs * cap_dprobs, axis=-1), cap_start)
    delta = lax.psum(delta_all, ("vid", "txt"))
    video_dscores = (
        video_probs * (video_dprobs - take_rows(delta, video_start, items_here)[..., None])
    ).astype(jnp.bfloat16)
    cap_dscores = (
        cap_probs * (cap_dprobs - take_rows(delta, cap_start, cap_items)[..., None])
    ).astype(jnp.bfloat16)
    video_dq = (
        jnp.einsum(
            "bhlk,bkhe->blhe",
            video_dscores,
            split_heads(video_keys),
            preferred_element_type=jnp.float32,
        )
        * scale
    ).reshape(items_here, lat_total, head_width)
    cap_dq = (
        jnp.einsum(
            "bhlk,bkhe->blhe",
            cap_dscores,
            split_heads(cap_keys),
            preferred_element_type=jnp.float32,
        )
        * scale
    ).reshape(cap_items, lat_total, head_width)
    query_all = jnp.zeros((items_total, lat_total, head_width), jnp.float32)
    query_all = place_sum(place_sum(query_all, video_dq, video_start), cap_dq, cap_start)
    d_queries = lax.psum_scatter(
        to_blocks(query_all, vid_count, txt_count), ("vid", "txt"), scatter_dimension=0, tiled=True
    )[0].astype(jnp.bfloat16)
    video_key_grad = (
        (
            jnp.einsum(
                "bhlk,blhe->bkhe",
                video_dscores,
                split_heads(video_queries),
                preferred_element_type=jnp.float32,
            )
            * scale
        )
        .reshape(items_here, video_here, head_width)
        .astype(jnp.bfloat16)
    )
    video_value_grad = (
        jnp.einsum("bhlk,blhe->bkhe", video_low, video_d_att, preferred_element_type=jnp.float32)
        .reshape(items_here, video_here, head_width)
        .astype(jnp.bfloat16)
    )
    caption_key_grad = (
        (
            jnp.einsum(
                "bhlk,blhe->bkhe",
                cap_dscores,
                split_heads(cap_queries),
                preferred_element_type=jnp.float32,
            )
            * scale
        )
        .reshape(cap_items, cap_here, head_width)
        .astype(jnp.bfloat16)
    )
    caption_value_grad = (
        jnp.einsum("bhlk,blhe->bkhe", cap_low, cap_d_att, preferred_element_type=jnp.float32)
        .reshape(cap_items, cap_here, head_width)
        .astype(jnp.bfloat16)
    )
    grad_query = jnp.einsum("bld,ble->de", lat_norm, d_queries, preferred_element_type=jnp.float32)
    d_lat_norm = lax.psum(
        jnp.einsum("ble,de->bld", d_queries, query_weight, preferred_element_type=jnp.float32),
        "head",
    )
    d_lat_back, grad_gain_latent = norm_back(lat_float, gain_latent, d_lat_norm)
    latent_grad = d_after + d_lat_back
    grad_key = jnp.einsum(
        "zsg,zsv->gv", video_normed, video_key_grad, preferred_element_type=jnp.float32
    ) + jnp.einsum(
        "zsg,zsv->gv", caption_normed, caption_key_grad, preferred_element_type=jnp.float32
    )
    grad_value = jnp.einsum(
        "zsg,zsv->gv", video_normed, video_value_grad, preferred_element_type=jnp.float32
    ) + jnp.einsum(
        "zsg,zsv->gv", caption_normed, caption_value_grad, preferred_element_type=jnp.float32
    )
    video_term = jnp.einsum(
        "ayt,ot->ayo", video_key_grad, key_matrix, preferred_element_type=jnp.float32
    ) + jnp.einsum(
        "ayt,ot->ayo", video_value_grad, value_matrix, preferred_element_type=jnp.float32
    )
    cap_term = jnp.einsum(
        "ayt,ot->ayo", caption_key_grad, key_matrix, preferred_element_type=jnp.float32
    ) + jnp.einsum(
        "ayt,ot->ayo", caption_value_grad, value_matrix, preferred_element_type=jnp.float32
    )
    d_video_norm, d_cap_norm = lax.psum((video_term, cap_term), "head")
    video_grad, video_gain_part = norm_back(video_float, gain_tokens, d_video_norm)
    caption_grad, cap_gain_part = norm_back(cap_float, gain_tokens, d_cap_norm)
    grad_gain_tokens = video_gain_part + cap_gain_part
    kept_here = jnp.sum(keep)
    (
        grad_query,
        grad_key,
        grad_value,
        grad_out,
        grad_up,
        grad_down,
        grad_gain_latent,
        grad_gain_tokens,
        grad_gain_mlp,
        kept_total,
    ) = lax.psum(
        (
            grad_query,
            grad_key,
            grad_value,
            grad_out,
            grad_up,
            grad_down,
            grad_gain_latent,
            grad_gain_tokens,
            grad_gain_mlp,
            kept_here,
        ),
        ("vid", "txt"),
    )
    kept_count = (kept_total / vid_count).astype(jnp.int32)
    return (
        latents_out,
        latent_grad,
        video_grad,
        caption_grad,
        grad_query,
        grad_key,
        grad_value,
        grad_out,
        grad_up,
        grad_down,
        grad_gain_latent,
        grad_gain_tokens,
        grad_gain_mlp,
        kept_count,
    )


def swap_cores(values):
    return lax.ppermute(values, "vid", [(0, 1), (1, 0)])


def head_shift(values, shift, count):
    return lax.ppermute(values, "head", [(i, (i - shift) % count) for i in range(count)])


def take_block(values, index, size, axis=0):
    return lax.dynamic_slice_in_dim(values, index * size, size, axis)


def head_chunks(part, place, count):
    low = part.astype(BF16)
    others = [
        lax.dynamic_index_in_dim(low, (place - shift) % count, 0, False)
        for shift in range(1, count)
    ]
    return [lax.dynamic_index_in_dim(part, place, 0, False)] + others


def head_exchange(chunks, count):
    return [head_shift(chunks[shift], shift, count) for shift in range(1, count)]


def head_sum(own, received):
    for part in received:
        own = own + part.astype(F32)
    return own.astype(BF16)


def gather_head(total, place, count):
    result = jnp.zeros((count,) + total.shape, BF16)
    result = lax.dynamic_update_index_in_dim(result, total, place, 0)
    for shift in range(1, count):
        result = lax.dynamic_update_index_in_dim(
            result, head_shift(total, shift, count), (place + shift) % count, 0
        )
    return result


def group_steps(count):
    return [(step, [(i, (i - step) % count) for i in range(count)]) for step in range(1, count)]


def reduce_over_cores(rows, core):
    half = rows.shape[0] // 2
    other = swap_cores(take_block(rows, 1 - core, half))
    return take_block(rows, core, half).astype(F32) + other.astype(F32), other


def reduce_over_group(half, place, count):
    part = half.shape[0] // count
    low = half.astype(BF16)
    total = take_block(half, place, part)
    for step, perm in group_steps(count):
        chunk = take_block(low, (place - step) % count, part)
        total = total + lax.ppermute(chunk, "txt", perm).astype(F32)
    return total.astype(BF16)


def gather_places(total, place, count):
    part = total.shape[0]
    mine = jnp.zeros((part * count, total.shape[1]), BF16)
    mine = lax.dynamic_update_slice_in_dim(mine, total, place * part, 0)
    for step, perm in group_steps(count):
        mine = lax.dynamic_update_slice_in_dim(
            mine, lax.ppermute(total, "txt", perm), (place + step) % count * part, 0
        )
    return mine


def gather_cores(mine, core):
    half = mine.shape[0]
    whole = jnp.zeros((2 * half, mine.shape[1]), BF16)
    whole = lax.dynamic_update_slice_in_dim(whole, mine, core * half, 0)
    return lax.dynamic_update_slice_in_dim(whole, swap_cores(mine), (1 - core) * half, 0)


def caption_perm(step, vid_count, txt_count, cores):
    pairs = []
    for v in range(vid_count):
        for t in range(txt_count):
            block = (t + step) % txt_count
            dest_txt = v * (txt_count // vid_count) + block // cores
            dest_vid = block % cores
            pairs.append((v * txt_count + t, dest_vid * txt_count + dest_txt))
    return pairs


PAIR = 128
BACK_COST = 3
F32 = jnp.float32
BF16 = jnp.bfloat16


def dot_nt(a, b):
    return lax.dot_general(a, b, (((1,), (1,)), ((), ())), preferred_element_type=F32)


def dot_nn(a, b):
    return lax.dot_general(a, b, (((1,), (0,)), ((), ())), preferred_element_type=F32)


def dot_tn(a, b):
    return lax.dot_general(a, b, (((0,), (0,)), ((), ())), preferred_element_type=F32)


def square(ref):
    return ref[...].reshape(D, D)


def two_heads(values):
    low = lax.broadcasted_iota(jnp.int32, values.shape, 1) < PAIR // 2
    zero = jnp.zeros_like(values)
    return jnp.concatenate([jnp.where(low, values, zero), jnp.where(low, zero, values)], axis=0)


def from_two_heads(both):
    n = both.shape[1] // 2
    first = lax.broadcasted_iota(jnp.int32, (PAIR, n), 0) < PAIR // 2
    return jnp.where(first, both[:, :n], both[:, n:]).T


def chunk_list(video, cap, size):
    return [(start, size) for start in range(0, video, size)] + [(video, cap)]


def norm_kernel(s_ref, own_ref, other_ref, gain_ref, out_ref):
    gain = gain_ref[...]
    start = 0
    for ref in (own_ref, other_ref):
        def chunk(c, carry, ref=ref, start=start):
            for part in range(2):
                at = pl.multiple_of(c * 128, 128) + 64 * part
                out_ref[pl.ds(start + at, 64), :] = layer_norm(
                    ref[pl.ds(at, 64), :].astype(F32), gain
                ).astype(BF16)
            return carry

        lax.fori_loop(0, ref.shape[0] // 128, chunk, 0)
        start += ref.shape[0]


def cap_mask(cap_ref):
    mask = cap_ref[:, pl.ds(D, PAIR)]
    return jnp.concatenate([mask, mask], axis=1).astype(F32) > 0.5


def forward_kernel(s_ref, tok_ref, cap_ref, gain_ref, lat_ref, gain_lat_ref, wq_ref, wkv_ref, *refs):
    q_ref, k_ref, v_ref, lse_ref, o_ref, s_scr, e_scr, wkv_scr = refs[-8:]
    keys, width = k_ref.shape
    cap = cap_ref.shape[0]
    step = (keys - cap) // 4
    latn = layer_norm(lat_ref[...].astype(F32), gain_lat_ref[...]).astype(BF16)
    queries = dot_nt(latn, wq_ref[...].reshape(width, D)).astype(BF16).astype(F32)
    q_ref[...] = (queries * 0.125).astype(BF16)

    @pl.when(pl.program_id(0) == 0)
    def _():
        wkv_scr[...] = wkv_ref[...].reshape(2 * width, D).T

    def project(rows, tokens):
        both = dot_nn(tokens, wkv_scr[...]).astype(BF16)
        k_ref[rows, :] = both[:, :width]
        v_ref[rows, :] = both[:, width:]

    def project_video(c, carry):
        rows = pl.ds(pl.multiple_of(c * step, 16), step)
        project(rows, tok_ref[rows, :])
        return carry

    lax.fori_loop(0, 4, project_video, 0)
    cap_rows = pl.ds(keys - cap, cap)
    project(cap_rows, layer_norm(cap_ref[:, pl.ds(0, D)].astype(F32), gain_ref[...]).astype(BF16))
    pieces = [pl.ds(start, 64) for start in range(0, keys, 64)]

    def pair(p, carry):
        cols = pl.ds(pl.multiple_of(p * PAIR, PAIR), PAIR)
        q2 = two_heads(q_ref[:, cols])
        s_scr[...] = dot_nt(k_ref[:, cols], q2)
        s_scr[cap_rows, :] = jnp.where(cap_mask(cap_ref), s_scr[cap_rows, :], -1e30)
        peak = s_scr[pieces[0], :]
        for rows in pieces[1:]:
            peak = jnp.maximum(peak, s_scr[rows, :])
        peak = jnp.max(peak, axis=0, keepdims=True)
        total = jnp.zeros((8, q2.shape[0]), F32)
        for rows in pieces:
            e = jnp.exp(s_scr[rows, :] - peak)
            e_scr[rows, :] = e.astype(BF16)
            total = total + jnp.sum(e.reshape(-1, 8, q2.shape[0]), axis=0)
        total = jnp.sum(total, axis=0, keepdims=True)
        out = dot_tn(v_ref[:, cols], e_scr[...])
        o_ref[:, cols] = from_two_heads(out / total)
        lse_ref[pl.ds(p, 1), :] = peak + jnp.log(total)
        return carry

    lax.fori_loop(0, width // PAIR, pair, 0)


def backward_kernel(
    s_ref, q_ref, k_ref, v_ref, lse_ref, o_ref, up_ref, attn_ref, cot_ref, own_ref, other_ref, cap_ref,
    wk_ref, wv_ref, gain_ref, tok_ref, wq_ref, wo_ref, lat_ref, gain_lat_ref, gain_mlp_ref,
    own_out, other_out, cap_out, lat_out, late_ref,
    dq_ref, dk_ref, dv_ref, s_scr, dp_scr, p_scr, ds_scr, up_scr, sums_ref, gain_out,
    datt_ref, after_ref,
):
    item = pl.program_id(0)
    keys = k_ref.shape[0]
    cap = cap_ref.shape[0]
    cap_rows = pl.ds(keys - cap, cap)
    pieces = [pl.ds(start, 64) for start in range(0, keys, 64)]

    @pl.when(item == 0)
    def _():
        gain_out[...] = jnp.zeros_like(gain_out)
        sums_ref[...] = jnp.zeros_like(sums_ref)

    def norm_back(x, up, gain, row):
        center = x - jnp.mean(x, axis=-1, keepdims=True)
        rate = lax.rsqrt(jnp.mean(center * center, axis=-1, keepdims=True) + 1e-05)
        hat = center * rate
        gain_out[pl.ds(8 * row, 8), :] += jnp.sum((up * hat).reshape(-1, 8, D), axis=0)
        scaled = up * gain
        first = jnp.mean(scaled, axis=-1, keepdims=True)
        second = jnp.mean(scaled * hat, axis=-1, keepdims=True)
        return rate * (scaled - first - hat * second)

    keep = (1 - s_ref[4 + item]).astype(F32)
    after_ref[...] = cot_ref[...].astype(F32) + norm_back(
        attn_ref[...], up_ref[...].astype(F32), gain_mlp_ref[...], 2
    )
    d_branch = after_ref[...].astype(BF16)
    datt_ref[...] = (dot_nt(d_branch, square(wo_ref)) * keep).astype(BF16)

    def pair(p, carry):
        cols = pl.ds(pl.multiple_of(p * PAIR, PAIR), PAIR)
        q2 = two_heads(q_ref[:, cols])
        d_att = datt_ref[:, cols]
        d2 = two_heads(d_att)
        prod = (d_att.astype(F32) * o_ref[:, cols]).T
        delta = jnp.concatenate(
            [
                jnp.sum(prod[: PAIR // 2], axis=0, keepdims=True),
                jnp.sum(prod[PAIR // 2 :], axis=0, keepdims=True),
            ],
            axis=1,
        )
        pairs_here = D // PAIR // lse_ref.shape[0]
        lse = lse_ref[p // pairs_here, pl.ds(p % pairs_here, 1), :]
        s_scr[...] = dot_nt(k_ref[:, cols], q2)
        dp_scr[...] = dot_nt(v_ref[:, cols], d2)
        s_scr[cap_rows, :] = jnp.where(cap_mask(cap_ref), s_scr[cap_rows, :], -1e30)
        for rows in pieces:
            probs = jnp.exp(s_scr[rows, :] - lse)
            p_scr[rows, :] = probs.astype(BF16)
            ds_scr[rows, :] = (probs * (dp_scr[rows, :] - delta)).astype(BF16)
        dv_ref[:, cols] = dot_nn(p_scr[...], d2).astype(BF16)
        dk_ref[:, cols] = dot_nn(ds_scr[...], q2).astype(BF16)
        dq = dot_tn(k_ref[:, cols], ds_scr[...])
        dq_ref[:, cols] = (from_two_heads(dq) * 0.125).astype(BF16)
        return carry

    lax.fori_loop(0, D // PAIR, pair, 0)
    gain = gain_ref[...]

    wide = sums_ref.shape[0] // 4
    window = pl.ds(pl.multiple_of(s_ref[2], PAIR), wide)
    video_rows = pl.ds(0, keys - cap)
    cap_norm = layer_norm(cap_ref[:, pl.ds(0, D)].astype(F32), gain).astype(BF16)
    latn = layer_norm(lat_ref[...].astype(F32), gain_lat_ref[...]).astype(BF16)
    sums_ref[pl.ds(0, wide), :] += dot_tn(dq_ref[:, window], latn)
    mixed = (o_ref[:, window] * keep).astype(BF16)
    sums_ref[pl.ds(3 * wide, wide), :] += dot_tn(mixed, after_ref[...].astype(BF16))

    def both(rows):
        return jnp.concatenate([dk_ref[rows, window], dv_ref[rows, window]], axis=1)

    sums_ref[pl.ds(wide, 2 * wide), :] += dot_tn(both(video_rows), tok_ref[...]) + dot_tn(
        both(cap_rows), cap_norm
    )

    half = lat_out.shape[0]
    lat_grad = after_ref[...] + norm_back(
        lat_ref[...].astype(F32), dot_nn(dq_ref[...], square(wq_ref)), gain_lat_ref[...], 1
    )
    lat_out[...] = lat_grad[:half]
    other_out[pl.ds(other_ref.shape[0], half), :] = lat_grad[half:].astype(BF16)

    start = 0
    for ref, out, size in ((own_ref, own_out, 256), (other_ref, other_out, 256), (cap_ref, cap_out, cap)):
        def chunk(c, carry, ref=ref, out=out, size=size, start=start):
            rows = pl.ds(pl.multiple_of(c * size, 16), size)
            key_rows = pl.ds(pl.multiple_of(start + c * size, 16), size)
            up_scr[pl.ds(0, size), :] = dot_nn(dk_ref[key_rows, :], square(wk_ref)) + dot_nn(
                dv_ref[key_rows, :], square(wv_ref)
            )
            for at in range(0, size, 32):
                piece = pl.ds(pl.multiple_of(c * size, 16) + at, 32)
                back = norm_back(
                    ref[piece, pl.ds(0, D)].astype(F32), up_scr[pl.ds(at, 32), :], gain, 0
                )
                out[piece, :] = back.astype(out.dtype)
            return carry

        lax.fori_loop(0, ref.shape[0] // size, chunk, 0)
        start += ref.shape[0]

    @pl.when(item == pl.num_programs(0) - 1)
    def _():
        width = D // 4
        for n in range(4):
            mine = pl.ds(pl.multiple_of(s_ref[3] + n * wide, PAIR // 2), width)
            late_ref[pl.ds(n * width, width), :] = sums_ref[mine, :].astype(BF16)
        gains = [jnp.sum(gain_out[pl.ds(8 * row, 8), :], axis=0, keepdims=True) for row in range(3)]
        kept = 4 - s_ref[4] - s_ref[5] - s_ref[6] - s_ref[7]
        gains.append(jnp.full((1, D), kept.astype(F32)))
        gains = jnp.concatenate(gains + [jnp.zeros((12, D), F32)], axis=0)
        late_ref[pl.ds(4 * width, 16), :] = gains.astype(BF16)
        spare = late_ref.shape[0] - 4 * width - 16
        late_ref[pl.ds(4 * width + 16, spare), :] = jnp.zeros((spare, D), BF16)


def place_kernel(s_ref, video_in, lat_in, video_part, lat_part, video_ref, lat_ref):
    video_ref[...] = video_part[...].astype(F32)

    @pl.when(pl.program_id(1) == 0)
    def _():
        lat_ref[...] = lat_part[...].astype(F32)


def local(
    latents,
    video_tokens,
    caption_tokens,
    caption_len,
    key_mask,
    drop_flags,
    gain_latent,
    gain_tokens,
    gain_mlp,
    query_weight,
    key_matrix,
    value_matrix,
    out_weight,
    up_weight,
    down_weight,
    cotangent,
):
    txt_count = lax.axis_size("txt")
    head_count = lax.axis_size("head")
    core = lax.axis_index("vid")
    place_index = lax.axis_index("txt")
    z = lax.axis_index("head")
    items_here = latents.shape[0]
    own = items_here // 2
    lat_half = latents.shape[1]
    lat_rows = 2 * lat_half
    video_here = video_tokens.shape[1]
    cap_here = caption_tokens.shape[1]
    cap_rows = cap_here * txt_count
    keys_here = 2 * video_here + cap_rows
    head_width = query_weight.shape[1]

    def dot(spec, a, b):
        return jnp.einsum(spec, a, b, preferred_element_type=F32)

    packed = jnp.stack([key_matrix.T, value_matrix.T, query_weight.T, out_weight])
    half = take_block(packed, core, 2)
    up1 = lax.ppermute(half, "head", [(0, 1), (1, 2), (2, 3)])
    down1 = lax.ppermute(half, "head", [(1, 0), (2, 1), (3, 2)])
    near_at = z // 2
    zero = jnp.int32(0)
    own_at = z % 2
    part_shape = (2, 2, 2, head_width, D)

    def place_chunk(whole, chunk, at_core, at_chunk):
        chunk = chunk.reshape((-1, 2, 1) + chunk.shape[-2:])
        return lax.dynamic_update_slice(whole, chunk, (at_core, zero, at_chunk, zero, zero))

    both_own = take_block(jnp.concatenate([latents, cotangent], axis=1), core, own)
    video_other = swap_cores(
        jnp.concatenate(
            [take_block(a, 1 - core, own) for a in (video_tokens, latents, cotangent)], axis=1
        )
    )
    both_other = video_other[:, video_here:]
    lat = jnp.concatenate([both_own[:, :lat_half], both_other[:, :lat_half]], axis=1)
    cot = jnp.concatenate([both_own[:, lat_half:], both_other[:, lat_half:]], axis=1)
    drop_own = take_block(drop_flags, core, own)
    keep = (1 - drop_own).astype(F32)
    window = z * head_width // PAIR * PAIR
    inside = z * head_width - window
    scalars = jnp.concatenate([jnp.stack([core, near_at, window, inside]), drop_own])
    scalars_far = jnp.concatenate([jnp.stack([core, 1 - near_at, window, inside]), drop_own])

    place_slots = place_index * cap_here + jnp.arange(cap_here, dtype=jnp.int32)
    cap_valid = (place_slots[None, :] < caption_len[:, None]) & (key_mask == 1)
    flags = jnp.broadcast_to(cap_valid.astype(BF16)[:, :, None], cap_valid.shape + (PAIR,))
    cap_message = jnp.concatenate([caption_tokens, flags], axis=2)
    def send_captions(message, steps):
        return [
            lax.ppermute(
                take_block(message, (place_index + step) % txt_count, own),
                ("vid", "txt"),
                caption_perm(step, 2, txt_count, 2),
            )
            for step in steps
        ]

    cap_parts = send_captions(cap_message, range(2))

    def item_spec(rows, width=D, first=0):
        return pl.BlockSpec((None, rows, width), lambda i, s: (first + i, 0, 0))

    def own_spec(rows, first=0):
        return pl.BlockSpec((None, rows, D), lambda i, s: (s[0] * own + first + i, 0, 0))

    def whole_spec(*shape):
        return pl.BlockSpec(shape, lambda i, s: (0,) * len(shape))

    def weight_spec(m):
        return pl.BlockSpec(
            (2, None, None, 2, head_width, D),
            lambda i, s: (0, m // 2, m % 2, 0, 0, 0),
            pipeline_mode=pl.Buffered(1),
        )

    def part_spec(at_core, first, count):
        return pl.BlockSpec(
            (None, count, 2, head_width, D),
            lambda i, s: (at_core, first, 0, 0, 0),
            pipeline_mode=pl.Buffered(1),
        )

    def half_spec(rows):
        return pl.BlockSpec((None, rows, 2 * head_width), lambda i, s: (i, 0, s[1]))

    row_spec = pl.BlockSpec((1, D), lambda i, s: (0, 0))

    def call(kernel, name, ins, outs, operands, micros, scratch=(), aliases={}, scalars=scalars, grid=own):
        return pl.pallas_call(
            kernel,
            name=name,
            grid_spec=pltpu.PrefetchScalarGridSpec(
                num_scalar_prefetch=1,
                grid=(grid,),
                in_specs=ins,
                out_specs=[spec for spec, _, _ in outs],
                scratch_shapes=list(scratch),
            ),
            out_shape=[jax.ShapeDtypeStruct(shape, dtype) for _, shape, dtype in outs],
            input_output_aliases=aliases,
            cost_estimate=pl.CostEstimate(
                flops=micros * 1100 * 10**6, transcendentals=0, bytes_accessed=micros * 10**6
            ),
            compiler_params=pltpu.CompilerParams(vmem_limit_bytes=56 << 20),
        )(scalars, *operands)

    def item_out(rows, dtype, width=D):
        return (item_spec(rows, width), (own, rows, width), dtype)

    gain_lat_row = gain_latent[None]
    gain_tok_row = gain_tokens[None]
    gain_mlp_row = gain_mlp[None]
    (tok_norm,) = call(
        norm_kernel,
        "token_norm",
        [own_spec(video_here), item_spec(video_here), row_spec],
        [item_out(2 * video_here, BF16)],
        (video_tokens, video_other, gain_tok_row),
        9,
    )
    tok_norm, up1, down1, cap_message = lax.optimization_barrier((tok_norm, up1, down1, cap_message))
    cap_parts = cap_parts + send_captions(cap_message, range(2, txt_count))
    cap = jnp.concatenate(cap_parts, axis=1)
    partner = jnp.where(z % 2 == 1, up1, down1)
    near = jnp.zeros(part_shape, BF16)
    near = place_chunk(near, packed.reshape((2, 2) + packed.shape[1:]), zero, own_at)
    near = place_chunk(near, partner, core, 1 - own_at)
    partner_other = swap_cores(partner)
    near = place_chunk(near, partner_other, 1 - core, 1 - own_at)
    up1, down1, half_then, _ = lax.optimization_barrier((up1, down1, half, partner_other))
    ring_up = lax.ppermute(jnp.where(z == 3, half_then, up1), "head", [(1, 2), (2, 3), (3, 0)])
    ring_down = lax.ppermute(jnp.where(z == 0, half_then, down1), "head", [(1, 0), (2, 1), (0, 3)])

    def forward(part, scalars, before=()):
        return call(
            forward_kernel,
            "attention_forward",
            [item_spec(2 * video_here), item_spec(cap_rows, D + PAIR), row_spec]
            + [item_spec(lat_rows), row_spec]
            + [part_spec(1, 0, 1), part_spec(0, 0, 2)]
            + [pl.BlockSpec(memory_space=pl.ANY)] * len(before),
            [
                (half_spec(lat_rows), (own, lat_rows, D), BF16),
                (half_spec(keys_here), (own, keys_here, D), BF16),
                (half_spec(keys_here), (own, keys_here, D), BF16),
                (
                    pl.BlockSpec((None, None, 8, 2 * lat_rows), lambda i, s: (i, s[1], 0, 0)),
                    (own, 2, 8, 2 * lat_rows),
                    F32,
                ),
                (half_spec(lat_rows), (own, lat_rows, D), F32),
            ],
            (tok_norm, cap, gain_tok_row, lat, gain_lat_row, part, part) + tuple(before),
            23,
            [
                pltpu.VMEM((keys_here, 2 * lat_rows), F32),
                pltpu.VMEM((keys_here, 2 * lat_rows), BF16),
                pltpu.VMEM((D, 4 * head_width), BF16),
            ],
            {8 + n: n for n in range(len(before))},
            scalars,
        )

    before = forward(near, scalars)
    before, up1, down1, ring_up, ring_down = lax.optimization_barrier(
        (before, up1, down1, ring_up, ring_down)
    )
    far_low = jnp.where(z == 1, down1, jnp.where(z == 2, ring_up, ring_down))
    far_high = jnp.where(z == 1, ring_down, jnp.where(z == 2, up1, ring_up))
    far_mine = jnp.stack([far_low, far_high], axis=1)
    far = jnp.zeros(part_shape, BF16)
    far = lax.dynamic_update_index_in_dim(far, far_mine, core, 0)
    far = lax.dynamic_update_index_in_dim(far, swap_cores(far_mine), 1 - core, 0)
    def both_halves(near, far):
        whole = jnp.zeros((2,) + near.shape, BF16)
        whole = lax.dynamic_update_index_in_dim(whole, near, near_at, 0)
        return lax.dynamic_update_index_in_dim(whole, far, 1 - near_at, 0)

    queries, keys, values, lse, attended = forward(far, scalars_far, before)
    w_out = both_halves(near[1, 1], far[1, 1]).reshape(D, D)
    lat_float = lat.astype(F32)
    mixed_in = (attended * keep[:, None, None]).astype(BF16)
    after_attn = lat_float + dot("ble,ed->bld", mixed_in, w_out)
    mlp_norm = layer_norm(after_attn, gain_mlp).astype(BF16)

    pre_act = dot("bld,df->blf", mlp_norm, up_weight)
    activ, gelu_pull = jax.vjp(gelu_exact, pre_act)
    activ = activ.astype(BF16)
    d_pre = gelu_pull(dot("bld,fd->blf", cot, down_weight))[0].astype(BF16)
    d_mlp_part = dot("blf,df->bld", d_pre, up_weight)
    d_mlp_part, activ, d_pre = lax.optimization_barrier((d_mlp_part, activ, d_pre))
    chunks = head_chunks(d_mlp_part, z, head_count)
    received = head_exchange(chunks, head_count)
    activ, d_pre, received[0] = lax.optimization_barrier((activ, d_pre, received[0]))
    d_mlp_total = head_sum(chunks[0], received)
    grad_down = dot("blf,bld->fd", activ, cot).astype(BF16)
    grad_up = dot("bld,blf->df", mlp_norm, d_pre).astype(BF16)
    near, far, _ = lax.optimization_barrier((near, far, d_mlp_part))
    weights = both_halves(near, far)
    early = jnp.where(core == 0, grad_up, grad_down).astype(F32)
    early = early + swap_cores(jnp.where(core == 0, grad_down, grad_up)).astype(F32)
    d_mlp_norm = gather_head(d_mlp_total, z, head_count)
    activ, _ = lax.optimization_barrier((activ, d_mlp_total))
    growth = head_chunks(dot("blf,fd->bld", activ, down_weight), z, head_count)
    d_mlp_norm = d_mlp_norm.reshape(after_attn.shape)
    growth, d_mlp_norm, weights, early = lax.optimization_barrier(
        (growth, d_mlp_norm, weights, early.astype(BF16))
    )
    early = lax.psum(early, "txt")
    growth_received = head_exchange(growth, head_count)

    late_size = 4 * head_width + 16
    late_size = late_size + -late_size % (32 * txt_count)
    pair_shape = (keys_here, 2 * lat_rows)
    video_grad, other_back, cap_back, latent_grad, late = call(
        backward_kernel,
        "attention_backward",
        [
            item_spec(lat_rows),
            item_spec(keys_here),
            item_spec(keys_here),
            pl.BlockSpec((None, 2, 8, 2 * lat_rows), lambda i, s: (i, 0, 0, 0)),
            item_spec(lat_rows),
            item_spec(lat_rows),
            item_spec(lat_rows),
            item_spec(lat_rows),
            own_spec(video_here),
            item_spec(video_here),
            item_spec(cap_rows, D + PAIR),
            weight_spec(0),
            weight_spec(1),
            row_spec,
            item_spec(2 * video_here),
            weight_spec(2),
            weight_spec(3),
            item_spec(lat_rows),
            row_spec,
            row_spec,
        ],
        [
            (own_spec(video_here), video_tokens.shape, F32),
            item_out(video_here + lat_half, BF16),
            item_out(cap_rows, BF16),
            (own_spec(lat_half), latents.shape, F32),
            (whole_spec(late_size, D), (late_size, D), BF16),
        ],
        (
            queries, keys, values, lse, attended, d_mlp_norm, after_attn, cot, video_tokens,
            video_other, cap, weights, weights, gain_tok_row, tok_norm, weights, weights, lat,
            gain_lat_row, gain_mlp_row,
        ),
        BACK_COST,
        [
            pltpu.VMEM((lat_rows, D), BF16),
            pltpu.VMEM((keys_here, D), BF16),
            pltpu.VMEM((keys_here, D), BF16),
            pltpu.VMEM(pair_shape, F32),
            pltpu.VMEM(pair_shape, F32),
            pltpu.VMEM(pair_shape, BF16),
            pltpu.VMEM(pair_shape, BF16),
            pltpu.VMEM((256, D), F32),
            pltpu.VMEM((8 * PAIR, D), F32),
            pltpu.VMEM((24, D), F32),
            pltpu.VMEM((lat_rows, D), BF16),
            pltpu.VMEM((lat_rows, D), F32),
        ],
    )
    def place(video_grad, latent_grad, part):
        piece = video_here
        return pl.pallas_call(
            place_kernel,
            name="place_rows",
            grid_spec=pltpu.PrefetchScalarGridSpec(
                num_scalar_prefetch=1,
                grid=(own, 1),
                in_specs=[
                    pl.BlockSpec(memory_space=pl.ANY),
                    pl.BlockSpec(memory_space=pl.ANY),
                    pl.BlockSpec((None, piece, D), lambda i, r, s: (i, r, 0)),
                    pl.BlockSpec((None, lat_half, D), lambda i, r, s: (i, video_here // lat_half, 0)),
                ],
                out_specs=[
                    pl.BlockSpec((None, piece, D), lambda i, r, s: ((1 - s[0]) * own + i, r, 0)),
                    pl.BlockSpec((None, lat_half, D), lambda i, r, s: ((1 - s[0]) * own + i, 0, 0)),
                ],
            ),
            out_shape=[
                jax.ShapeDtypeStruct(video_tokens.shape, F32),
                jax.ShapeDtypeStruct(latents.shape, F32),
            ],
            input_output_aliases={1: 0, 2: 1},
            cost_estimate=pl.CostEstimate(
                flops=6 * 10**9, transcendentals=0, bytes_accessed=10**7
            ),
        )(scalars, video_grad, latent_grad, part, part)

    early, growth_received, late = lax.optimization_barrier((early, growth_received, late))
    late_half, late_swapped = reduce_over_cores(late, core)
    other_back, early, _ = lax.optimization_barrier((other_back, early, late_swapped))
    other_here = swap_cores(other_back)
    growth_received, _ = lax.optimization_barrier((growth_received, late_swapped))
    growth = head_sum(growth[0], growth_received)
    early_other = swap_cores(early)
    late_total = reduce_over_group(late_half, place_index, txt_count)
    late_total, growth, early_other, other_here, cap_back = lax.optimization_barrier(
        (late_total, growth, early_other, other_here, cap_back)
    )
    growth = gather_head(growth, z, head_count)
    cap_parts = []
    for step in range(txt_count):
        perm = [(b, a) for a, b in caption_perm(step, 2, txt_count, 2)]
        cap_parts.append(
            lax.ppermute(cap_back[:, step * cap_here : (step + 1) * cap_here], ("vid", "txt"), perm)
        )
    late = gather_places(late_total, place_index, txt_count)
    video_grad, latent_grad = place(video_grad, latent_grad, other_here)
    late, video_grad, latent_grad, cap_parts, growth = lax.optimization_barrier(
        (late, video_grad, latent_grad, cap_parts, growth)
    )
    late = gather_cores(late, core).astype(F32)
    caption_grad = jnp.zeros((txt_count, own, cap_here, D), F32)
    for step, part in enumerate(cap_parts):
        caption_grad = lax.dynamic_update_index_in_dim(
            caption_grad, part.astype(F32), (place_index + step) % txt_count, 0
        )
    caption_grad = caption_grad.reshape(caption_tokens.shape)
    out_mine = (after_attn + growth.reshape(after_attn.shape).astype(F32)).astype(BF16)
    gains = late[4 * head_width :]

    def give_back(values):
        other = swap_cores(values[:, lat_half:].astype(BF16)).astype(values.dtype)
        whole = jnp.zeros((items_here, lat_half, D), values.dtype)
        whole = lax.dynamic_update_slice_in_dim(whole, values[:, :lat_half], core * own, 0)
        return lax.dynamic_update_slice_in_dim(whole, other, (1 - core) * own, 0)

    latents_out = give_back(out_mine)
    kept_count = gains[3, 0].astype(jnp.int32)
    return (
        latents_out,
        latent_grad,
        video_grad,
        caption_grad,
        late[:head_width].T,
        late[head_width : 2 * head_width].T,
        late[2 * head_width : 3 * head_width].T,
        late[3 * head_width : 4 * head_width],
        jnp.where(core == 0, early, early_other).astype(F32),
        jnp.where(core == 0, early_other, early).astype(F32),
        gains[1],
        gains[0],
        gains[2],
        kept_count,
    )


def fits(mesh):
    shape = mesh.shape
    return shape["vid"] == 2 and shape["txt"] == 4 and shape["head"] == 4


def solution(mesh):
    in_specs = (
        P("txt", "vid", None),
        P("txt", "vid", None),
        P("vid", "txt", None),
        P("vid"),
        P("vid", "txt"),
        P("txt"),
        P(),
        P(),
        P(),
        P(None, "head"),
        P(None, "head"),
        P(None, "head"),
        P("head", None),
        P(None, "head"),
        P("head", None),
        P("txt", "vid", None),
    )
    out_specs = (
        P("txt", "vid", None),
        P("txt", "vid", None),
        P("txt", "vid", None),
        P("vid", "txt", None),
        P(None, "head"),
        P(None, "head"),
        P(None, "head"),
        P("head", None),
        P(None, "head"),
        P("head", None),
        P(),
        P(),
        P(),
        P(),
    )
    return jax.shard_map(local if fits(mesh) else local_general, mesh=mesh, in_specs=in_specs, out_specs=out_specs, check_vma=False)
```

```python
import functools
import math

import jax
import jax.numpy as jnp
from jax import lax
from jax.experimental import pallas as pl
from jax.experimental.pallas import tpu as pltpu
from jax.sharding import PartitionSpec as P

D = 768
HEADS = 12


def combined_all(part, axis, combine):
    gathered = jax.tree.map(lambda a: lax.all_gather(a, axis), part)

    def take(source):
        return jax.tree.map(lambda a: lax.dynamic_index_in_dim(a, source, 0, False), gathered)

    return lax.fori_loop(
        1, lax.axis_size(axis), lambda source, state: combine(state, take(source)), take(0)
    )


def layer_norm(values, gain):
    center = values - jnp.mean(values, axis=-1, keepdims=True)
    spread = jnp.mean(center * center, axis=-1, keepdims=True)
    return center * lax.rsqrt(spread + 1e-05) * gain


def norm_back(values, gain, upstream):
    result, pullback = jax.vjp(layer_norm, values, gain)
    return pullback(upstream)


def gelu_exact(values):
    return jax.nn.gelu(values, approximate=False)


def combine_stats(first, second):
    peak = jnp.maximum(first[0], second[0])
    total = first[1] * jnp.exp(first[0] - peak) + second[1] * jnp.exp(second[0] - peak)
    return (peak, total)


def to_blocks(whole, vid_count, txt_count):
    items, rows, width = whole.shape
    split = whole.reshape(txt_count, items // txt_count, vid_count, rows // vid_count, width)
    return split.transpose(2, 0, 1, 3, 4).reshape(
        vid_count * txt_count, items // txt_count, rows // vid_count, width
    )


def from_blocks(blocked, vid_count, txt_count):
    count, items_here, rows_here, width = blocked.shape
    split = blocked.reshape(vid_count, txt_count, items_here, rows_here, width)
    return split.transpose(1, 2, 0, 3, 4).reshape(
        txt_count * items_here, vid_count * rows_here, width
    )


def place_sum(whole, part, start):
    current = lax.dynamic_slice_in_dim(whole, start, part.shape[0], 0)
    return lax.dynamic_update_slice_in_dim(whole, current + part, start, 0)


def place_stats(peak_all, total_all, peak, total, start):
    old_peak = lax.dynamic_slice_in_dim(peak_all, start, peak.shape[0], 0)
    old_total = lax.dynamic_slice_in_dim(total_all, start, peak.shape[0], 0)
    new_peak, new_total = combine_stats((old_peak, old_total), (peak, total))
    peak_all = lax.dynamic_update_slice_in_dim(peak_all, new_peak, start, 0)
    total_all = lax.dynamic_update_slice_in_dim(total_all, new_total, start, 0)
    return (peak_all, total_all)


def take_rows(whole, start, count):
    return lax.dynamic_slice_in_dim(whole, start, count, 0)


def local_general(
    latents,
    video_tokens,
    caption_tokens,
    caption_len,
    key_mask,
    drop_flags,
    gain_latent,
    gain_tokens,
    gain_mlp,
    query_weight,
    key_matrix,
    value_matrix,
    out_weight,
    up_weight,
    down_weight,
    cotangent,
):
    vid_count = lax.axis_size("vid")
    txt_count = lax.axis_size("txt")
    vid_index = lax.axis_index("vid")
    txt_index = lax.axis_index("txt")
    items_here = latents.shape[0]
    cap_items = caption_tokens.shape[0]
    items_total = items_here * txt_count
    head_width = query_weight.shape[1]
    head_size = D // HEADS
    heads_here = head_width // head_size
    scale = 1.0 / math.sqrt(head_size)
    video_here = video_tokens.shape[1]
    cap_here = caption_tokens.shape[1]
    video_start = txt_index * items_here
    cap_start = vid_index * cap_items
    keep = (1 - drop_flags).astype(jnp.float32)
    slots = txt_index * cap_here + jnp.arange(cap_here, dtype=jnp.int32)
    cap_valid = (slots[None, :] < caption_len[:, None]) & (key_mask == 1)
    cap_mask = cap_valid[:, None, None, :]

    def split_heads(values):
        return values.reshape(values.shape[0], values.shape[1], heads_here, head_size)

    lat_float = latents.astype(jnp.float32)
    lat_norm = layer_norm(lat_float, gain_latent).astype(jnp.bfloat16)
    queries = jnp.einsum(
        "bld,de->ble", lat_norm, query_weight, preferred_element_type=jnp.float32
    ).astype(jnp.bfloat16)
    all_queries = from_blocks(
        lax.all_gather(queries[None], ("vid", "txt"), axis=0, tiled=True), vid_count, txt_count
    )
    lat_total = all_queries.shape[1]
    video_queries = take_rows(all_queries, video_start, items_here)
    cap_queries = take_rows(all_queries, cap_start, cap_items)
    video_float = video_tokens.astype(jnp.float32)
    cap_float = caption_tokens.astype(jnp.float32)
    video_normed = layer_norm(video_float, gain_tokens).astype(jnp.bfloat16)
    caption_normed = layer_norm(cap_float, gain_tokens).astype(jnp.bfloat16)
    video_keys = jnp.einsum(
        "flc,co->flo", video_normed, key_matrix, preferred_element_type=jnp.float32
    ).astype(jnp.bfloat16)
    video_values = jnp.einsum(
        "flc,co->flo", video_normed, value_matrix, preferred_element_type=jnp.float32
    ).astype(jnp.bfloat16)
    cap_keys = jnp.einsum(
        "flc,co->flo", caption_normed, key_matrix, preferred_element_type=jnp.float32
    ).astype(jnp.bfloat16)
    cap_values = jnp.einsum(
        "flc,co->flo", caption_normed, value_matrix, preferred_element_type=jnp.float32
    ).astype(jnp.bfloat16)
    video_scores = (
        jnp.einsum(
            "blhe,bkhe->bhlk",
            split_heads(video_queries),
            split_heads(video_keys),
            preferred_element_type=jnp.float32,
        )
        * scale
    )
    cap_scores = (
        jnp.einsum(
            "blhe,bkhe->bhlk",
            split_heads(cap_queries),
            split_heads(cap_keys),
            preferred_element_type=jnp.float32,
        )
        * scale
    )
    cap_scores = jnp.where(cap_mask, cap_scores, -1e30)
    video_peak = jnp.max(video_scores, axis=-1)
    video_total = jnp.sum(jnp.exp(video_scores - video_peak[..., None]), axis=-1)
    cap_peak = jnp.max(cap_scores, axis=-1)
    cap_total = jnp.sum(
        jnp.where(cap_mask, jnp.exp(cap_scores - cap_peak[..., None]), 0.0), axis=-1
    )
    peak_all = jnp.full((items_total, heads_here, lat_total), -1e30, jnp.float32)
    total_all = jnp.zeros((items_total, heads_here, lat_total), jnp.float32)
    peak_all, total_all = place_stats(peak_all, total_all, video_peak, video_total, video_start)
    peak_all, total_all = place_stats(peak_all, total_all, cap_peak, cap_total, cap_start)
    peak, total = combined_all((peak_all, total_all), ("vid", "txt"), combine_stats)
    video_probs = (
        jnp.exp(video_scores - take_rows(peak, video_start, items_here)[..., None])
        / take_rows(total, video_start, items_here)[..., None]
    )
    cap_probs = jnp.where(
        cap_mask,
        jnp.exp(cap_scores - take_rows(peak, cap_start, cap_items)[..., None])
        / take_rows(total, cap_start, cap_items)[..., None],
        0.0,
    )
    video_low = video_probs.astype(jnp.bfloat16)
    cap_low = cap_probs.astype(jnp.bfloat16)
    video_part = jnp.einsum(
        "bhlk,bkhe->blhe", video_low, split_heads(video_values), preferred_element_type=jnp.float32
    ).reshape(items_here, lat_total, head_width)
    cap_part = jnp.einsum(
        "bhlk,bkhe->blhe", cap_low, split_heads(cap_values), preferred_element_type=jnp.float32
    ).reshape(cap_items, lat_total, head_width)
    value_all = jnp.zeros((items_total, lat_total, head_width), jnp.float32)
    value_all = place_sum(place_sum(value_all, video_part, video_start), cap_part, cap_start)
    attended = lax.psum_scatter(
        to_blocks(value_all, vid_count, txt_count), ("vid", "txt"), scatter_dimension=0, tiled=True
    )[0]
    mixed_in = (attended * keep[:, None, None]).astype(jnp.bfloat16)
    branch = lax.psum(
        jnp.einsum("ble,ed->bld", mixed_in, out_weight, preferred_element_type=jnp.float32), "head"
    )
    after_attn = lat_float + branch
    mlp_norm = layer_norm(after_attn, gain_mlp).astype(jnp.bfloat16)
    pre_act = jnp.einsum("bld,df->blf", mlp_norm, up_weight, preferred_element_type=jnp.float32)
    activ = gelu_exact(pre_act).astype(jnp.bfloat16)
    growth = lax.psum(
        jnp.einsum("blf,fd->bld", activ, down_weight, preferred_element_type=jnp.float32).astype(
            jnp.bfloat16
        ),
        "head",
    ).astype(jnp.float32)
    latents_out = (after_attn + growth).astype(jnp.bfloat16)
    grad_down = jnp.einsum("blf,bld->fd", activ, cotangent, preferred_element_type=jnp.float32)
    d_activ = jnp.einsum("bld,fd->blf", cotangent, down_weight, preferred_element_type=jnp.float32)
    d_pre = jax.vjp(gelu_exact, pre_act)[1](d_activ)[0].astype(jnp.bfloat16)
    grad_up = jnp.einsum("bld,blf->df", mlp_norm, d_pre, preferred_element_type=jnp.float32)
    d_mlp_norm = lax.psum(
        jnp.einsum("blf,df->bld", d_pre, up_weight, preferred_element_type=jnp.float32), "head"
    )
    d_after_norm, grad_gain_mlp = norm_back(after_attn, gain_mlp, d_mlp_norm)
    d_after = cotangent.astype(jnp.float32) + d_after_norm
    d_branch = d_after.astype(jnp.bfloat16)
    grad_out = jnp.einsum("ble,bld->ed", mixed_in, d_branch, preferred_element_type=jnp.float32)
    d_att = (
        jnp.einsum("bld,ed->ble", d_branch, out_weight, preferred_element_type=jnp.float32)
        * keep[:, None, None]
    ).astype(jnp.bfloat16)
    all_d_att = from_blocks(
        lax.all_gather(d_att[None], ("vid", "txt"), axis=0, tiled=True), vid_count, txt_count
    )
    video_d_att = split_heads(take_rows(all_d_att, video_start, items_here))
    cap_d_att = split_heads(take_rows(all_d_att, cap_start, cap_items))
    video_dprobs = jnp.einsum(
        "blhe,bkhe->bhlk",
        video_d_att,
        split_heads(video_values),
        preferred_element_type=jnp.float32,
    )
    cap_dprobs = jnp.einsum(
        "blhe,bkhe->bhlk", cap_d_att, split_heads(cap_values), preferred_element_type=jnp.float32
    )
    delta_all = jnp.zeros((items_total, heads_here, lat_total), jnp.float32)
    delta_all = place_sum(delta_all, jnp.sum(video_probs * video_dprobs, axis=-1), video_start)
    delta_all = place_sum(delta_all, jnp.sum(cap_probs * cap_dprobs, axis=-1), cap_start)
    delta = lax.psum(delta_all, ("vid", "txt"))
    video_dscores = (
        video_probs * (video_dprobs - take_rows(delta, video_start, items_here)[..., None])
    ).astype(jnp.bfloat16)
    cap_dscores = (
        cap_probs * (cap_dprobs - take_rows(delta, cap_start, cap_items)[..., None])
    ).astype(jnp.bfloat16)
    video_dq = (
        jnp.einsum(
            "bhlk,bkhe->blhe",
            video_dscores,
            split_heads(video_keys),
            preferred_element_type=jnp.float32,
        )
        * scale
    ).reshape(items_here, lat_total, head_width)
    cap_dq = (
        jnp.einsum(
            "bhlk,bkhe->blhe",
            cap_dscores,
            split_heads(cap_keys),
            preferred_element_type=jnp.float32,
        )
        * scale
    ).reshape(cap_items, lat_total, head_width)
    query_all = jnp.zeros((items_total, lat_total, head_width), jnp.float32)
    query_all = place_sum(place_sum(query_all, video_dq, video_start), cap_dq, cap_start)
    d_queries = lax.psum_scatter(
        to_blocks(query_all, vid_count, txt_count), ("vid", "txt"), scatter_dimension=0, tiled=True
    )[0].astype(jnp.bfloat16)
    video_key_grad = (
        (
            jnp.einsum(
                "bhlk,blhe->bkhe",
                video_dscores,
                split_heads(video_queries),
                preferred_element_type=jnp.float32,
            )
            * scale
        )
        .reshape(items_here, video_here, head_width)
        .astype(jnp.bfloat16)
    )
    video_value_grad = (
        jnp.einsum("bhlk,blhe->bkhe", video_low, video_d_att, preferred_element_type=jnp.float32)
        .reshape(items_here, video_here, head_width)
        .astype(jnp.bfloat16)
    )
    caption_key_grad = (
        (
            jnp.einsum(
                "bhlk,blhe->bkhe",
                cap_dscores,
                split_heads(cap_queries),
                preferred_element_type=jnp.float32,
            )
            * scale
        )
        .reshape(cap_items, cap_here, head_width)
        .astype(jnp.bfloat16)
    )
    caption_value_grad = (
        jnp.einsum("bhlk,blhe->bkhe", cap_low, cap_d_att, preferred_element_type=jnp.float32)
        .reshape(cap_items, cap_here, head_width)
        .astype(jnp.bfloat16)
    )
    grad_query = jnp.einsum("bld,ble->de", lat_norm, d_queries, preferred_element_type=jnp.float32)
    d_lat_norm = lax.psum(
        jnp.einsum("ble,de->bld", d_queries, query_weight, preferred_element_type=jnp.float32),
        "head",
    )
    d_lat_back, grad_gain_latent = norm_back(lat_float, gain_latent, d_lat_norm)
    latent_grad = d_after + d_lat_back
    grad_key = jnp.einsum(
        "zsg,zsv->gv", video_normed, video_key_grad, preferred_element_type=jnp.float32
    ) + jnp.einsum(
        "zsg,zsv->gv", caption_normed, caption_key_grad, preferred_element_type=jnp.float32
    )
    grad_value = jnp.einsum(
        "zsg,zsv->gv", video_normed, video_value_grad, preferred_element_type=jnp.float32
    ) + jnp.einsum(
        "zsg,zsv->gv", caption_normed, caption_value_grad, preferred_element_type=jnp.float32
    )
    video_term = jnp.einsum(
        "ayt,ot->ayo", video_key_grad, key_matrix, preferred_element_type=jnp.float32
    ) + jnp.einsum(
        "ayt,ot->ayo", video_value_grad, value_matrix, preferred_element_type=jnp.float32
    )
    cap_term = jnp.einsum(
        "ayt,ot->ayo", caption_key_grad, key_matrix, preferred_element_type=jnp.float32
    ) + jnp.einsum(
        "ayt,ot->ayo", caption_value_grad, value_matrix, preferred_element_type=jnp.float32
    )
    d_video_norm, d_cap_norm = lax.psum((video_term, cap_term), "head")
    video_grad, video_gain_part = norm_back(video_float, gain_tokens, d_video_norm)
    caption_grad, cap_gain_part = norm_back(cap_float, gain_tokens, d_cap_norm)
    grad_gain_tokens = video_gain_part + cap_gain_part
    kept_here = jnp.sum(keep)
    (
        grad_query,
        grad_key,
        grad_value,
        grad_out,
        grad_up,
        grad_down,
        grad_gain_latent,
        grad_gain_tokens,
        grad_gain_mlp,
        kept_total,
    ) = lax.psum(
        (
            grad_query,
            grad_key,
            grad_value,
            grad_out,
            grad_up,
            grad_down,
            grad_gain_latent,
            grad_gain_tokens,
            grad_gain_mlp,
            kept_here,
        ),
        ("vid", "txt"),
    )
    kept_count = (kept_total / vid_count).astype(jnp.int32)
    return (
        latents_out,
        latent_grad,
        video_grad,
        caption_grad,
        grad_query,
        grad_key,
        grad_value,
        grad_out,
        grad_up,
        grad_down,
        grad_gain_latent,
        grad_gain_tokens,
        grad_gain_mlp,
        kept_count,
    )


def swap_cores(values):
    return lax.ppermute(values, "vid", [(0, 1), (1, 0)])


def head_shift(values, shift, count):
    return lax.ppermute(values, "head", [(i, (i - shift) % count) for i in range(count)])


def take_block(values, index, size, axis=0):
    return lax.dynamic_slice_in_dim(values, index * size, size, axis)


def head_chunks(part, place, count):
    low = part.astype(BF16)
    others = [
        lax.dynamic_index_in_dim(low, (place - shift) % count, 0, False)
        for shift in range(1, count)
    ]
    return [lax.dynamic_index_in_dim(part, place, 0, False)] + others


def head_exchange(chunks, count):
    return [head_shift(chunks[shift], shift, count) for shift in range(1, count)]


def head_sum(own, received):
    for part in received:
        own = own + part.astype(F32)
    return own.astype(BF16)


def gather_head(total, place, count):
    result = jnp.zeros((count,) + total.shape, BF16)
    result = lax.dynamic_update_index_in_dim(result, total, place, 0)
    for shift in range(1, count):
        result = lax.dynamic_update_index_in_dim(
            result, head_shift(total, shift, count), (place + shift) % count, 0
        )
    return result


def group_steps(count):
    return [(step, [(i, (i - step) % count) for i in range(count)]) for step in range(1, count)]


def reduce_over_cores(rows, core):
    half = rows.shape[0] // 2
    other = swap_cores(take_block(rows, 1 - core, half))
    return take_block(rows, core, half).astype(F32) + other.astype(F32), other


def reduce_over_group(half, place, count):
    part = half.shape[0] // count
    low = half.astype(BF16)
    total = take_block(half, place, part)
    for step, perm in group_steps(count):
        chunk = take_block(low, (place - step) % count, part)
        total = total + lax.ppermute(chunk, "txt", perm).astype(F32)
    return total.astype(BF16)


def gather_places(total, place, count):
    part = total.shape[0]
    mine = jnp.zeros((part * count, total.shape[1]), BF16)
    mine = lax.dynamic_update_slice_in_dim(mine, total, place * part, 0)
    for step, perm in group_steps(count):
        mine = lax.dynamic_update_slice_in_dim(
            mine, lax.ppermute(total, "txt", perm), (place + step) % count * part, 0
        )
    return mine


def gather_cores(mine, core):
    half = mine.shape[0]
    whole = jnp.zeros((2 * half, mine.shape[1]), BF16)
    whole = lax.dynamic_update_slice_in_dim(whole, mine, core * half, 0)
    return lax.dynamic_update_slice_in_dim(whole, swap_cores(mine), (1 - core) * half, 0)


def caption_perm(step, vid_count, txt_count, cores):
    pairs = []
    for v in range(vid_count):
        for t in range(txt_count):
            block = (t + step) % txt_count
            dest_txt = v * (txt_count // vid_count) + block // cores
            dest_vid = block % cores
            pairs.append((v * txt_count + t, dest_vid * txt_count + dest_txt))
    return pairs


PAIR = 128
BACK_COST = 3
F32 = jnp.float32
BF16 = jnp.bfloat16


def dot_nt(a, b):
    return lax.dot_general(a, b, (((1,), (1,)), ((), ())), preferred_element_type=F32)


def dot_nn(a, b):
    return lax.dot_general(a, b, (((1,), (0,)), ((), ())), preferred_element_type=F32)


def dot_tn(a, b):
    return lax.dot_general(a, b, (((0,), (0,)), ((), ())), preferred_element_type=F32)


def square(ref):
    return ref[...].reshape(D, D)


def two_heads(values):
    low = lax.broadcasted_iota(jnp.int32, values.shape, 1) < PAIR // 2
    zero = jnp.zeros_like(values)
    return jnp.concatenate([jnp.where(low, values, zero), jnp.where(low, zero, values)], axis=0)


def from_two_heads(both):
    n = both.shape[1] // 2
    first = lax.broadcasted_iota(jnp.int32, (PAIR, n), 0) < PAIR // 2
    return jnp.where(first, both[:, :n], both[:, n:]).T


def chunk_list(video, cap, size):
    return [(start, size) for start in range(0, video, size)] + [(video, cap)]


def norm_kernel(s_ref, own_ref, other_ref, gain_ref, out_ref):
    gain = gain_ref[...]
    start = 0
    for ref in (own_ref, other_ref):
        def chunk(c, carry, ref=ref, start=start):
            for part in range(2):
                at = pl.multiple_of(c * 128, 128) + 64 * part
                out_ref[pl.ds(start + at, 64), :] = layer_norm(
                    ref[pl.ds(at, 64), :].astype(F32), gain
                ).astype(BF16)
            return carry

        lax.fori_loop(0, ref.shape[0] // 128, chunk, 0)
        start += ref.shape[0]


def cap_mask(cap_ref):
    mask = cap_ref[:, pl.ds(D, PAIR)]
    return jnp.concatenate([mask, mask], axis=1).astype(F32) > 0.5


def forward_kernel(s_ref, tok_ref, cap_ref, gain_ref, lat_ref, gain_lat_ref, wq_ref, wkv_ref, *refs):
    q_ref, k_ref, v_ref, lse_ref, o_ref, s_scr, e_scr, wkv_scr = refs[-8:]
    keys, width = k_ref.shape
    cap = cap_ref.shape[0]
    step = (keys - cap) // 4
    latn = layer_norm(lat_ref[...].astype(F32), gain_lat_ref[...]).astype(BF16)
    queries = dot_nt(latn, wq_ref[...].reshape(width, D)).astype(BF16).astype(F32)
    q_ref[...] = (queries * 0.125).astype(BF16)

    @pl.when(pl.program_id(0) == 0)
    def _():
        wkv_scr[...] = wkv_ref[...].reshape(2 * width, D).T

    def project(rows, tokens):
        both = dot_nn(tokens, wkv_scr[...]).astype(BF16)
        k_ref[rows, :] = both[:, :width]
        v_ref[rows, :] = both[:, width:]

    def project_video(c, carry):
        rows = pl.ds(pl.multiple_of(c * step, 16), step)
        project(rows, tok_ref[rows, :])
        return carry

    lax.fori_loop(0, 4, project_video, 0)
    cap_rows = pl.ds(keys - cap, cap)
    project(cap_rows, layer_norm(cap_ref[:, pl.ds(0, D)].astype(F32), gain_ref[...]).astype(BF16))
    pieces = [pl.ds(start, 64) for start in range(0, keys, 64)]

    def pair(p, carry):
        cols = pl.ds(pl.multiple_of(p * PAIR, PAIR), PAIR)
        q2 = two_heads(q_ref[:, cols])
        s_scr[...] = dot_nt(k_ref[:, cols], q2)
        s_scr[cap_rows, :] = jnp.where(cap_mask(cap_ref), s_scr[cap_rows, :], -1e30)
        peak = s_scr[pieces[0], :]
        for rows in pieces[1:]:
            peak = jnp.maximum(peak, s_scr[rows, :])
        peak = jnp.max(peak, axis=0, keepdims=True)
        total = jnp.zeros((8, q2.shape[0]), F32)
        for rows in pieces:
            e = jnp.exp(s_scr[rows, :] - peak)
            e_scr[rows, :] = e.astype(BF16)
            total = total + jnp.sum(e.reshape(-1, 8, q2.shape[0]), axis=0)
        total = jnp.sum(total, axis=0, keepdims=True)
        out = dot_tn(v_ref[:, cols], e_scr[...])
        o_ref[:, cols] = from_two_heads(out / total)
        lse_ref[pl.ds(p, 1), :] = peak + jnp.log(total)
        return carry

    lax.fori_loop(0, width // PAIR, pair, 0)


def backward_kernel(
    s_ref, q_ref, k_ref, v_ref, lse_ref, o_ref, up_ref, attn_ref, cot_ref, own_ref, other_ref, cap_ref,
    wk_ref, wv_ref, gain_ref, tok_ref, wq_ref, wo_ref, lat_ref, gain_lat_ref, gain_mlp_ref,
    own_out, other_out, cap_out, lat_out, late_ref,
    dq_ref, dk_ref, dv_ref, s_scr, dp_scr, p_scr, ds_scr, up_scr, sums_ref, gain_out,
    datt_ref, after_ref,
):
    item = pl.program_id(0)
    keys = k_ref.shape[0]
    cap = cap_ref.shape[0]
    cap_rows = pl.ds(keys - cap, cap)
    pieces = [pl.ds(start, 64) for start in range(0, keys, 64)]

    @pl.when(item == 0)
    def _():
        gain_out[...] = jnp.zeros_like(gain_out)
        sums_ref[...] = jnp.zeros_like(sums_ref)

    def norm_back(x, up, gain, row):
        center = x - jnp.mean(x, axis=-1, keepdims=True)
        rate = lax.rsqrt(jnp.mean(center * center, axis=-1, keepdims=True) + 1e-05)
        hat = center * rate
        gain_out[pl.ds(8 * row, 8), :] += jnp.sum((up * hat).reshape(-1, 8, D), axis=0)
        scaled = up * gain
        first = jnp.mean(scaled, axis=-1, keepdims=True)
        second = jnp.mean(scaled * hat, axis=-1, keepdims=True)
        return rate * (scaled - first - hat * second)

    keep = (1 - s_ref[4 + item]).astype(F32)
    after_ref[...] = cot_ref[...].astype(F32) + norm_back(
        attn_ref[...], up_ref[...].astype(F32), gain_mlp_ref[...], 2
    )
    d_branch = after_ref[...].astype(BF16)
    datt_ref[...] = (dot_nt(d_branch, square(wo_ref)) * keep).astype(BF16)

    def pair(p, carry):
        cols = pl.ds(pl.multiple_of(p * PAIR, PAIR), PAIR)
        q2 = two_heads(q_ref[:, cols])
        d_att = datt_ref[:, cols]
        d2 = two_heads(d_att)
        prod = (d_att.astype(F32) * o_ref[:, cols]).T
        delta = jnp.concatenate(
            [
                jnp.sum(prod[: PAIR // 2], axis=0, keepdims=True),
                jnp.sum(prod[PAIR // 2 :], axis=0, keepdims=True),
            ],
            axis=1,
        )
        pairs_here = D // PAIR // lse_ref.shape[0]
        lse = lse_ref[p // pairs_here, pl.ds(p % pairs_here, 1), :]
        s_scr[...] = dot_nt(k_ref[:, cols], q2)
        dp_scr[...] = dot_nt(v_ref[:, cols], d2)
        s_scr[cap_rows, :] = jnp.where(cap_mask(cap_ref), s_scr[cap_rows, :], -1e30)
        for rows in pieces:
            probs = jnp.exp(s_scr[rows, :] - lse)
            p_scr[rows, :] = probs.astype(BF16)
            ds_scr[rows, :] = (probs * (dp_scr[rows, :] - delta)).astype(BF16)
        dv_ref[:, cols] = dot_nn(p_scr[...], d2).astype(BF16)
        dk_ref[:, cols] = dot_nn(ds_scr[...], q2).astype(BF16)
        dq = dot_tn(k_ref[:, cols], ds_scr[...])
        dq_ref[:, cols] = (from_two_heads(dq) * 0.125).astype(BF16)
        return carry

    lax.fori_loop(0, D // PAIR, pair, 0)
    gain = gain_ref[...]

    wide = sums_ref.shape[0] // 4
    window = pl.ds(pl.multiple_of(s_ref[2], PAIR), wide)
    video_rows = pl.ds(0, keys - cap)
    cap_norm = layer_norm(cap_ref[:, pl.ds(0, D)].astype(F32), gain).astype(BF16)
    latn = layer_norm(lat_ref[...].astype(F32), gain_lat_ref[...]).astype(BF16)
    sums_ref[pl.ds(0, wide), :] += dot_tn(dq_ref[:, window], latn)
    mixed = (o_ref[:, window] * keep).astype(BF16)
    sums_ref[pl.ds(3 * wide, wide), :] += dot_tn(mixed, after_ref[...].astype(BF16))

    def both(rows):
        return jnp.concatenate([dk_ref[rows, window], dv_ref[rows, window]], axis=1)

    sums_ref[pl.ds(wide, 2 * wide), :] += dot_tn(both(video_rows), tok_ref[...]) + dot_tn(
        both(cap_rows), cap_norm
    )

    half = lat_out.shape[0]
    lat_grad = after_ref[...] + norm_back(
        lat_ref[...].astype(F32), dot_nn(dq_ref[...], square(wq_ref)), gain_lat_ref[...], 1
    )
    lat_out[...] = lat_grad[:half]
    other_out[pl.ds(other_ref.shape[0], half), :] = lat_grad[half:].astype(BF16)

    start = 0
    for ref, out, size in ((own_ref, own_out, 256), (other_ref, other_out, 256), (cap_ref, cap_out, cap)):
        def chunk(c, carry, ref=ref, out=out, size=size, start=start):
            rows = pl.ds(pl.multiple_of(c * size, 16), size)
            key_rows = pl.ds(pl.multiple_of(start + c * size, 16), size)
            up_scr[pl.ds(0, size), :] = dot_nn(dk_ref[key_rows, :], square(wk_ref)) + dot_nn(
                dv_ref[key_rows, :], square(wv_ref)
            )
            for at in range(0, size, 32):
                piece = pl.ds(pl.multiple_of(c * size, 16) + at, 32)
                back = norm_back(
                    ref[piece, pl.ds(0, D)].astype(F32), up_scr[pl.ds(at, 32), :], gain, 0
                )
                out[piece, :] = back.astype(out.dtype)
            return carry

        lax.fori_loop(0, ref.shape[0] // size, chunk, 0)
        start += ref.shape[0]

    @pl.when(item == pl.num_programs(0) - 1)
    def _():
        width = D // 4
        for n in range(4):
            mine = pl.ds(pl.multiple_of(s_ref[3] + n * wide, PAIR // 2), width)
            late_ref[pl.ds(n * width, width), :] = sums_ref[mine, :].astype(BF16)
        gains = [jnp.sum(gain_out[pl.ds(8 * row, 8), :], axis=0, keepdims=True) for row in range(3)]
        kept = 4 - s_ref[4] - s_ref[5] - s_ref[6] - s_ref[7]
        gains.append(jnp.full((1, D), kept.astype(F32)))
        gains = jnp.concatenate(gains + [jnp.zeros((12, D), F32)], axis=0)
        late_ref[pl.ds(4 * width, 16), :] = gains.astype(BF16)
        spare = late_ref.shape[0] - 4 * width - 16
        late_ref[pl.ds(4 * width + 16, spare), :] = jnp.zeros((spare, D), BF16)


def place_kernel(s_ref, video_in, lat_in, video_part, lat_part, video_ref, lat_ref):
    video_ref[...] = video_part[...].astype(F32)

    @pl.when(pl.program_id(1) == 0)
    def _():
        lat_ref[...] = lat_part[...].astype(F32)


def local(
    latents,
    video_tokens,
    caption_tokens,
    caption_len,
    key_mask,
    drop_flags,
    gain_latent,
    gain_tokens,
    gain_mlp,
    query_weight,
    key_matrix,
    value_matrix,
    out_weight,
    up_weight,
    down_weight,
    cotangent,
):
    txt_count = lax.axis_size("txt")
    head_count = lax.axis_size("head")
    core = lax.axis_index("vid")
    place_index = lax.axis_index("txt")
    z = lax.axis_index("head")
    items_here = latents.shape[0]
    own = items_here // 2
    lat_half = latents.shape[1]
    lat_rows = 2 * lat_half
    video_here = video_tokens.shape[1]
    cap_here = caption_tokens.shape[1]
    cap_rows = cap_here * txt_count
    keys_here = 2 * video_here + cap_rows
    head_width = query_weight.shape[1]

    def dot(spec, a, b):
        return jnp.einsum(spec, a, b, preferred_element_type=F32)

    packed = jnp.stack([key_matrix.T, value_matrix.T, query_weight.T, out_weight])
    half = take_block(packed, core, 2)
    up1 = lax.ppermute(half, "head", [(0, 1), (1, 2), (2, 3)])
    down1 = lax.ppermute(half, "head", [(1, 0), (2, 1), (3, 2)])
    near_at = z // 2
    zero = jnp.int32(0)
    own_at = z % 2
    part_shape = (2, 2, 2, head_width, D)

    def place_chunk(whole, chunk, at_core, at_chunk):
        chunk = chunk.reshape((-1, 2, 1) + chunk.shape[-2:])
        return lax.dynamic_update_slice(whole, chunk, (at_core, zero, at_chunk, zero, zero))

    both_own = take_block(jnp.concatenate([latents, cotangent], axis=1), core, own)
    video_other = swap_cores(
        jnp.concatenate(
            [take_block(a, 1 - core, own) for a in (video_tokens, latents, cotangent)], axis=1
        )
    )
    both_other = video_other[:, video_here:]
    lat = jnp.concatenate([both_own[:, :lat_half], both_other[:, :lat_half]], axis=1)
    cot = jnp.concatenate([both_own[:, lat_half:], both_other[:, lat_half:]], axis=1)
    drop_own = take_block(drop_flags, core, own)
    keep = (1 - drop_own).astype(F32)
    window = z * head_width // PAIR * PAIR
    inside = z * head_width - window
    scalars = jnp.concatenate([jnp.stack([core, near_at, window, inside]), drop_own])
    scalars_far = jnp.concatenate([jnp.stack([core, 1 - near_at, window, inside]), drop_own])

    place_slots = place_index * cap_here + jnp.arange(cap_here, dtype=jnp.int32)
    cap_valid = (place_slots[None, :] < caption_len[:, None]) & (key_mask == 1)
    flags = jnp.broadcast_to(cap_valid.astype(BF16)[:, :, None], cap_valid.shape + (PAIR,))
    cap_message = jnp.concatenate([caption_tokens, flags], axis=2)
    def send_captions(message, steps):
        return [
            lax.ppermute(
                take_block(message, (place_index + step) % txt_count, own),
                ("vid", "txt"),
                caption_perm(step, 2, txt_count, 2),
            )
            for step in steps
        ]

    cap_parts = send_captions(cap_message, range(txt_count))

    def item_spec(rows, width=D, first=0):
        return pl.BlockSpec((None, rows, width), lambda i, s: (first + i, 0, 0))

    def own_spec(rows, first=0):
        return pl.BlockSpec((None, rows, D), lambda i, s: (s[0] * own + first + i, 0, 0))

    def whole_spec(*shape):
        return pl.BlockSpec(shape, lambda i, s: (0,) * len(shape))

    def weight_spec(m):
        return pl.BlockSpec(
            (2, None, None, 2, head_width, D),
            lambda i, s: (0, m // 2, m % 2, 0, 0, 0),
            pipeline_mode=pl.Buffered(1),
        )

    def part_spec(at_core, first, count):
        return pl.BlockSpec(
            (None, count, 2, head_width, D),
            lambda i, s: (at_core, first, 0, 0, 0),
            pipeline_mode=pl.Buffered(1),
        )

    def half_spec(rows):
        return pl.BlockSpec((None, rows, 2 * head_width), lambda i, s: (i, 0, s[1]))

    row_spec = pl.BlockSpec((1, D), lambda i, s: (0, 0))

    def call(kernel, name, ins, outs, operands, micros, scratch=(), aliases={}, scalars=scalars, grid=own):
        return pl.pallas_call(
            kernel,
            name=name,
            grid_spec=pltpu.PrefetchScalarGridSpec(
                num_scalar_prefetch=1,
                grid=(grid,),
                in_specs=ins,
                out_specs=[spec for spec, _, _ in outs],
                scratch_shapes=list(scratch),
            ),
            out_shape=[jax.ShapeDtypeStruct(shape, dtype) for _, shape, dtype in outs],
            input_output_aliases=aliases,
            cost_estimate=pl.CostEstimate(
                flops=micros * 1100 * 10**6, transcendentals=0, bytes_accessed=micros * 10**6
            ),
            compiler_params=pltpu.CompilerParams(vmem_limit_bytes=56 << 20),
        )(scalars, *operands)

    def item_out(rows, dtype, width=D):
        return (item_spec(rows, width), (own, rows, width), dtype)

    gain_lat_row = gain_latent[None]
    gain_tok_row = gain_tokens[None]
    gain_mlp_row = gain_mlp[None]
    (tok_norm,) = call(
        norm_kernel,
        "token_norm",
        [own_spec(video_here), item_spec(video_here), row_spec],
        [item_out(2 * video_here, BF16)],
        (video_tokens, video_other, gain_tok_row),
        9,
    )
    tok_norm, up1, down1, cap_parts = lax.optimization_barrier((tok_norm, up1, down1, cap_parts))
    cap = jnp.concatenate(cap_parts, axis=1)
    partner = jnp.where(z % 2 == 1, up1, down1)
    near = jnp.zeros(part_shape, BF16)
    near = place_chunk(near, packed.reshape((2, 2) + packed.shape[1:]), zero, own_at)
    near = place_chunk(near, partner, core, 1 - own_at)
    partner_other = swap_cores(partner)
    near = place_chunk(near, partner_other, 1 - core, 1 - own_at)
    up1, down1, half_then, _ = lax.optimization_barrier((up1, down1, half, partner_other))
    ring_up = lax.ppermute(jnp.where(z == 3, half_then, up1), "head", [(1, 2), (2, 3), (3, 0)])
    ring_down = lax.ppermute(jnp.where(z == 0, half_then, down1), "head", [(1, 0), (2, 1), (0, 3)])

    def forward(part, scalars, before=()):
        return call(
            forward_kernel,
            "attention_forward",
            [item_spec(2 * video_here), item_spec(cap_rows, D + PAIR), row_spec]
            + [item_spec(lat_rows), row_spec]
            + [part_spec(1, 0, 1), part_spec(0, 0, 2)]
            + [pl.BlockSpec(memory_space=pl.ANY)] * len(before),
            [
                (half_spec(lat_rows), (own, lat_rows, D), BF16),
                (half_spec(keys_here), (own, keys_here, D), BF16),
                (half_spec(keys_here), (own, keys_here, D), BF16),
                (
                    pl.BlockSpec((None, None, 8, 2 * lat_rows), lambda i, s: (i, s[1], 0, 0)),
                    (own, 2, 8, 2 * lat_rows),
                    F32,
                ),
                (half_spec(lat_rows), (own, lat_rows, D), F32),
            ],
            (tok_norm, cap, gain_tok_row, lat, gain_lat_row, part, part) + tuple(before),
            23,
            [
                pltpu.VMEM((keys_here, 2 * lat_rows), F32),
                pltpu.VMEM((keys_here, 2 * lat_rows), BF16),
                pltpu.VMEM((D, 4 * head_width), BF16),
            ],
            {8 + n: n for n in range(len(before))},
            scalars,
        )

    before = forward(near, scalars)
    before, up1, down1, ring_up, ring_down = lax.optimization_barrier(
        (before, up1, down1, ring_up, ring_down)
    )
    far_low = jnp.where(z == 1, down1, jnp.where(z == 2, ring_up, ring_down))
    far_high = jnp.where(z == 1, ring_down, jnp.where(z == 2, up1, ring_up))
    far_mine = jnp.stack([far_low, far_high], axis=1)
    far = jnp.zeros(part_shape, BF16)
    far = lax.dynamic_update_index_in_dim(far, far_mine, core, 0)
    far = lax.dynamic_update_index_in_dim(far, swap_cores(far_mine), 1 - core, 0)
    def both_halves(near, far):
        whole = jnp.zeros((2,) + near.shape, BF16)
        whole = lax.dynamic_update_index_in_dim(whole, near, near_at, 0)
        return lax.dynamic_update_index_in_dim(whole, far, 1 - near_at, 0)

    queries, keys, values, lse, attended = forward(far, scalars_far, before)
    w_out = both_halves(near[1, 1], far[1, 1]).reshape(D, D)
    lat_float = lat.astype(F32)
    mixed_in = (attended * keep[:, None, None]).astype(BF16)
    after_attn = lat_float + dot("ble,ed->bld", mixed_in, w_out)
    mlp_norm = layer_norm(after_attn, gain_mlp).astype(BF16)

    pre_act = dot("bld,df->blf", mlp_norm, up_weight)
    activ, gelu_pull = jax.vjp(gelu_exact, pre_act)
    activ = activ.astype(BF16)
    d_pre = gelu_pull(dot("bld,fd->blf", cot, down_weight))[0].astype(BF16)
    d_mlp_part = dot("blf,df->bld", d_pre, up_weight)
    d_mlp_part, activ, d_pre = lax.optimization_barrier((d_mlp_part, activ, d_pre))
    chunks = head_chunks(d_mlp_part, z, head_count)
    received = head_exchange(chunks, head_count)
    activ, d_pre, received[0] = lax.optimization_barrier((activ, d_pre, received[0]))
    d_mlp_total = head_sum(chunks[0], received)
    grad_down = dot("blf,bld->fd", activ, cot).astype(BF16)
    grad_up = dot("bld,blf->df", mlp_norm, d_pre).astype(BF16)
    near, far, _ = lax.optimization_barrier((near, far, d_mlp_part))
    weights = both_halves(near, far)
    early = jnp.where(core == 0, grad_up, grad_down).astype(F32)
    early = early + swap_cores(jnp.where(core == 0, grad_down, grad_up)).astype(F32)
    d_mlp_norm = gather_head(d_mlp_total, z, head_count)
    activ, _ = lax.optimization_barrier((activ, d_mlp_total))
    growth = head_chunks(dot("blf,fd->bld", activ, down_weight), z, head_count)
    d_mlp_norm = d_mlp_norm.reshape(after_attn.shape)
    growth, d_mlp_norm, weights, early = lax.optimization_barrier(
        (growth, d_mlp_norm, weights, early.astype(BF16))
    )
    early = lax.psum(early, "txt")
    growth_received = head_exchange(growth, head_count)

    late_size = 4 * head_width + 16
    late_size = late_size + -late_size % (32 * txt_count)
    pair_shape = (keys_here, 2 * lat_rows)
    video_grad, other_back, cap_back, latent_grad, late = call(
        backward_kernel,
        "attention_backward",
        [
            item_spec(lat_rows),
            item_spec(keys_here),
            item_spec(keys_here),
            pl.BlockSpec((None, 2, 8, 2 * lat_rows), lambda i, s: (i, 0, 0, 0)),
            item_spec(lat_rows),
            item_spec(lat_rows),
            item_spec(lat_rows),
            item_spec(lat_rows),
            own_spec(video_here),
            item_spec(video_here),
            item_spec(cap_rows, D + PAIR),
            weight_spec(0),
            weight_spec(1),
            row_spec,
            item_spec(2 * video_here),
            weight_spec(2),
            weight_spec(3),
            item_spec(lat_rows),
            row_spec,
            row_spec,
        ],
        [
            (own_spec(video_here), video_tokens.shape, F32),
            item_out(video_here + lat_half, BF16),
            item_out(cap_rows, BF16),
            (own_spec(lat_half), latents.shape, F32),
            (whole_spec(late_size, D), (late_size, D), BF16),
        ],
        (
            queries, keys, values, lse, attended, d_mlp_norm, after_attn, cot, video_tokens,
            video_other, cap, weights, weights, gain_tok_row, tok_norm, weights, weights, lat,
            gain_lat_row, gain_mlp_row,
        ),
        BACK_COST,
        [
            pltpu.VMEM((lat_rows, D), BF16),
            pltpu.VMEM((keys_here, D), BF16),
            pltpu.VMEM((keys_here, D), BF16),
            pltpu.VMEM(pair_shape, F32),
            pltpu.VMEM(pair_shape, F32),
            pltpu.VMEM(pair_shape, BF16),
            pltpu.VMEM(pair_shape, BF16),
            pltpu.VMEM((256, D), F32),
            pltpu.VMEM((8 * PAIR, D), F32),
            pltpu.VMEM((24, D), F32),
            pltpu.VMEM((lat_rows, D), BF16),
            pltpu.VMEM((lat_rows, D), F32),
        ],
    )
    def place(video_grad, latent_grad, part):
        piece = video_here
        return pl.pallas_call(
            place_kernel,
            name="place_rows",
            grid_spec=pltpu.PrefetchScalarGridSpec(
                num_scalar_prefetch=1,
                grid=(own, 1),
                in_specs=[
                    pl.BlockSpec(memory_space=pl.ANY),
                    pl.BlockSpec(memory_space=pl.ANY),
                    pl.BlockSpec((None, piece, D), lambda i, r, s: (i, r, 0)),
                    pl.BlockSpec((None, lat_half, D), lambda i, r, s: (i, video_here // lat_half, 0)),
                ],
                out_specs=[
                    pl.BlockSpec((None, piece, D), lambda i, r, s: ((1 - s[0]) * own + i, r, 0)),
                    pl.BlockSpec((None, lat_half, D), lambda i, r, s: ((1 - s[0]) * own + i, 0, 0)),
                ],
            ),
            out_shape=[
                jax.ShapeDtypeStruct(video_tokens.shape, F32),
                jax.ShapeDtypeStruct(latents.shape, F32),
            ],
            input_output_aliases={1: 0, 2: 1},
            cost_estimate=pl.CostEstimate(
                flops=6 * 10**9, transcendentals=0, bytes_accessed=10**7
            ),
        )(scalars, video_grad, latent_grad, part, part)

    early, growth_received, late = lax.optimization_barrier((early, growth_received, late))
    late_half, late_swapped = reduce_over_cores(late, core)
    other_back, early, _ = lax.optimization_barrier((other_back, early, late_swapped))
    other_here = swap_cores(other_back)
    growth_received, _ = lax.optimization_barrier((growth_received, late_swapped))
    growth = head_sum(growth[0], growth_received)
    early_other = swap_cores(early)
    late_total = reduce_over_group(late_half, place_index, txt_count)
    late_total, growth, early_other, other_here, cap_back = lax.optimization_barrier(
        (late_total, growth, early_other, other_here, cap_back)
    )
    growth = gather_head(growth, z, head_count)
    cap_parts = []
    for step in range(txt_count):
        perm = [(b, a) for a, b in caption_perm(step, 2, txt_count, 2)]
        cap_parts.append(
            lax.ppermute(cap_back[:, step * cap_here : (step + 1) * cap_here], ("vid", "txt"), perm)
        )
    late = gather_places(late_total, place_index, txt_count)
    video_grad, latent_grad = place(video_grad, latent_grad, other_here)
    late, video_grad, latent_grad, cap_parts, growth = lax.optimization_barrier(
        (late, video_grad, latent_grad, cap_parts, growth)
    )
    late = gather_cores(late, core).astype(F32)
    caption_grad = jnp.zeros((txt_count, own, cap_here, D), F32)
    for step, part in enumerate(cap_parts):
        caption_grad = lax.dynamic_update_index_in_dim(
            caption_grad, part.astype(F32), (place_index + step) % txt_count, 0
        )
    caption_grad = caption_grad.reshape(caption_tokens.shape)
    out_mine = (after_attn + growth.reshape(after_attn.shape).astype(F32)).astype(BF16)
    gains = late[4 * head_width :]

    def give_back(values):
        other = swap_cores(values[:, lat_half:].astype(BF16)).astype(values.dtype)
        whole = jnp.zeros((items_here, lat_half, D), values.dtype)
        whole = lax.dynamic_update_slice_in_dim(whole, values[:, :lat_half], core * own, 0)
        return lax.dynamic_update_slice_in_dim(whole, other, (1 - core) * own, 0)

    latents_out = give_back(out_mine)
    kept_count = gains[3, 0].astype(jnp.int32)
    return (
        latents_out,
        latent_grad,
        video_grad,
        caption_grad,
        late[:head_width].T,
        late[head_width : 2 * head_width].T,
        late[2 * head_width : 3 * head_width].T,
        late[3 * head_width : 4 * head_width],
        jnp.where(core == 0, early, early_other).astype(F32),
        jnp.where(core == 0, early_other, early).astype(F32),
        gains[1],
        gains[0],
        gains[2],
        kept_count,
    )


def fits(mesh):
    shape = mesh.shape
    return shape["vid"] == 2 and shape["txt"] == 4 and shape["head"] == 4


def solution(mesh):
    in_specs = (
        P("txt", "vid", None),
        P("txt", "vid", None),
        P("vid", "txt", None),
        P("vid"),
        P("vid", "txt"),
        P("txt"),
        P(),
        P(),
        P(),
        P(None, "head"),
        P(None, "head"),
        P(None, "head"),
        P("head", None),
        P(None, "head"),
        P("head", None),
        P("txt", "vid", None),
    )
    out_specs = (
        P("txt", "vid", None),
        P("txt", "vid", None),
        P("txt", "vid", None),
        P("vid", "txt", None),
        P(None, "head"),
        P(None, "head"),
        P(None, "head"),
        P("head", None),
        P(None, "head"),
        P("head", None),
        P(),
        P(),
        P(),
        P(),
    )
    return jax.shard_map(local if fits(mesh) else local_general, mesh=mesh, in_specs=in_specs, out_specs=out_specs, check_vma=False)
```

```python
import functools
import math

import jax
import jax.numpy as jnp
from jax import lax
from jax.experimental import pallas as pl
from jax.experimental.pallas import tpu as pltpu
from jax.sharding import PartitionSpec as P

D = 768
HEADS = 12


def combined_all(part, axis, combine):
    gathered = jax.tree.map(lambda a: lax.all_gather(a, axis), part)

    def take(source):
        return jax.tree.map(lambda a: lax.dynamic_index_in_dim(a, source, 0, False), gathered)

    return lax.fori_loop(
        1, lax.axis_size(axis), lambda source, state: combine(state, take(source)), take(0)
    )


def layer_norm(values, gain):
    center = values - jnp.mean(values, axis=-1, keepdims=True)
    spread = jnp.mean(center * center, axis=-1, keepdims=True)
    return center * lax.rsqrt(spread + 1e-05) * gain


def norm_back(values, gain, upstream):
    result, pullback = jax.vjp(layer_norm, values, gain)
    return pullback(upstream)


def gelu_exact(values):
    return jax.nn.gelu(values, approximate=False)


def combine_stats(first, second):
    peak = jnp.maximum(first[0], second[0])
    total = first[1] * jnp.exp(first[0] - peak) + second[1] * jnp.exp(second[0] - peak)
    return (peak, total)


def to_blocks(whole, vid_count, txt_count):
    items, rows, width = whole.shape
    split = whole.reshape(txt_count, items // txt_count, vid_count, rows // vid_count, width)
    return split.transpose(2, 0, 1, 3, 4).reshape(
        vid_count * txt_count, items // txt_count, rows // vid_count, width
    )


def from_blocks(blocked, vid_count, txt_count):
    count, items_here, rows_here, width = blocked.shape
    split = blocked.reshape(vid_count, txt_count, items_here, rows_here, width)
    return split.transpose(1, 2, 0, 3, 4).reshape(
        txt_count * items_here, vid_count * rows_here, width
    )


def place_sum(whole, part, start):
    current = lax.dynamic_slice_in_dim(whole, start, part.shape[0], 0)
    return lax.dynamic_update_slice_in_dim(whole, current + part, start, 0)


def place_stats(peak_all, total_all, peak, total, start):
    old_peak = lax.dynamic_slice_in_dim(peak_all, start, peak.shape[0], 0)
    old_total = lax.dynamic_slice_in_dim(total_all, start, peak.shape[0], 0)
    new_peak, new_total = combine_stats((old_peak, old_total), (peak, total))
    peak_all = lax.dynamic_update_slice_in_dim(peak_all, new_peak, start, 0)
    total_all = lax.dynamic_update_slice_in_dim(total_all, new_total, start, 0)
    return (peak_all, total_all)


def take_rows(whole, start, count):
    return lax.dynamic_slice_in_dim(whole, start, count, 0)


def local_general(
    latents,
    video_tokens,
    caption_tokens,
    caption_len,
    key_mask,
    drop_flags,
    gain_latent,
    gain_tokens,
    gain_mlp,
    query_weight,
    key_matrix,
    value_matrix,
    out_weight,
    up_weight,
    down_weight,
    cotangent,
):
    vid_count = lax.axis_size("vid")
    txt_count = lax.axis_size("txt")
    vid_index = lax.axis_index("vid")
    txt_index = lax.axis_index("txt")
    items_here = latents.shape[0]
    cap_items = caption_tokens.shape[0]
    items_total = items_here * txt_count
    head_width = query_weight.shape[1]
    head_size = D // HEADS
    heads_here = head_width // head_size
    scale = 1.0 / math.sqrt(head_size)
    video_here = video_tokens.shape[1]
    cap_here = caption_tokens.shape[1]
    video_start = txt_index * items_here
    cap_start = vid_index * cap_items
    keep = (1 - drop_flags).astype(jnp.float32)
    slots = txt_index * cap_here + jnp.arange(cap_here, dtype=jnp.int32)
    cap_valid = (slots[None, :] < caption_len[:, None]) & (key_mask == 1)
    cap_mask = cap_valid[:, None, None, :]

    def split_heads(values):
        return values.reshape(values.shape[0], values.shape[1], heads_here, head_size)

    lat_float = latents.astype(jnp.float32)
    lat_norm = layer_norm(lat_float, gain_latent).astype(jnp.bfloat16)
    queries = jnp.einsum(
        "bld,de->ble", lat_norm, query_weight, preferred_element_type=jnp.float32
    ).astype(jnp.bfloat16)
    all_queries = from_blocks(
        lax.all_gather(queries[None], ("vid", "txt"), axis=0, tiled=True), vid_count, txt_count
    )
    lat_total = all_queries.shape[1]
    video_queries = take_rows(all_queries, video_start, items_here)
    cap_queries = take_rows(all_queries, cap_start, cap_items)
    video_float = video_tokens.astype(jnp.float32)
    cap_float = caption_tokens.astype(jnp.float32)
    video_normed = layer_norm(video_float, gain_tokens).astype(jnp.bfloat16)
    caption_normed = layer_norm(cap_float, gain_tokens).astype(jnp.bfloat16)
    video_keys = jnp.einsum(
        "flc,co->flo", video_normed, key_matrix, preferred_element_type=jnp.float32
    ).astype(jnp.bfloat16)
    video_values = jnp.einsum(
        "flc,co->flo", video_normed, value_matrix, preferred_element_type=jnp.float32
    ).astype(jnp.bfloat16)
    cap_keys = jnp.einsum(
        "flc,co->flo", caption_normed, key_matrix, preferred_element_type=jnp.float32
    ).astype(jnp.bfloat16)
    cap_values = jnp.einsum(
        "flc,co->flo", caption_normed, value_matrix, preferred_element_type=jnp.float32
    ).astype(jnp.bfloat16)
    video_scores = (
        jnp.einsum(
            "blhe,bkhe->bhlk",
            split_heads(video_queries),
            split_heads(video_keys),
            preferred_element_type=jnp.float32,
        )
        * scale
    )
    cap_scores = (
        jnp.einsum(
            "blhe,bkhe->bhlk",
            split_heads(cap_queries),
            split_heads(cap_keys),
            preferred_element_type=jnp.float32,
        )
        * scale
    )
    cap_scores = jnp.where(cap_mask, cap_scores, -1e30)
    video_peak = jnp.max(video_scores, axis=-1)
    video_total = jnp.sum(jnp.exp(video_scores - video_peak[..., None]), axis=-1)
    cap_peak = jnp.max(cap_scores, axis=-1)
    cap_total = jnp.sum(
        jnp.where(cap_mask, jnp.exp(cap_scores - cap_peak[..., None]), 0.0), axis=-1
    )
    peak_all = jnp.full((items_total, heads_here, lat_total), -1e30, jnp.float32)
    total_all = jnp.zeros((items_total, heads_here, lat_total), jnp.float32)
    peak_all, total_all = place_stats(peak_all, total_all, video_peak, video_total, video_start)
    peak_all, total_all = place_stats(peak_all, total_all, cap_peak, cap_total, cap_start)
    peak, total = combined_all((peak_all, total_all), ("vid", "txt"), combine_stats)
    video_probs = (
        jnp.exp(video_scores - take_rows(peak, video_start, items_here)[..., None])
        / take_rows(total, video_start, items_here)[..., None]
    )
    cap_probs = jnp.where(
        cap_mask,
        jnp.exp(cap_scores - take_rows(peak, cap_start, cap_items)[..., None])
        / take_rows(total, cap_start, cap_items)[..., None],
        0.0,
    )
    video_low = video_probs.astype(jnp.bfloat16)
    cap_low = cap_probs.astype(jnp.bfloat16)
    video_part = jnp.einsum(
        "bhlk,bkhe->blhe", video_low, split_heads(video_values), preferred_element_type=jnp.float32
    ).reshape(items_here, lat_total, head_width)
    cap_part = jnp.einsum(
        "bhlk,bkhe->blhe", cap_low, split_heads(cap_values), preferred_element_type=jnp.float32
    ).reshape(cap_items, lat_total, head_width)
    value_all = jnp.zeros((items_total, lat_total, head_width), jnp.float32)
    value_all = place_sum(place_sum(value_all, video_part, video_start), cap_part, cap_start)
    attended = lax.psum_scatter(
        to_blocks(value_all, vid_count, txt_count), ("vid", "txt"), scatter_dimension=0, tiled=True
    )[0]
    mixed_in = (attended * keep[:, None, None]).astype(jnp.bfloat16)
    branch = lax.psum(
        jnp.einsum("ble,ed->bld", mixed_in, out_weight, preferred_element_type=jnp.float32), "head"
    )
    after_attn = lat_float + branch
    mlp_norm = layer_norm(after_attn, gain_mlp).astype(jnp.bfloat16)
    pre_act = jnp.einsum("bld,df->blf", mlp_norm, up_weight, preferred_element_type=jnp.float32)
    activ = gelu_exact(pre_act).astype(jnp.bfloat16)
    growth = lax.psum(
        jnp.einsum("blf,fd->bld", activ, down_weight, preferred_element_type=jnp.float32).astype(
            jnp.bfloat16
        ),
        "head",
    ).astype(jnp.float32)
    latents_out = (after_attn + growth).astype(jnp.bfloat16)
    grad_down = jnp.einsum("blf,bld->fd", activ, cotangent, preferred_element_type=jnp.float32)
    d_activ = jnp.einsum("bld,fd->blf", cotangent, down_weight, preferred_element_type=jnp.float32)
    d_pre = jax.vjp(gelu_exact, pre_act)[1](d_activ)[0].astype(jnp.bfloat16)
    grad_up = jnp.einsum("bld,blf->df", mlp_norm, d_pre, preferred_element_type=jnp.float32)
    d_mlp_norm = lax.psum(
        jnp.einsum("blf,df->bld", d_pre, up_weight, preferred_element_type=jnp.float32), "head"
    )
    d_after_norm, grad_gain_mlp = norm_back(after_attn, gain_mlp, d_mlp_norm)
    d_after = cotangent.astype(jnp.float32) + d_after_norm
    d_branch = d_after.astype(jnp.bfloat16)
    grad_out = jnp.einsum("ble,bld->ed", mixed_in, d_branch, preferred_element_type=jnp.float32)
    d_att = (
        jnp.einsum("bld,ed->ble", d_branch, out_weight, preferred_element_type=jnp.float32)
        * keep[:, None, None]
    ).astype(jnp.bfloat16)
    all_d_att = from_blocks(
        lax.all_gather(d_att[None], ("vid", "txt"), axis=0, tiled=True), vid_count, txt_count
    )
    video_d_att = split_heads(take_rows(all_d_att, video_start, items_here))
    cap_d_att = split_heads(take_rows(all_d_att, cap_start, cap_items))
    video_dprobs = jnp.einsum(
        "blhe,bkhe->bhlk",
        video_d_att,
        split_heads(video_values),
        preferred_element_type=jnp.float32,
    )
    cap_dprobs = jnp.einsum(
        "blhe,bkhe->bhlk", cap_d_att, split_heads(cap_values), preferred_element_type=jnp.float32
    )
    delta_all = jnp.zeros((items_total, heads_here, lat_total), jnp.float32)
    delta_all = place_sum(delta_all, jnp.sum(video_probs * video_dprobs, axis=-1), video_start)
    delta_all = place_sum(delta_all, jnp.sum(cap_probs * cap_dprobs, axis=-1), cap_start)
    delta = lax.psum(delta_all, ("vid", "txt"))
    video_dscores = (
        video_probs * (video_dprobs - take_rows(delta, video_start, items_here)[..., None])
    ).astype(jnp.bfloat16)
    cap_dscores = (
        cap_probs * (cap_dprobs - take_rows(delta, cap_start, cap_items)[..., None])
    ).astype(jnp.bfloat16)
    video_dq = (
        jnp.einsum(
            "bhlk,bkhe->blhe",
            video_dscores,
            split_heads(video_keys),
            preferred_element_type=jnp.float32,
        )
        * scale
    ).reshape(items_here, lat_total, head_width)
    cap_dq = (
        jnp.einsum(
            "bhlk,bkhe->blhe",
            cap_dscores,
            split_heads(cap_keys),
            preferred_element_type=jnp.float32,
        )
        * scale
    ).reshape(cap_items, lat_total, head_width)
    query_all = jnp.zeros((items_total, lat_total, head_width), jnp.float32)
    query_all = place_sum(place_sum(query_all, video_dq, video_start), cap_dq, cap_start)
    d_queries = lax.psum_scatter(
        to_blocks(query_all, vid_count, txt_count), ("vid", "txt"), scatter_dimension=0, tiled=True
    )[0].astype(jnp.bfloat16)
    video_key_grad = (
        (
            jnp.einsum(
                "bhlk,blhe->bkhe",
                video_dscores,
                split_heads(video_queries),
                preferred_element_type=jnp.float32,
            )
            * scale
        )
        .reshape(items_here, video_here, head_width)
        .astype(jnp.bfloat16)
    )
    video_value_grad = (
        jnp.einsum("bhlk,blhe->bkhe", video_low, video_d_att, preferred_element_type=jnp.float32)
        .reshape(items_here, video_here, head_width)
        .astype(jnp.bfloat16)
    )
    caption_key_grad = (
        (
            jnp.einsum(
                "bhlk,blhe->bkhe",
                cap_dscores,
                split_heads(cap_queries),
                preferred_element_type=jnp.float32,
            )
            * scale
        )
        .reshape(cap_items, cap_here, head_width)
        .astype(jnp.bfloat16)
    )
    caption_value_grad = (
        jnp.einsum("bhlk,blhe->bkhe", cap_low, cap_d_att, preferred_element_type=jnp.float32)
        .reshape(cap_items, cap_here, head_width)
        .astype(jnp.bfloat16)
    )
    grad_query = jnp.einsum("bld,ble->de", lat_norm, d_queries, preferred_element_type=jnp.float32)
    d_lat_norm = lax.psum(
        jnp.einsum("ble,de->bld", d_queries, query_weight, preferred_element_type=jnp.float32),
        "head",
    )
    d_lat_back, grad_gain_latent = norm_back(lat_float, gain_latent, d_lat_norm)
    latent_grad = d_after + d_lat_back
    grad_key = jnp.einsum(
        "zsg,zsv->gv", video_normed, video_key_grad, preferred_element_type=jnp.float32
    ) + jnp.einsum(
        "zsg,zsv->gv", caption_normed, caption_key_grad, preferred_element_type=jnp.float32
    )
    grad_value = jnp.einsum(
        "zsg,zsv->gv", video_normed, video_value_grad, preferred_element_type=jnp.float32
    ) + jnp.einsum(
        "zsg,zsv->gv", caption_normed, caption_value_grad, preferred_element_type=jnp.float32
    )
    video_term = jnp.einsum(
        "ayt,ot->ayo", video_key_grad, key_matrix, preferred_element_type=jnp.float32
    ) + jnp.einsum(
        "ayt,ot->ayo", video_value_grad, value_matrix, preferred_element_type=jnp.float32
    )
    cap_term = jnp.einsum(
        "ayt,ot->ayo", caption_key_grad, key_matrix, preferred_element_type=jnp.float32
    ) + jnp.einsum(
        "ayt,ot->ayo", caption_value_grad, value_matrix, preferred_element_type=jnp.float32
    )
    d_video_norm, d_cap_norm = lax.psum((video_term, cap_term), "head")
    video_grad, video_gain_part = norm_back(video_float, gain_tokens, d_video_norm)
    caption_grad, cap_gain_part = norm_back(cap_float, gain_tokens, d_cap_norm)
    grad_gain_tokens = video_gain_part + cap_gain_part
    kept_here = jnp.sum(keep)
    (
        grad_query,
        grad_key,
        grad_value,
        grad_out,
        grad_up,
        grad_down,
        grad_gain_latent,
        grad_gain_tokens,
        grad_gain_mlp,
        kept_total,
    ) = lax.psum(
        (
            grad_query,
            grad_key,
            grad_value,
            grad_out,
            grad_up,
            grad_down,
            grad_gain_latent,
            grad_gain_tokens,
            grad_gain_mlp,
            kept_here,
        ),
        ("vid", "txt"),
    )
    kept_count = (kept_total / vid_count).astype(jnp.int32)
    return (
        latents_out,
        latent_grad,
        video_grad,
        caption_grad,
        grad_query,
        grad_key,
        grad_value,
        grad_out,
        grad_up,
        grad_down,
        grad_gain_latent,
        grad_gain_tokens,
        grad_gain_mlp,
        kept_count,
    )


def swap_cores(values):
    return lax.ppermute(values, "vid", [(0, 1), (1, 0)])


def head_shift(values, shift, count):
    return lax.ppermute(values, "head", [(i, (i - shift) % count) for i in range(count)])


def take_block(values, index, size, axis=0):
    return lax.dynamic_slice_in_dim(values, index * size, size, axis)


def head_chunks(part, place, count):
    low = part.astype(BF16)
    others = [
        lax.dynamic_index_in_dim(low, (place - shift) % count, 0, False)
        for shift in range(1, count)
    ]
    return [lax.dynamic_index_in_dim(part, place, 0, False)] + others


def head_exchange(chunks, count):
    return [head_shift(chunks[shift], shift, count) for shift in range(1, count)]


def head_sum(own, received):
    for part in received:
        own = own + part.astype(F32)
    return own.astype(BF16)


def gather_head(total, place, count):
    result = jnp.zeros((count,) + total.shape, BF16)
    result = lax.dynamic_update_index_in_dim(result, total, place, 0)
    for shift in range(1, count):
        result = lax.dynamic_update_index_in_dim(
            result, head_shift(total, shift, count), (place + shift) % count, 0
        )
    return result


def group_steps(count):
    return [(step, [(i, (i - step) % count) for i in range(count)]) for step in range(1, count)]


def reduce_over_cores(rows, core):
    half = rows.shape[0] // 2
    other = swap_cores(take_block(rows, 1 - core, half))
    return take_block(rows, core, half).astype(F32) + other.astype(F32), other


def reduce_over_group(half, place, count):
    part = half.shape[0] // count
    low = half.astype(BF16)
    total = take_block(half, place, part)
    for step, perm in group_steps(count):
        chunk = take_block(low, (place - step) % count, part)
        total = total + lax.ppermute(chunk, "txt", perm).astype(F32)
    return total.astype(BF16)


def gather_places(total, place, count):
    part = total.shape[0]
    mine = jnp.zeros((part * count, total.shape[1]), BF16)
    mine = lax.dynamic_update_slice_in_dim(mine, total, place * part, 0)
    for step, perm in group_steps(count):
        mine = lax.dynamic_update_slice_in_dim(
            mine, lax.ppermute(total, "txt", perm), (place + step) % count * part, 0
        )
    return mine


def gather_cores(mine, core):
    half = mine.shape[0]
    whole = jnp.zeros((2 * half, mine.shape[1]), BF16)
    whole = lax.dynamic_update_slice_in_dim(whole, mine, core * half, 0)
    return lax.dynamic_update_slice_in_dim(whole, swap_cores(mine), (1 - core) * half, 0)


def caption_perm(step, vid_count, txt_count, cores):
    pairs = []
    for v in range(vid_count):
        for t in range(txt_count):
            block = (t + step) % txt_count
            dest_txt = v * (txt_count // vid_count) + block // cores
            dest_vid = block % cores
            pairs.append((v * txt_count + t, dest_vid * txt_count + dest_txt))
    return pairs


PAIR = 128
BACK_COST = 3
F32 = jnp.float32
BF16 = jnp.bfloat16


def dot_nt(a, b):
    return lax.dot_general(a, b, (((1,), (1,)), ((), ())), preferred_element_type=F32)


def dot_nn(a, b):
    return lax.dot_general(a, b, (((1,), (0,)), ((), ())), preferred_element_type=F32)


def dot_tn(a, b):
    return lax.dot_general(a, b, (((0,), (0,)), ((), ())), preferred_element_type=F32)


def square(ref):
    return ref[...].reshape(D, D)


def two_heads(values):
    low = lax.broadcasted_iota(jnp.int32, values.shape, 1) < PAIR // 2
    zero = jnp.zeros_like(values)
    return jnp.concatenate([jnp.where(low, values, zero), jnp.where(low, zero, values)], axis=0)


def from_two_heads(both):
    n = both.shape[1] // 2
    first = lax.broadcasted_iota(jnp.int32, (PAIR, n), 0) < PAIR // 2
    return jnp.where(first, both[:, :n], both[:, n:]).T


def chunk_list(video, cap, size):
    return [(start, size) for start in range(0, video, size)] + [(video, cap)]


def norm_kernel(s_ref, own_ref, other_ref, gain_ref, out_ref):
    gain = gain_ref[...]
    start = 0
    for ref in (own_ref, other_ref):
        def chunk(c, carry, ref=ref, start=start):
            for part in range(2):
                at = pl.multiple_of(c * 128, 128) + 64 * part
                out_ref[pl.ds(start + at, 64), :] = layer_norm(
                    ref[pl.ds(at, 64), :].astype(F32), gain
                ).astype(BF16)
            return carry

        lax.fori_loop(0, ref.shape[0] // 128, chunk, 0)
        start += ref.shape[0]


def cap_mask(cap_ref):
    mask = cap_ref[:, pl.ds(D, PAIR)]
    return jnp.concatenate([mask, mask], axis=1).astype(F32) > 0.5


def forward_kernel(s_ref, tok_ref, cap_ref, gain_ref, lat_ref, gain_lat_ref, wq_ref, wkv_ref, *refs):
    q_ref, k_ref, v_ref, lse_ref, o_ref, s_scr, e_scr, wkv_scr = refs[-8:]
    keys, width = k_ref.shape
    cap = cap_ref.shape[0]
    step = (keys - cap) // 4
    latn = layer_norm(lat_ref[...].astype(F32), gain_lat_ref[...]).astype(BF16)
    queries = dot_nt(latn, wq_ref[...].reshape(width, D)).astype(BF16).astype(F32)
    q_ref[...] = (queries * 0.125).astype(BF16)

    @pl.when(pl.program_id(0) == 0)
    def _():
        wkv_scr[...] = wkv_ref[...].reshape(2 * width, D).T

    def project(rows, tokens):
        both = dot_nn(tokens, wkv_scr[...]).astype(BF16)
        k_ref[rows, :] = both[:, :width]
        v_ref[rows, :] = both[:, width:]

    def project_video(c, carry):
        rows = pl.ds(pl.multiple_of(c * step, 16), step)
        project(rows, tok_ref[rows, :])
        return carry

    lax.fori_loop(0, 4, project_video, 0)
    cap_rows = pl.ds(keys - cap, cap)
    project(cap_rows, layer_norm(cap_ref[:, pl.ds(0, D)].astype(F32), gain_ref[...]).astype(BF16))
    pieces = [pl.ds(start, 64) for start in range(0, keys, 64)]

    def pair(p, carry):
        cols = pl.ds(pl.multiple_of(p * PAIR, PAIR), PAIR)
        q2 = two_heads(q_ref[:, cols])
        s_scr[...] = dot_nt(k_ref[:, cols], q2)
        s_scr[cap_rows, :] = jnp.where(cap_mask(cap_ref), s_scr[cap_rows, :], -1e30)
        peak = s_scr[pieces[0], :]
        for rows in pieces[1:]:
            peak = jnp.maximum(peak, s_scr[rows, :])
        peak = jnp.max(peak, axis=0, keepdims=True)
        total = jnp.zeros((8, q2.shape[0]), F32)
        for rows in pieces:
            e = jnp.exp(s_scr[rows, :] - peak)
            e_scr[rows, :] = e.astype(BF16)
            total = total + jnp.sum(e.reshape(-1, 8, q2.shape[0]), axis=0)
        total = jnp.sum(total, axis=0, keepdims=True)
        out = dot_tn(v_ref[:, cols], e_scr[...])
        o_ref[:, cols] = from_two_heads(out / total)
        lse_ref[pl.ds(p, 1), :] = peak + jnp.log(total)
        return carry

    lax.fori_loop(0, width // PAIR, pair, 0)


def backward_kernel(
    s_ref, q_ref, k_ref, v_ref, lse_ref, o_ref, up_ref, attn_ref, cot_ref, own_ref, other_ref, cap_ref,
    wk_ref, wv_ref, gain_ref, tok_ref, wq_ref, wo_ref, lat_ref, gain_lat_ref, gain_mlp_ref,
    own_out, other_out, cap_out, lat_out, late_ref,
    dq_ref, dk_ref, dv_ref, s_scr, dp_scr, p_scr, ds_scr, up_scr, sums_ref, gain_out,
    datt_ref, after_ref,
):
    item = pl.program_id(0)
    keys = k_ref.shape[0]
    cap = cap_ref.shape[0]
    cap_rows = pl.ds(keys - cap, cap)
    pieces = [pl.ds(start, 64) for start in range(0, keys, 64)]

    @pl.when(item == 0)
    def _():
        gain_out[...] = jnp.zeros_like(gain_out)
        sums_ref[...] = jnp.zeros_like(sums_ref)

    def norm_back(x, up, gain, row):
        center = x - jnp.mean(x, axis=-1, keepdims=True)
        rate = lax.rsqrt(jnp.mean(center * center, axis=-1, keepdims=True) + 1e-05)
        hat = center * rate
        gain_out[pl.ds(8 * row, 8), :] += jnp.sum((up * hat).reshape(-1, 8, D), axis=0)
        scaled = up * gain
        first = jnp.mean(scaled, axis=-1, keepdims=True)
        second = jnp.mean(scaled * hat, axis=-1, keepdims=True)
        return rate * (scaled - first - hat * second)

    keep = (1 - s_ref[4 + item]).astype(F32)
    after_ref[...] = cot_ref[...].astype(F32) + norm_back(
        attn_ref[...], up_ref[...].astype(F32), gain_mlp_ref[...], 2
    )
    d_branch = after_ref[...].astype(BF16)
    datt_ref[...] = (dot_nt(d_branch, square(wo_ref)) * keep).astype(BF16)

    def pair(p, carry):
        cols = pl.ds(pl.multiple_of(p * PAIR, PAIR), PAIR)
        q2 = two_heads(q_ref[:, cols])
        d_att = datt_ref[:, cols]
        d2 = two_heads(d_att)
        prod = (d_att.astype(F32) * o_ref[:, cols]).T
        delta = jnp.concatenate(
            [
                jnp.sum(prod[: PAIR // 2], axis=0, keepdims=True),
                jnp.sum(prod[PAIR // 2 :], axis=0, keepdims=True),
            ],
            axis=1,
        )
        pairs_here = D // PAIR // lse_ref.shape[0]
        lse = lse_ref[p // pairs_here, pl.ds(p % pairs_here, 1), :]
        s_scr[...] = dot_nt(k_ref[:, cols], q2)
        dp_scr[...] = dot_nt(v_ref[:, cols], d2)
        s_scr[cap_rows, :] = jnp.where(cap_mask(cap_ref), s_scr[cap_rows, :], -1e30)
        for rows in pieces:
            probs = jnp.exp(s_scr[rows, :] - lse)
            p_scr[rows, :] = probs.astype(BF16)
            ds_scr[rows, :] = (probs * (dp_scr[rows, :] - delta)).astype(BF16)
        dv_ref[:, cols] = dot_nn(p_scr[...], d2).astype(BF16)
        dk_ref[:, cols] = dot_nn(ds_scr[...], q2).astype(BF16)
        dq = dot_tn(k_ref[:, cols], ds_scr[...])
        dq_ref[:, cols] = (from_two_heads(dq) * 0.125).astype(BF16)
        return carry

    lax.fori_loop(0, D // PAIR, pair, 0)
    gain = gain_ref[...]

    wide = sums_ref.shape[0] // 4
    window = pl.ds(pl.multiple_of(s_ref[2], PAIR), wide)
    video_rows = pl.ds(0, keys - cap)
    cap_norm = layer_norm(cap_ref[:, pl.ds(0, D)].astype(F32), gain).astype(BF16)
    latn = layer_norm(lat_ref[...].astype(F32), gain_lat_ref[...]).astype(BF16)
    sums_ref[pl.ds(0, wide), :] += dot_tn(dq_ref[:, window], latn)
    mixed = (o_ref[:, window] * keep).astype(BF16)
    sums_ref[pl.ds(3 * wide, wide), :] += dot_tn(mixed, after_ref[...].astype(BF16))

    def both(rows):
        return jnp.concatenate([dk_ref[rows, window], dv_ref[rows, window]], axis=1)

    sums_ref[pl.ds(wide, 2 * wide), :] += dot_tn(both(video_rows), tok_ref[...]) + dot_tn(
        both(cap_rows), cap_norm
    )

    half = lat_out.shape[0]
    lat_grad = after_ref[...] + norm_back(
        lat_ref[...].astype(F32), dot_nn(dq_ref[...], square(wq_ref)), gain_lat_ref[...], 1
    )
    lat_out[...] = lat_grad[:half]
    other_out[pl.ds(other_ref.shape[0], half), :] = lat_grad[half:].astype(BF16)

    start = 0
    for ref, out, size in ((own_ref, own_out, 256), (other_ref, other_out, 256), (cap_ref, cap_out, cap)):
        def chunk(c, carry, ref=ref, out=out, size=size, start=start):
            rows = pl.ds(pl.multiple_of(c * size, 16), size)
            key_rows = pl.ds(pl.multiple_of(start + c * size, 16), size)
            up_scr[pl.ds(0, size), :] = dot_nn(dk_ref[key_rows, :], square(wk_ref)) + dot_nn(
                dv_ref[key_rows, :], square(wv_ref)
            )
            for at in range(0, size, 32):
                piece = pl.ds(pl.multiple_of(c * size, 16) + at, 32)
                back = norm_back(
                    ref[piece, pl.ds(0, D)].astype(F32), up_scr[pl.ds(at, 32), :], gain, 0
                )
                out[piece, :] = back.astype(out.dtype)
            return carry

        lax.fori_loop(0, ref.shape[0] // size, chunk, 0)
        start += ref.shape[0]

    @pl.when(item == pl.num_programs(0) - 1)
    def _():
        width = D // 4
        for n in range(4):
            mine = pl.ds(pl.multiple_of(s_ref[3] + n * wide, PAIR // 2), width)
            late_ref[pl.ds(n * width, width), :] = sums_ref[mine, :].astype(BF16)
        gains = [jnp.sum(gain_out[pl.ds(8 * row, 8), :], axis=0, keepdims=True) for row in range(3)]
        kept = 4 - s_ref[4] - s_ref[5] - s_ref[6] - s_ref[7]
        gains.append(jnp.full((1, D), kept.astype(F32)))
        gains = jnp.concatenate(gains + [jnp.zeros((12, D), F32)], axis=0)
        late_ref[pl.ds(4 * width, 16), :] = gains.astype(BF16)
        spare = late_ref.shape[0] - 4 * width - 16
        late_ref[pl.ds(4 * width + 16, spare), :] = jnp.zeros((spare, D), BF16)


def place_kernel(s_ref, video_in, lat_in, video_part, lat_part, video_ref, lat_ref):
    video_ref[...] = video_part[...].astype(F32)

    @pl.when(pl.program_id(1) == 0)
    def _():
        lat_ref[...] = lat_part[...].astype(F32)


def local(
    latents,
    video_tokens,
    caption_tokens,
    caption_len,
    key_mask,
    drop_flags,
    gain_latent,
    gain_tokens,
    gain_mlp,
    query_weight,
    key_matrix,
    value_matrix,
    out_weight,
    up_weight,
    down_weight,
    cotangent,
):
    txt_count = lax.axis_size("txt")
    head_count = lax.axis_size("head")
    core = lax.axis_index("vid")
    place_index = lax.axis_index("txt")
    z = lax.axis_index("head")
    items_here = latents.shape[0]
    own = items_here // 2
    lat_half = latents.shape[1]
    lat_rows = 2 * lat_half
    video_here = video_tokens.shape[1]
    cap_here = caption_tokens.shape[1]
    cap_rows = cap_here * txt_count
    keys_here = 2 * video_here + cap_rows
    head_width = query_weight.shape[1]

    def dot(spec, a, b):
        return jnp.einsum(spec, a, b, preferred_element_type=F32)

    packed = jnp.stack([key_matrix.T, value_matrix.T, query_weight.T, out_weight])
    half = take_block(packed, core, 2)
    up1 = lax.ppermute(half, "head", [(0, 1), (1, 2), (2, 3)])
    down1 = lax.ppermute(half, "head", [(1, 0), (2, 1), (3, 2)])
    near_at = z // 2
    zero = jnp.int32(0)
    own_at = z % 2
    part_shape = (2, 2, 2, head_width, D)

    def place_chunk(whole, chunk, at_core, at_chunk):
        chunk = chunk.reshape((-1, 2, 1) + chunk.shape[-2:])
        return lax.dynamic_update_slice(whole, chunk, (at_core, zero, at_chunk, zero, zero))

    both_own = take_block(jnp.concatenate([latents, cotangent], axis=1), core, own)
    video_other = swap_cores(
        jnp.concatenate(
            [take_block(a, 1 - core, own) for a in (video_tokens, latents, cotangent)], axis=1
        )
    )
    both_other = video_other[:, video_here:]
    lat = jnp.concatenate([both_own[:, :lat_half], both_other[:, :lat_half]], axis=1)
    cot = jnp.concatenate([both_own[:, lat_half:], both_other[:, lat_half:]], axis=1)
    drop_own = take_block(drop_flags, core, own)
    keep = (1 - drop_own).astype(F32)
    window = z * head_width // PAIR * PAIR
    inside = z * head_width - window
    scalars = jnp.concatenate([jnp.stack([core, near_at, window, inside]), drop_own])
    scalars_far = jnp.concatenate([jnp.stack([core, 1 - near_at, window, inside]), drop_own])

    place_slots = place_index * cap_here + jnp.arange(cap_here, dtype=jnp.int32)
    cap_valid = (place_slots[None, :] < caption_len[:, None]) & (key_mask == 1)
    flags = jnp.broadcast_to(cap_valid.astype(BF16)[:, :, None], cap_valid.shape + (PAIR,))
    cap_message = jnp.concatenate([caption_tokens, flags], axis=2)
    def send_captions(message, steps):
        return [
            lax.ppermute(
                take_block(message, (place_index + step) % txt_count, own),
                ("vid", "txt"),
                caption_perm(step, 2, txt_count, 2),
            )
            for step in steps
        ]

    cap_parts = send_captions(cap_message, range(txt_count))

    def item_spec(rows, width=D, first=0):
        return pl.BlockSpec((None, rows, width), lambda i, s: (first + i, 0, 0))

    def own_spec(rows, first=0):
        return pl.BlockSpec((None, rows, D), lambda i, s: (s[0] * own + first + i, 0, 0))

    def whole_spec(*shape):
        return pl.BlockSpec(shape, lambda i, s: (0,) * len(shape))

    def weight_spec(m):
        return pl.BlockSpec(
            (2, None, None, 2, head_width, D),
            lambda i, s: (0, m // 2, m % 2, 0, 0, 0),
            pipeline_mode=pl.Buffered(1),
        )

    def part_spec(at_core, first, count):
        return pl.BlockSpec(
            (None, count, 2, head_width, D),
            lambda i, s: (at_core, first, 0, 0, 0),
            pipeline_mode=pl.Buffered(1),
        )

    def half_spec(rows):
        return pl.BlockSpec((None, rows, 2 * head_width), lambda i, s: (i, 0, s[1]))

    row_spec = pl.BlockSpec((1, D), lambda i, s: (0, 0))

    def call(kernel, name, ins, outs, operands, micros, scratch=(), aliases={}, scalars=scalars, grid=own):
        return pl.pallas_call(
            kernel,
            name=name,
            grid_spec=pltpu.PrefetchScalarGridSpec(
                num_scalar_prefetch=1,
                grid=(grid,),
                in_specs=ins,
                out_specs=[spec for spec, _, _ in outs],
                scratch_shapes=list(scratch),
            ),
            out_shape=[jax.ShapeDtypeStruct(shape, dtype) for _, shape, dtype in outs],
            input_output_aliases=aliases,
            cost_estimate=pl.CostEstimate(
                flops=micros * 1100 * 10**6, transcendentals=0, bytes_accessed=micros * 10**6
            ),
            compiler_params=pltpu.CompilerParams(vmem_limit_bytes=56 << 20),
        )(scalars, *operands)

    def item_out(rows, dtype, width=D):
        return (item_spec(rows, width), (own, rows, width), dtype)

    gain_lat_row = gain_latent[None]
    gain_tok_row = gain_tokens[None]
    gain_mlp_row = gain_mlp[None]
    (tok_norm,) = call(
        norm_kernel,
        "token_norm",
        [own_spec(video_here), item_spec(video_here), row_spec],
        [item_out(2 * video_here, BF16)],
        (video_tokens, video_other, gain_tok_row),
        9,
    )
    tok_norm, up1, down1, cap_parts = lax.optimization_barrier((tok_norm, up1, down1, cap_parts))
    cap = jnp.concatenate(cap_parts, axis=1)
    partner = jnp.where(z % 2 == 1, up1, down1)
    near = jnp.zeros(part_shape, BF16)
    near = place_chunk(near, packed.reshape((2, 2) + packed.shape[1:]), zero, own_at)
    near = place_chunk(near, partner, core, 1 - own_at)
    partner_other = swap_cores(partner)
    near = place_chunk(near, partner_other, 1 - core, 1 - own_at)
    up1, down1, half_then, _ = lax.optimization_barrier((up1, down1, half, partner_other))
    ring_up = lax.ppermute(jnp.where(z == 3, half_then, up1), "head", [(1, 2), (2, 3), (3, 0)])
    ring_down = lax.ppermute(jnp.where(z == 0, half_then, down1), "head", [(1, 0), (2, 1), (0, 3)])

    def forward(part, scalars, before=()):
        return call(
            forward_kernel,
            "attention_forward",
            [item_spec(2 * video_here), item_spec(cap_rows, D + PAIR), row_spec]
            + [item_spec(lat_rows), row_spec]
            + [part_spec(1, 0, 1), part_spec(0, 0, 2)]
            + [pl.BlockSpec(memory_space=pl.ANY)] * len(before),
            [
                (half_spec(lat_rows), (own, lat_rows, D), BF16),
                (half_spec(keys_here), (own, keys_here, D), BF16),
                (half_spec(keys_here), (own, keys_here, D), BF16),
                (
                    pl.BlockSpec((None, None, 8, 2 * lat_rows), lambda i, s: (i, s[1], 0, 0)),
                    (own, 2, 8, 2 * lat_rows),
                    F32,
                ),
                (half_spec(lat_rows), (own, lat_rows, D), F32),
            ],
            (tok_norm, cap, gain_tok_row, lat, gain_lat_row, part, part) + tuple(before),
            23,
            [
                pltpu.VMEM((keys_here, 2 * lat_rows), F32),
                pltpu.VMEM((keys_here, 2 * lat_rows), BF16),
                pltpu.VMEM((D, 4 * head_width), BF16),
            ],
            {8 + n: n for n in range(len(before))},
            scalars,
        )

    before = forward(near, scalars)
    before, up1, down1, ring_up, ring_down = lax.optimization_barrier(
        (before, up1, down1, ring_up, ring_down)
    )
    far_low = jnp.where(z == 1, down1, jnp.where(z == 2, ring_up, ring_down))
    far_high = jnp.where(z == 1, ring_down, jnp.where(z == 2, up1, ring_up))
    far_mine = jnp.stack([far_low, far_high], axis=1)
    far = jnp.zeros(part_shape, BF16)
    far = lax.dynamic_update_index_in_dim(far, far_mine, core, 0)
    far = lax.dynamic_update_index_in_dim(far, swap_cores(far_mine), 1 - core, 0)
    def both_halves(near, far):
        whole = jnp.zeros((2,) + near.shape, BF16)
        whole = lax.dynamic_update_index_in_dim(whole, near, near_at, 0)
        return lax.dynamic_update_index_in_dim(whole, far, 1 - near_at, 0)

    queries, keys, values, lse, attended = forward(far, scalars_far, before)
    w_out = both_halves(near[1, 1], far[1, 1]).reshape(D, D)
    lat_float = lat.astype(F32)
    mixed_in = (attended * keep[:, None, None]).astype(BF16)
    after_attn = lat_float + dot("ble,ed->bld", mixed_in, w_out)
    mlp_norm = layer_norm(after_attn, gain_mlp).astype(BF16)

    pre_act = dot("bld,df->blf", mlp_norm, up_weight)
    activ, gelu_pull = jax.vjp(gelu_exact, pre_act)
    activ = activ.astype(BF16)
    d_pre = gelu_pull(dot("bld,fd->blf", cot, down_weight))[0].astype(BF16)
    d_mlp_part = dot("blf,df->bld", d_pre, up_weight)
    d_mlp_part, activ, d_pre = lax.optimization_barrier((d_mlp_part, activ, d_pre))
    chunks = head_chunks(d_mlp_part, z, head_count)
    received = head_exchange(chunks, head_count)
    activ, d_pre, received[0] = lax.optimization_barrier((activ, d_pre, received[0]))
    d_mlp_total = head_sum(chunks[0], received)
    grad_down = dot("blf,bld->fd", activ, cot).astype(BF16)
    grad_up = dot("bld,blf->df", mlp_norm, d_pre).astype(BF16)
    near, far, _ = lax.optimization_barrier((near, far, d_mlp_part))
    weights = both_halves(near, far)
    early = jnp.where(core == 0, grad_up, grad_down).astype(F32)
    early = early + swap_cores(jnp.where(core == 0, grad_down, grad_up)).astype(F32)
    d_mlp_norm = gather_head(d_mlp_total, z, head_count)
    activ, _ = lax.optimization_barrier((activ, d_mlp_total))
    growth = head_chunks(dot("blf,fd->bld", activ, down_weight), z, head_count)
    d_mlp_norm = d_mlp_norm.reshape(after_attn.shape)
    growth, d_mlp_norm, weights, early = lax.optimization_barrier(
        (growth, d_mlp_norm, weights, early.astype(BF16))
    )
    early = lax.psum(early, "txt")
    growth_received = head_exchange(growth, head_count)

    late_size = 4 * head_width + 16
    late_size = late_size + -late_size % (32 * txt_count)
    pair_shape = (keys_here, 2 * lat_rows)
    video_grad, other_back, cap_back, latent_grad, late = call(
        backward_kernel,
        "attention_backward",
        [
            item_spec(lat_rows),
            item_spec(keys_here),
            item_spec(keys_here),
            pl.BlockSpec((None, 2, 8, 2 * lat_rows), lambda i, s: (i, 0, 0, 0)),
            item_spec(lat_rows),
            item_spec(lat_rows),
            item_spec(lat_rows),
            item_spec(lat_rows),
            own_spec(video_here),
            item_spec(video_here),
            item_spec(cap_rows, D + PAIR),
            weight_spec(0),
            weight_spec(1),
            row_spec,
            item_spec(2 * video_here),
            weight_spec(2),
            weight_spec(3),
            item_spec(lat_rows),
            row_spec,
            row_spec,
        ],
        [
            (own_spec(video_here), video_tokens.shape, F32),
            item_out(video_here + lat_half, BF16),
            item_out(cap_rows, BF16),
            (own_spec(lat_half), latents.shape, F32),
            (whole_spec(late_size, D), (late_size, D), BF16),
        ],
        (
            queries, keys, values, lse, attended, d_mlp_norm, after_attn, cot, video_tokens,
            video_other, cap, weights, weights, gain_tok_row, tok_norm, weights, weights, lat,
            gain_lat_row, gain_mlp_row,
        ),
        BACK_COST,
        [
            pltpu.VMEM((lat_rows, D), BF16),
            pltpu.VMEM((keys_here, D), BF16),
            pltpu.VMEM((keys_here, D), BF16),
            pltpu.VMEM(pair_shape, F32),
            pltpu.VMEM(pair_shape, F32),
            pltpu.VMEM(pair_shape, BF16),
            pltpu.VMEM(pair_shape, BF16),
            pltpu.VMEM((256, D), F32),
            pltpu.VMEM((8 * PAIR, D), F32),
            pltpu.VMEM((24, D), F32),
            pltpu.VMEM((lat_rows, D), BF16),
            pltpu.VMEM((lat_rows, D), F32),
        ],
    )
    def place(video_grad, latent_grad, part):
        piece = video_here
        return pl.pallas_call(
            place_kernel,
            name="place_rows",
            grid_spec=pltpu.PrefetchScalarGridSpec(
                num_scalar_prefetch=1,
                grid=(own, 1),
                in_specs=[
                    pl.BlockSpec(memory_space=pl.ANY),
                    pl.BlockSpec(memory_space=pl.ANY),
                    pl.BlockSpec((None, piece, D), lambda i, r, s: (i, r, 0)),
                    pl.BlockSpec((None, lat_half, D), lambda i, r, s: (i, video_here // lat_half, 0)),
                ],
                out_specs=[
                    pl.BlockSpec((None, piece, D), lambda i, r, s: ((1 - s[0]) * own + i, r, 0)),
                    pl.BlockSpec((None, lat_half, D), lambda i, r, s: ((1 - s[0]) * own + i, 0, 0)),
                ],
            ),
            out_shape=[
                jax.ShapeDtypeStruct(video_tokens.shape, F32),
                jax.ShapeDtypeStruct(latents.shape, F32),
            ],
            input_output_aliases={1: 0, 2: 1},
            cost_estimate=pl.CostEstimate(
                flops=6 * 10**9, transcendentals=0, bytes_accessed=10**7
            ),
        )(scalars, video_grad, latent_grad, part, part)

    early, growth_received, late = lax.optimization_barrier((early, growth_received, late))
    late_half, late_swapped = reduce_over_cores(late, core)
    other_back, early, _ = lax.optimization_barrier((other_back, early, late_swapped))
    other_here = swap_cores(other_back)
    growth_received, _ = lax.optimization_barrier((growth_received, late_swapped))
    growth = head_sum(growth[0], growth_received)
    early_other = swap_cores(early)
    late_total = reduce_over_group(late_half, place_index, txt_count)
    late_total, growth, early_other, other_here, cap_back = lax.optimization_barrier(
        (late_total, growth, early_other, other_here, cap_back)
    )
    growth = gather_head(growth, z, head_count)
    cap_parts = []
    for step in range(txt_count):
        perm = [(b, a) for a, b in caption_perm(step, 2, txt_count, 2)]
        cap_parts.append(
            lax.ppermute(cap_back[:, step * cap_here : (step + 1) * cap_here], ("vid", "txt"), perm)
        )
    late = gather_places(late_total, place_index, txt_count)
    video_grad, latent_grad = place(video_grad, latent_grad, other_here)
    late, video_grad, latent_grad = lax.optimization_barrier((late, video_grad, latent_grad))
    late = gather_cores(late, core).astype(F32)
    caption_grad = jnp.zeros((txt_count, own, cap_here, D), F32)
    for step, part in enumerate(cap_parts):
        caption_grad = lax.dynamic_update_index_in_dim(
            caption_grad, part.astype(F32), (place_index + step) % txt_count, 0
        )
    caption_grad = caption_grad.reshape(caption_tokens.shape)
    out_mine = (after_attn + growth.reshape(after_attn.shape).astype(F32)).astype(BF16)
    gains = late[4 * head_width :]

    def give_back(values):
        other = swap_cores(values[:, lat_half:].astype(BF16)).astype(values.dtype)
        whole = jnp.zeros((items_here, lat_half, D), values.dtype)
        whole = lax.dynamic_update_slice_in_dim(whole, values[:, :lat_half], core * own, 0)
        return lax.dynamic_update_slice_in_dim(whole, other, (1 - core) * own, 0)

    latents_out = give_back(out_mine)
    kept_count = gains[3, 0].astype(jnp.int32)
    return (
        latents_out,
        latent_grad,
        video_grad,
        caption_grad,
        late[:head_width].T,
        late[head_width : 2 * head_width].T,
        late[2 * head_width : 3 * head_width].T,
        late[3 * head_width : 4 * head_width],
        jnp.where(core == 0, early, early_other).astype(F32),
        jnp.where(core == 0, early_other, early).astype(F32),
        gains[1],
        gains[0],
        gains[2],
        kept_count,
    )


def fits(mesh):
    shape = mesh.shape
    return shape["vid"] == 2 and shape["txt"] == 4 and shape["head"] == 4


def solution(mesh):
    in_specs = (
        P("txt", "vid", None),
        P("txt", "vid", None),
        P("vid", "txt", None),
        P("vid"),
        P("vid", "txt"),
        P("txt"),
        P(),
        P(),
        P(),
        P(None, "head"),
        P(None, "head"),
        P(None, "head"),
        P("head", None),
        P(None, "head"),
        P("head", None),
        P("txt", "vid", None),
    )
    out_specs = (
        P("txt", "vid", None),
        P("txt", "vid", None),
        P("txt", "vid", None),
        P("vid", "txt", None),
        P(None, "head"),
        P(None, "head"),
        P(None, "head"),
        P("head", None),
        P(None, "head"),
        P("head", None),
        P(),
        P(),
        P(),
        P(),
    )
    return jax.shard_map(local if fits(mesh) else local_general, mesh=mesh, in_specs=in_specs, out_specs=out_specs, check_vma=False)
```
